32 devices in a mesh: dp: 4 (over y, core), ctx: 4 (over z), tp: 2 (over x).
Axes of the slice: x: 2, y: 2, z: 4, core: 2. Of those that a mesh axis runs over, the one named last changes fastest.
Arguments:
- tokens: bfloat16 [8, 640, 512], P('dp', 'ctx'), may hold values from -6 to 6
- cotangent: bfloat16 [8, 640, 512], P('dp', 'ctx'), may hold values from -6 to 6
- routes: int32 [8, 640, 2], P('dp', 'ctx'), may hold values from 0 to 15, as said below
- slot_index: int32 [8, 640, 2], P('dp', 'ctx'), may hold values from 0 to 30, as said below
- token_mask: int32 [8, 640], P('dp', 'ctx'), may hold values from 0 to 1, as said below
- image_mask: int32 [8], P('dp'), may hold values from 0 to 1, as said below
- adapter_set: int32 [8], P('dp'), may hold values from 0 to 3
- first_gain: float32 [512], replicated, may hold values from 0.5 to 1.5
- first_shift: float32 [512], replicated, may hold values from -0.5 to 0.5
- second_gain: float32 [512], replicated, may hold values from 0.5 to 1.5
- second_shift: float32 [512], replicated, may hold values from -0.5 to 0.5
- attend_weight: bfloat16 [512, 3, 512], P('dp', None, 'tp'), may hold values from -0.25 to 0.25
- mixing_weight: bfloat16 [512, 512], P('dp', 'tp'), may hold values from -0.75 to 0.75
- router_weight: bfloat16 [512, 16], P('dp'), may hold values from -0.1875 to 0.1875
- expand_weight: bfloat16 [16, 512, 2048], P('dp', None, 'tp'), may hold values from -0.25 to 0.25
- shrink_weight: bfloat16 [16, 2048, 512], P('dp', 'tp'), may hold values from -2 to 2
- attend_down: bfloat16 [4, 512, 16], replicated, may hold values from -0.25 to 0.25
- attend_up: bfloat16 [4, 16, 3, 512], replicated, may hold values from -0.75 to 0.75
- mixing_down: bfloat16 [4, 512, 16], replicated, may hold values from -0.25 to 0.25
- mixing_up: bfloat16 [4, 16, 512], replicated, may hold values from -1.5 to 1.5
- router_down: bfloat16 [4, 512, 16], replicated, may hold values from -0.25 to 0.25
- router_up: bfloat16 [4, 16, 16], replicated, may hold values from -0.75 to 0.75
- expand_down: bfloat16 [4, 16, 512, 16], replicated, may hold values from -0.25 to 0.25
- expand_up: bfloat16 [4, 16, 16, 2048], replicated, may hold values from -0.75 to 0.75
- shrink_down: bfloat16 [4, 16, 2048, 16], replicated, may hold values from -0.125 to 0.125
- shrink_up: bfloat16 [4, 16, 16, 512], replicated, may hold values from -6 to 6
Outputs:
- layer_out: bfloat16 [8, 640, 512], P('dp', 'ctx')
- tokens_grad: bfloat16 [8, 640, 512], P('dp', 'ctx')
- grad_attend_down: float32 [4, 512, 16], replicated
- grad_attend_up: float32 [4, 16, 3, 512], replicated
- grad_mixing_down: float32 [4, 512, 16], replicated
- grad_mixing_up: float32 [4, 16, 512], replicated
- grad_router_down: float32 [4, 512, 16], replicated
- grad_router_up: float32 [4, 16, 16], replicated
- grad_expand_down: float32 [4, 16, 512, 16], replicated
- grad_expand_up: float32 [4, 16, 16, 2048], replicated
- grad_shrink_down: float32 [4, 16, 2048, 16], replicated
- grad_shrink_up: float32 [4, 16, 16, 512], replicated
The draws below stay inside these ranges and needn't reach their ends.
Inputs may be any that keep to these rules, and one draw needn't show every extreme that they name: `routes`: each token names two different experts. In every image block of 160 positions the first 31 tokens name one common expert first. `slot_index`: A pair's value is the number of earlier pairs (positions in order, a token's first expert before its second) of the same image block that name the same expert and belong to live tokens; pairs of tokens that are not live and pairs counted 30 or more hold 30, which means dropped. `token_mask`: the real tokens of each image are a prefix of more than half of its 640 positions. `image_mask`: the first image is real, and at least one image is a pad.
All inputs are finite; a program needn't handle non-finite values.
Results may differ from the reference program's by a relative error of at most 0.022.
Values may be sent and summed in bfloat16 or wider, within the bound.
A program may use at most 192 MiB of HBM per device.

```python
import math
import jax
import jax.numpy as jnp
from jax import lax

D = 512
HEADS = 8
HD = 64
FF = 2048
EXPERTS = 16
TOP = 2
RANK = 16
SETS = 4
TOK_CTX = 160
CAP = 30
SEQ = 640
IMAGES = 8
N_CTX = 4


def layout_draw(key):
    seeded = jax.random.fold_in(key, 101)
    streams = jax.random.split(seeded, 6)
    block_count = SEQ // TOK_CTX
    primary = jax.random.randint(streams[0], (IMAGES, SEQ), 0, EXPERTS)
    offsets = jax.random.randint(streams[1], (IMAGES, SEQ), 1, EXPERTS)
    forced = jax.random.randint(streams[2], (IMAGES, block_count), 0, EXPERTS)
    places = jnp.arange(SEQ)
    forced_tokens = jnp.repeat(forced, TOK_CTX, axis=1)
    primary = jnp.where((places % TOK_CTX)[None, :] <= CAP, forced_tokens, primary)
    secondary = (primary + offsets) % EXPERTS
    route_ids = jnp.stack([primary, secondary], axis=-1).astype(jnp.int32)
    lengths = jax.random.randint(streams[3], (IMAGES, 1), SEQ // 2 + 1, SEQ + 1)
    token_live = (places[None, :] < lengths).astype(jnp.int32)
    image_live = jax.random.randint(streams[4], (IMAGES,), 0, 2).astype(jnp.int32)
    pad_image = jax.random.randint(streams[5], (), 1, IMAGES)
    image_live = jnp.where(jnp.arange(IMAGES) == pad_image, 0, image_live)
    image_live = image_live.at[0].set(1).astype(jnp.int32)
    both_live = token_live * image_live[:, None]
    pair_ids = route_ids.reshape(IMAGES, block_count, TOK_CTX * TOP)
    pair_live = jnp.repeat(both_live, TOP, axis=1).reshape(IMAGES, block_count, TOK_CTX * TOP)
    matches = (pair_ids[..., None] == jnp.arange(EXPERTS)).astype(jnp.int32)
    counted = matches * pair_live[..., None]
    earlier = jnp.cumsum(counted, axis=2) - counted
    ranks = jnp.sum(earlier * matches, axis=-1)
    slot_ids = jnp.where((pair_live > 0) & (ranks < CAP), ranks, CAP)
    slot_ids = slot_ids.reshape(IMAGES, SEQ, TOP).astype(jnp.int32)
    return (route_ids, slot_ids, token_live, image_live)


def draw_routes(key, part):
    return layout_draw(key)[0]


def draw_slot_index(key, part):
    return layout_draw(key)[1]


def draw_token_mask(key, part):
    return layout_draw(key)[2]


def draw_image_mask(key, part):
    return layout_draw(key)[3]


def touch_ends(entries, rng, least, top_value):
    dims = entries.shape
    index_at = [jax.random.randint(jax.random.fold_in(rng, axis), (), 0, dims[axis]) for axis in range(len(dims))]
    entries = entries.at[tuple(index_at)].set(least)
    longest = dims.index(max(dims))
    index_at[longest] = (index_at[longest] + 1) % dims[longest]
    return entries.at[tuple(index_at)].set(top_value)


def block_levels(own_key, extent, cuts, smallest, largest):
    gain, own = 1.0, jax.random.fold_in(own_key, 6)
    for dim, blocks in cuts:
        heights = jnp.exp(jax.random.uniform(jax.random.fold_in(own, dim), (blocks,), jnp.float32, smallest / len(cuts), largest / len(cuts)))
        gain = gain * jnp.repeat(heights, extent[dim] // blocks).reshape([-1 if axis == dim else 1 for axis in range(len(extent))])
    return gain


def gaussian(own_key, shape, scale, most, cuts=(), held_as=jnp.bfloat16):
    loudness = block_levels(own_key, shape, cuts, -0.22, 0.18) if cuts else 1.0
    array = jax.random.normal(own_key, shape, jnp.float32) * scale * loudness
    return jnp.minimum(jnp.maximum(array, -most), most).astype(held_as)


def setup_inputs(seed: int = 0) -> dict:
    key_list = jax.random.split(jax.random.key(seed), 27)
    return {
        "tokens": gaussian(key_list[0], (IMAGES, SEQ, D), 1.0, 6.0, ((0, 4), (1, 4))),
        "cotangent": gaussian(key_list[1], (IMAGES, SEQ, D), 1.0, 6.0, ((0, 4), (1, 4))),
        "routes": draw_routes(jax.random.fold_in(key_list[26], 71), 0),
        "slot_index": draw_slot_index(jax.random.fold_in(key_list[26], 71), 0),
        "token_mask": draw_token_mask(jax.random.fold_in(key_list[26], 71), 0),
        "image_mask": draw_image_mask(jax.random.fold_in(key_list[26], 71), 0),
        "adapter_set": touch_ends(jax.random.randint(key_list[6], (IMAGES,), 0, SETS), jax.random.fold_in(key_list[6], 1), 0, SETS - 1).astype(jnp.int32),
        "first_gain": jnp.clip(1.0 + 0.1 * jax.random.normal(key_list[7], (D,), jnp.float32), 0.5, 1.5),
        "first_shift": gaussian(key_list[8], (D,), 0.1, 0.5, (), jnp.float32),
        "second_gain": jnp.clip(1.0 + 0.1 * jax.random.normal(key_list[9], (D,), jnp.float32), 0.5, 1.5),
        "second_shift": gaussian(key_list[10], (D,), 0.1, 0.5, (), jnp.float32),
        "attend_weight": gaussian(key_list[11], (D, 3, HEADS * HD), D ** -0.5, 0.25, ((0, 4), (2, 2))),
        "mixing_weight": gaussian(key_list[12], (D, HEADS * HD), HD ** -0.5, 0.75, ((0, 4), (1, 2))),
        "router_weight": gaussian(key_list[13], (D, EXPERTS), (2 * D) ** -0.5, 0.1875, ((0, 4),)),
        "expand_weight": gaussian(key_list[14], (EXPERTS, D, FF), D ** -0.5, 0.25, ((0, 4), (2, 2))),
        "shrink_weight": gaussian(key_list[15], (EXPERTS, FF, D), (max(FF // 256, 1)) ** -0.5, 2.0, ((0, 4), (1, 2))),
        "attend_down": gaussian(key_list[16], (SETS, D, RANK), D ** -0.5, 0.25),
        "attend_up": gaussian(key_list[17], (SETS, RANK, 3, HEADS * HD), (4 * RANK) ** -0.5, 0.75),
        "mixing_down": gaussian(key_list[18], (SETS, HEADS * HD, RANK), (HEADS * HD) ** -0.5, 0.25),
        "mixing_up": gaussian(key_list[19], (SETS, RANK, D), RANK ** -0.5, 1.5),
        "router_down": gaussian(key_list[20], (SETS, D, RANK), D ** -0.5, 0.25),
        "router_up": gaussian(key_list[21], (SETS, RANK, EXPERTS), (4 * RANK) ** -0.5, 0.75),
        "expand_down": gaussian(key_list[22], (SETS, EXPERTS, D, RANK), D ** -0.5, 0.25),
        "expand_up": gaussian(key_list[23], (SETS, EXPERTS, RANK, FF), (4 * RANK) ** -0.5, 0.75),
        "shrink_down": gaussian(key_list[24], (SETS, EXPERTS, FF, RANK), FF ** -0.5, 0.125),
        "shrink_up": gaussian(key_list[25], (SETS, EXPERTS, RANK, D), 1 ** -0.5, 6.0),
    }


HIGH = lax.Precision.HIGHEST
EPSILON = 1e-06
MASKED = -1e+30

@jax.custom_vjp
def low(v):
    return lax.optimization_barrier(v.astype(jnp.bfloat16)).astype(jnp.float32)

@jax.custom_vjp
def low_back(v):
    return v

def low_keep(v):
    return (low(v), None)

def low_pass(kept, grad):
    return (grad,)

def back_keep(v):
    return (v, None)

def back_low(kept, grad):
    return (low(grad),)
low.defvjp(low_keep, low_pass)
low_back.defvjp(back_keep, back_low)

def matmul(left_side, right_side):
    return jnp.dot(left_side, right_side, precision=HIGH)

def normalize(values, gain_row, shift_row):
    centred = values - lax.optimization_barrier(jnp.mean(values, axis=-1, keepdims=True))
    spread = lax.optimization_barrier(jnp.mean(centred * centred, axis=-1, keepdims=True))
    return centred * lax.rsqrt(spread + EPSILON) * gain_row + shift_row

def choose(values, set_rows):
    return values * jnp.repeat(set_rows, RANK, axis=-1)

def softmax_rows(values):
    row_top = lax.optimization_barrier(jnp.max(values, axis=-1, keepdims=True))
    powers = jnp.exp(values - row_top)
    return powers / lax.optimization_barrier(jnp.sum(powers, axis=-1, keepdims=True))

def prepare(adapters):
    attend_a, attend_b, mixing_a, mixing_b, router_a, router_b, expand_a, expand_b, shrink_a, shrink_b = adapters
    set_width = SETS * RANK
    return (jnp.transpose(attend_a, (1, 0, 2)).reshape(D, set_width), attend_b.reshape(set_width, 3 * HEADS * HD), jnp.transpose(mixing_a, (1, 0, 2)).reshape(HEADS * HD, set_width), mixing_b.reshape(set_width, D), jnp.transpose(router_a, (1, 0, 2)).reshape(D, set_width), router_b.reshape(set_width, EXPERTS), jnp.transpose(expand_a, (1, 2, 0, 3)).reshape(EXPERTS, D, set_width), jnp.transpose(expand_b, (1, 0, 2, 3)).reshape(EXPERTS, set_width, FF), jnp.transpose(shrink_a, (1, 2, 0, 3)).reshape(EXPERTS, FF, set_width), jnp.transpose(shrink_b, (1, 0, 2, 3)).reshape(EXPERTS, set_width, D))

def expert_rows(set_rows):

    def apply_rows(mapped):
        rows_in, up_w, down_w, up_a, up_b, down_a, down_b = mapped
        first_low = low_back(low(choose(matmul(rows_in, up_a), set_rows)))
        before = low_back(matmul(rows_in, up_w) + matmul(first_low, up_b))
        active = low(jax.nn.gelu(before, approximate=False))
        second_low = low_back(low(choose(matmul(active, down_a), set_rows)))
        return low_back(low(matmul(active, down_w) + matmul(second_low, down_b)))
    return jax.checkpoint(apply_rows)

def group_layer(block_data, frozen, prepared):
    inputs, route_ids, slot_ids, live_ids, set_ids = block_data
    gain_one, shift_one, gain_two, shift_two, attend_w, mixing_w, router_w, expand_w, shrink_w = frozen
    attend_a, attend_b, mixing_a, mixing_b, router_a, router_b, expand_a, expand_b, shrink_a, shrink_b = prepared
    image_count = inputs.shape[0]
    token_count = image_count * SEQ
    flat_in = inputs.reshape(token_count, D)
    set_hot = (set_ids[:, None] == jnp.arange(SETS).astype(jnp.int32)[None, :]).astype(jnp.float32)
    token_sets = jnp.repeat(set_hot, SEQ, axis=0)
    normed_one = low(normalize(flat_in, gain_one, shift_one))
    attend_lift = low_back(low(choose(matmul(normed_one, attend_a), token_sets)))
    joined_rows = matmul(normed_one, attend_w.reshape(D, 3 * HEADS * HD)) + matmul(attend_lift, attend_b)
    joined_rows = joined_rows.reshape(image_count, SEQ, 3, HEADS, HD)
    queries = low_back(low(joined_rows[:, :, 0]))
    keyset = low_back(low(joined_rows[:, :, 1]))
    valueset = low_back(low(joined_rows[:, :, 2]))
    score_scale = HD ** (-0.5)
    scores = low_back(jnp.einsum('iqhd,ikhd->ihqk', queries, keyset, precision=HIGH) * score_scale)
    scores = jnp.where(live_ids[:, None, None, :] > 0, scores, MASKED)
    weights = low(softmax_rows(scores))
    mixed_heads = jnp.einsum('ihqk,ikhd->iqhd', weights, valueset, precision=HIGH)
    head_mix = low_back(low(mixed_heads.reshape(token_count, HEADS * HD)))
    mixing_lift = low_back(low(choose(matmul(head_mix, mixing_a), token_sets)))
    attended = low_back(matmul(head_mix, mixing_w.T) + matmul(mixing_lift, mixing_b))
    hidden = flat_in + attended
    expert_in = low(normalize(hidden, gain_two, shift_two))
    router_lift = low_back(low(choose(matmul(expert_in, router_a), token_sets)))
    logits = low_back(matmul(expert_in, router_w) + matmul(router_lift, router_b))
    gate_probs = softmax_rows(logits)
    flat_routes = route_ids.reshape(token_count, TOP)
    route_hot = (flat_routes[..., None] == jnp.arange(EXPERTS).astype(jnp.int32)).astype(jnp.float32)
    gate_values = lax.optimization_barrier(jnp.sum(gate_probs[:, None, :] * route_hot, axis=-1))
    block_rows = image_count * N_CTX * CAP
    token_place = jnp.arange(token_count).astype(jnp.int32)
    block_index = token_place // SEQ * N_CTX + token_place % SEQ // TOK_CTX
    flat_slots = slot_ids.reshape(token_count, TOP)
    kept_pairs = flat_slots < CAP
    target = jnp.where(kept_pairs, flat_routes * block_rows + block_index[:, None] * CAP + flat_slots, 0)
    target = target.reshape(-1).astype(jnp.int32)
    kept_float = kept_pairs.reshape(-1, 1).astype(jnp.float32)
    sent_rows = low_back(jnp.repeat(expert_in, TOP, axis=0)) * kept_float
    buffer = jnp.zeros((EXPERTS * block_rows, D), jnp.float32).at[target].add(sent_rows)
    row_sets = jnp.repeat(set_hot, N_CTX * CAP, axis=0)
    expert_out = lax.map(expert_rows(row_sets), (buffer.reshape(EXPERTS, block_rows, D), expand_w, shrink_w, expand_a, expand_b, shrink_a, shrink_b))
    returned = expert_out.reshape(EXPERTS * block_rows, D)[target] * kept_float
    returned = returned.reshape(token_count, TOP, D)
    output = hidden + lax.optimization_barrier(jnp.sum(gate_values[..., None] * returned, axis=1))
    return output.reshape(image_count, SEQ, D)

def reference(tokens, cotangent, routes, slot_index, token_mask, image_mask, adapter_set, first_gain, first_shift, second_gain, second_shift, attend_weight, mixing_weight, router_weight, expand_weight, shrink_weight, attend_down, attend_up, mixing_down, mixing_up, router_down, router_up, expand_down, expand_up, shrink_down, shrink_up):
    frozen = tuple((member.astype(jnp.float32) for member in (first_gain, first_shift, second_gain, second_shift, attend_weight, mixing_weight, router_weight, expand_weight, shrink_weight)))
    live_ids = (token_mask * image_mask[:, None]).astype(jnp.int32)
    group_size = math.gcd(IMAGES, max(1, 4096 // SEQ))
    group_count = IMAGES // group_size

    def shaped(values):
        return values.reshape((group_count, group_size) + values.shape[1:])

    def forward(inputs, *adapters):
        prepared = prepare(adapters)

        def one_group(block_data):
            return group_layer(block_data, frozen, prepared)
        stacked = lax.map(jax.checkpoint(one_group), (shaped(inputs), shaped(routes), shaped(slot_index), shaped(live_ids), shaped(adapter_set)))
        return stacked.reshape(IMAGES, SEQ, D)
    adapter_list = tuple((member.astype(jnp.float32) for member in (attend_down, attend_up, mixing_down, mixing_up, router_down, router_up, expand_down, expand_up, shrink_down, shrink_up)))
    output, pullback = jax.vjp(forward, tokens.astype(jnp.float32), *adapter_list)
    weighted = cotangent.astype(jnp.float32) * live_ids[..., None].astype(jnp.float32)
    gradients = pullback(weighted)
    return (output.astype(jnp.bfloat16), gradients[0].astype(jnp.bfloat16), gradients[1], gradients[2], gradients[3], gradients[4], gradients[5], gradients[6], gradients[7], gradients[8], gradients[9], gradients[10])
```

```python
import functools

import jax
import jax.numpy as jnp
from jax import lax
from jax.experimental import pallas as pl
from jax.experimental.pallas import tpu as pltpu
from jax.sharding import PartitionSpec as P

D = 512
HEADS = 8
HD = 64
FF = 2048
EXPERTS = 16
TOP = 2
RANK = 16
SETS = 4
CAP = 30
SLOTS = 32
WIDTH = SETS * RANK

EPSILON = 1e-06
MASKED = -1e30
SQRT_HALF = 0.7071067811865476
INV_ROOT_TWO_PI = 0.3989422804014327
F32 = jnp.float32
BF16 = jnp.bfloat16
MESH = pl.DeviceIdType.MESH
ANY = pl.BlockSpec(memory_space=pl.ANY)
IN_VMEM = pl.BlockSpec(memory_space=pltpu.VMEM)


def matmul(left_side, right_side):
    return jnp.dot(left_side, right_side, preferred_element_type=F32)


def inner_rows(left_side, right_side):
    return lax.dot_general(
        left_side, right_side, (((0,), (0,)), ((), ())), preferred_element_type=F32
    )


def times_transposed(left_side, right_side):
    return lax.dot_general(
        left_side, right_side, (((1,), (1,)), ((), ())), preferred_element_type=F32
    )


def normalize(values, gain_row, shift_row):
    centred = values - jnp.mean(values, axis=-1, keepdims=True)
    spread = jnp.mean(centred * centred, axis=-1, keepdims=True)
    factor = lax.rsqrt(spread + EPSILON)
    normed = centred * factor
    return (normed * gain_row + shift_row, normed, factor)


def normalize_back(grad_out, normed, factor, gain_row):
    scaled = grad_out * gain_row
    return factor * (
        scaled
        - jnp.mean(scaled, axis=-1, keepdims=True)
        - normed * jnp.mean(scaled * normed, axis=-1, keepdims=True)
    )


class Wire:
    def __init__(self, send, recv, local=None):
        self.send, self.recv, self.local = send, recv, local
        self.used = self.used_local = 0

    def copy(self, src, dst, device):
        k = self.used
        self.used += 1
        return pltpu.make_async_remote_copy(
            src_ref=src,
            dst_ref=dst,
            send_sem=self.send.at[k],
            recv_sem=self.recv.at[k],
            device_id=device,
            device_id_type=MESH,
        )

    def near(self, src, dst):
        k = self.used_local
        self.used_local += 1
        return pltpu.make_async_copy(src, dst, self.local.at[k])


class Place:
    def __init__(self, sizes):
        self.dp_size, self.ctx_size, self.tp_size = sizes
        self.chips = self.dp_size // 2
        self.dp = lax.axis_index("dp")
        self.ctx = lax.axis_index("ctx")
        self.tp = lax.axis_index("tp")
        self.chip = lax.div(self.dp, 2)
        self.core = lax.rem(self.dp, 2)
        self.sibling = self.chip * 2 + (1 - self.core)

    def ahead(self, i, j):
        return (
            lax.rem(self.chip + i, self.chips) * 2 + self.core,
            lax.rem(self.tp + j, self.tp_size),
        )

    def behind(self, i, j):
        return self.ahead(self.chips - i, self.tp_size - j)

    def offsets(self, over_tp=True):
        return [
            (i, j)
            for i in range(self.chips)
            for j in range(self.tp_size if over_tp else 1)
            if i or j
        ]

    def greet(self, with_ctx):
        barrier = pltpu.get_barrier_semaphore()
        count = 0
        for i, j in self.offsets():
            dp, tp = self.ahead(i, j)
            pl.semaphore_signal(
                barrier, inc=1, device_id={"dp": dp, "tp": tp}, device_id_type=MESH
            )
            count += 1
        pl.semaphore_signal(
            barrier, inc=1, device_id={"dp": self.sibling}, device_id_type=MESH
        )
        count += 1
        if with_ctx:
            for i in range(1, self.ctx_size):
                pl.semaphore_signal(
                    barrier,
                    inc=1,
                    device_id={"ctx": lax.rem(self.ctx + i, self.ctx_size)},
                    device_id_type=MESH,
                )
                count += 1
        pl.semaphore_wait(barrier, count)


def gather_plane_start(place, wire, items):
    flights, done = [], []
    for source, slot, over_tp in items:
        for i, j in place.offsets(over_tp):
            dp, tp = place.ahead(i, j)
            copy = wire.copy(source, slot(place.dp, place.tp), {"dp": dp, "tp": tp})
            copy.start()
            flights.append((copy, slot(*place.behind(i, j))))
    for source, slot, _ in items:
        copy = wire.copy(source, slot(place.dp, place.tp), {"dp": place.sibling})
        copy.start()
        done.append(copy)
        copy = wire.near(source, slot(place.dp, place.tp))
        copy.start()
        done.append(copy)
    return flights, done


def gather_plane_end(place, wire, flights, done):
    for copy, got in flights:
        copy.wait_recv()
        onward = wire.copy(got, got, {"dp": place.sibling})
        onward.start()
        done.append(onward)
    for copy, _ in flights:
        copy.wait_send()
    for copy in done:
        copy.wait()


def plane_copies(place, flags):
    sent = sum(len(place_offsets(place, f)) for f in flags)
    return sent, len(flags)


def place_offsets(sizes, over_tp):
    chips = sizes[0] // 2
    return chips * (sizes[2] if over_tp else 1) - 1


def semaphores(remote, near):
    return [
        pltpu.SemaphoreType.DMA((remote,)),
        pltpu.SemaphoreType.DMA((remote,)),
        pltpu.SemaphoreType.DMA((near,)),
    ]


def comm_params(number):
    return pltpu.CompilerParams(
        collective_id=number, has_side_effects=True, vmem_limit_bytes=48 << 20
    )


def gather_ctx_start(place, wire, source, slot):
    flights = []
    for i in range(1, place.ctx_size):
        copy = wire.copy(
            source,
            slot(place.ctx, place.tp),
            {"ctx": lax.rem(place.ctx + i, place.ctx_size)},
        )
        copy.start()
        flights.append(
            (copy, slot(lax.rem(place.ctx - i + place.ctx_size, place.ctx_size), place.tp))
        )
    return flights


def start_kernel(
    sizes, tokens, weights, mixing, router, cotangent, ints,
    tokens_all, weights_all, mixing_all, router_all, cotangent_all, ints_all, ctx_ints,
    send, recv, local,
):
    place = Place(sizes)
    wire = Wire(send, recv, local)
    place.greet(True)
    rows, lanes = mixing.shape
    half = tokens.shape[1] // place.tp_size
    other_tp = lax.rem(place.tp + 1, 2)

    def token_slot(ctx, tp):
        start = pl.multiple_of(ctx * tokens.shape[1] + tp * half, 16)
        return tokens_all.at[:, pl.ds(start, half), :]

    def at_rows(dp):
        return pl.ds(pl.multiple_of(dp * rows, 16), rows)

    def at_lanes(tp):
        return pl.ds(pl.multiple_of(tp * lanes, 128), lanes)

    mine = tokens.at[:, pl.ds(pl.multiple_of(place.tp * half, 16), half), :]
    token_flights = gather_ctx_start(place, wire, mine, token_slot)
    int_flights = gather_ctx_start(place, wire, ints, lambda ctx, tp: ctx_ints.at[ctx])
    flights, done = gather_plane_start(
        place,
        wire,
        [
            (weights, lambda dp, tp: weights_all.at[:, at_rows(dp), at_lanes(tp)], True),
            (mixing, lambda dp, tp: mixing_all.at[at_rows(dp), at_lanes(tp)], True),
            (ints, lambda dp, tp: ints_all.at[pl.ds(dp * 2, 2)], False),
            (router, lambda dp, tp: router_all.at[dp], False),
            (cotangent, lambda dp, tp: cotangent_all.at[pl.ds(dp * 2, 2)], False),
        ],
    )
    whole = tokens_all.at[:, pl.ds(pl.multiple_of(place.ctx * tokens.shape[1], 16), tokens.shape[1]), :]
    for src, dst in ((tokens, whole), (ints, ctx_ints.at[place.ctx])):
        copy = wire.near(src, dst)
        copy.start()
        done.append(copy)
    for copy, got in token_flights:
        copy.wait_recv()
        onward = wire.copy(got, got, {"tp": other_tp})
        onward.start()
        done.append(onward)
    for copy, _ in int_flights:
        copy.wait()
    for copy, _ in token_flights:
        copy.wait_send()
    gather_plane_end(place, wire, flights, done)


def start_gather(sizes, tokens, weights, mixing, router, cotangent, ints):
    dp, ctx, tp = sizes
    rows, lanes = mixing.shape
    images, block = tokens.shape[:2]
    full, part = place_offsets(sizes, True), place_offsets(sizes, False)
    remote = 3 * (ctx - 1) + 4 * full + 6 * part + 5
    return pl.pallas_call(
        functools.partial(start_kernel, sizes),
        out_shape=(
            jax.ShapeDtypeStruct((images, ctx * block, D), BF16),
            jax.ShapeDtypeStruct((3, dp * rows, tp * lanes), BF16),
            jax.ShapeDtypeStruct((dp * rows, tp * lanes), BF16),
            jax.ShapeDtypeStruct((dp,) + router.shape, BF16),
            jax.ShapeDtypeStruct((dp * images, block, D), BF16),
            jax.ShapeDtypeStruct((dp * images,) + ints.shape[1:], jnp.int32),
            jax.ShapeDtypeStruct((ctx,) + ints.shape, jnp.int32),
        ),
        in_specs=[ANY] * 6,
        out_specs=(ANY,) * 7,
        scratch_shapes=semaphores(remote, 7),
        compiler_params=comm_params(1),
    )(tokens, weights, mixing, router, cotangent, ints)


def expert_in_kernel(sizes, own, gathered, send, recv, local):
    place = Place(sizes)
    wire = Wire(send, recv, local)
    place.greet(False)
    half = own.shape[1]

    def slot(dp, tp):
        return gathered.at[pl.ds(dp * 2, 2), pl.ds(pl.multiple_of(tp * half, 16), half), :]

    flights, done = gather_plane_start(place, wire, [(own, slot, True)])
    gather_plane_end(place, wire, flights, done)


def expert_in_gather(sizes, own):
    dp, ctx, tp = sizes
    images, half = own.shape[:2]
    return pl.pallas_call(
        functools.partial(expert_in_kernel, sizes),
        out_shape=jax.ShapeDtypeStruct((dp * images, tp * half, D), BF16),
        in_specs=[ANY],
        out_specs=ANY,
        scratch_shapes=semaphores(2 * place_offsets(sizes, True) + 1, 1),
        compiler_params=comm_params(2),
    )(own)


def return_kernel(sizes, partial, received, from_sibling, paired, send, recv, local):
    place = Place(sizes)
    wire = Wire(send, recv, local)
    place.greet(False)
    swap = wire.copy(partial.at[1 - place.core], from_sibling, {"dp": place.sibling})
    swap.start()
    swap.wait_recv()
    copies = []
    for i, j in place.offsets() + [(0, 0)]:
        dp, tp = place.ahead(i, j)
        chip = lax.div(dp, 2)
        paired[chip, tp] = (
            partial[place.core, chip, tp].astype(F32) + from_sibling[chip, tp].astype(F32)
        ).astype(BF16)
        index = i * place.tp_size + j
        if index:
            copy = wire.copy(paired.at[chip, tp], received.at[index], {"dp": dp, "tp": tp})
        else:
            copy = wire.near(paired.at[chip, tp], received.at[0])
        copy.start()
        copies.append(copy)
    for copy in copies:
        copy.wait()
    swap.wait_send()


def return_rows(sizes, partial):
    dp, ctx, tp = sizes
    count, lanes = partial.shape[3:]
    chips = dp // 2
    return pl.pallas_call(
        functools.partial(return_kernel, sizes),
        out_shape=jax.ShapeDtypeStruct((chips * tp, count, lanes), BF16),
        in_specs=[IN_VMEM],
        out_specs=ANY,
        scratch_shapes=[
            pltpu.VMEM((chips, tp, count, lanes), BF16),
            pltpu.VMEM((chips, tp, count, lanes), BF16),
        ]
        + semaphores(chips * tp, 1),
        compiler_params=comm_params(3),
    )(partial)


def heads_kernel(sizes, own, gathered, send, recv, local):
    place = Place(sizes)
    wire = Wire(send, recv, local)
    place.greet(True)
    half = own.shape[1]
    other_tp = lax.rem(place.tp + 1, 2)

    def slot(ctx, tp):
        start = pl.multiple_of((ctx * place.tp_size + tp) * half, 16)
        return gathered.at[:, pl.ds(start, half), :]

    flights = gather_ctx_start(place, wire, own, slot)
    swap = wire.copy(own, slot(place.ctx, place.tp), {"tp": other_tp})
    swap.start()
    here = wire.near(own, slot(place.ctx, place.tp))
    here.start()
    done = [swap, here]
    for copy, got in flights:
        copy.wait_recv()
        onward = wire.copy(got, got, {"tp": other_tp})
        onward.start()
        done.append(onward)
    for copy, _ in flights:
        copy.wait_send()
    for copy in done:
        copy.wait()


def heads_gather(sizes, own):
    dp, ctx, tp = sizes
    images, half, lanes = own.shape
    return pl.pallas_call(
        functools.partial(heads_kernel, sizes),
        out_shape=jax.ShapeDtypeStruct((images, ctx * tp * half, lanes), BF16),
        in_specs=[ANY],
        out_specs=ANY,
        scratch_shapes=semaphores(2 * (ctx - 1) + 1, 1),
        compiler_params=comm_params(4),
    )(own)


def add_rounded(*parts):
    total = parts[0].astype(F32)
    for part in parts[1:]:
        total = total + part.astype(F32)
    return total.astype(BF16)


def finish_kernel(
    sizes, first, second, small, out_own, grad_own,
    first_all, second_all, small_all, out_all, grad_all,
    second_got, small_got, second_sum, small_sum,
    first_end, second_end, small_end,
    first_mid, second_mid, small_mid,
    first_stage, second_stage, small_stage,
    first_final, second_final, small_final,
    send, recv, local,
):
    place = Place(sizes)
    wire = Wire(send, recv, local)
    plane = place.dp_size * place.tp_size
    me = place.dp * place.tp_size + place.tp
    is_mid = jnp.logical_and(place.ctx >= 1, place.ctx <= 2)
    is_end = jnp.logical_not(is_mid)
    inner = lax.div(place.ctx, 2)
    outer_half = 1 - inner
    partner = jnp.where(is_mid, inner * 3, 1 + inner)
    other_mid = 2 - inner
    other_tp = lax.rem(place.tp + 1, 2)
    half = out_own.shape[1]
    experts = first.shape[0]

    barrier = pltpu.get_barrier_semaphore()
    peers = []
    for k in range(1, plane):
        peer = lax.rem(me + k, plane)
        peers.append((lax.div(peer, place.tp_size), lax.rem(peer, place.tp_size)))
        pl.semaphore_signal(
            barrier, inc=1, device_id={"dp": peers[-1][0], "tp": peers[-1][1]}, device_id_type=MESH
        )
    pl.semaphore_signal(barrier, inc=1, device_id={"ctx": partner}, device_id_type=MESH)

    @pl.when(is_mid)
    def _():
        pl.semaphore_signal(barrier, inc=1, device_id={"ctx": other_mid}, device_id_type=MESH)

    pl.semaphore_wait(barrier, plane + jnp.where(is_mid, 1, 0))

    swap = wire.copy(second.at[other_tp], second_got, {"tp": other_tp})
    swap.start()
    spread = []
    for k, (dp, tp) in enumerate(peers):
        copy = wire.copy(
            small.at[dp * place.tp_size + tp], small_got.at[k], {"dp": dp, "tp": tp}
        )
        copy.start()
        spread.append(copy)
    outs = []
    for own, gathered in ((out_own, out_all), (grad_own, grad_all)):
        spot = gathered.at[:, pl.ds(pl.multiple_of(place.tp * half, 16), half), :]
        outs.append(wire.copy(own, spot, {"tp": other_tp}))
        outs.append(wire.near(own, spot))

    chunks = [
        (
            first.at[e], first_end.at[e], first_mid.at[e], first_stage.at[e],
            first_final.at[e], functools.partial(lambda e, dp, tp: first_all.at[dp, tp, e], e),
        )
        for e in range(experts)
    ]
    chunks.append(
        (second_sum, second_end, second_mid, second_stage, second_final,
         lambda dp, tp: second_all.at[dp, tp])
    )
    chunks.append(
        (small_sum, small_end, small_mid, small_stage, small_final,
         lambda dp, tp: small_all.at[dp, tp])
    )

    flows = []
    for mine, end, mid, stage, final, slot in chunks:
        flows.append(
            dict(
                outer=wire.copy(mine.at[outer_half], end.at[outer_half], {"ctx": partner}),
                inner=wire.copy(mine.at[inner], end.at[inner], {"ctx": partner}),
                cross=wire.copy(stage, mid, {"ctx": other_mid}),
                back=wire.copy(final.at[inner], final.at[inner], {"ctx": partner}),
                share=wire.copy(final.at[inner], final.at[inner], {"ctx": other_mid}),
                pass_on=wire.copy(final.at[outer_half], final.at[outer_half], {"ctx": partner}),
            )
        )

    def send_ends(k):
        @pl.when(is_end)
        def _():
            flows[k]["outer"].start()
            flows[k]["inner"].start()

    for k in range(experts):
        send_ends(k)
    swap.wait()
    second_sum[...] = add_rounded(second[place.tp], second_got[...])
    send_ends(experts)
    for copy in spread:
        copy.wait()
    total = small[me].astype(F32)
    for k in range(plane - 1):
        total = total + small_got[k].astype(F32)
    small_sum[...] = total.astype(BF16).reshape(small_sum.shape)
    send_ends(experts + 1)

    def mid_first(k):
        mine, end, mid, stage, final, slot = chunks[k]

        @pl.when(is_mid)
        def _():
            flows[k]["outer"].wait_recv()
            stage[...] = add_rounded(mine[outer_half], end[outer_half])
            flows[k]["cross"].start()

    def mid_second(k):
        mine, end, mid, stage, final, slot = chunks[k]

        @pl.when(is_mid)
        def _():
            flows[k]["inner"].wait_recv()
            flows[k]["cross"].wait_recv()
            final[inner] = add_rounded(mine[inner], end[inner], mid[...])
            flows[k]["share"].start()
            flows[k]["back"].start()

    def settle(k):
        @pl.when(is_mid)
        def _():
            flows[k]["share"].wait_recv()
            flows[k]["pass_on"].start()

        @pl.when(is_end)
        def _():
            flows[k]["back"].wait_recv()
            flows[k]["pass_on"].wait_recv()

    squared = place.chips == 2 and place.tp_size == 2
    done = []
    plane_flights = []

    def plane_send(k):
        final, slot = chunks[k][4], chunks[k][5]
        spot = slot(place.dp, place.tp)
        flights = []
        for i, j in place.offsets():
            if squared and i and j:
                continue
            dp, tp = place.ahead(i, j)
            copy = wire.copy(final, spot, {"dp": dp, "tp": tp})
            copy.start()
            flights.append((copy, i, j))
        for copy in (wire.copy(final, spot, {"dp": place.sibling}), wire.near(final, spot)):
            copy.start()
            done.append(copy)
        plane_flights.append(flights)

    def to_sibling(ref):
        copy = wire.copy(ref, ref, {"dp": place.sibling})
        copy.start()
        done.append(copy)

    diagonals = []

    def plane_forward(k):
        slot = chunks[k][5]
        for copy, i, j in plane_flights[k]:
            copy.wait_recv()
            got = slot(*place.behind(i, j))
            if squared:
                part = 0 if j else 1
                dp, tp = place.ahead(1 - i, 1 - j)
                onward = wire.copy(got.at[part], got.at[part], {"dp": dp, "tp": tp})
                onward.start()
                diagonals.append((onward, slot(*place.behind(1, 1)).at[part]))
            to_sibling(got)
            copy.wait_send()

    def plane_diagonal():
        while diagonals:
            copy, got = diagonals.pop(0)
            copy.wait_recv()
            to_sibling(got)
            copy.wait_send()

    count = len(chunks)
    for k in range(count + 3):
        if k < count:
            mid_first(k)
        if 1 <= k < count + 1:
            mid_second(k - 1)
        if 2 <= k < count + 2:
            settle(k - 2)
            plane_send(k - 2)
        if k == 2:
            for copy in outs:
                copy.start()
        if k >= 3:
            plane_diagonal()
            plane_forward(k - 3)
    plane_diagonal()

    @pl.when(is_end)
    def _():
        for flow in flows:
            flow["outer"].wait_send()
            flow["inner"].wait_send()

    @pl.when(is_mid)
    def _():
        for flow in flows:
            for name in ("cross", "back", "share", "pass_on"):
                flow[name].wait_send()

    for copy in outs + done:
        copy.wait()


def finish(sizes, first, second, small, out_own, grad_own):
    dp, ctx, tp = sizes
    experts, _, width, lanes = first.shape
    part = second.shape[1:]
    rows = small.shape[1]
    small_part = (2, rows // 2, 128)
    plane = dp * tp
    images, half = out_own.shape[:2]
    chunks = experts + 2
    offsets = place_offsets(sizes, True)
    per_chunk = 6 + 2 * offsets + 1 + 4
    remote = chunks * per_chunk + plane + 2

    def buffers(make):
        return [make((experts, 2, width, lanes), 1), make(part, 0), make(small_part, 0)]

    def full(shape, lead):
        return pltpu.VMEM(shape, BF16)

    def one(shape, lead):
        return pltpu.VMEM(shape[:lead] + shape[lead + 1 :], BF16)

    return pl.pallas_call(
        functools.partial(finish_kernel, sizes),
        out_shape=(
            jax.ShapeDtypeStruct((dp, tp) + first.shape, BF16),
            jax.ShapeDtypeStruct((dp, tp) + part, BF16),
            jax.ShapeDtypeStruct((dp, tp) + small_part, BF16),
            jax.ShapeDtypeStruct((images, tp * half, D), BF16),
            jax.ShapeDtypeStruct((images, tp * half, D), BF16),
        ),
        in_specs=[IN_VMEM] * 3 + [ANY] * 2,
        out_specs=(ANY,) * 5,
        scratch_shapes=[
            pltpu.VMEM(part, BF16),
            pltpu.VMEM((plane - 1, rows, 128), BF16),
            pltpu.VMEM(part, BF16),
            pltpu.VMEM(small_part, BF16),
        ]
        + buffers(full)
        + buffers(one)
        + buffers(one)
        + buffers(full)
        + semaphores(remote, chunks + 2),
        compiler_params=comm_params(5),
    )(first, second, small, out_own, grad_own)


def per_device(
    sizes,
    tokens,
    cotangent,
    routes,
    slot_index,
    token_mask,
    image_mask,
    adapter_set,
    first_gain,
    first_shift,
    second_gain,
    second_shift,
    attend_weight,
    mixing_weight,
    router_weight,
    expand_weight,
    shrink_weight,
    attend_down,
    attend_up,
    mixing_down,
    mixing_up,
    router_down,
    router_up,
    expand_down,
    expand_up,
    shrink_down,
    shrink_up,
):
    dp_size, ctx_size, tp_size = sizes
    plane = dp_size * tp_size
    images, block = tokens.shape[:2]
    half = block // tp_size
    count = images * half
    seq = ctx_size * block
    all_images = dp_size * images
    local_experts, _, hidden_half = expand_weight.shape
    ctx_index, tp_index, dp_index = (lax.axis_index(a) for a in ("ctx", "tp", "dp"))
    owned = dp_index * local_experts
    ff_start = tp_index * hidden_half
    own_start = ctx_index * block + tp_index * half

    live = token_mask * image_mask[:, None]
    ints = jnp.concatenate(
        [
            jnp.transpose(routes, (0, 2, 1)),
            jnp.transpose(slot_index, (0, 2, 1)),
            live[:, None, :],
            jnp.broadcast_to(adapter_set[:, None, None], (images, 3, block)),
        ],
        axis=1,
    )
    tokens_all, weights_all, mixing_all, router_parts, cotangent_all, ints_all, ctx_ints = (
        start_gather(
            sizes,
            tokens,
            jnp.transpose(attend_weight, (1, 0, 2)),
            mixing_weight,
            jnp.transpose(router_weight, (1, 0)),
            cotangent,
            ints,
        )
    )
    router_t = jnp.transpose(router_parts, (1, 0, 2)).reshape(EXPERTS, D)

    attend_low = jnp.transpose(attend_down, (0, 2, 1)).reshape(WIDTH, D)
    attend_high = jnp.transpose(attend_up, (2, 0, 1, 3)).reshape(3, WIDTH, D)
    mixing_low = jnp.transpose(mixing_down, (0, 2, 1)).reshape(WIDTH, D)
    mixing_high = mixing_up.reshape(WIDTH, D)
    router_low = jnp.transpose(router_down, (0, 2, 1)).reshape(WIDTH, D)
    router_high = router_up.reshape(WIDTH, EXPERTS)

    def picker(sets, repeat):
        hot = (sets[:, None] == jnp.arange(WIDTH)[None, :] // RANK).astype(F32)
        return jnp.repeat(hot, repeat, axis=0)

    def own_rows(values):
        return lax.dynamic_slice_in_dim(values, own_start, half, 1)

    def own_block(values):
        return lax.dynamic_slice_in_dim(values, tp_index * half, half, 1)

    key_live = jnp.transpose(ctx_ints[:, :, 4, :], (1, 0, 2)).reshape(images, seq)
    flat = tokens_all.reshape(images * seq, D).astype(F32)
    attend_in = normalize(flat, first_gain, first_shift)[0].astype(BF16)
    attend_lift = (times_transposed(attend_in, attend_low) * picker(adapter_set, seq)).astype(BF16)
    joined = (
        jnp.einsum("td,pdf->ptf", attend_in, weights_all, preferred_element_type=F32)
        + jnp.einsum("tr,prf->ptf", attend_lift, attend_high, preferred_element_type=F32)
    ).astype(BF16)
    joined = joined.reshape(3, images, seq, HEADS, HD)
    queries_all, keys_all, values_all = joined[0], joined[1], joined[2]
    queries = own_rows(queries_all)
    scale = HD**-0.5
    key_open = (key_live > 0)[:, None, None, :]
    scores = (
        jnp.einsum("iqhd,ikhd->ihqk", queries, keys_all, preferred_element_type=F32) * scale
    )
    scores = jnp.where(key_open, scores, MASKED)
    row_top = jnp.max(scores, axis=-1, keepdims=True)
    powers = jnp.exp(scores - row_top)
    row_total = jnp.sum(powers, axis=-1, keepdims=True)
    weights_att = (powers / row_total).astype(BF16)
    head_mix = jnp.einsum("ihqk,ikhd->iqhd", weights_att, values_all, preferred_element_type=F32)
    head_mix = head_mix.astype(BF16).reshape(count, D)
    log_total = jnp.maximum(row_top + jnp.log(row_total), -1e29)

    own_sets = picker(adapter_set, half)
    mixing_lift = (times_transposed(head_mix, mixing_low) * own_sets).astype(BF16)
    own_in = own_block(tokens).reshape(count, D).astype(F32)
    hidden = own_in + times_transposed(head_mix, mixing_all) + matmul(mixing_lift, mixing_high)
    normed_two, unit_two, factor_two = normalize(hidden, second_gain, second_shift)
    expert_in = normed_two.astype(BF16)

    expert_in_all = expert_in_gather(sizes, expert_in.reshape(images, half, D))

    image_sets = ints_all[:, 5, 0]

    def router(rows_in, sets):
        lift = (times_transposed(rows_in, router_low) * sets).astype(BF16)
        logits = times_transposed(rows_in, router_t) + matmul(lift, router_high)
        top = jnp.max(logits, axis=-1, keepdims=True)
        powers = jnp.exp(logits - top)
        return lift, powers / jnp.sum(powers, axis=-1, keepdims=True)

    _, gate_all = router(expert_in_all.reshape(all_images * block, D), picker(image_sets, block))
    gate_all = gate_all.reshape(all_images, block, EXPERTS)
    expert_ids = jnp.arange(EXPERTS)[None, None, :]
    lanes_local = local_experts * SLOTS
    slot_ids = jnp.arange(lanes_local)[None, :, None]
    table = jnp.zeros((all_images, lanes_local, block), F32)
    gated = jnp.zeros((all_images, lanes_local, block), F32)
    for k in range(TOP):
        route, slot = ints_all[:, k, :], ints_all[:, TOP + k, :]
        gate = jnp.sum(gate_all * (route[..., None] == expert_ids), axis=-1)
        near = jnp.logical_and(route >= owned, route < owned + local_experts)
        target = jnp.where(
            jnp.logical_and(slot < CAP, near), (route - owned) * SLOTS + slot, -1
        )
        hot = (slot_ids == target[:, None, :]).astype(F32)
        table = table + hot
        gated = gated + hot * gate[:, None, :]
    slot_gate = jnp.sum(gated, axis=-1, keepdims=True)
    table = table.astype(BF16)

    def to_slots(values):
        rows = jnp.einsum("ist,itd->isd", table, values, preferred_element_type=F32)
        return rows

    def by_expert(values):
        split = values.reshape(all_images, local_experts, SLOTS, values.shape[-1])
        return jnp.transpose(split, (1, 0, 2, 3)).reshape(
            local_experts, all_images * SLOTS, values.shape[-1]
        )

    def by_image(values):
        split = values.reshape(local_experts, all_images, SLOTS, values.shape[-1])
        return jnp.transpose(split, (1, 0, 2, 3)).reshape(
            all_images, lanes_local, values.shape[-1]
        )

    rows_in = by_expert(to_slots(expert_in_all).astype(BF16))
    grad_slots = to_slots(cotangent_all)
    grad_out = by_expert((grad_slots * slot_gate).astype(BF16))
    slot_sets = picker(image_sets, SLOTS)[None]

    def local_adapter(values):
        return lax.dynamic_slice_in_dim(values, owned, local_experts, 1)

    first_a = jnp.transpose(local_adapter(expand_down), (1, 0, 3, 2)).reshape(
        local_experts, WIDTH, D
    )
    first_b = lax.dynamic_slice_in_dim(local_adapter(expand_up), ff_start, hidden_half, 3)
    first_b = jnp.transpose(first_b, (1, 0, 2, 3)).reshape(local_experts, WIDTH, hidden_half)
    second_a = lax.dynamic_slice_in_dim(local_adapter(shrink_down), ff_start, hidden_half, 2)
    second_a = jnp.transpose(second_a, (1, 0, 3, 2)).reshape(local_experts, WIDTH, hidden_half)
    second_b = jnp.transpose(local_adapter(shrink_up), (1, 0, 2, 3)).reshape(
        local_experts, WIDTH, D
    )

    def each(spec, left, right):
        return jnp.einsum(spec, left, right, preferred_element_type=F32)

    lifted = (each("ecd,erd->ecr", rows_in, first_a) * slot_sets).astype(BF16)
    before = each("ecd,edf->ecf", rows_in, expand_weight) + each(
        "ecr,erf->ecf", lifted, first_b
    )
    phi = 0.5 * (1.0 + lax.erf(before * SQRT_HALF))
    active = (before * phi).astype(BF16)
    slope = phi + before * INV_ROOT_TWO_PI * jnp.exp(-0.5 * before * before)
    lowered = (each("ecf,erf->ecr", active, second_a) * slot_sets).astype(BF16)
    expert_out = each("ecf,efd->ecd", active, shrink_weight) + each(
        "ecr,erd->ecd", lowered, second_b
    )
    grad_lowered = (each("ecd,erd->ecr", grad_out, second_b) * slot_sets).astype(BF16)
    grad_active = each("ecd,efd->ecf", grad_out, shrink_weight) + each(
        "ecr,erf->ecf", grad_lowered, second_a
    )
    grad_before = (grad_active * slope).astype(BF16)
    grad_lifted = (each("ecf,erf->ecr", grad_before, first_b) * slot_sets).astype(BF16)
    grad_rows = each("ecf,edf->ecd", grad_before, expand_weight) + each(
        "ecr,erd->ecd", grad_lifted, first_a
    )
    first_grads = jnp.stack(
        [
            each("ecr,ecf->erf", lifted, grad_before),
            each("ecr,ecf->erf", grad_lowered, active),
        ],
        axis=1,
    ).astype(BF16)
    second_grads = jnp.stack(
        [
            each("ecr,ecd->erd", grad_lifted, rows_in),
            each("ecr,ecd->erd", lowered, grad_out),
        ]
    ).astype(BF16)
    second_grads = jnp.transpose(
        second_grads.reshape(2, local_experts, WIDTH, tp_size, D // tp_size), (3, 0, 1, 2, 4)
    )
    out_slots = by_image(expert_out)
    gate_grads = jnp.sum(out_slots * grad_slots, axis=-1, keepdims=True)
    lane_experts = jnp.arange(128)[None, None, :]
    slot_experts = owned + jnp.arange(lanes_local)[None, :, None] // SLOTS
    payload = jnp.concatenate(
        [
            (out_slots * slot_gate).astype(BF16),
            by_image(grad_rows.astype(BF16)),
            jnp.where(lane_experts == slot_experts, gate_grads, 0.0).astype(BF16),
        ],
        axis=-1,
    )
    partial = jnp.einsum("ist,isd->itd", table, payload, preferred_element_type=F32).astype(BF16)
    lanes = payload.shape[-1]
    partial = partial.reshape(dp_size // 2, 2, images, tp_size, half, lanes)
    partial = jnp.transpose(partial, (1, 0, 3, 2, 4, 5)).reshape(
        2, dp_size // 2, tp_size, count, lanes
    )
    received = return_rows(sizes, partial)
    summed = jnp.sum(received.astype(F32), axis=0)
    returned, grad_from_experts, grad_probs = (
        summed[:, :D],
        summed[:, D : 2 * D],
        summed[:, 2 * D : 2 * D + EXPERTS],
    )

    layer_out = (hidden + returned).astype(BF16)
    own_live = own_block(live).reshape(count, 1).astype(F32)
    grad_output = own_block(cotangent).reshape(count, D).astype(F32) * own_live
    router_lift, gate_probs = router(expert_in, own_sets)
    grad_logits = (
        gate_probs * (grad_probs - jnp.sum(grad_probs * gate_probs, axis=-1, keepdims=True))
    ).astype(BF16)
    grad_router_lift = (times_transposed(grad_logits, router_high) * own_sets).astype(BF16)
    grad_expert_in = (
        grad_from_experts + matmul(grad_logits, router_t) + matmul(grad_router_lift, router_low)
    )
    grad_hidden = grad_output + normalize_back(grad_expert_in, unit_two, factor_two, second_gain)
    grad_attended = grad_hidden.astype(BF16)
    grad_mixing_lift = (times_transposed(grad_attended, mixing_high) * own_sets).astype(BF16)
    grad_heads = (matmul(grad_attended, mixing_all) + matmul(grad_mixing_lift, mixing_low)).astype(
        BF16
    )
    delta = jnp.sum(
        (grad_heads.astype(F32) * head_mix.astype(F32)).reshape(images, half, HEADS, HD), axis=-1
    )
    log_rows = jnp.transpose(log_total[..., 0], (0, 2, 1))

    def parts_of(values, number):
        parts, rest = [], values
        for _ in range(number):
            parts.append(lax.reduce_precision(rest, 8, 7))
            rest = rest - parts[-1]
        return [part.astype(BF16) for part in parts]

    extra = parts_of(log_rows, 3) + parts_of(delta, 2)
    extra.append(jnp.zeros((images, half, 128 - len(extra) * HEADS), BF16))
    heads_all = heads_gather(
        sizes, jnp.concatenate([grad_heads.reshape(images, half, D)] + extra, axis=-1)
    )
    grad_heads_all = heads_all[:, :, :D].reshape(images, seq, HEADS, HD)
    more = heads_all[:, :, D:].astype(F32)

    def stat(first, number):
        total = more[:, :, first * HEADS : (first + 1) * HEADS]
        for k in range(first + 1, first + number):
            total = total + more[:, :, k * HEADS : (k + 1) * HEADS]
        return jnp.transpose(total, (0, 2, 1))[:, :, None, :]

    log_all, delta_all = stat(0, 3), stat(3, 2)

    own_grads = grad_heads.reshape(images, half, HEADS, HD)
    probs = jnp.exp(scores - log_total)
    grad_probs_att = jnp.einsum(
        "iqhd,ikhd->ihqk", own_grads, values_all, preferred_element_type=F32
    )
    delta_rows = jnp.transpose(delta, (0, 2, 1))[..., None]
    grad_scores = (probs * (grad_probs_att - delta_rows)).astype(BF16)
    grad_queries = (
        jnp.einsum("ihqk,ikhd->iqhd", grad_scores, keys_all, preferred_element_type=F32) * scale
    )
    own_keys, own_values = own_rows(keys_all), own_rows(values_all)
    own_open = (own_rows(key_live) > 0)[:, None, :, None]
    scores_t = (
        jnp.einsum("ikhd,iqhd->ihkq", own_keys, queries_all, preferred_element_type=F32) * scale
    )
    probs_t = jnp.exp(jnp.where(own_open, scores_t, MASKED) - log_all)
    grad_probs_t = jnp.einsum(
        "ikhd,iqhd->ihkq", own_values, grad_heads_all, preferred_element_type=F32
    )
    grad_scores_t = (probs_t * (grad_probs_t - delta_all)).astype(BF16)
    grad_keys = (
        jnp.einsum("ihkq,iqhd->ikhd", grad_scores_t, queries_all, preferred_element_type=F32)
        * scale
    )
    grad_values = jnp.einsum(
        "ihkq,iqhd->ikhd", probs_t.astype(BF16), grad_heads_all, preferred_element_type=F32
    )
    grad_joined = jnp.stack([grad_queries, grad_keys, grad_values]).astype(BF16)
    grad_joined = grad_joined.reshape(3, count, D)
    own_attend_in = own_rows(attend_in.reshape(images, seq, D)).reshape(count, D)
    own_attend_lift = own_rows(attend_lift.reshape(images, seq, WIDTH)).reshape(count, WIDTH)
    grad_attend_lift = (
        jnp.einsum("ptf,prf->tr", grad_joined, attend_high, preferred_element_type=F32) * own_sets
    ).astype(BF16)
    grad_attend_in = jnp.einsum(
        "ptf,pdf->td", grad_joined, weights_all, preferred_element_type=F32
    ) + matmul(grad_attend_lift, attend_low)
    _, unit_one, factor_one = normalize(own_in, first_gain, first_shift)
    tokens_grad = (
        grad_hidden + normalize_back(grad_attend_in, unit_one, factor_one, first_gain)
    ).astype(BF16)

    small = jnp.concatenate(
        [inner_rows(own_attend_lift, grad_joined[p]) for p in range(3)]
        + [
            inner_rows(grad_attend_lift, own_attend_in),
            inner_rows(grad_mixing_lift, head_mix),
            inner_rows(mixing_lift, grad_attended),
            inner_rows(grad_router_lift, expert_in),
            jnp.pad(inner_rows(router_lift, grad_logits), ((0, 0), (0, 128 - EXPERTS))),
        ],
        axis=1,
    ).astype(BF16)
    lanes_small = small.shape[1]
    needed = WIDTH * lanes_small // 128
    rows = -(-needed // (plane * 16)) * 16
    small = jnp.pad(small.reshape(needed, 128), ((0, plane * rows - needed), (0, 0)))
    first_all, second_all, small_all, out_all, grad_all = finish(
        sizes,
        first_grads,
        second_grads,
        small.reshape(plane, rows, 128),
        layer_out.reshape(images, half, D),
        tokens_grad.reshape(images, half, D),
    )
    small_all = small_all.reshape(plane * rows, 128)[:needed].reshape(WIDTH, lanes_small)
    small_all = small_all.astype(F32).reshape(SETS, RANK, lanes_small)

    def piece(k):
        return small_all[:, :, k * D : (k + 1) * D]

    def flipped(values):
        return jnp.swapaxes(values, -1, -2)

    wide = first_all.reshape(dp_size, tp_size, local_experts, 2, SETS, RANK, hidden_half)
    wide = jnp.transpose(wide, (3, 4, 0, 2, 5, 1, 6)).reshape(
        2, SETS, EXPERTS, RANK, tp_size * hidden_half
    ).astype(F32)
    narrow = second_all.reshape(dp_size, tp_size, 2, local_experts, SETS, RANK, D // tp_size)
    narrow = jnp.transpose(narrow, (2, 4, 0, 3, 5, 1, 6)).reshape(
        2, SETS, EXPERTS, RANK, D
    ).astype(F32)
    return (
        out_all,
        grad_all,
        flipped(piece(3)),
        jnp.stack([piece(0), piece(1), piece(2)], axis=2),
        flipped(piece(4)),
        piece(5),
        flipped(piece(6)),
        small_all[:, :, 7 * D : 7 * D + EXPERTS],
        flipped(narrow[0]),
        wide[0],
        flipped(wide[1]),
        narrow[1],
    )


def solution(mesh):
    sizes = (mesh.shape["dp"], mesh.shape["ctx"], mesh.shape["tp"])
    tokens_spec = P("dp", "ctx", None)
    in_specs = (
        (tokens_spec,) * 4
        + (P("dp", "ctx"), P("dp"), P("dp"))
        + (P(),) * 4
        + (P("dp", None, "tp"), P("dp", "tp"), P("dp", None))
        + (P("dp", None, "tp"), P("dp", "tp", None))
        + (P(),) * 10
    )
    out_specs = (tokens_spec,) * 2 + (P(),) * 10
    return jax.shard_map(
        functools.partial(per_device, sizes),
        mesh=mesh,
        in_specs=in_specs,
        out_specs=out_specs,
        check_vma=False,
    )
```

```python
import functools

import jax
import jax.numpy as jnp
from jax import lax
from jax.experimental import pallas as pl
from jax.experimental.pallas import tpu as pltpu
from jax.sharding import PartitionSpec as P

D = 512
HEADS = 8
HD = 64
FF = 2048
EXPERTS = 16
TOP = 2
RANK = 16
SETS = 4
CAP = 30
SLOTS = 32
WIDTH = SETS * RANK

EPSILON = 1e-06
MASKED = -1e30
SQRT_HALF = 0.7071067811865476
INV_ROOT_TWO_PI = 0.3989422804014327
F32 = jnp.float32
BF16 = jnp.bfloat16
MESH = pl.DeviceIdType.MESH
ANY = pl.BlockSpec(memory_space=pl.ANY)
IN_VMEM = pl.BlockSpec(memory_space=pltpu.VMEM)


def matmul(left_side, right_side):
    return jnp.dot(left_side, right_side, preferred_element_type=F32)


def inner_rows(left_side, right_side):
    return lax.dot_general(
        left_side, right_side, (((0,), (0,)), ((), ())), preferred_element_type=F32
    )


def times_transposed(left_side, right_side):
    return lax.dot_general(
        left_side, right_side, (((1,), (1,)), ((), ())), preferred_element_type=F32
    )


def normalize(values, gain_row, shift_row):
    centred = values - jnp.mean(values, axis=-1, keepdims=True)
    spread = jnp.mean(centred * centred, axis=-1, keepdims=True)
    factor = lax.rsqrt(spread + EPSILON)
    normed = centred * factor
    return (normed * gain_row + shift_row, normed, factor)


def normalize_back(grad_out, normed, factor, gain_row):
    scaled = grad_out * gain_row
    return factor * (
        scaled
        - jnp.mean(scaled, axis=-1, keepdims=True)
        - normed * jnp.mean(scaled * normed, axis=-1, keepdims=True)
    )


class Wire:
    def __init__(self, send, recv, local=None):
        self.send, self.recv, self.local = send, recv, local
        self.used = self.used_local = 0

    def copy(self, src, dst, device):
        k = self.used
        self.used += 1
        return pltpu.make_async_remote_copy(
            src_ref=src,
            dst_ref=dst,
            send_sem=self.send.at[k],
            recv_sem=self.recv.at[k],
            device_id=device,
            device_id_type=MESH,
        )

    def near(self, src, dst):
        k = self.used_local
        self.used_local += 1
        return pltpu.make_async_copy(src, dst, self.local.at[k])


class Place:
    def __init__(self, sizes):
        self.dp_size, self.ctx_size, self.tp_size = sizes
        self.chips = self.dp_size // 2
        self.dp = lax.axis_index("dp")
        self.ctx = lax.axis_index("ctx")
        self.tp = lax.axis_index("tp")
        self.chip = lax.div(self.dp, 2)
        self.core = lax.rem(self.dp, 2)
        self.sibling = self.chip * 2 + (1 - self.core)

    def ahead(self, i, j):
        return (
            lax.rem(self.chip + i, self.chips) * 2 + self.core,
            lax.rem(self.tp + j, self.tp_size),
        )

    def behind(self, i, j):
        return self.ahead(self.chips - i, self.tp_size - j)

    def offsets(self, over_tp=True):
        return [
            (i, j)
            for i in range(self.chips)
            for j in range(self.tp_size if over_tp else 1)
            if i or j
        ]

    def greet(self, with_ctx):
        barrier = pltpu.get_barrier_semaphore()
        count = 0
        for i, j in self.offsets():
            dp, tp = self.ahead(i, j)
            pl.semaphore_signal(
                barrier, inc=1, device_id={"dp": dp, "tp": tp}, device_id_type=MESH
            )
            count += 1
        pl.semaphore_signal(
            barrier, inc=1, device_id={"dp": self.sibling}, device_id_type=MESH
        )
        count += 1
        if with_ctx:
            for i in range(1, self.ctx_size):
                pl.semaphore_signal(
                    barrier,
                    inc=1,
                    device_id={"ctx": lax.rem(self.ctx + i, self.ctx_size)},
                    device_id_type=MESH,
                )
                count += 1
        pl.semaphore_wait(barrier, count)


def gather_plane_start(place, wire, items):
    flights, done = [], []
    for source, slot, over_tp in items:
        for i, j in place.offsets(over_tp):
            dp, tp = place.ahead(i, j)
            copy = wire.copy(source, slot(place.dp, place.tp), {"dp": dp, "tp": tp})
            copy.start()
            flights.append((copy, slot(*place.behind(i, j))))
    for source, slot, _ in items:
        copy = wire.copy(source, slot(place.dp, place.tp), {"dp": place.sibling})
        copy.start()
        done.append(copy)
        copy = wire.near(source, slot(place.dp, place.tp))
        copy.start()
        done.append(copy)
    return flights, done


def gather_plane_end(place, wire, flights, done):
    for copy, got in flights:
        copy.wait_recv()
        onward = wire.copy(got, got, {"dp": place.sibling})
        onward.start()
        done.append(onward)
    for copy, _ in flights:
        copy.wait_send()
    for copy in done:
        copy.wait()


def plane_copies(place, flags):
    sent = sum(len(place_offsets(place, f)) for f in flags)
    return sent, len(flags)


def place_offsets(sizes, over_tp):
    chips = sizes[0] // 2
    return chips * (sizes[2] if over_tp else 1) - 1


def semaphores(remote, near):
    return [
        pltpu.SemaphoreType.DMA((remote,)),
        pltpu.SemaphoreType.DMA((remote,)),
        pltpu.SemaphoreType.DMA((near,)),
    ]


def comm_params(number):
    return pltpu.CompilerParams(
        collective_id=number, has_side_effects=True, vmem_limit_bytes=48 << 20
    )


def gather_ctx_start(place, wire, source, slot):
    flights = []
    for i in range(1, place.ctx_size):
        copy = wire.copy(
            source,
            slot(place.ctx, place.tp),
            {"ctx": lax.rem(place.ctx + i, place.ctx_size)},
        )
        copy.start()
        flights.append(
            (copy, slot(lax.rem(place.ctx - i + place.ctx_size, place.ctx_size), place.tp))
        )
    return flights


def start_kernel(
    sizes, tokens, weights, mixing, router, cotangent, ints,
    tokens_all, weights_all, mixing_all, router_all, cotangent_all, ints_all, ctx_ints,
    send, recv, local,
):
    place = Place(sizes)
    wire = Wire(send, recv, local)
    place.greet(True)
    rows, lanes = mixing.shape
    half = tokens.shape[1] // place.tp_size
    other_tp = lax.rem(place.tp + 1, 2)

    def token_slot(ctx, tp):
        start = pl.multiple_of(ctx * tokens.shape[1] + tp * half, 16)
        return tokens_all.at[:, pl.ds(start, half), :]

    def at_rows(dp):
        return pl.ds(pl.multiple_of(dp * rows, 16), rows)

    def at_lanes(tp):
        return pl.ds(pl.multiple_of(tp * lanes, 128), lanes)

    mine = tokens.at[:, pl.ds(pl.multiple_of(place.tp * half, 16), half), :]
    token_flights = gather_ctx_start(place, wire, mine, token_slot)
    int_flights = gather_ctx_start(place, wire, ints, lambda ctx, tp: ctx_ints.at[ctx])
    flights, done = gather_plane_start(
        place,
        wire,
        [
            (weights, lambda dp, tp: weights_all.at[:, at_rows(dp), at_lanes(tp)], True),
            (mixing, lambda dp, tp: mixing_all.at[at_rows(dp), at_lanes(tp)], True),
            (ints, lambda dp, tp: ints_all.at[pl.ds(dp * 2, 2)], False),
            (router, lambda dp, tp: router_all.at[dp], False),
            (cotangent, lambda dp, tp: cotangent_all.at[pl.ds(dp * 2, 2)], False),
        ],
    )
    whole = tokens_all.at[:, pl.ds(pl.multiple_of(place.ctx * tokens.shape[1], 16), tokens.shape[1]), :]
    for src, dst in ((tokens, whole), (ints, ctx_ints.at[place.ctx])):
        copy = wire.near(src, dst)
        copy.start()
        done.append(copy)
    for copy, got in token_flights:
        copy.wait_recv()
        onward = wire.copy(got, got, {"tp": other_tp})
        onward.start()
        done.append(onward)
    for copy, _ in int_flights:
        copy.wait()
    for copy, _ in token_flights:
        copy.wait_send()
    gather_plane_end(place, wire, flights, done)


def start_gather(sizes, tokens, weights, mixing, router, cotangent, ints):
    dp, ctx, tp = sizes
    rows, lanes = mixing.shape
    images, block = tokens.shape[:2]
    full, part = place_offsets(sizes, True), place_offsets(sizes, False)
    remote = 3 * (ctx - 1) + 4 * full + 6 * part + 5
    return pl.pallas_call(
        functools.partial(start_kernel, sizes),
        out_shape=(
            jax.ShapeDtypeStruct((images, ctx * block, D), BF16),
            jax.ShapeDtypeStruct((3, dp * rows, tp * lanes), BF16),
            jax.ShapeDtypeStruct((dp * rows, tp * lanes), BF16),
            jax.ShapeDtypeStruct((dp,) + router.shape, BF16),
            jax.ShapeDtypeStruct((dp * images, block, D), BF16),
            jax.ShapeDtypeStruct((dp * images,) + ints.shape[1:], jnp.int32),
            jax.ShapeDtypeStruct((ctx,) + ints.shape, jnp.int32),
        ),
        in_specs=[ANY] * 6,
        out_specs=(ANY,) * 7,
        scratch_shapes=semaphores(remote, 7),
        compiler_params=comm_params(1),
    )(tokens, weights, mixing, router, cotangent, ints)


def expert_in_kernel(sizes, own, gathered, send, recv, local):
    place = Place(sizes)
    wire = Wire(send, recv, local)
    place.greet(False)
    half = own.shape[1]

    def slot(dp, tp):
        return gathered.at[pl.ds(dp * 2, 2), pl.ds(pl.multiple_of(tp * half, 16), half), :]

    flights, done = gather_plane_start(place, wire, [(own, slot, True)])
    gather_plane_end(place, wire, flights, done)


def expert_in_gather(sizes, own):
    dp, ctx, tp = sizes
    images, half = own.shape[:2]
    return pl.pallas_call(
        functools.partial(expert_in_kernel, sizes),
        out_shape=jax.ShapeDtypeStruct((dp * images, tp * half, D), BF16),
        in_specs=[ANY],
        out_specs=ANY,
        scratch_shapes=semaphores(2 * place_offsets(sizes, True) + 1, 1),
        compiler_params=comm_params(2),
    )(own)


def return_kernel(sizes, partial, received, from_sibling, paired, send, recv, local):
    place = Place(sizes)
    wire = Wire(send, recv, local)
    place.greet(False)
    swap = wire.copy(partial.at[1 - place.core], from_sibling, {"dp": place.sibling})
    swap.start()
    swap.wait_recv()
    copies = []
    for i, j in place.offsets() + [(0, 0)]:
        dp, tp = place.ahead(i, j)
        chip = lax.div(dp, 2)
        paired[chip, tp] = (
            partial[place.core, chip, tp].astype(F32) + from_sibling[chip, tp].astype(F32)
        ).astype(BF16)
        index = i * place.tp_size + j
        if index:
            copy = wire.copy(paired.at[chip, tp], received.at[index], {"dp": dp, "tp": tp})
        else:
            copy = wire.near(paired.at[chip, tp], received.at[0])
        copy.start()
        copies.append(copy)
    for copy in copies:
        copy.wait()
    swap.wait_send()


def return_rows(sizes, partial):
    dp, ctx, tp = sizes
    count, lanes = partial.shape[3:]
    chips = dp // 2
    return pl.pallas_call(
        functools.partial(return_kernel, sizes),
        out_shape=jax.ShapeDtypeStruct((chips * tp, count, lanes), BF16),
        in_specs=[IN_VMEM],
        out_specs=ANY,
        scratch_shapes=[
            pltpu.VMEM((chips, tp, count, lanes), BF16),
            pltpu.VMEM((chips, tp, count, lanes), BF16),
        ]
        + semaphores(chips * tp, 1),
        compiler_params=comm_params(3),
    )(partial)


def heads_kernel(sizes, own, stats, gathered, stats_all, send, recv, local):
    place = Place(sizes)
    wire = Wire(send, recv, local)
    place.greet(True)
    half = own.shape[1]
    other_tp = lax.rem(place.tp + 1, 2)

    def rows_slot(ctx, tp):
        start = pl.multiple_of((ctx * place.tp_size + tp) * half, 16)
        return gathered.at[:, pl.ds(start, half), :]

    def stats_slot(ctx, tp):
        return stats_all.at[ctx * place.tp_size + tp]

    done, flights = [], []
    for source, slot in ((own, rows_slot), (stats, stats_slot)):
        flights += gather_ctx_start(place, wire, source, slot)
    for source, slot in ((own, rows_slot), (stats, stats_slot)):
        spot = slot(place.ctx, place.tp)
        for copy in (wire.copy(source, spot, {"tp": other_tp}), wire.near(source, spot)):
            copy.start()
            done.append(copy)
    for copy, got in flights:
        copy.wait_recv()
        onward = wire.copy(got, got, {"tp": other_tp})
        onward.start()
        done.append(onward)
    for copy, _ in flights:
        copy.wait_send()
    for copy in done:
        copy.wait()


def heads_gather(sizes, own, stats):
    dp, ctx, tp = sizes
    images, half, lanes = own.shape
    return pl.pallas_call(
        functools.partial(heads_kernel, sizes),
        out_shape=(
            jax.ShapeDtypeStruct((images, ctx * tp * half, lanes), BF16),
            jax.ShapeDtypeStruct((ctx * tp,) + stats.shape, BF16),
        ),
        in_specs=[ANY] * 2,
        out_specs=(ANY,) * 2,
        scratch_shapes=semaphores(2 * (2 * (ctx - 1) + 1), 2),
        compiler_params=comm_params(4),
    )(own, stats)


def add_rounded(*parts):
    total = parts[0].astype(F32)
    for part in parts[1:]:
        total = total + part.astype(F32)
    return total.astype(BF16)


def finish_kernel(
    sizes, first, second, small, out_own, grad_own,
    first_all, second_all, small_all, out_all, grad_all,
    second_got, small_got, second_sum, small_sum,
    first_end, second_end, small_end,
    first_mid, second_mid, small_mid,
    first_stage, second_stage, small_stage,
    first_final, second_final, small_final,
    send, recv, local,
):
    place = Place(sizes)
    wire = Wire(send, recv, local)
    plane = place.dp_size * place.tp_size
    me = place.dp * place.tp_size + place.tp
    is_mid = jnp.logical_and(place.ctx >= 1, place.ctx <= 2)
    is_end = jnp.logical_not(is_mid)
    inner = lax.div(place.ctx, 2)
    outer_half = 1 - inner
    partner = jnp.where(is_mid, inner * 3, 1 + inner)
    other_mid = 2 - inner
    other_tp = lax.rem(place.tp + 1, 2)
    half = out_own.shape[1]
    experts = first.shape[0]

    barrier = pltpu.get_barrier_semaphore()
    peers = []
    for k in range(1, plane):
        peer = lax.rem(me + k, plane)
        peers.append((lax.div(peer, place.tp_size), lax.rem(peer, place.tp_size)))
        pl.semaphore_signal(
            barrier, inc=1, device_id={"dp": peers[-1][0], "tp": peers[-1][1]}, device_id_type=MESH
        )
    pl.semaphore_signal(barrier, inc=1, device_id={"ctx": partner}, device_id_type=MESH)

    @pl.when(is_mid)
    def _():
        pl.semaphore_signal(barrier, inc=1, device_id={"ctx": other_mid}, device_id_type=MESH)

    pl.semaphore_wait(barrier, plane + jnp.where(is_mid, 1, 0))

    swap = wire.copy(second.at[other_tp], second_got, {"tp": other_tp})
    swap.start()
    spread = []
    for k, (dp, tp) in enumerate(peers):
        copy = wire.copy(
            small.at[dp * place.tp_size + tp], small_got.at[k], {"dp": dp, "tp": tp}
        )
        copy.start()
        spread.append(copy)
    outs = []
    for own, gathered in ((out_own, out_all), (grad_own, grad_all)):
        spot = gathered.at[:, pl.ds(pl.multiple_of(place.tp * half, 16), half), :]
        outs.append(wire.copy(own, spot, {"tp": other_tp}))
        outs.append(wire.near(own, spot))

    chunks = [
        (
            first.at[e], first_end.at[e], first_mid.at[e], first_stage.at[e],
            first_final.at[e], functools.partial(lambda e, dp, tp: first_all.at[dp, tp, e], e),
        )
        for e in range(experts)
    ]
    chunks.append(
        (second_sum, second_end, second_mid, second_stage, second_final,
         lambda dp, tp: second_all.at[dp, tp])
    )
    chunks.append(
        (small_sum, small_end, small_mid, small_stage, small_final,
         lambda dp, tp: small_all.at[dp, tp])
    )

    flows = []
    for mine, end, mid, stage, final, slot in chunks:
        flows.append(
            dict(
                outer=wire.copy(mine.at[outer_half], end.at[outer_half], {"ctx": partner}),
                inner=wire.copy(mine.at[inner], end.at[inner], {"ctx": partner}),
                cross=wire.copy(stage, mid, {"ctx": other_mid}),
                back=wire.copy(final.at[inner], final.at[inner], {"ctx": partner}),
                share=wire.copy(final.at[inner], final.at[inner], {"ctx": other_mid}),
                pass_on=wire.copy(final.at[outer_half], final.at[outer_half], {"ctx": partner}),
            )
        )

    def send_ends(k):
        @pl.when(is_end)
        def _():
            flows[k]["outer"].start()
            flows[k]["inner"].start()

    for k in range(experts):
        send_ends(k)
    swap.wait()
    second_sum[...] = add_rounded(second[place.tp], second_got[...])
    send_ends(experts)
    for copy in spread:
        copy.wait()
    total = small[me].astype(F32)
    for k in range(plane - 1):
        total = total + small_got[k].astype(F32)
    small_sum[...] = total.astype(BF16).reshape(small_sum.shape)
    send_ends(experts + 1)

    def mid_first(k):
        mine, end, mid, stage, final, slot = chunks[k]

        @pl.when(is_mid)
        def _():
            flows[k]["outer"].wait_recv()
            stage[...] = add_rounded(mine[outer_half], end[outer_half])
            flows[k]["cross"].start()

    def mid_second(k):
        mine, end, mid, stage, final, slot = chunks[k]

        @pl.when(is_mid)
        def _():
            flows[k]["inner"].wait_recv()
            flows[k]["cross"].wait_recv()
            final[inner] = add_rounded(mine[inner], end[inner], mid[...])
            flows[k]["share"].start()
            flows[k]["back"].start()

    def settle(k):
        @pl.when(is_mid)
        def _():
            flows[k]["share"].wait_recv()
            flows[k]["pass_on"].start()

        @pl.when(is_end)
        def _():
            flows[k]["back"].wait_recv()
            flows[k]["pass_on"].wait_recv()

    squared = place.chips == 2 and place.tp_size == 2
    done = []
    plane_flights = []

    def plane_send(k):
        final, slot = chunks[k][4], chunks[k][5]
        spot = slot(place.dp, place.tp)
        flights = []
        for i, j in place.offsets():
            if squared and i and j:
                continue
            dp, tp = place.ahead(i, j)
            copy = wire.copy(final, spot, {"dp": dp, "tp": tp})
            copy.start()
            flights.append((copy, i, j))
        for copy in (wire.copy(final, spot, {"dp": place.sibling}), wire.near(final, spot)):
            copy.start()
            done.append(copy)
        plane_flights.append(flights)

    def to_sibling(ref):
        copy = wire.copy(ref, ref, {"dp": place.sibling})
        copy.start()
        done.append(copy)

    diagonals = []

    def plane_forward(k):
        slot = chunks[k][5]
        for copy, i, j in plane_flights[k]:
            copy.wait_recv()
            got = slot(*place.behind(i, j))
            if squared:
                part = 0 if j else 1
                dp, tp = place.ahead(1 - i, 1 - j)
                onward = wire.copy(got.at[part], got.at[part], {"dp": dp, "tp": tp})
                onward.start()
                diagonals.append((onward, slot(*place.behind(1, 1)).at[part]))
            to_sibling(got)
            copy.wait_send()

    def plane_diagonal():
        while diagonals:
            copy, got = diagonals.pop(0)
            copy.wait_recv()
            to_sibling(got)
            copy.wait_send()

    count = len(chunks)
    for k in range(count + 3):
        if k < count:
            mid_first(k)
        if 1 <= k < count + 1:
            mid_second(k - 1)
        if 2 <= k < count + 2:
            settle(k - 2)
            plane_send(k - 2)
        if k == 2:
            for copy in outs:
                copy.start()
        if k >= 3:
            plane_diagonal()
            plane_forward(k - 3)
    plane_diagonal()

    @pl.when(is_end)
    def _():
        for flow in flows:
            flow["outer"].wait_send()
            flow["inner"].wait_send()

    @pl.when(is_mid)
    def _():
        for flow in flows:
            for name in ("cross", "back", "share", "pass_on"):
                flow[name].wait_send()

    for copy in outs + done:
        copy.wait()


def finish(sizes, first, second, small, out_own, grad_own):
    dp, ctx, tp = sizes
    experts, _, width, lanes = first.shape
    part = second.shape[1:]
    rows = small.shape[1]
    small_part = (2, rows // 2, 128)
    plane = dp * tp
    images, half = out_own.shape[:2]
    chunks = experts + 2
    offsets = place_offsets(sizes, True)
    per_chunk = 6 + 2 * offsets + 1 + 4
    remote = chunks * per_chunk + plane + 2

    def buffers(make):
        return [make((experts, 2, width, lanes), 1), make(part, 0), make(small_part, 0)]

    def full(shape, lead):
        return pltpu.VMEM(shape, BF16)

    def one(shape, lead):
        return pltpu.VMEM(shape[:lead] + shape[lead + 1 :], BF16)

    return pl.pallas_call(
        functools.partial(finish_kernel, sizes),
        out_shape=(
            jax.ShapeDtypeStruct((dp, tp) + first.shape, BF16),
            jax.ShapeDtypeStruct((dp, tp) + part, BF16),
            jax.ShapeDtypeStruct((dp, tp) + small_part, BF16),
            jax.ShapeDtypeStruct((images, tp * half, D), BF16),
            jax.ShapeDtypeStruct((images, tp * half, D), BF16),
        ),
        in_specs=[IN_VMEM] * 3 + [ANY] * 2,
        out_specs=(ANY,) * 5,
        scratch_shapes=[
            pltpu.VMEM(part, BF16),
            pltpu.VMEM((plane - 1, rows, 128), BF16),
            pltpu.VMEM(part, BF16),
            pltpu.VMEM(small_part, BF16),
        ]
        + buffers(full)
        + buffers(one)
        + buffers(one)
        + buffers(full)
        + semaphores(remote, chunks + 2),
        compiler_params=comm_params(5),
    )(first, second, small, out_own, grad_own)


def put_lanes(columns, width):
    lane = lax.broadcasted_iota(jnp.int32, (columns[0].shape[0], width), 1)
    total = jnp.zeros((columns[0].shape[0], width), F32)
    for k, column in enumerate(columns):
        total = jnp.where(lane == k, column, total)
    return total


def half_masks():
    lane = lax.broadcasted_iota(jnp.int32, (1, 2 * HD), 1)
    even = (lane < HD).astype(F32)
    return even, 1.0 - even


def stack_pair(rows, masks, factor=1.0):
    wide = rows.astype(F32) * factor
    return jnp.concatenate([wide * masks[0], wide * masks[1]], axis=0).astype(BF16)


def join_pair(rows, masks):
    half = rows.shape[0] // 2
    return rows[:half] * masks[0] + rows[half:] * masks[1]


def attend_kernel(
    place, tokens, weights, mixing, live_keys, picks, attend_low, attend_high, mixing_low,
    mixing_high, gains,
    joined, own_in, own_lift, head_mix_out, log_out, mixing_lift_out, hidden_out, expert_in_out,
    lift_scratch,
):
    images, seq = tokens.shape[:2]
    half = head_mix_out.shape[0] // images
    own_start = pl.multiple_of(place[0], 16)
    block = seq // 2

    def project(k, _):
        i, r = lax.div(k, 2), pl.multiple_of(lax.rem(k, 2) * block, 16)
        rows = tokens[i, pl.ds(r, block), :].astype(F32)
        normed = normalize(rows, gains[0:1, :], gains[1:2, :])[0].astype(BF16)
        lift = (times_transposed(normed, attend_low[...]) * picks[pl.ds(i, 1), :]).astype(BF16)
        lift_scratch[i, pl.ds(r, block), :] = lift
        for p in range(3):
            joined[p, i, pl.ds(r, block), :] = (
                matmul(normed, weights[p]) + matmul(lift, attend_high[p])
            ).astype(BF16)
        return 0

    lax.fori_loop(0, images * 2, project, 0)
    masks = half_masks()
    scale = HD**-0.5
    mix_parts = []
    for i in range(images):
        open_keys = live_keys[i : i + 1, :] > 0
        rows = tokens[i, pl.ds(own_start, half), :].astype(F32)
        own_in[i] = normalize(rows, gains[0:1, :], gains[1:2, :])[0].astype(BF16)
        own_lift[i] = lift_scratch[i, pl.ds(own_start, half), :]
        logs = []
        for j in range(HEADS // 2):
            lanes = slice(j * 2 * HD, (j + 1) * 2 * HD)
            q = stack_pair(joined[0, i, pl.ds(own_start, half), lanes], masks, scale)
            scores = times_transposed(q, joined[1, i, :, lanes])
            scores = jnp.where(open_keys, scores, MASKED)
            top = jnp.max(scores, axis=-1, keepdims=True)
            powers = jnp.exp(scores - top)
            total = jnp.sum(powers, axis=-1, keepdims=True)
            weights_att = (powers * (1.0 / total)).astype(BF16)
            mixed = join_pair(matmul(weights_att, joined[2, i, :, lanes]), masks)
            head_mix_out[i * half : (i + 1) * half, lanes] = mixed.astype(BF16)
            log = jnp.maximum(top + jnp.log(total), -1e29)
            logs += [log[:half], log[half:]]
        log_out[i * half : (i + 1) * half, :] = put_lanes(logs, 128)
        mix = head_mix_out[i * half : (i + 1) * half, :]
        lift = (times_transposed(mix, mixing_low[...]) * picks[i : i + 1, :]).astype(BF16)
        mixing_lift_out[i * half : (i + 1) * half, :] = lift
        hidden = rows + times_transposed(mix, mixing[...]) + matmul(lift, mixing_high[...])
        hidden_out[i * half : (i + 1) * half, :] = hidden
        expert_in_out[i] = normalize(hidden, gains[2:3, :], gains[3:4, :])[0].astype(BF16)


def attend(half, place, *operands):
    images, seq = operands[0].shape[:2]
    count = images * half

    def out(*shape, dtype=BF16):
        return jax.ShapeDtypeStruct(shape, dtype)

    return pl.pallas_call(
        attend_kernel,
        out_shape=(
            out(3, images, seq, D),
            out(images, half, D),
            out(images, half, WIDTH),
            out(count, D),
            out(count, 128, dtype=F32),
            out(count, WIDTH),
            out(count, D, dtype=F32),
            out(images, half, D),
        ),
        in_specs=[pl.BlockSpec(memory_space=pltpu.SMEM)] + [IN_VMEM] * len(operands),
        out_specs=(IN_VMEM,) * 8,
        scratch_shapes=[pltpu.VMEM((images, seq, WIDTH), BF16)],
        compiler_params=pltpu.CompilerParams(vmem_limit_bytes=48 << 20),
    )(place, *operands)


def experts_kernel(
    place, rows_all, cot_all, ints, picks, picks_t, router_t, router_low, router_high_t,
    up_weight, down_weight, first_a, first_b, second_a, second_b,
    first_grads, second_grads, partial,
    table, rows_in, grad_slots, gates, payload,
):
    e = pl.program_id(0)
    last = pl.num_programs(0) - 1
    experts, count = rows_in.shape[:2]
    images, block = rows_all.shape[:2]
    owned = place[1]
    slots = experts * SLOTS
    half = block // second_grads.shape[0]

    @pl.when(e == 0)
    def _():
        def dispatch(i, _):
            rows = rows_all[i]
            lift = times_transposed(router_low[...], rows) * picks_t[i]
            logits = times_transposed(router_t[...], rows) + matmul(
                router_high_t[...], lift.astype(BF16)
            )
            powers = jnp.exp(logits - jnp.max(logits, axis=0, keepdims=True))
            probs = powers / jnp.sum(powers, axis=0, keepdims=True)
            numbers = ints[i]
            expert = lax.broadcasted_iota(jnp.int32, (EXPERTS, block), 0)
            slot = lax.broadcasted_iota(jnp.int32, (slots, block), 0)
            hot = jnp.zeros((slots, block), F32)
            gated = jnp.zeros((slots, block), F32)
            for k in range(TOP):
                route, place_in = numbers[k : k + 1, :], numbers[TOP + k : TOP + k + 1, :]
                gate = jnp.sum(jnp.where(expert == route, probs, 0.0), axis=0, keepdims=True)
                local = route - owned
                here = (local >= 0) & (local < experts) & (place_in < CAP)
                target = jnp.where(here, local * SLOTS + place_in, -1)
                match = slot == target
                hot = jnp.where(match, 1.0, hot)
                gated = jnp.where(match, gate, gated)
            hot = hot.astype(BF16)
            table[i] = hot
            gate_column = jnp.broadcast_to(jnp.sum(gated, axis=1, keepdims=True), (slots, 128))
            picked = matmul(hot, rows).astype(BF16)
            grads = matmul(hot, cot_all[i]).astype(BF16)
            at = pl.ds(pl.multiple_of(i * SLOTS, SLOTS), SLOTS)
            for n in range(experts):
                part = slice(n * SLOTS, (n + 1) * SLOTS)
                rows_in[n, at, :] = picked[part]
                grad_slots[n, at, :] = grads[part]
                gates[n, at, :] = gate_column[part]
            return 0

        lax.fori_loop(0, images, dispatch, 0)

    rows = rows_in[e]
    grads = grad_slots[e].astype(F32)
    gate = gates[e][:, 0:1]
    sets = jnp.broadcast_to(picks[...][:, None, :], (images, SLOTS, WIDTH)).reshape(count, WIDTH)
    a_first, b_first = first_a[:, 0].reshape(WIDTH, D), first_b[:, 0].reshape(WIDTH, -1)
    a_second, b_second = second_a[:, 0].reshape(WIDTH, -1), second_b[:, 0].reshape(WIDTH, D)
    lifted = (times_transposed(rows, a_first) * sets).astype(BF16)
    before = matmul(rows, up_weight[0]) + matmul(lifted, b_first)
    phi = 0.5 * (1.0 + lax.erf(before * SQRT_HALF))
    active = (before * phi).astype(BF16)
    slope = phi + before * (INV_ROOT_TWO_PI * jnp.exp(-0.5 * before * before))
    lowered = (times_transposed(active, a_second) * sets).astype(BF16)
    out = matmul(active, down_weight[0]) + matmul(lowered, b_second)
    grad_out = (grads * gate).astype(BF16)
    grad_lowered = (times_transposed(grad_out, b_second) * sets).astype(BF16)
    grad_active = times_transposed(grad_out, down_weight[0]) + matmul(grad_lowered, a_second)
    grad_before = (grad_active * slope).astype(BF16)
    grad_lifted = (times_transposed(grad_before, b_first) * sets).astype(BF16)
    grad_rows = times_transposed(grad_before, up_weight[0]) + matmul(grad_lifted, a_first)
    first_grads[0, 0] = inner_rows(lifted, grad_before).astype(BF16)
    first_grads[0, 1] = inner_rows(grad_lowered, active).astype(BF16)
    pieces = second_grads.shape[0]
    lanes = D // pieces
    for number, value in (
        (0, inner_rows(grad_lifted, rows)),
        (1, inner_rows(lowered, grad_out)),
    ):
        for t in range(pieces):
            second_grads[t, number, e] = value[:, t * lanes : (t + 1) * lanes].astype(BF16)
    lane = lax.broadcasted_iota(jnp.int32, (count, 128), 1)
    gate_grads = jnp.sum(out * grads, axis=1, keepdims=True)
    gated_out = (out * gate).astype(BF16).reshape(images, SLOTS, D)
    grad_rows = grad_rows.astype(BF16).reshape(images, SLOTS, D)
    gate_grads = jnp.where(lane == owned + e, gate_grads, 0.0).astype(BF16)
    gate_grads = gate_grads.reshape(images, SLOTS, 128)
    at = pl.ds(pl.multiple_of(e * SLOTS, SLOTS), SLOTS)
    payload[:, at, 0:D] = gated_out
    payload[:, at, D : 2 * D] = grad_rows
    payload[:, at, 2 * D :] = gate_grads

    @pl.when(e == last)
    def _():
        def combine(i, _):
            dp, local = lax.div(i, 2), lax.rem(i, 2)
            rows = inner_rows(table[i], payload[i]).astype(BF16)
            core, chip = lax.rem(dp, 2), lax.div(dp, 2)
            for t in range(partial.shape[2]):
                partial[core, chip, t, local] = rows[t * half : (t + 1) * half]
            return 0

        lax.fori_loop(0, images, combine, 0)


def run_experts(
    sizes, place, rows_all, cot_all, ints, picks, picks_t, router_t, router_low, router_high_t,
    up_weight, down_weight, first_a, first_b, second_a, second_b,
):
    dp, ctx, tp = sizes
    experts, _, hidden = up_weight.shape
    images, block = rows_all.shape[:2]
    half = block // tp
    lanes = 2 * D + 128
    count = images * SLOTS

    def whole(array):
        return pl.BlockSpec(array.shape, lambda e, place: (0,) * array.ndim)

    def adapter(size, split):
        return pl.BlockSpec(
            (SETS, 1, RANK, size),
            lambda e, place: (0, place[1] + e, 0, place[2] if split else 0),
        )

    second_shape = (tp, 2, experts, WIDTH, D // tp)
    partial_shape = (2, dp // 2, tp, images // dp, half, lanes)
    return pl.pallas_call(
        experts_kernel,
        grid_spec=pltpu.PrefetchScalarGridSpec(
            num_scalar_prefetch=1,
            grid=(experts,),
            in_specs=[
                whole(a)
                for a in (
                    rows_all, cot_all, ints, picks, picks_t, router_t, router_low, router_high_t,
                )
            ]
            + [
                pl.BlockSpec((1, D, hidden), lambda e, place: (e, 0, 0)),
                pl.BlockSpec((1, hidden, D), lambda e, place: (e, 0, 0)),
                adapter(D, False),
                adapter(hidden, True),
                adapter(hidden, True),
                adapter(D, False),
            ],
            out_specs=[
                pl.BlockSpec((1, 2, WIDTH, hidden), lambda e, place: (e, 0, 0, 0)),
                pl.BlockSpec(second_shape, lambda e, place: (0,) * 5),
                pl.BlockSpec(partial_shape, lambda e, place: (0,) * 6),
            ],
            scratch_shapes=[
                pltpu.VMEM((images, experts * SLOTS, block), BF16),
                pltpu.VMEM((experts, count, D), BF16),
                pltpu.VMEM((experts, count, D), BF16),
                pltpu.VMEM((experts, count, 128), F32),
                pltpu.VMEM((images, experts * SLOTS, lanes), BF16),
            ],
        ),
        out_shape=[
            jax.ShapeDtypeStruct((experts, 2, WIDTH, hidden), BF16),
            jax.ShapeDtypeStruct(second_shape, BF16),
            jax.ShapeDtypeStruct(partial_shape, BF16),
        ],
        compiler_params=pltpu.CompilerParams(vmem_limit_bytes=56 << 20),
    )(
        place, rows_all, cot_all, ints, picks, picks_t, router_t, router_low, router_high_t,
        up_weight, down_weight, first_a, first_b, second_a, second_b,
    )


def split_sum(values, ones):
    high = values.astype(BF16)
    low = (values - high.astype(F32)).astype(BF16)
    return matmul(high, ones) + matmul(low, ones)


def middle_kernel(
    place, received, hidden_in, expert_in, cotangent, live, picks, router_t, router_low,
    router_high, mixing, mixing_low, mixing_high, head_mix, mixing_lift, logs, gains,
    layer_out, grad_hidden_out, heads_out, stats_out, delta_out, tiles,
):
    images, half = expert_in.shape[:2]
    count = images * half
    start = pl.multiple_of(place[3], 16)
    total = received[0].astype(F32)
    for k in range(1, received.shape[0]):
        total = total + received[k].astype(F32)
    hidden = hidden_in[...]
    layer_out[...] = (hidden + total[:, :D]).astype(BF16).reshape(images, half, D)
    grad_probs = total[:, 2 * D : 2 * D + EXPERTS]
    own_sets = jnp.concatenate(
        [jnp.broadcast_to(picks[i : i + 1, :], (half, WIDTH)) for i in range(images)], axis=0
    )
    grad_output = jnp.concatenate(
        [cotangent[i, pl.ds(start, half), :] for i in range(images)], axis=0
    ).astype(F32) * live[...]
    rows = expert_in[...].reshape(count, D)
    router_lift = (times_transposed(rows, router_low[...]) * own_sets).astype(BF16)
    logits = times_transposed(rows, router_t[...]) + matmul(router_lift, router_high[...])
    powers = jnp.exp(logits - jnp.max(logits, axis=-1, keepdims=True))
    gate_probs = powers / jnp.sum(powers, axis=-1, keepdims=True)
    grad_logits = (
        gate_probs * (grad_probs - jnp.sum(grad_probs * gate_probs, axis=-1, keepdims=True))
    ).astype(BF16)
    grad_router_lift = (times_transposed(grad_logits, router_high[...]) * own_sets).astype(BF16)
    grad_expert_in = (
        total[:, D : 2 * D]
        + matmul(grad_logits, router_t[...])
        + matmul(grad_router_lift, router_low[...])
    )
    _, unit, factor = normalize(hidden, gains[2:3, :], gains[3:4, :])
    grad_hidden = grad_output + normalize_back(grad_expert_in, unit, factor, gains[2:3, :])
    grad_hidden_out[...] = grad_hidden
    grad_attended = grad_hidden.astype(BF16)
    grad_mixing_lift = (times_transposed(grad_attended, mixing_high[...]) * own_sets).astype(BF16)
    grad_heads = (
        matmul(grad_attended, mixing[...]) + matmul(grad_mixing_lift, mixing_low[...])
    ).astype(BF16)
    heads_out[...] = grad_heads.reshape(images, half, D)
    mix = head_mix[...]
    lane = lax.broadcasted_iota(jnp.int32, (D, 128), 1)
    head = lax.div(lax.broadcasted_iota(jnp.int32, (D, 128), 0), HD)
    ones = (lane == head).astype(F32).astype(BF16)
    delta = split_sum(grad_heads.astype(F32) * mix.astype(F32), ones)
    delta_out[...] = delta
    log = logs[...]
    for i in range(images):
        part = slice(i * half, (i + 1) * half)
        pad = jnp.zeros((128 - half, 128), F32)
        stats = [jnp.concatenate([v[part], pad], axis=0).T[:HEADS] for v in (log, delta)]
        row = 0
        for rest, number in zip(stats, (3, 2)):
            for _ in range(number):
                high = rest.astype(BF16)
                stats_out[i, row : row + HEADS, :] = high
                rest = rest - high.astype(F32)
                row += HEADS
    products = (
        inner_rows(grad_mixing_lift, mix),
        inner_rows(mixing_lift[...], grad_attended),
        inner_rows(grad_router_lift, rows),
    )
    tile = 0
    for product in products:
        for k in range(D // 128):
            tiles[tile * WIDTH : (tile + 1) * WIDTH, :] = product[
                :, k * 128 : (k + 1) * 128
            ].astype(BF16)
            tile += 1
    wide_logits = jnp.concatenate(
        [grad_logits, jnp.zeros((count, 128 - EXPERTS), BF16)], axis=1
    )
    tiles[tile * WIDTH : (tile + 1) * WIDTH, :] = inner_rows(router_lift, wide_logits).astype(BF16)


def middle(place, *operands):
    images, half = operands[2].shape[:2]
    count = images * half
    tiles = 3 * (D // 128) + 1
    return pl.pallas_call(
        middle_kernel,
        out_shape=(
            jax.ShapeDtypeStruct((images, half, D), BF16),
            jax.ShapeDtypeStruct((count, D), F32),
            jax.ShapeDtypeStruct((images, half, D), BF16),
            jax.ShapeDtypeStruct((images, 5 * HEADS, 128), BF16),
            jax.ShapeDtypeStruct((count, 128), F32),
            jax.ShapeDtypeStruct((tiles * WIDTH, 128), BF16),
        ),
        in_specs=[pl.BlockSpec(memory_space=pltpu.SMEM)] + [IN_VMEM] * len(operands),
        out_specs=(IN_VMEM,) * 6,
        compiler_params=pltpu.CompilerParams(vmem_limit_bytes=48 << 20),
    )(place, *operands)


def attend_back_kernel(
    place, joined, heads_all, stats_all, heads, logs, delta, live_keys, live_own, tokens, own_in,
    own_lift, grad_hidden, weights, attend_low, attend_high, picks, gains, tiles_in,
    tokens_grad, small, grads,
):
    images, seq = joined.shape[1:3]
    half = heads.shape[1]
    own_start = pl.multiple_of(place[0], 16)
    start = pl.multiple_of(place[3], 16)
    own = pl.ds(own_start, half)
    masks = half_masks()
    scale = HD**-0.5
    blocks = seq // half
    for i in range(images):
        part = slice(i * half, (i + 1) * half)
        open_keys = live_keys[i : i + 1, :] > 0
        open_own = live_own[part] > 0
        open_own = jnp.concatenate([open_own, open_own], axis=0)
        stats = jnp.concatenate(
            [stats_all[n, i][:, :half].astype(F32) for n in range(blocks)], axis=1
        )
        log_t = stats[0:HEADS] + stats[HEADS : 2 * HEADS] + stats[2 * HEADS : 3 * HEADS]
        delta_t = stats[3 * HEADS : 4 * HEADS] + stats[4 * HEADS :]
        log_own, delta_own = logs[part], delta[part]
        for j in range(HEADS // 2):
            lanes = slice(j * 2 * HD, (j + 1) * 2 * HD)
            q_all, k_all, v_all = (joined[p, i, :, lanes] for p in range(3))
            g_all = heads_all[i, :, lanes]

            def column(values):
                return jnp.concatenate(
                    [values[:, 2 * j : 2 * j + 1], values[:, 2 * j + 1 : 2 * j + 2]], axis=0
                )

            def row(values):
                return jnp.concatenate(
                    [
                        jnp.broadcast_to(values[2 * j + n : 2 * j + n + 1, :], (half, seq))
                        for n in range(2)
                    ],
                    axis=0,
                )

            q = stack_pair(joined[0, i, own, lanes], masks, scale)
            g = stack_pair(heads[i, :, lanes], masks)
            scores = jnp.where(open_keys, times_transposed(q, k_all), MASKED)
            probs = jnp.exp(scores - column(log_own))
            grad_probs = times_transposed(g, v_all)
            grad_scores = (probs * (grad_probs - column(delta_own))).astype(BF16)
            grads[0, part, lanes] = (
                join_pair(matmul(grad_scores, k_all), masks) * scale
            ).astype(BF16)
            k = stack_pair(joined[1, i, own, lanes], masks, scale)
            v = stack_pair(joined[2, i, own, lanes], masks)
            scores = jnp.where(open_own, times_transposed(k, q_all), MASKED)
            probs = jnp.exp(scores - row(log_t))
            grad_probs = times_transposed(v, g_all)
            grad_scores = (probs * (grad_probs - row(delta_t))).astype(BF16)
            grads[1, part, lanes] = (
                join_pair(matmul(grad_scores, q_all), masks) * scale
            ).astype(BF16)
            grads[2, part, lanes] = join_pair(matmul(probs.astype(BF16), g_all), masks).astype(
                BF16
            )
    own_sets = jnp.concatenate(
        [jnp.broadcast_to(picks[i : i + 1, :], (half, WIDTH)) for i in range(images)], axis=0
    )
    lift = times_transposed(grads[0], attend_high[0])
    into = times_transposed(grads[0], weights[0])
    for p in range(1, 3):
        lift = lift + times_transposed(grads[p], attend_high[p])
        into = into + times_transposed(grads[p], weights[p])
    lift = (lift * own_sets).astype(BF16)
    into = into + matmul(lift, attend_low[...])
    flat = jnp.concatenate(
        [tokens[i, pl.ds(start, half), :] for i in range(images)], axis=0
    ).astype(F32)
    _, unit, factor = normalize(flat, gains[0:1, :], gains[1:2, :])
    result = grad_hidden[...] + normalize_back(into, unit, factor, gains[0:1, :])
    tokens_grad[...] = result.astype(BF16).reshape(images, half, D)
    rows_in = own_in[...].reshape(images * half, D)
    lift_in = own_lift[...].reshape(images * half, WIDTH)
    products = [inner_rows(lift_in, grads[p]) for p in range(3)] + [inner_rows(lift, rows_in)]
    tile = 0
    for product in products:
        for n in range(D // 128):
            small[tile * WIDTH : (tile + 1) * WIDTH, :] = product[
                :, n * 128 : (n + 1) * 128
            ].astype(BF16)
            tile += 1
    done = tile * WIDTH + tiles_in.shape[0]
    small[tile * WIDTH : done, :] = tiles_in[...]
    if done < small.shape[0]:
        small[done:, :] = jnp.zeros((small.shape[0] - done, 128), BF16)


def attend_back(small_rows, place, *operands):
    images, half = operands[3].shape[:2]
    count = images * half
    return pl.pallas_call(
        attend_back_kernel,
        out_shape=(
            jax.ShapeDtypeStruct((images, half, D), BF16),
            jax.ShapeDtypeStruct((small_rows, 128), BF16),
        ),
        in_specs=[pl.BlockSpec(memory_space=pltpu.SMEM)] + [IN_VMEM] * len(operands),
        out_specs=(IN_VMEM,) * 2,
        scratch_shapes=[pltpu.VMEM((3, count, D), BF16)],
        compiler_params=pltpu.CompilerParams(vmem_limit_bytes=48 << 20),
    )(place, *operands)


def assemble_kernel(
    first, second, small, up, down_t, narrow_t, narrow,
    attend_down, attend_up, mixing_down, mixing_up, router_down, router_up,
):
    lanes, part = first.shape[-1], second.shape[-1]
    for tp in range(first.shape[1]):
        for half, out in ((0, up), (1, down_t)):
            out[:, 0, :, tp * lanes : (tp + 1) * lanes] = (
                first[0, tp, 0, half].astype(F32).reshape(SETS, RANK, lanes)
            )
        for half, out in ((0, narrow_t), (1, narrow)):
            out[:, 0, :, tp * part : (tp + 1) * part] = (
                second[0, tp, half, 0].astype(F32).reshape(SETS, RANK, part)
            )

    @pl.when(pl.program_id(0) == 0)
    def _():
        def tile(k):
            return small[k * WIDTH : (k + 1) * WIDTH, :].astype(F32).reshape(SETS, RANK, 128)

        count = D // 128
        for p in range(3):
            for k in range(count):
                attend_up[:, p, :, k * 128 : (k + 1) * 128] = tile(p * count + k)
        for p, out in enumerate((attend_down, mixing_down, mixing_up, router_down)):
            for k in range(count):
                out[:, :, k * 128 : (k + 1) * 128] = tile((p + 3) * count + k)
        router_up[...] = tile(7 * count)[:, :, :EXPERTS]


def assemble(first, second, small):
    dp, tp, experts, _, width, lanes = first.shape
    part = second.shape[-1]

    def split(e):
        return lax.div(e, experts), lax.rem(e, experts)

    def expert_out(size):
        return (
            jax.ShapeDtypeStruct((SETS, EXPERTS, RANK, size), F32),
            pl.BlockSpec((SETS, 1, RANK, size), lambda e: (0, e, 0, 0)),
        )

    def whole_out(*shape):
        return (
            jax.ShapeDtypeStruct(shape, F32),
            pl.BlockSpec(shape, lambda e: (0,) * len(shape)),
        )

    outs = (
        [expert_out(FF)] * 2
        + [expert_out(D)] * 2
        + [whole_out(SETS, RANK, D), whole_out(SETS, 3, RANK, D)]
        + [whole_out(SETS, RANK, D)] * 3
        + [whole_out(SETS, RANK, EXPERTS)]
    )
    return pl.pallas_call(
        assemble_kernel,
        grid=(EXPERTS,),
        out_shape=[out[0] for out in outs],
        in_specs=[
            pl.BlockSpec(
                (1, tp, 1, 2, width, lanes), lambda e: (split(e)[0], 0, split(e)[1], 0, 0, 0)
            ),
            pl.BlockSpec(
                (1, tp, 2, 1, width, part), lambda e: (split(e)[0], 0, 0, split(e)[1], 0, 0)
            ),
            pl.BlockSpec(small.shape, lambda e: (0, 0)),
        ],
        out_specs=[out[1] for out in outs],
        compiler_params=pltpu.CompilerParams(vmem_limit_bytes=32 << 20),
    )(first, second, small)


def per_device(
    sizes,
    tokens,
    cotangent,
    routes,
    slot_index,
    token_mask,
    image_mask,
    adapter_set,
    first_gain,
    first_shift,
    second_gain,
    second_shift,
    attend_weight,
    mixing_weight,
    router_weight,
    expand_weight,
    shrink_weight,
    attend_down,
    attend_up,
    mixing_down,
    mixing_up,
    router_down,
    router_up,
    expand_down,
    expand_up,
    shrink_down,
    shrink_up,
):
    dp_size, ctx_size, tp_size = sizes
    plane = dp_size * tp_size
    images, block = tokens.shape[:2]
    half = block // tp_size
    count = images * half
    seq = ctx_size * block
    all_images = dp_size * images
    local_experts, _, hidden_half = expand_weight.shape
    ctx_index, tp_index, dp_index = (lax.axis_index(a) for a in ("ctx", "tp", "dp"))
    place = jnp.stack(
        [
            ctx_index * block + tp_index * half,
            dp_index * local_experts,
            tp_index,
            tp_index * half,
        ]
    ).astype(jnp.int32)

    live = token_mask * image_mask[:, None]
    ints = jnp.concatenate(
        [
            jnp.transpose(routes, (0, 2, 1)),
            jnp.transpose(slot_index, (0, 2, 1)),
            live[:, None, :],
            jnp.broadcast_to(adapter_set[:, None, None], (images, 3, block)),
        ],
        axis=1,
    )
    tokens_all, weights_all, mixing_all, router_parts, cotangent_all, ints_all, ctx_ints = (
        start_gather(
            sizes,
            tokens,
            jnp.transpose(attend_weight, (1, 0, 2)),
            mixing_weight,
            jnp.transpose(router_weight, (1, 0)),
            cotangent,
            ints,
        )
    )
    router_t = jnp.transpose(router_parts, (1, 0, 2)).reshape(EXPERTS, D)

    attend_low = jnp.transpose(attend_down, (0, 2, 1)).reshape(WIDTH, D)
    attend_high = jnp.transpose(attend_up, (2, 0, 1, 3)).reshape(3, WIDTH, D)
    mixing_low = jnp.transpose(mixing_down, (0, 2, 1)).reshape(WIDTH, D)
    mixing_high = mixing_up.reshape(WIDTH, D)
    router_low = jnp.transpose(router_down, (0, 2, 1)).reshape(WIDTH, D)
    router_high = router_up.reshape(WIDTH, EXPERTS)
    gains = jnp.stack([first_gain, first_shift, second_gain, second_shift])

    def picker(sets):
        return (sets[:, None] == jnp.arange(WIDTH)[None, :] // RANK).astype(F32)

    own_picks = picker(adapter_set)
    key_live = jnp.transpose(ctx_ints[:, :, 4, :], (1, 0, 2)).reshape(images, seq)
    own_live = (
        lax.dynamic_slice_in_dim(live, tp_index * half, half, 1).reshape(count, 1).astype(F32)
    )
    joined, own_in, own_lift, head_mix, logs, mixing_lift, hidden, expert_in = attend(
        half, place, tokens_all, weights_all, mixing_all, key_live, own_picks, attend_low,
        attend_high, mixing_low, mixing_high, gains,
    )
    expert_in_all = expert_in_gather(sizes, expert_in)
    picks = picker(ints_all[:, 5, 0])
    first_grads, second_grads, partial = run_experts(
        sizes, place, expert_in_all, cotangent_all, ints_all, picks, picks[:, :, None], router_t,
        router_low, jnp.transpose(router_high), expand_weight, shrink_weight,
        jnp.transpose(expand_down, (0, 1, 3, 2)),
        expand_up,
        jnp.transpose(shrink_down, (0, 1, 3, 2)),
        shrink_up,
    )
    received = return_rows(
        sizes, partial.reshape(2, dp_size // 2, tp_size, count, partial.shape[-1])
    )
    layer_out, grad_hidden, heads, stats, delta, tiles = middle(
        place, received, hidden, expert_in, cotangent, own_live, own_picks, router_t, router_low,
        router_high, mixing_all, mixing_low, mixing_high, head_mix, mixing_lift, logs, gains,
    )
    heads_all, stats_all = heads_gather(sizes, heads, stats)
    needed = (7 * (D // 128) + 1) * WIDTH
    rows = -(-needed // (plane * 16)) * 16
    tokens_grad, small = attend_back(
        plane * rows, place, joined, heads_all, stats_all, heads, logs, delta, key_live, own_live,
        tokens, own_in, own_lift, grad_hidden, weights_all, attend_low, attend_high, own_picks,
        gains, tiles,
    )
    first_all, second_all, small_all, out_all, grad_all = finish(
        sizes, first_grads, second_grads, small.reshape(plane, rows, 128), layer_out, tokens_grad
    )
    wide = assemble(first_all, second_all, small_all.reshape(plane * rows, 128))

    def flipped(values):
        return jnp.swapaxes(values, -1, -2)

    return (
        out_all,
        grad_all,
        flipped(wide[4]),
        jnp.transpose(wide[5], (0, 2, 1, 3)),
        flipped(wide[6]),
        wide[7],
        flipped(wide[8]),
        wide[9],
        flipped(wide[2]),
        wide[0],
        flipped(wide[1]),
        wide[3],
    )


def solution(mesh):
    sizes = (mesh.shape["dp"], mesh.shape["ctx"], mesh.shape["tp"])
    tokens_spec = P("dp", "ctx", None)
    in_specs = (
        (tokens_spec,) * 4
        + (P("dp", "ctx"), P("dp"), P("dp"))
        + (P(),) * 4
        + (P("dp", None, "tp"), P("dp", "tp"), P("dp", None))
        + (P("dp", None, "tp"), P("dp", "tp", None))
        + (P(),) * 10
    )
    out_specs = (tokens_spec,) * 2 + (P(),) * 10
    return jax.shard_map(
        functools.partial(per_device, sizes),
        mesh=mesh,
        in_specs=in_specs,
        out_specs=out_specs,
        check_vma=False,
    )
```

```python
import functools

import jax
import jax.numpy as jnp
from jax import lax
from jax.experimental import pallas as pl
from jax.experimental.pallas import tpu as pltpu
from jax.sharding import PartitionSpec as P

D = 512
HEADS = 8
HD = 64
FF = 2048
EXPERTS = 16
TOP = 2
RANK = 16
SETS = 4
CAP = 30
SLOTS = 32
WIDTH = SETS * RANK

EPSILON = 1e-06
MASKED = -1e30
SQRT_HALF = 0.7071067811865476
INV_ROOT_TWO_PI = 0.3989422804014327
F32 = jnp.float32
BF16 = jnp.bfloat16
MESH = pl.DeviceIdType.MESH
ANY = pl.BlockSpec(memory_space=pl.ANY)
IN_VMEM = pl.BlockSpec(memory_space=pltpu.VMEM)


def matmul(left_side, right_side):
    return jnp.dot(left_side, right_side, preferred_element_type=F32)


def inner_rows(left_side, right_side):
    return lax.dot_general(
        left_side, right_side, (((0,), (0,)), ((), ())), preferred_element_type=F32
    )


def times_transposed(left_side, right_side):
    return lax.dot_general(
        left_side, right_side, (((1,), (1,)), ((), ())), preferred_element_type=F32
    )


def normalize(values, gain_row, shift_row):
    centred = values - jnp.mean(values, axis=-1, keepdims=True)
    spread = jnp.mean(centred * centred, axis=-1, keepdims=True)
    factor = lax.rsqrt(spread + EPSILON)
    normed = centred * factor
    return (normed * gain_row + shift_row, normed, factor)


def normalize_back(grad_out, normed, factor, gain_row):
    scaled = grad_out * gain_row
    return factor * (
        scaled
        - jnp.mean(scaled, axis=-1, keepdims=True)
        - normed * jnp.mean(scaled * normed, axis=-1, keepdims=True)
    )


class Wire:
    def __init__(self, send, recv, local=None):
        self.send, self.recv, self.local = send, recv, local
        self.used = self.used_local = 0

    def copy(self, src, dst, device):
        k = self.used
        self.used += 1
        return pltpu.make_async_remote_copy(
            src_ref=src,
            dst_ref=dst,
            send_sem=self.send.at[k],
            recv_sem=self.recv.at[k],
            device_id=device,
            device_id_type=MESH,
        )

    def near(self, src, dst):
        k = self.used_local
        self.used_local += 1
        return pltpu.make_async_copy(src, dst, self.local.at[k])


class Place:
    def __init__(self, sizes):
        self.dp_size, self.ctx_size, self.tp_size = sizes
        self.chips = self.dp_size // 2
        self.dp = lax.axis_index("dp")
        self.ctx = lax.axis_index("ctx")
        self.tp = lax.axis_index("tp")
        self.chip = lax.div(self.dp, 2)
        self.core = lax.rem(self.dp, 2)
        self.sibling = self.chip * 2 + (1 - self.core)

    def ahead(self, i, j):
        return (
            lax.rem(self.chip + i, self.chips) * 2 + self.core,
            lax.rem(self.tp + j, self.tp_size),
        )

    def behind(self, i, j):
        return self.ahead(self.chips - i, self.tp_size - j)

    def offsets(self, over_tp=True):
        return [
            (i, j)
            for i in range(self.chips)
            for j in range(self.tp_size if over_tp else 1)
            if i or j
        ]

    def greet(self, with_ctx):
        barrier = pltpu.get_barrier_semaphore()
        count = 0
        for i, j in self.offsets():
            dp, tp = self.ahead(i, j)
            pl.semaphore_signal(
                barrier, inc=1, device_id={"dp": dp, "tp": tp}, device_id_type=MESH
            )
            count += 1
        pl.semaphore_signal(
            barrier, inc=1, device_id={"dp": self.sibling}, device_id_type=MESH
        )
        count += 1
        if with_ctx:
            for i in range(1, self.ctx_size):
                pl.semaphore_signal(
                    barrier,
                    inc=1,
                    device_id={"ctx": lax.rem(self.ctx + i, self.ctx_size)},
                    device_id_type=MESH,
                )
                count += 1
        pl.semaphore_wait(barrier, count)


def gather_plane_start(place, wire, items):
    flights, done = [], []
    for source, slot, over_tp in items:
        for i, j in place.offsets(over_tp):
            dp, tp = place.ahead(i, j)
            copy = wire.copy(source, slot(place.dp, place.tp), {"dp": dp, "tp": tp})
            copy.start()
            flights.append((copy, slot(*place.behind(i, j))))
    for source, slot, _ in items:
        copy = wire.copy(source, slot(place.dp, place.tp), {"dp": place.sibling})
        copy.start()
        done.append(copy)
        copy = wire.near(source, slot(place.dp, place.tp))
        copy.start()
        done.append(copy)
    return flights, done


def gather_plane_end(place, wire, flights, done):
    for copy, got in flights:
        copy.wait_recv()
        onward = wire.copy(got, got, {"dp": place.sibling})
        onward.start()
        done.append(onward)
    for copy, _ in flights:
        copy.wait_send()
    for copy in done:
        copy.wait()


def plane_copies(place, flags):
    sent = sum(len(place_offsets(place, f)) for f in flags)
    return sent, len(flags)


def place_offsets(sizes, over_tp):
    chips = sizes[0] // 2
    return chips * (sizes[2] if over_tp else 1) - 1


def semaphores(remote, near):
    return [
        pltpu.SemaphoreType.DMA((remote,)),
        pltpu.SemaphoreType.DMA((remote,)),
        pltpu.SemaphoreType.DMA((near,)),
    ]


def comm_params(number):
    return pltpu.CompilerParams(
        collective_id=number, has_side_effects=True, vmem_limit_bytes=48 << 20
    )


def gather_ctx_start(place, wire, source, slot):
    flights = []
    for i in range(1, place.ctx_size):
        copy = wire.copy(
            source,
            slot(place.ctx, place.tp),
            {"ctx": lax.rem(place.ctx + i, place.ctx_size)},
        )
        copy.start()
        flights.append(
            (copy, slot(lax.rem(place.ctx - i + place.ctx_size, place.ctx_size), place.tp))
        )
    return flights


def start_kernel(
    sizes, tokens, weights, mixing, router, cotangent, ints,
    tokens_all, weights_all, mixing_all, router_all, cotangent_all, ints_all, ctx_ints,
    send, recv, local,
):
    place = Place(sizes)
    wire = Wire(send, recv, local)
    place.greet(True)
    rows, lanes = mixing.shape
    half = tokens.shape[1] // place.tp_size
    other_tp = lax.rem(place.tp + 1, 2)

    def token_slot(ctx, tp):
        start = pl.multiple_of(ctx * tokens.shape[1] + tp * half, 16)
        return tokens_all.at[:, pl.ds(start, half), :]

    def at_rows(dp):
        return pl.ds(pl.multiple_of(dp * rows, 16), rows)

    def at_lanes(tp):
        return pl.ds(pl.multiple_of(tp * lanes, 128), lanes)

    mine = tokens.at[:, pl.ds(pl.multiple_of(place.tp * half, 16), half), :]
    token_flights = gather_ctx_start(place, wire, mine, token_slot)
    int_flights = gather_ctx_start(place, wire, ints, lambda ctx, tp: ctx_ints.at[ctx])
    flights, done = gather_plane_start(
        place,
        wire,
        [
            (weights, lambda dp, tp: weights_all.at[:, at_rows(dp), at_lanes(tp)], True),
            (mixing, lambda dp, tp: mixing_all.at[at_rows(dp), at_lanes(tp)], True),
            (ints, lambda dp, tp: ints_all.at[pl.ds(dp * 2, 2)], False),
            (router, lambda dp, tp: router_all.at[dp], False),
            (cotangent, lambda dp, tp: cotangent_all.at[pl.ds(dp * 2, 2)], False),
        ],
    )
    whole = tokens_all.at[:, pl.ds(pl.multiple_of(place.ctx * tokens.shape[1], 16), tokens.shape[1]), :]
    for src, dst in ((tokens, whole), (ints, ctx_ints.at[place.ctx])):
        copy = wire.near(src, dst)
        copy.start()
        done.append(copy)
    for copy, got in token_flights:
        copy.wait_recv()
        onward = wire.copy(got, got, {"tp": other_tp})
        onward.start()
        done.append(onward)
    for copy, _ in int_flights:
        copy.wait()
    for copy, _ in token_flights:
        copy.wait_send()
    gather_plane_end(place, wire, flights, done)


def start_gather(sizes, tokens, weights, mixing, router, cotangent, ints):
    dp, ctx, tp = sizes
    rows, lanes = mixing.shape
    images, block = tokens.shape[:2]
    full, part = place_offsets(sizes, True), place_offsets(sizes, False)
    remote = 3 * (ctx - 1) + 4 * full + 6 * part + 5
    return pl.pallas_call(
        functools.partial(start_kernel, sizes),
        out_shape=(
            jax.ShapeDtypeStruct((images, ctx * block, D), BF16),
            jax.ShapeDtypeStruct((3, dp * rows, tp * lanes), BF16),
            jax.ShapeDtypeStruct((dp * rows, tp * lanes), BF16),
            jax.ShapeDtypeStruct((dp,) + router.shape, BF16),
            jax.ShapeDtypeStruct((dp * images, block, D), BF16),
            jax.ShapeDtypeStruct((dp * images,) + ints.shape[1:], jnp.int32),
            jax.ShapeDtypeStruct((ctx,) + ints.shape, jnp.int32),
        ),
        in_specs=[ANY] * 6,
        out_specs=(ANY,) * 7,
        scratch_shapes=semaphores(remote, 7),
        compiler_params=comm_params(1),
    )(tokens, weights, mixing, router, cotangent, ints)


def expert_in_kernel(sizes, own, gathered, send, recv, local):
    place = Place(sizes)
    wire = Wire(send, recv, local)
    place.greet(False)
    half = own.shape[1]

    def slot(dp, tp):
        return gathered.at[pl.ds(dp * 2, 2), pl.ds(pl.multiple_of(tp * half, 16), half), :]

    flights, done = gather_plane_start(place, wire, [(own, slot, True)])
    gather_plane_end(place, wire, flights, done)


def expert_in_gather(sizes, own):
    dp, ctx, tp = sizes
    images, half = own.shape[:2]
    return pl.pallas_call(
        functools.partial(expert_in_kernel, sizes),
        out_shape=jax.ShapeDtypeStruct((dp * images, tp * half, D), BF16),
        in_specs=[ANY],
        out_specs=ANY,
        scratch_shapes=semaphores(2 * place_offsets(sizes, True) + 1, 1),
        compiler_params=comm_params(2),
    )(own)


def add_rounded(*parts):
    total = parts[0].astype(F32)
    for part in parts[1:]:
        total = total + part.astype(F32)
    return total.astype(BF16)


def put_lanes(columns, width):
    lane = lax.broadcasted_iota(jnp.int32, (columns[0].shape[0], width), 1)
    total = jnp.zeros((columns[0].shape[0], width), F32)
    for k, column in enumerate(columns):
        total = jnp.where(lane == k, column, total)
    return total


def half_masks():
    lane = lax.broadcasted_iota(jnp.int32, (1, 2 * HD), 1)
    even = (lane < HD).astype(F32)
    return even, 1.0 - even


def stack_pair(rows, masks, factor=1.0):
    wide = rows.astype(F32) * factor
    return jnp.concatenate([wide * masks[0], wide * masks[1]], axis=0).astype(BF16)


def join_pair(rows, masks):
    half = rows.shape[0] // 2
    return rows[:half] * masks[0] + rows[half:] * masks[1]


def attend_kernel(
    place, tokens, weights, mixing, live_keys, picks, attend_low, attend_high, mixing_low,
    mixing_high, gains,
    joined, own_in, own_lift, head_mix_out, log_out, mixing_lift_out, hidden_out, expert_in_out,
    lift_scratch,
):
    images, seq = tokens.shape[:2]
    half = head_mix_out.shape[0] // images
    own_start = pl.multiple_of(place[0], 16)
    block = seq // 2

    def project(k, _):
        i, r = lax.div(k, 2), pl.multiple_of(lax.rem(k, 2) * block, 16)
        rows = tokens[i, pl.ds(r, block), :].astype(F32)
        normed = normalize(rows, gains[0:1, :], gains[1:2, :])[0].astype(BF16)
        lift = (times_transposed(normed, attend_low[...]) * picks[pl.ds(i, 1), :]).astype(BF16)
        lift_scratch[i, pl.ds(r, block), :] = lift
        for p in range(3):
            joined[p, i, pl.ds(r, block), :] = (
                matmul(normed, weights[p]) + matmul(lift, attend_high[p])
            ).astype(BF16)
        return 0

    lax.fori_loop(0, images * 2, project, 0)
    masks = half_masks()
    scale = HD**-0.5
    mix_parts = []
    for i in range(images):
        open_keys = live_keys[i : i + 1, :] > 0
        rows = tokens[i, pl.ds(own_start, half), :].astype(F32)
        own_in[i] = normalize(rows, gains[0:1, :], gains[1:2, :])[0].astype(BF16)
        own_lift[i] = lift_scratch[i, pl.ds(own_start, half), :]
        logs = []
        for j in range(HEADS // 2):
            lanes = slice(j * 2 * HD, (j + 1) * 2 * HD)
            q = stack_pair(joined[0, i, pl.ds(own_start, half), lanes], masks, scale)
            scores = times_transposed(q, joined[1, i, :, lanes])
            scores = jnp.where(open_keys, scores, MASKED)
            top = jnp.max(scores, axis=-1, keepdims=True)
            powers = jnp.exp(scores - top)
            total = jnp.sum(powers, axis=-1, keepdims=True)
            weights_att = (powers * (1.0 / total)).astype(BF16)
            mixed = join_pair(matmul(weights_att, joined[2, i, :, lanes]), masks)
            head_mix_out[i * half : (i + 1) * half, lanes] = mixed.astype(BF16)
            log = jnp.maximum(top + jnp.log(total), -1e29)
            logs += [log[:half], log[half:]]
        log_out[i * half : (i + 1) * half, :] = put_lanes(logs, 128)
        mix = head_mix_out[i * half : (i + 1) * half, :]
        lift = (times_transposed(mix, mixing_low[...]) * picks[i : i + 1, :]).astype(BF16)
        mixing_lift_out[i * half : (i + 1) * half, :] = lift
        hidden = rows + times_transposed(mix, mixing[...]) + matmul(lift, mixing_high[...])
        hidden_out[i * half : (i + 1) * half, :] = hidden
        expert_in_out[i] = normalize(hidden, gains[2:3, :], gains[3:4, :])[0].astype(BF16)


def attend(half, place, *operands):
    images, seq = operands[0].shape[:2]
    count = images * half

    def out(*shape, dtype=BF16):
        return jax.ShapeDtypeStruct(shape, dtype)

    return pl.pallas_call(
        attend_kernel,
        out_shape=(
            out(3, images, seq, D),
            out(images, half, D),
            out(images, half, WIDTH),
            out(count, D),
            out(count, 128, dtype=F32),
            out(count, WIDTH),
            out(count, D, dtype=F32),
            out(images, half, D),
        ),
        in_specs=[pl.BlockSpec(memory_space=pltpu.SMEM)] + [IN_VMEM] * len(operands),
        out_specs=(IN_VMEM,) * 8,
        scratch_shapes=[pltpu.VMEM((images, seq, WIDTH), BF16)],
        compiler_params=pltpu.CompilerParams(vmem_limit_bytes=48 << 20),
    )(place, *operands)


def experts_kernel(
    place, rows_all, cot_all, ints, picks, picks_t, router_t, router_low, router_high_t,
    up_weight, down_weight, first_a, first_b, second_a, second_b,
    first_grads, second_grads, partial,
    table, rows_in, grad_slots, gates, payload,
):
    e = pl.program_id(0)
    last = pl.num_programs(0) - 1
    experts, count = rows_in.shape[:2]
    images, block = rows_all.shape[:2]
    owned = place[1]
    slots = experts * SLOTS
    half = block // second_grads.shape[0]

    @pl.when(e == 0)
    def _():
        def dispatch(i, _):
            rows = rows_all[i]
            lift = times_transposed(router_low[...], rows) * picks_t[i]
            logits = times_transposed(router_t[...], rows) + matmul(
                router_high_t[...], lift.astype(BF16)
            )
            powers = jnp.exp(logits - jnp.max(logits, axis=0, keepdims=True))
            probs = powers / jnp.sum(powers, axis=0, keepdims=True)
            numbers = ints[i]
            expert = lax.broadcasted_iota(jnp.int32, (EXPERTS, block), 0)
            slot = lax.broadcasted_iota(jnp.int32, (slots, block), 0)
            hot = jnp.zeros((slots, block), F32)
            gated = jnp.zeros((slots, block), F32)
            for k in range(TOP):
                route, place_in = numbers[k : k + 1, :], numbers[TOP + k : TOP + k + 1, :]
                gate = jnp.sum(jnp.where(expert == route, probs, 0.0), axis=0, keepdims=True)
                local = route - owned
                here = (local >= 0) & (local < experts) & (place_in < CAP)
                target = jnp.where(here, local * SLOTS + place_in, -1)
                match = slot == target
                hot = jnp.where(match, 1.0, hot)
                gated = jnp.where(match, gate, gated)
            hot = hot.astype(BF16)
            table[i] = hot
            gate_column = jnp.broadcast_to(jnp.sum(gated, axis=1, keepdims=True), (slots, 128))
            picked = matmul(hot, rows).astype(BF16)
            grads = matmul(hot, cot_all[i]).astype(BF16)
            at = pl.ds(pl.multiple_of(i * SLOTS, SLOTS), SLOTS)
            for n in range(experts):
                part = slice(n * SLOTS, (n + 1) * SLOTS)
                rows_in[n, at, :] = picked[part]
                grad_slots[n, at, :] = grads[part]
                gates[n, at, :] = gate_column[part]
            return 0

        lax.fori_loop(0, images, dispatch, 0)

    rows = rows_in[e]
    grads = grad_slots[e].astype(F32)
    gate = gates[e][:, 0:1]
    sets = jnp.broadcast_to(picks[...][:, None, :], (images, SLOTS, WIDTH)).reshape(count, WIDTH)
    a_first, b_first = first_a[:, 0].reshape(WIDTH, D), first_b[:, 0].reshape(WIDTH, -1)
    a_second, b_second = second_a[:, 0].reshape(WIDTH, -1), second_b[:, 0].reshape(WIDTH, D)
    lifted = (times_transposed(rows, a_first) * sets).astype(BF16)
    before = matmul(rows, up_weight[0]) + matmul(lifted, b_first)
    phi = 0.5 * (1.0 + lax.erf(before * SQRT_HALF))
    active = (before * phi).astype(BF16)
    slope = phi + before * (INV_ROOT_TWO_PI * jnp.exp(-0.5 * before * before))
    lowered = (times_transposed(active, a_second) * sets).astype(BF16)
    out = matmul(active, down_weight[0]) + matmul(lowered, b_second)
    grad_out = (grads * gate).astype(BF16)
    grad_lowered = (times_transposed(grad_out, b_second) * sets).astype(BF16)
    grad_active = times_transposed(grad_out, down_weight[0]) + matmul(grad_lowered, a_second)
    grad_before = (grad_active * slope).astype(BF16)
    grad_lifted = (times_transposed(grad_before, b_first) * sets).astype(BF16)
    grad_rows = times_transposed(grad_before, up_weight[0]) + matmul(grad_lifted, a_first)
    first_grads[0, 0] = inner_rows(lifted, grad_before).astype(BF16)
    first_grads[0, 1] = inner_rows(grad_lowered, active).astype(BF16)
    pieces = second_grads.shape[0]
    lanes = D // pieces
    for number, value in (
        (0, inner_rows(grad_lifted, rows)),
        (1, inner_rows(lowered, grad_out)),
    ):
        for t in range(pieces):
            second_grads[t, number, e] = value[:, t * lanes : (t + 1) * lanes].astype(BF16)
    lane = lax.broadcasted_iota(jnp.int32, (count, 128), 1)
    gate_grads = jnp.sum(out * grads, axis=1, keepdims=True)
    gated_out = (out * gate).astype(BF16).reshape(images, SLOTS, D)
    grad_rows = grad_rows.astype(BF16).reshape(images, SLOTS, D)
    gate_grads = jnp.where(lane == owned + e, gate_grads, 0.0).astype(BF16)
    gate_grads = gate_grads.reshape(images, SLOTS, 128)
    at = pl.ds(pl.multiple_of(e * SLOTS, SLOTS), SLOTS)
    payload[:, at, 0:D] = grad_rows
    payload[:, at, D : D + 128] = gate_grads
    payload[:, at, D + 128 :] = gated_out

    @pl.when(e == last)
    def _():
        def combine(i, _):
            dp, local = lax.div(i, 2), lax.rem(i, 2)
            rows = inner_rows(table[i], payload[i]).astype(BF16)
            core, chip = lax.rem(dp, 2), lax.div(dp, 2)
            for t in range(partial.shape[2]):
                partial[core, chip, t, local] = rows[t * half : (t + 1) * half]
            return 0

        lax.fori_loop(0, images, combine, 0)


def run_experts(
    sizes, place, rows_all, cot_all, ints, picks, picks_t, router_t, router_low, router_high_t,
    up_weight, down_weight, first_a, first_b, second_a, second_b,
):
    dp, ctx, tp = sizes
    experts, _, hidden = up_weight.shape
    images, block = rows_all.shape[:2]
    half = block // tp
    lanes = 2 * D + 128
    count = images * SLOTS

    def whole(array):
        return pl.BlockSpec(array.shape, lambda e, place: (0,) * array.ndim)

    def adapter(size, split):
        return pl.BlockSpec(
            (SETS, 1, RANK, size),
            lambda e, place: (0, place[1] + e, 0, place[2] if split else 0),
        )

    second_shape = (tp, 2, experts, WIDTH, D // tp)
    partial_shape = (2, dp // 2, tp, images // dp, half, lanes)
    return pl.pallas_call(
        experts_kernel,
        grid_spec=pltpu.PrefetchScalarGridSpec(
            num_scalar_prefetch=1,
            grid=(experts,),
            in_specs=[
                whole(a)
                for a in (
                    rows_all, cot_all, ints, picks, picks_t, router_t, router_low, router_high_t,
                )
            ]
            + [
                pl.BlockSpec((1, D, hidden), lambda e, place: (e, 0, 0)),
                pl.BlockSpec((1, hidden, D), lambda e, place: (e, 0, 0)),
                adapter(D, False),
                adapter(hidden, True),
                adapter(hidden, True),
                adapter(D, False),
            ],
            out_specs=[
                pl.BlockSpec((1, 2, WIDTH, hidden), lambda e, place: (e, 0, 0, 0)),
                pl.BlockSpec(second_shape, lambda e, place: (0,) * 5),
                pl.BlockSpec(partial_shape, lambda e, place: (0,) * 6),
            ],
            scratch_shapes=[
                pltpu.VMEM((images, experts * SLOTS, block), BF16),
                pltpu.VMEM((experts, count, D), BF16),
                pltpu.VMEM((experts, count, D), BF16),
                pltpu.VMEM((experts, count, 128), F32),
                pltpu.VMEM((images, experts * SLOTS, lanes), BF16),
            ],
        ),
        out_shape=[
            jax.ShapeDtypeStruct((experts, 2, WIDTH, hidden), BF16),
            jax.ShapeDtypeStruct(second_shape, BF16),
            jax.ShapeDtypeStruct(partial_shape, BF16),
        ],
        compiler_params=pltpu.CompilerParams(vmem_limit_bytes=56 << 20),
    )(
        place, rows_all, cot_all, ints, picks, picks_t, router_t, router_low, router_high_t,
        up_weight, down_weight, first_a, first_b, second_a, second_b,
    )


def split_sum(values, ones):
    high = values.astype(BF16)
    low = (values - high.astype(F32)).astype(BF16)
    return matmul(high, ones) + matmul(low, ones)


class Chain:
    def __init__(self, place, wire, sources, slots):
        self.place, n = place, place.ctx_size
        self.steps = n - 1
        other_tp = lax.rem(place.tp + 1, 2)
        self.right, self.left, self.over_right, self.over_left = {}, {}, {}, {}
        self.own = []
        for source, slot in zip(sources, slots):
            here = slot(place.ctx, place.tp)
            self.own.append(wire.copy(source, here, {"tp": other_tp}))
            self.own.append(wire.near(source, here))
        for s in range(1, n):
            back = [slot(jnp.maximum(place.ctx - (s - 1), 0), place.tp) for slot in slots]
            ahead = [slot(jnp.minimum(place.ctx + (s - 1), n - 1), place.tp) for slot in slots]
            got_right = [slot(jnp.maximum(place.ctx - s, 0), place.tp) for slot in slots]
            got_left = [slot(jnp.minimum(place.ctx + s, n - 1), place.tp) for slot in slots]
            to_right = {"ctx": jnp.minimum(place.ctx + 1, n - 1)}
            to_left = {"ctx": jnp.maximum(place.ctx - 1, 0)}
            self.right[s] = [
                wire.copy(a if s == 1 else b, b, to_right) for a, b in zip(sources, back)
            ]
            self.left[s] = [
                wire.copy(a if s == 1 else b, b, to_left) for a, b in zip(sources, ahead)
            ]
            self.over_right[s] = [wire.copy(b, b, {"tp": other_tp}) for b in got_right]
            self.over_left[s] = [wire.copy(b, b, {"tp": other_tp}) for b in got_left]

    def sends_right(self, s):
        return jnp.logical_and(self.place.ctx >= s - 1, self.place.ctx < self.steps)

    def sends_left(self, s):
        return jnp.logical_and(self.place.ctx <= self.steps + 1 - s, self.place.ctx > 0)

    def gets_right(self, s):
        return self.place.ctx >= s

    def gets_left(self, s):
        return self.place.ctx <= self.steps - s

    @staticmethod
    def all_of(copies, verb):
        for copy in copies:
            getattr(copy, verb)()

    def start(self):
        pl.when(self.sends_right(1))(lambda: self.all_of(self.right[1], "start"))
        pl.when(self.sends_left(1))(lambda: self.all_of(self.left[1], "start"))
        self.all_of(self.own, "start")

    def step(self, s):
        def passed(got, over, onward, sends):
            def run():
                self.all_of(got[s], "wait_recv")
                if s < self.steps:
                    pl.when(sends(s + 1))(lambda: self.all_of(onward[s + 1], "start"))
                self.all_of(over[s], "start")

            return run

        pl.when(self.gets_right(s))(
            passed(self.right, self.over_right, self.right, self.sends_right)
        )
        pl.when(self.gets_left(s))(passed(self.left, self.over_left, self.left, self.sends_left))

    def end(self):
        self.all_of(self.own, "wait")
        for s in range(1, self.steps + 1):
            pl.when(self.gets_right(s))(lambda: self.all_of(self.over_right[s], "wait"))
            pl.when(self.gets_left(s))(lambda: self.all_of(self.over_left[s], "wait"))

    def drain(self):
        for s in range(1, self.steps + 1):
            pl.when(self.sends_right(s))(lambda: self.all_of(self.right[s], "wait_send"))
            pl.when(self.sends_left(s))(lambda: self.all_of(self.left[s], "wait_send"))

    @staticmethod
    def remote(n, arrays):
        return arrays * (1 + 4 * (n - 1))


def back_kernel(
    sizes,
    partial, first, second, hidden_in, expert_in, cotangent, live, picks, router_t, router_low,
    router_high, mixing, mixing_low, mixing_high, head_mix, mixing_lift, logs, gains, joined,
    live_keys, tokens, own_in, own_lift, weights, attend_low, attend_high,
    first_all, second_all, early_all, late_all, out_all, grad_all,
    from_sibling, paired, received, second_got, early_got, late_got,
    second_sum, early_sum, late_sum, early, late,
    first_end, second_end, early_end, late_end,
    first_mid, second_mid, early_mid, late_mid,
    first_stage, second_stage, early_stage, late_stage,
    first_final, second_final, early_final, late_final,
    out_own, grad_own, grad_hidden, heads, stats, delta, heads_all, stats_all, grads,
    send, recv, local,
):
    place = Place(sizes)
    wire = Wire(send, recv, local)
    plane = place.dp_size * place.tp_size
    me = place.dp * place.tp_size + place.tp
    is_mid = jnp.logical_and(place.ctx >= 1, place.ctx <= 2)
    is_end = jnp.logical_not(is_mid)
    inner = lax.div(place.ctx, 2)
    outer_half = 1 - inner
    partner = jnp.where(is_mid, inner * 3, 1 + inner)
    other_mid = 2 - inner
    other_tp = lax.rem(place.tp + 1, 2)
    images, half = expert_in.shape[:2]
    count = images * half
    experts = first.shape[0]
    start = pl.multiple_of(place.tp * half, 16)
    own_start = pl.multiple_of(place.ctx * tokens.shape[1] + place.tp * half, 16)
    critical = D + 128

    barrier = pltpu.get_barrier_semaphore()
    peers = []
    for k in range(1, plane):
        peer = lax.rem(me + k, plane)
        peers.append((lax.div(peer, place.tp_size), lax.rem(peer, place.tp_size)))
        pl.semaphore_signal(
            barrier, inc=1, device_id={"dp": peers[-1][0], "tp": peers[-1][1]}, device_id_type=MESH
        )
    pl.semaphore_signal(barrier, inc=1, device_id={"ctx": partner}, device_id_type=MESH)

    @pl.when(is_mid)
    def _():
        pl.semaphore_signal(barrier, inc=1, device_id={"ctx": other_mid}, device_id_type=MESH)

    pl.semaphore_wait(barrier, plane + jnp.where(is_mid, 1, 0))

    chunks = [
        (
            first.at[e], first_end.at[e], first_mid.at[e], first_stage.at[e],
            first_final.at[e], functools.partial(lambda e, dp, tp: first_all.at[dp, tp, e], e),
        )
        for e in range(experts)
    ]
    chunks += [
        (second_sum, second_end, second_mid, second_stage, second_final,
         lambda dp, tp: second_all.at[dp, tp]),
        (early_sum, early_end, early_mid, early_stage, early_final,
         lambda dp, tp: early_all.at[dp, tp]),
        (late_sum, late_end, late_mid, late_stage, late_final,
         lambda dp, tp: late_all.at[dp, tp]),
    ]
    flows = []
    for mine, end, mid, stage, final, slot in chunks:
        flows.append(
            dict(
                outer=wire.copy(mine.at[outer_half], end.at[outer_half], {"ctx": partner}),
                inner=wire.copy(mine.at[inner], end.at[inner], {"ctx": partner}),
                cross=wire.copy(stage, mid, {"ctx": other_mid}),
                back=wire.copy(final.at[inner], final.at[inner], {"ctx": partner}),
                share=wire.copy(final.at[inner], final.at[inner], {"ctx": other_mid}),
                pass_on=wire.copy(final.at[outer_half], final.at[outer_half], {"ctx": partner}),
            )
        )
    late_waits = []

    def send_end(k):
        @pl.when(is_end)
        def _():
            flows[k]["outer"].start()
            flows[k]["inner"].start()

    def mid_first(k):
        mine, end, mid, stage, final, slot = chunks[k]

        @pl.when(is_mid)
        def _():
            flows[k]["outer"].wait_recv()
            stage[...] = add_rounded(mine[outer_half], end[outer_half])
            flows[k]["cross"].start()

    def mid_second(k):
        mine, end, mid, stage, final, slot = chunks[k]

        @pl.when(is_mid)
        def _():
            flows[k]["inner"].wait_recv()
            flows[k]["cross"].wait_recv()
            final[inner] = add_rounded(mine[inner], end[inner], mid[...])
            flows[k]["share"].start()
            flows[k]["back"].start()

    squared = place.chips == 2 and place.tp_size == 2
    plane_flights, diagonals = {}, {}

    def settle(k):
        @pl.when(is_mid)
        def _():
            flows[k]["share"].wait_recv()
            flows[k]["pass_on"].start()

        @pl.when(is_end)
        def _():
            flows[k]["back"].wait_recv()
            flows[k]["pass_on"].wait_recv()

        final, slot = chunks[k][4], chunks[k][5]
        spot = slot(place.dp, place.tp)
        plane_flights[k] = []
        for i, j in place.offsets():
            if squared and i and j:
                continue
            dp, tp = place.ahead(i, j)
            copy = wire.copy(final, spot, {"dp": dp, "tp": tp})
            copy.start()
            plane_flights[k].append((copy, i, j))
        for copy in (wire.copy(final, spot, {"dp": place.sibling}), wire.near(final, spot)):
            copy.start()
            late_waits.append(copy)

    def to_sibling(ref):
        copy = wire.copy(ref, ref, {"dp": place.sibling})
        copy.start()
        late_waits.append(copy)

    def forward(k):
        slot = chunks[k][5]
        for copy, i, j in sorted(plane_flights[k], key=lambda f: f[1]):
            copy.wait_recv()
            got = slot(*place.behind(i, j))
            if squared and j:
                dp, tp = place.ahead(1, 0)
                diagonals[k] = wire.copy(got, got, {"dp": dp, "tp": tp})
                diagonals[k].start()
            to_sibling(got)

    def diagonal(k):
        if squared:
            diagonals[k].wait_recv()
            to_sibling(chunks[k][5](*place.behind(1, 1)))

    stages = (mid_first, mid_second, settle, forward, diagonal)
    reached = [0] * len(chunks)
    SUM, FINAL, SENT, ONWARD, DONE = range(1, 6)

    def go(k, stage):
        while reached[k] < stage:
            stages[reached[k]](k)
            reached[k] += 1

    def go_first(*pairs):
        for k, stage in pairs:
            if k < experts:
                go(k, stage)

    second_at, early_at, late_at = experts, experts + 1, experts + 2

    def spread_start(values, got):
        rows = got.shape[1]
        copies = []
        for k, (dp, tp) in enumerate(peers):
            at = pl.ds(pl.multiple_of((dp * place.tp_size + tp) * rows, 16), rows)
            copy = wire.copy(values.at[at], got.at[k], {"dp": dp, "tp": tp})
            copy.start()
            copies.append(copy)
        return copies

    def spread_end(copies, values, got, total):
        rows = got.shape[1]
        for copy in copies:
            copy.wait()
        added = values[pl.ds(pl.multiple_of(me * rows, 16), rows), :].astype(F32)
        for k in range(plane - 1):
            added = added + got[k].astype(F32)
        total[...] = added.astype(BF16).reshape(total.shape)

    swap = wire.copy(partial.at[1 - place.core], from_sibling, {"dp": place.sibling})
    swap.start()
    second_swap = wire.copy(second.at[other_tp], second_got, {"tp": other_tp})
    second_swap.start()
    for k in range(experts):
        send_end(k)
    swap.wait_recv()
    returns = []
    for lanes in (slice(0, critical), slice(critical, critical + D)):
        copies = []
        for i, j in place.offsets() + [(0, 0)]:
            dp, tp = place.ahead(i, j)
            chip = lax.div(dp, 2)
            index = i * place.tp_size + j
            if index:
                paired[chip, tp, :, lanes] = add_rounded(
                    partial[place.core, chip, tp, :, lanes], from_sibling[chip, tp, :, lanes]
                )
                copy = wire.copy(
                    paired.at[chip, tp, :, lanes],
                    received.at[index, :, lanes],
                    {"dp": dp, "tp": tp},
                )
                copy.start()
                copies.append(copy)
            else:
                received[0, :, lanes] = add_rounded(
                    partial[place.core, chip, tp, :, lanes], from_sibling[chip, tp, :, lanes]
                )
        returns.append(copies)
    late_sends = [swap] + returns[0] + returns[1]

    go_first((0, SUM))
    second_swap.wait()
    second_sum[...] = add_rounded(second[place.tp], second_got[...])
    send_end(second_at)
    go_first((1, SUM), (0, FINAL), (2, SUM), (1, FINAL), (0, SENT))
    for copy in returns[0]:
        copy.wait_recv()

    own_sets = jnp.concatenate(
        [jnp.broadcast_to(picks[i : i + 1, :], (half, WIDTH)) for i in range(images)], axis=0
    )
    total = received[0, :, :critical].astype(F32)
    for k in range(1, received.shape[0]):
        total = total + received[k, :, :critical].astype(F32)
    hidden = hidden_in[...]
    grad_probs = total[:, D : D + EXPERTS]
    grad_output = (
        jnp.concatenate([cotangent[i, pl.ds(start, half), :] for i in range(images)], axis=0)
    ).astype(F32) * live[...]
    rows = expert_in[...].reshape(count, D)
    router_lift = (times_transposed(rows, router_low[...]) * own_sets).astype(BF16)
    logits = times_transposed(rows, router_t[...]) + matmul(router_lift, router_high[...])
    powers = jnp.exp(logits - jnp.max(logits, axis=-1, keepdims=True))
    gate_probs = powers / jnp.sum(powers, axis=-1, keepdims=True)
    grad_logits = (
        gate_probs * (grad_probs - jnp.sum(grad_probs * gate_probs, axis=-1, keepdims=True))
    ).astype(BF16)
    grad_router_lift = (times_transposed(grad_logits, router_high[...]) * own_sets).astype(BF16)
    grad_expert_in = (
        total[:, :D]
        + matmul(grad_logits, router_t[...])
        + matmul(grad_router_lift, router_low[...])
    )
    _, unit, factor = normalize(hidden, gains[2:3, :], gains[3:4, :])
    grad_rows = grad_output + normalize_back(grad_expert_in, unit, factor, gains[2:3, :])
    grad_hidden[...] = grad_rows
    grad_attended = grad_rows.astype(BF16)
    grad_mixing_lift = (times_transposed(grad_attended, mixing_high[...]) * own_sets).astype(BF16)
    grad_heads = (
        matmul(grad_attended, mixing[...]) + matmul(grad_mixing_lift, mixing_low[...])
    ).astype(BF16)
    heads[...] = grad_heads.reshape(images, half, D)
    mix = head_mix[...]
    lane = lax.broadcasted_iota(jnp.int32, (D, 128), 1)
    head = lax.div(lax.broadcasted_iota(jnp.int32, (D, 128), 0), HD)
    ones = (lane == head).astype(F32).astype(BF16)
    delta_rows = split_sum(grad_heads.astype(F32) * mix.astype(F32), ones)
    delta[...] = delta_rows
    log_rows = logs[...]
    for i in range(images):
        part = slice(i * half, (i + 1) * half)
        pad = jnp.zeros((128 - half, 128), F32)
        turned = [
            jnp.concatenate([v[part], pad], axis=0).T[:HEADS] for v in (log_rows, delta_rows)
        ]
        row = 0
        for rest, number in zip(turned, (3, 2)):
            for _ in range(number):
                high = rest.astype(BF16)
                stats[i, row : row + HEADS, :] = high
                rest = rest - high.astype(F32)
                row += HEADS

    def rows_slot(ctx, tp):
        at = pl.multiple_of((ctx * place.tp_size + tp) * half, 16)
        return heads_all.at[:, pl.ds(at, half), :]

    chain = Chain(
        place, wire, [heads, stats],
        [rows_slot, lambda ctx, tp: stats_all.at[ctx * place.tp_size + tp]],
    )
    chain.start()

    def put_tiles(target, products):
        tile = 0
        for product in products:
            for n in range(product.shape[1] // 128):
                target[tile * WIDTH : (tile + 1) * WIDTH, :] = product[
                    :, n * 128 : (n + 1) * 128
                ].astype(BF16)
                tile += 1
        if tile * WIDTH < target.shape[0]:
            target[tile * WIDTH :, :] = jnp.zeros(
                (target.shape[0] - tile * WIDTH, 128), BF16
            )

    wide_logits = jnp.concatenate(
        [grad_logits, jnp.zeros((count, 128 - EXPERTS), BF16)], axis=1
    )
    put_tiles(
        early,
        (
            inner_rows(grad_mixing_lift, mix),
            inner_rows(mixing_lift[...], grad_attended),
            inner_rows(grad_router_lift, rows),
            inner_rows(router_lift, wide_logits),
        ),
    )
    early_spread = spread_start(early, early_got)
    go_first((3, SUM), (2, FINAL), (1, SENT))
    chain.step(1)
    go(second_at, SUM)
    go_first((3, FINAL), (2, SENT))
    chain.step(2)
    go_first((0, ONWARD))
    for s in range(3, chain.steps + 1):
        chain.step(s)
    spread_end(early_spread, early, early_got, early_sum)
    send_end(early_at)
    go(second_at, FINAL)
    go_first((3, SENT))
    chain.end()

    own = pl.ds(own_start, half)
    masks = half_masks()
    scale = HD**-0.5

    def heads_back(i, j):
        part = slice(i * half, (i + 1) * half)
        lanes = slice(j * 2 * HD, (j + 1) * 2 * HD)
        open_keys = live_keys[i : i + 1, :] > 0
        open_own = live[part] > 0
        open_own = jnp.concatenate([open_own, open_own], axis=0)
        found = jnp.concatenate(
            [stats_all[n, i][:, :half].astype(F32) for n in range(stats_all.shape[0])], axis=1
        )
        log_t = found[0:HEADS] + found[HEADS : 2 * HEADS] + found[2 * HEADS : 3 * HEADS]
        delta_t = found[3 * HEADS : 4 * HEADS] + found[4 * HEADS :]
        q_all, k_all, v_all = (joined[p, i, :, lanes] for p in range(3))
        g_all = heads_all[i, :, lanes]

        def column(values):
            return jnp.concatenate(
                [values[:, 2 * j : 2 * j + 1], values[:, 2 * j + 1 : 2 * j + 2]], axis=0
            )

        def across(values):
            return jnp.concatenate(
                [
                    jnp.broadcast_to(values[2 * j + n : 2 * j + n + 1, :], (half, values.shape[1]))
                    for n in range(2)
                ],
                axis=0,
            )

        q = stack_pair(joined[0, i, own, lanes], masks, scale)
        g = stack_pair(heads[i, :, lanes], masks)
        scores = jnp.where(open_keys, times_transposed(q, k_all), MASKED)
        probs = jnp.exp(scores - column(logs[part]))
        grad_probs_att = times_transposed(g, v_all)
        grad_scores = (probs * (grad_probs_att - column(delta[part]))).astype(BF16)
        grads[0, part, lanes] = (join_pair(matmul(grad_scores, k_all), masks) * scale).astype(BF16)
        k = stack_pair(joined[1, i, own, lanes], masks, scale)
        v = stack_pair(joined[2, i, own, lanes], masks)
        scores = jnp.where(open_own, times_transposed(k, q_all), MASKED)
        probs = jnp.exp(scores - across(log_t))
        grad_probs_att = times_transposed(v, g_all)
        grad_scores = (probs * (grad_probs_att - across(delta_t))).astype(BF16)
        grads[1, part, lanes] = (join_pair(matmul(grad_scores, q_all), masks) * scale).astype(BF16)
        grads[2, part, lanes] = join_pair(matmul(probs.astype(BF16), g_all), masks).astype(BF16)

    for i in range(images):
        for j in range(HEADS // 2):
            heads_back(i, j)
        if i == 0:
            go(early_at, SUM)
            go(second_at, SENT)
            go_first((1, ONWARD), (2, ONWARD), (0, DONE))
    go(early_at, FINAL)
    lift = times_transposed(grads[0], attend_high[0])
    into = times_transposed(grads[0], weights[0])
    for p in range(1, 3):
        lift = lift + times_transposed(grads[p], attend_high[p])
        into = into + times_transposed(grads[p], weights[p])
    lift = (lift * own_sets).astype(BF16)
    lift_in = own_lift[...].reshape(count, WIDTH)
    put_tiles(
        late,
        [inner_rows(lift_in, grads[p]) for p in range(3)]
        + [inner_rows(lift, own_in[...].reshape(count, D))],
    )
    late_spread = spread_start(late, late_got)
    into = into + matmul(lift, attend_low[...])
    flat = jnp.concatenate(
        [tokens[i, pl.ds(start, half), :] for i in range(images)], axis=0
    ).astype(F32)
    _, unit, factor = normalize(flat, gains[0:1, :], gains[1:2, :])
    result = grad_hidden[...] + normalize_back(into, unit, factor, gains[0:1, :])
    grad_own[...] = result.astype(BF16).reshape(images, half, D)
    for copy in returns[1]:
        copy.wait_recv()
    total = hidden_in[...]
    for k in range(received.shape[0]):
        total = total + received[k, :, critical:].astype(F32)
    out_own[...] = total.astype(BF16).reshape(images, half, D)
    for values, gathered in ((out_own, out_all), (grad_own, grad_all)):
        spot = gathered.at[:, pl.ds(start, half), :]
        for copy in (wire.copy(values, spot, {"tp": other_tp}), wire.near(values, spot)):
            copy.start()
            late_waits.append(copy)
    spread_end(late_spread, late, late_got, late_sum)
    send_end(late_at)
    go(early_at, SENT)
    go_first((1, DONE), (3, ONWARD))
    go(late_at, SUM)
    go_first((2, DONE))
    go(second_at, ONWARD)
    go(late_at, FINAL)
    go_first((3, DONE))
    go(late_at, SENT)
    go(early_at, ONWARD)
    go(second_at, DONE)
    go(late_at, ONWARD)
    for k in range(len(chunks)):
        go(k, DONE)

    @pl.when(is_end)
    def _():
        for flow in flows:
            flow["outer"].wait_send()
            flow["inner"].wait_send()

    @pl.when(is_mid)
    def _():
        for flow in flows:
            for name in ("cross", "back", "share", "pass_on"):
                flow[name].wait_send()

    chain.drain()
    for copy in late_sends:
        copy.wait_send()
    for k in plane_flights:
        for copy, _, _ in plane_flights[k]:
            copy.wait_send()
    for k in diagonals:
        diagonals[k].wait_send()
    for copy in late_waits:
        copy.wait()


def back(sizes, partial, first, second, *operands):
    dp, ctx, tp = sizes
    assert ctx == 4 and tp == 2
    experts, _, width, lanes = first.shape
    part = second.shape[1:]
    plane = dp * tp
    chips = dp // 2
    count, sent = partial.shape[3:]
    images = operands[1].shape[0]
    half = count // images
    seq = ctx * tp * half

    def small_rows(tiles):
        return -(-tiles * WIDTH // (plane * 16)) * 16

    early_rows, late_rows = small_rows(3 * (D // 128) + 1), small_rows(4 * (D // 128))
    small = [(2, rows // 2, 128) for rows in (early_rows, late_rows)]
    chunks = experts + 3
    offsets = place_offsets(sizes, True)
    remote = (
        chunks * (6 + 2 * offsets + 1)
        + 2
        + 2 * offsets
        + 2 * (plane - 1)
        + Chain.remote(ctx, 2)
        + 2
    )

    def vmem(*shape, dtype=BF16):
        return pltpu.VMEM(shape, dtype)

    shapes = [(experts, 2, width, lanes), part] + small
    halves = [(experts, width, lanes)] + [shape[1:] for shape in shapes[1:]]
    return pl.pallas_call(
        functools.partial(back_kernel, sizes),
        out_shape=(
            jax.ShapeDtypeStruct((dp, tp) + first.shape, BF16),
            jax.ShapeDtypeStruct((dp, tp) + part, BF16),
            jax.ShapeDtypeStruct((dp, tp) + small[0], BF16),
            jax.ShapeDtypeStruct((dp, tp) + small[1], BF16),
            jax.ShapeDtypeStruct((images, tp * half, D), BF16),
            jax.ShapeDtypeStruct((images, tp * half, D), BF16),
        ),
        in_specs=[IN_VMEM] * (3 + len(operands)),
        out_specs=(ANY,) * 6,
        scratch_shapes=[
            vmem(chips, tp, count, sent),
            vmem(chips, tp, count, sent),
            vmem(chips * tp, count, sent),
            vmem(*part),
            vmem(plane - 1, early_rows, 128),
            vmem(plane - 1, late_rows, 128),
            vmem(*part),
            vmem(*small[0]),
            vmem(*small[1]),
            vmem(plane * early_rows, 128),
            vmem(plane * late_rows, 128),
        ]
        + [vmem(*shape) for shape in shapes]
        + [vmem(*shape) for shape in halves]
        + [vmem(*shape) for shape in halves]
        + [vmem(*shape) for shape in shapes]
        + [
            vmem(images, half, D),
            vmem(images, half, D),
            vmem(count, D, dtype=F32),
            vmem(images, half, D),
            vmem(images, 5 * HEADS, 128),
            vmem(count, 128, dtype=F32),
            vmem(images, seq, D),
            vmem(ctx * tp, images, 5 * HEADS, 128),
            vmem(3, count, D),
        ]
        + semaphores(remote, chunks + 2 + 2),
        compiler_params=pltpu.CompilerParams(
            collective_id=3, has_side_effects=True, vmem_limit_bytes=56 << 20
        ),
    )(partial, first, second, *operands)


def assemble_kernel(
    first, second, early, late, up, down_t, narrow_t, narrow,
    attend_down, attend_up, mixing_down, mixing_up, router_down, router_up,
):
    lanes, part = first.shape[-1], second.shape[-1]
    for tp in range(first.shape[1]):
        for half, out in ((0, up), (1, down_t)):
            out[:, 0, :, tp * lanes : (tp + 1) * lanes] = (
                first[0, tp, 0, half].astype(F32).reshape(SETS, RANK, lanes)
            )
        for half, out in ((0, narrow_t), (1, narrow)):
            out[:, 0, :, tp * part : (tp + 1) * part] = (
                second[0, tp, half, 0].astype(F32).reshape(SETS, RANK, part)
            )

    @pl.when(pl.program_id(0) == 0)
    def _():
        def tile(small, k):
            return small[k * WIDTH : (k + 1) * WIDTH, :].astype(F32).reshape(SETS, RANK, 128)

        count = D // 128
        for p in range(3):
            for k in range(count):
                attend_up[:, p, :, k * 128 : (k + 1) * 128] = tile(late, p * count + k)
        for k in range(count):
            attend_down[:, :, k * 128 : (k + 1) * 128] = tile(late, 3 * count + k)
        for p, out in enumerate((mixing_down, mixing_up, router_down)):
            for k in range(count):
                out[:, :, k * 128 : (k + 1) * 128] = tile(early, p * count + k)
        router_up[...] = tile(early, 3 * count)[:, :, :EXPERTS]


def assemble(first, second, early, late):
    dp, tp, experts, _, width, lanes = first.shape
    part = second.shape[-1]

    def split(e):
        return lax.div(e, experts), lax.rem(e, experts)

    def expert_out(size):
        return (
            jax.ShapeDtypeStruct((SETS, EXPERTS, RANK, size), F32),
            pl.BlockSpec((SETS, 1, RANK, size), lambda e: (0, e, 0, 0)),
        )

    def whole_out(*shape):
        return (
            jax.ShapeDtypeStruct(shape, F32),
            pl.BlockSpec(shape, lambda e: (0,) * len(shape)),
        )

    outs = (
        [expert_out(FF)] * 2
        + [expert_out(D)] * 2
        + [whole_out(SETS, RANK, D), whole_out(SETS, 3, RANK, D)]
        + [whole_out(SETS, RANK, D)] * 3
        + [whole_out(SETS, RANK, EXPERTS)]
    )
    return pl.pallas_call(
        assemble_kernel,
        grid=(EXPERTS,),
        out_shape=[out[0] for out in outs],
        in_specs=[
            pl.BlockSpec(
                (1, tp, 1, 2, width, lanes), lambda e: (split(e)[0], 0, split(e)[1], 0, 0, 0)
            ),
            pl.BlockSpec(
                (1, tp, 2, 1, width, part), lambda e: (split(e)[0], 0, 0, split(e)[1], 0, 0)
            ),
            pl.BlockSpec(early.shape, lambda e: (0, 0)),
            pl.BlockSpec(late.shape, lambda e: (0, 0)),
        ],
        out_specs=[out[1] for out in outs],
        compiler_params=pltpu.CompilerParams(vmem_limit_bytes=32 << 20),
    )(first, second, early, late)


def per_device(
    sizes,
    tokens,
    cotangent,
    routes,
    slot_index,
    token_mask,
    image_mask,
    adapter_set,
    first_gain,
    first_shift,
    second_gain,
    second_shift,
    attend_weight,
    mixing_weight,
    router_weight,
    expand_weight,
    shrink_weight,
    attend_down,
    attend_up,
    mixing_down,
    mixing_up,
    router_down,
    router_up,
    expand_down,
    expand_up,
    shrink_down,
    shrink_up,
):
    dp_size, ctx_size, tp_size = sizes
    images, block = tokens.shape[:2]
    half = block // tp_size
    count = images * half
    seq = ctx_size * block
    all_images = dp_size * images
    local_experts, _, hidden_half = expand_weight.shape
    ctx_index, tp_index, dp_index = (lax.axis_index(a) for a in ("ctx", "tp", "dp"))
    place = jnp.stack(
        [
            ctx_index * block + tp_index * half,
            dp_index * local_experts,
            tp_index,
            tp_index * half,
        ]
    ).astype(jnp.int32)

    live = token_mask * image_mask[:, None]
    ints = jnp.concatenate(
        [
            jnp.transpose(routes, (0, 2, 1)),
            jnp.transpose(slot_index, (0, 2, 1)),
            live[:, None, :],
            jnp.broadcast_to(adapter_set[:, None, None], (images, 3, block)),
        ],
        axis=1,
    )
    tokens_all, weights_all, mixing_all, router_parts, cotangent_all, ints_all, ctx_ints = (
        start_gather(
            sizes,
            tokens,
            jnp.transpose(attend_weight, (1, 0, 2)),
            mixing_weight,
            jnp.transpose(router_weight, (1, 0)),
            cotangent,
            ints,
        )
    )
    router_t = jnp.transpose(router_parts, (1, 0, 2)).reshape(EXPERTS, D)

    attend_low = jnp.transpose(attend_down, (0, 2, 1)).reshape(WIDTH, D)
    attend_high = jnp.transpose(attend_up, (2, 0, 1, 3)).reshape(3, WIDTH, D)
    mixing_low = jnp.transpose(mixing_down, (0, 2, 1)).reshape(WIDTH, D)
    mixing_high = mixing_up.reshape(WIDTH, D)
    router_low = jnp.transpose(router_down, (0, 2, 1)).reshape(WIDTH, D)
    router_high = router_up.reshape(WIDTH, EXPERTS)
    gains = jnp.stack([first_gain, first_shift, second_gain, second_shift])

    def picker(sets):
        return (sets[:, None] == jnp.arange(WIDTH)[None, :] // RANK).astype(F32)

    own_picks = picker(adapter_set)
    key_live = jnp.transpose(ctx_ints[:, :, 4, :], (1, 0, 2)).reshape(images, seq)
    own_live = (
        lax.dynamic_slice_in_dim(live, tp_index * half, half, 1).reshape(count, 1).astype(F32)
    )
    joined, own_in, own_lift, head_mix, logs, mixing_lift, hidden, expert_in = attend(
        half, place, tokens_all, weights_all, mixing_all, key_live, own_picks, attend_low,
        attend_high, mixing_low, mixing_high, gains,
    )
    expert_in_all = expert_in_gather(sizes, expert_in)
    picks = picker(ints_all[:, 5, 0])
    first_grads, second_grads, partial = run_experts(
        sizes, place, expert_in_all, cotangent_all, ints_all, picks, picks[:, :, None], router_t,
        router_low, jnp.transpose(router_high), expand_weight, shrink_weight,
        jnp.transpose(expand_down, (0, 1, 3, 2)),
        expand_up,
        jnp.transpose(shrink_down, (0, 1, 3, 2)),
        shrink_up,
    )
    first_all, second_all, early_all, late_all, out_all, grad_all = back(
        sizes,
        partial.reshape(2, dp_size // 2, tp_size, count, partial.shape[-1]),
        first_grads, second_grads, hidden, expert_in, cotangent, own_live, own_picks, router_t,
        router_low, router_high, mixing_all, mixing_low, mixing_high, head_mix, mixing_lift, logs,
        gains, joined, key_live, tokens, own_in, own_lift, weights_all, attend_low, attend_high,
    )
    wide = assemble(
        first_all, second_all, early_all.reshape(-1, 128), late_all.reshape(-1, 128)
    )

    def flipped(values):
        return jnp.swapaxes(values, -1, -2)

    return (
        out_all,
        grad_all,
        flipped(wide[4]),
        jnp.transpose(wide[5], (0, 2, 1, 3)),
        flipped(wide[6]),
        wide[7],
        flipped(wide[8]),
        wide[9],
        flipped(wide[2]),
        wide[0],
        flipped(wide[1]),
        wide[3],
    )


def solution(mesh):
    sizes = (mesh.shape["dp"], mesh.shape["ctx"], mesh.shape["tp"])
    tokens_spec = P("dp", "ctx", None)
    in_specs = (
        (tokens_spec,) * 4
        + (P("dp", "ctx"), P("dp"), P("dp"))
        + (P(),) * 4
        + (P("dp", None, "tp"), P("dp", "tp"), P("dp", None))
        + (P("dp", None, "tp"), P("dp", "tp", None))
        + (P(),) * 10
    )
    out_specs = (tokens_spec,) * 2 + (P(),) * 10
    return jax.shard_map(
        functools.partial(per_device, sizes),
        mesh=mesh,
        in_specs=in_specs,
        out_specs=out_specs,
        check_vma=False,
    )
```

```python
import functools
import types

import jax
import jax.numpy as jnp
from jax import lax
from jax.experimental import pallas as pl
from jax.experimental.pallas import tpu as pltpu
from jax.sharding import PartitionSpec as P

D = 512
HEADS = 8
HD = 64
FF = 2048
EXPERTS = 16
TOP = 2
RANK = 16
SETS = 4
CAP = 30
SLOTS = 32
WIDTH = SETS * RANK
LIVE_ROW = 2 * TOP
SET_ROW = LIVE_ROW + 1
CRITICAL = D + 128
EXPERT_ROWS = 256

EPSILON = 1e-06
MASKED = -1e30
SQRT_HALF = 0.7071067811865476
INV_ROOT_TWO_PI = 0.3989422804014327
F32 = jnp.float32
BF16 = jnp.bfloat16
MESH = pl.DeviceIdType.MESH
ANY = pl.BlockSpec(memory_space=pl.ANY)
IN_SMEM = pl.BlockSpec(memory_space=pltpu.SMEM)
IN_VMEM = pl.BlockSpec(memory_space=pltpu.VMEM)


def matmul(left_side, right_side):
    return jnp.dot(left_side, right_side, preferred_element_type=F32)


def inner_rows(left_side, right_side):
    return lax.dot_general(
        left_side, right_side, (((0,), (0,)), ((), ())), preferred_element_type=F32
    )


def times_transposed(left_side, right_side):
    return lax.dot_general(
        left_side, right_side, (((1,), (1,)), ((), ())), preferred_element_type=F32
    )


def normalize(values, gain_row, shift_row):
    centred = values - jnp.mean(values, axis=-1, keepdims=True)
    spread = jnp.mean(centred * centred, axis=-1, keepdims=True)
    factor = lax.rsqrt(spread + EPSILON)
    normed = centred * factor
    return (normed * gain_row + shift_row, normed, factor)


def normalize_back(grad_out, normed, factor, gain_row):
    scaled = grad_out * gain_row
    return factor * (
        scaled
        - jnp.mean(scaled, axis=-1, keepdims=True)
        - normed * jnp.mean(scaled * normed, axis=-1, keepdims=True)
    )


def add_rounded(*parts):
    total = parts[0].astype(F32)
    for part in parts[1:]:
        total = total + part.astype(F32)
    return total.astype(BF16)


def split_sum(values, ones):
    high = values.astype(BF16)
    low = (values - high.astype(F32)).astype(BF16)
    return matmul(high, ones) + matmul(low, ones)


def put_lanes(columns, width):
    lane = lax.broadcasted_iota(jnp.int32, (columns[0].shape[0], width), 1)
    total = jnp.zeros((columns[0].shape[0], width), F32)
    for k, column in enumerate(columns):
        total = jnp.where(lane == k, column, total)
    return total


def half_masks():
    lane = lax.broadcasted_iota(jnp.int32, (1, 2 * HD), 1)
    even = (lane < HD).astype(F32)
    return even, 1.0 - even


def stack_pair(rows, masks, factor=1.0):
    wide = rows.astype(F32) * factor
    return jnp.concatenate([wide * masks[0], wide * masks[1]], axis=0).astype(BF16)


def join_pair(rows, masks):
    half = rows.shape[0] // 2
    return rows[:half] * masks[0] + rows[half:] * masks[1]


def small_rows(tiles, plane):
    return -(-tiles * WIDTH // (plane * 16)) * 16


class Wire:
    def __init__(self, send, recv, local):
        self.send, self.recv, self.local = send, recv, local
        self.used = self.used_local = 0

    def copy(self, src, dst, device):
        k = self.used
        self.used += 1
        assert k < self.send.shape[0]
        return pltpu.make_async_remote_copy(
            src_ref=src,
            dst_ref=dst,
            send_sem=self.send.at[k],
            recv_sem=self.recv.at[k],
            device_id=device,
            device_id_type=MESH,
        )

    def near(self, src, dst):
        k = self.used_local
        self.used_local += 1
        assert k < self.local.shape[0]
        return pltpu.make_async_copy(src, dst, self.local.at[k])


class Place:
    def __init__(self, sizes):
        self.dp_size, self.ctx_size, self.tp_size = sizes
        self.chips = self.dp_size // 2
        self.plane = self.dp_size * self.tp_size
        self.dp = lax.axis_index("dp")
        self.ctx = lax.axis_index("ctx")
        self.tp = lax.axis_index("tp")
        self.chip = lax.div(self.dp, 2)
        self.core = lax.rem(self.dp, 2)
        self.sibling = self.chip * 2 + (1 - self.core)
        self.other_tp = lax.rem(self.tp + 1, 2)
        self.me = self.dp * self.tp_size + self.tp
        self.is_mid = jnp.logical_and(self.ctx >= 1, self.ctx <= 2)
        self.is_end = jnp.logical_not(self.is_mid)
        self.inner = lax.div(self.ctx, 2)
        self.partner = jnp.where(self.is_mid, self.inner * 3, 1 + self.inner)
        self.other_mid = 2 - self.inner
        self.peers = []
        for k in range(1, self.plane):
            peer = lax.rem(self.me + k, self.plane)
            self.peers.append((lax.div(peer, self.tp_size), lax.rem(peer, self.tp_size)))

    def ahead(self, i, j):
        return (
            lax.rem(self.chip + i, self.chips) * 2 + self.core,
            lax.rem(self.tp + j, self.tp_size),
        )

    def behind(self, i, j):
        return self.ahead(self.chips - i, self.tp_size - j)

    def offsets(self, over_tp=True):
        return [
            (i, j)
            for i in range(self.chips)
            for j in range(self.tp_size if over_tp else 1)
            if i or j
        ]

    def greet(self):
        barrier = pltpu.get_barrier_semaphore()
        for dp, tp in self.peers:
            pl.semaphore_signal(
                barrier, inc=1, device_id={"dp": dp, "tp": tp}, device_id_type=MESH
            )
        pl.semaphore_signal(
            barrier, inc=1, device_id={"ctx": self.partner}, device_id_type=MESH
        )

        @pl.when(self.is_mid)
        def _():
            pl.semaphore_signal(
                barrier, inc=1, device_id={"ctx": self.other_mid}, device_id_type=MESH
            )

        pl.semaphore_wait(barrier, self.plane + jnp.where(self.is_mid, 1, 0))


class Spread:
    def __init__(self, place, wire, source, slot, over_tp=True, direct=False, near=True):
        self.place, self.wire, self.source, self.slot = place, wire, source, slot
        self.over_tp = over_tp
        self.relay = over_tp and not direct and place.chips == 2 and place.tp_size == 2
        self.near = near
        self.flights, self.across, self.beside, self.here = [], None, [], None

    def to_sibling(self, source, spot):
        copy = self.wire.copy(source, spot, {"dp": self.place.sibling})
        copy.start()
        self.beside.append(copy)

    def start(self):
        place = self.place
        spot = self.slot(place.dp, place.tp)
        for i, j in place.offsets(self.over_tp):
            if self.relay and i and j:
                continue
            dp, tp = place.ahead(i, j)
            copy = self.wire.copy(self.source, spot, {"dp": dp, "tp": tp})
            copy.start()
            self.flights.append((copy, i, j))
        self.to_sibling(self.source, spot)
        if self.near:
            self.here = self.wire.near(self.source, spot)
            self.here.start()

    def forward(self):
        for copy, i, j in sorted(self.flights, key=lambda f: f[1]):
            copy.wait_recv()
            got = self.slot(*self.place.behind(i, j))
            if self.relay and j:
                dp, tp = self.place.ahead(1, 0)
                self.across = self.wire.copy(got, got, {"dp": dp, "tp": tp})
                self.across.start()
            self.to_sibling(got, got)

    def diagonal(self):
        if self.relay:
            self.across.wait_recv()
            got = self.slot(*self.place.behind(1, 1))
            self.to_sibling(got, got)

    def finish(self):
        for copy in self.beside:
            copy.wait_recv()
        if self.near:
            self.here.wait()

    def drain(self):
        for copy, _, _ in self.flights:
            copy.wait_send()
        if self.relay:
            self.across.wait_send()
        for copy in self.beside:
            copy.wait_send()

    @staticmethod
    def remote(sizes, over_tp=True):
        return 2 * (sizes[0] // 2 * (sizes[2] if over_tp else 1) - 1) + 1


class Chain:
    def __init__(self, place, wire, sources, slots, over, with_own):
        self.place, n = place, place.ctx_size
        self.steps = n - 1
        to_tp = {"tp": place.other_tp}
        self.right, self.left, self.over_right, self.over_left = {}, {}, {}, {}
        self.own, self.here = [], []
        for source, slot in zip(sources, slots):
            spot = slot(place.ctx, place.tp)
            if with_own:
                self.own.append(wire.copy(source, spot, to_tp))
                self.here.append(wire.near(source, spot))
        for s in range(1, n):
            back = [slot(jnp.maximum(place.ctx - (s - 1), 0), place.tp) for slot in slots]
            ahead = [slot(jnp.minimum(place.ctx + (s - 1), n - 1), place.tp) for slot in slots]
            got_right = [slot(jnp.maximum(place.ctx - s, 0), place.tp) for slot in slots]
            got_left = [slot(jnp.minimum(place.ctx + s, n - 1), place.tp) for slot in slots]
            to_right = {"ctx": jnp.minimum(place.ctx + 1, n - 1)}
            to_left = {"ctx": jnp.maximum(place.ctx - 1, 0)}
            self.right[s] = [
                wire.copy(a if s == 1 else b, b, to_right) for a, b in zip(sources, back)
            ]
            self.left[s] = [
                wire.copy(a if s == 1 else b, b, to_left) for a, b in zip(sources, ahead)
            ]
            self.over_right[s] = [wire.copy(b, b, to_tp) for b, o in zip(got_right, over) if o]
            self.over_left[s] = [wire.copy(b, b, to_tp) for b, o in zip(got_left, over) if o]

    def sends_right(self, s):
        return jnp.logical_and(self.place.ctx >= s - 1, self.place.ctx < self.steps)

    def sends_left(self, s):
        return jnp.logical_and(self.place.ctx <= self.steps + 1 - s, self.place.ctx > 0)

    def gets_right(self, s):
        return self.place.ctx >= s

    def gets_left(self, s):
        return self.place.ctx <= self.steps - s

    @staticmethod
    def all_of(copies, verb):
        for copy in copies:
            getattr(copy, verb)()

    def start(self):
        pl.when(self.sends_right(1))(lambda: self.all_of(self.right[1], "start"))
        pl.when(self.sends_left(1))(lambda: self.all_of(self.left[1], "start"))
        self.all_of(self.own + self.here, "start")

    def step(self, s):
        def passed(got, over, sends):
            def run():
                self.all_of(got[s], "wait_recv")
                if s < self.steps:
                    pl.when(sends(s + 1))(lambda: self.all_of(got[s + 1], "start"))
                self.all_of(over[s], "start")

            return run

        pl.when(self.gets_right(s))(passed(self.right, self.over_right, self.sends_right))
        pl.when(self.gets_left(s))(passed(self.left, self.over_left, self.sends_left))

    def landed(self, s):
        pl.when(self.gets_right(s))(lambda: self.all_of(self.over_right[s], "wait_recv"))
        pl.when(self.gets_left(s))(lambda: self.all_of(self.over_left[s], "wait_recv"))

    def finish_own(self):
        self.all_of(self.own, "wait_recv")
        self.all_of(self.here, "wait")

    def drain(self):
        self.all_of(self.own, "wait_send")
        for s in range(1, self.steps + 1):
            pl.when(self.gets_right(s))(lambda: self.all_of(self.over_right[s], "wait_send"))
            pl.when(self.gets_left(s))(lambda: self.all_of(self.over_left[s], "wait_send"))
            pl.when(self.sends_right(s))(lambda: self.all_of(self.right[s], "wait_send"))
            pl.when(self.sends_left(s))(lambda: self.all_of(self.left[s], "wait_send"))

    @staticmethod
    def remote(n, arrays):
        return arrays * (1 + 4 * (n - 1))


def layer_kernel(sizes, names, *refs):
    r = types.SimpleNamespace(**dict(zip(names, refs)))
    place = Place(sizes)
    wire = Wire(r.send, r.recv, r.local)
    plane = place.plane
    images, block = r.tokens.shape[:2]
    half = block // place.tp_size
    count = images * half
    seq = place.ctx_size * block
    experts, _, hidden_units = r.up_weight.shape
    all_images = place.dp_size * images
    owned = place.dp * experts
    start = pl.multiple_of(place.tp * half, 16)
    own_start = pl.multiple_of(place.ctx * block + place.tp * half, 16)
    own = pl.ds(own_start, half)
    masks = half_masks()
    scale = HD**-0.5

    pending = {}

    def load(name, source, target):
        pending[name] = wire.near(source, target)
        pending[name].start()

    def need(*wanted):
        for name in wanted:
            if name in pending:
                pending.pop(name).wait()

    whole = pl.ds(pl.multiple_of(place.ctx * block, 16), block)
    load("tokens", r.tokens, r.tokens_all.at[:, whole, :])
    for name in (
        "attend_low", "attend_high", "mixing_low", "mixing_high", "router_low", "router_high",
    ):
        load(name, getattr(r, name), getattr(r, "v_" + name))
    wide = pl.ds(pl.multiple_of(place.tp * hidden_units, 128), hidden_units)
    for e in range(experts):
        load(("a_first", e), r.first_a.at[:, owned + e], r.v_first_a.at[e])
        load(("b_first", e), r.first_b.at[:, owned + e, :, wide], r.v_first_b.at[e])
        load(("up", e), r.up_weight.at[e], r.v_up.at[e])
        load(("a_second", e), r.second_a.at[:, owned + e, :, wide], r.v_second_a.at[e])
        load(("b_second", e), r.second_b.at[:, owned + e], r.v_second_b.at[e])
        load(("down", e), r.down_weight.at[e], r.v_down.at[e])
    r.ints[:, 0:TOP, :] = r.routes_t[...]
    r.ints[:, TOP : 2 * TOP, :] = r.slots_t[...]
    lane_set = lax.div(lax.broadcasted_iota(jnp.int32, (1, WIDTH), 1), RANK)
    picks = []
    for i in range(images):
        r.ints[i, LIVE_ROW : LIVE_ROW + 1, :] = r.token_mask[i : i + 1, :] * r.image_mask[i]
        r.ints[i, SET_ROW:, :] = jnp.full((8 - SET_ROW, block), r.adapter_set[i], jnp.int32)
        picks.append((lane_set == r.adapter_set[i]).astype(F32))
    gain_one, shift_one = r.gains[0:1, :], r.gains[1:2, :]
    gain_two, shift_two = r.gains[2:3, :], r.gains[3:4, :]

    place.greet()

    rows, lanes = r.mixing.shape

    def at_rows(dp):
        return pl.ds(pl.multiple_of(dp * rows, 16), rows)

    def at_lanes(tp):
        return pl.ds(pl.multiple_of(tp * lanes, 128), lanes)

    def token_slot(ctx, tp):
        at = pl.multiple_of(ctx * block + tp * half, 16)
        return r.tokens_all.at[:, pl.ds(at, half), :]

    tokens_chain = Chain(
        place, wire, [r.tokens.at[:, pl.ds(start, half), :], r.ints],
        [token_slot, lambda ctx, tp: r.ctx_ints.at[ctx]], [True, False], False,
    )
    weights = Spread(
        place, wire, r.weights, lambda dp, tp: r.weights_all.at[:, at_rows(dp), at_lanes(tp)]
    )
    mixing = Spread(
        place, wire, r.mixing, lambda dp, tp: r.mixing_all.at[at_rows(dp), at_lanes(tp)]
    )
    numbers = Spread(
        place, wire, r.ints, lambda dp, tp: r.ints_all.at[pl.ds(dp * 2, 2)], over_tp=False
    )
    router = Spread(place, wire, r.router, lambda dp, tp: r.router_all.at[dp], over_tp=False)
    cotangents = Spread(
        place, wire, r.cotangent, lambda dp, tp: r.cot_all.at[pl.ds(dp * 2, 2)], over_tp=False
    )
    r.ctx_ints[place.ctx] = r.ints[...]
    tokens_chain.start()
    weights.start()
    numbers.start()
    router.start()
    mixing.start()
    cotangents.start()
    weights.forward()
    tokens_chain.step(1)
    weights.diagonal()
    tokens_chain.step(2)
    numbers.forward()
    router.forward()
    weights.finish()
    need("tokens", "attend_low", "attend_high")

    block_picks = jnp.concatenate(
        [jnp.broadcast_to(pick, (block, WIDTH)) for pick in picks], axis=0
    )
    own_sets = jnp.concatenate(
        [jnp.broadcast_to(pick, (half, WIDTH)) for pick in picks], axis=0
    )
    attend_low = r.v_attend_low[...].reshape(WIDTH, D)

    def high(p):
        return r.v_attend_high[:, p].reshape(WIDTH, D)

    def project(k, _):
        ctx = place.ctx
        first = jnp.where(ctx == 3, 2, ctx + 1)
        second = jnp.where(ctx == 0, 2, jnp.where(ctx == 1, 0, 1))
        third = jnp.where(ctx < 2, 3, 0)
        which = jnp.where(
            k == 0, ctx, jnp.where(k == 1, first, jnp.where(k == 2, second, third))
        )
        at = pl.ds(pl.multiple_of(which * block, 16), block)
        values = jnp.concatenate([r.tokens_all[i, at, :] for i in range(images)], axis=0)
        normed = normalize(values.astype(F32), gain_one, shift_one)[0].astype(BF16)
        lift = (times_transposed(normed, attend_low) * block_picks).astype(BF16)
        for i in range(images):
            r.lift_all[i, at, :] = lift[i * block : (i + 1) * block]
        for p in range(3):
            made = (matmul(normed, r.weights_all[p]) + matmul(lift, high(p))).astype(BF16)
            for i in range(images):
                r.joined[p, i, at, :] = made[i * block : (i + 1) * block]
        return 0

    def project_blocks(low, up):
        lax.fori_loop(low, up, project, 0)

    project_blocks(0, 1)
    tokens_chain.step(3)
    tokens_chain.landed(1)
    mixing.forward()
    project_blocks(1, 2)
    tokens_chain.landed(2)
    project_blocks(2, 3)
    cotangents.forward()
    mixing.diagonal()
    tokens_chain.landed(3)
    project_blocks(3, 4)
    mixing.finish()
    need("mixing_low", "mixing_high")
    mixing_low = r.v_mixing_low[...].reshape(WIDTH, D)
    mixing_high = r.v_mixing_high[...].reshape(WIDTH, D)

    def open_keys(i):
        return (
            jnp.concatenate(
                [
                    r.ctx_ints[n, i, LIVE_ROW : LIVE_ROW + 1, :]
                    for n in range(place.ctx_size)
                ],
                axis=1,
            )
            > 0
        )

    for i in range(images):
        r.keys_open[i : i + 1, :] = open_keys(i).astype(F32)
        token_rows = r.tokens_all[i, own, :].astype(F32)
        r.own_in[i] = normalize(token_rows, gain_one, shift_one)[0].astype(BF16)
        keys_open = r.keys_open[i : i + 1, :] > 0
        part = slice(i * half, (i + 1) * half)
        logs = []
        for j in range(HEADS // 2):
            at = slice(j * 2 * HD, (j + 1) * 2 * HD)
            q = stack_pair(r.joined[0, i, own, at], masks, scale)
            scores = times_transposed(q, r.joined[1, i, :, at])
            scores = jnp.where(keys_open, scores, MASKED)
            top = jnp.max(scores, axis=-1, keepdims=True)
            powers = jnp.exp(scores - top)
            total = jnp.sum(powers, axis=-1, keepdims=True)
            weights_att = (powers * (1.0 / total)).astype(BF16)
            mixed = join_pair(matmul(weights_att, r.joined[2, i, :, at]), masks)
            r.head_mix[part, at] = mixed.astype(BF16)
            log = jnp.maximum(top + jnp.log(total), -1e29)
            logs += [log[:half], log[half:]]
        r.logs[part, :] = put_lanes(logs, 128)
        mix = r.head_mix[part, :]
        lift = (times_transposed(mix, mixing_low) * picks[i]).astype(BF16)
        r.mixing_lift[part, :] = lift
        hidden = token_rows + times_transposed(mix, r.mixing_all[...]) + matmul(lift, mixing_high)
        r.hidden[part, :] = hidden
        r.expert_in[i] = normalize(hidden, gain_two, shift_two)[0].astype(BF16)

    def rows_slot(dp, tp):
        at = pl.multiple_of(tp * half, 16)
        return r.rows_all.at[pl.ds(dp * 2, 2), pl.ds(at, half), :]

    expert_rows = Spread(place, wire, r.expert_in, rows_slot, direct=True)
    expert_rows.start()

    slots = experts * SLOTS
    cotangents.finish()
    numbers.finish()
    router.finish()
    need("router_low", "router_high")
    router_low = r.v_router_low[...].reshape(WIDTH, D)
    router_high = r.v_router_high[...].reshape(WIDTH, EXPERTS)
    r.router_t[...] = jnp.concatenate([r.router_all[n] for n in range(place.dp_size)], axis=1)

    def targets(given, k):
        route, slot = given[k : k + 1, :], given[TOP + k : TOP + k + 1, :]
        local = route - owned
        here = (local >= 0) & (local < experts) & (slot < CAP)
        return jnp.where(here, local * SLOTS + slot, -1)

    def fill_slots(i, target, values):
        at = pl.ds(pl.multiple_of(i * SLOTS, SLOTS), SLOTS)
        for n in range(experts):
            target[n, at, :] = values[n * SLOTS : (n + 1) * SLOTS]

    def make_table(i, _):
        given = r.ints_all[i]
        slot = lax.broadcasted_iota(jnp.int32, (slots, block), 0)
        hot = jnp.zeros((slots, block), F32)
        for k in range(TOP):
            hot = jnp.where(slot == targets(given, k), 1.0, hot)
        hot = hot.astype(BF16)
        r.table[i] = hot
        fill_slots(i, r.grad_slots, matmul(hot, r.cot_all[i]).astype(BF16))
        return 0

    lax.fori_loop(0, all_images, make_table, 0)
    expert_rows.forward()
    expert_rows.finish()

    def dispatch(i, _):
        values = r.rows_all[i]
        given = r.ints_all[i]
        set_column = lax.div(lax.broadcasted_iota(jnp.int32, (WIDTH, 1), 0), RANK)
        pick = (set_column == given[SET_ROW : SET_ROW + 1, 0:1]).astype(F32)
        lift = (times_transposed(router_low, values) * pick).astype(BF16)
        logits = times_transposed(r.router_t[...], values) + inner_rows(router_high, lift)
        powers = jnp.exp(logits - jnp.max(logits, axis=0, keepdims=True))
        probs = powers / jnp.sum(powers, axis=0, keepdims=True)
        expert = lax.broadcasted_iota(jnp.int32, (EXPERTS, block), 0)
        slot = lax.broadcasted_iota(jnp.int32, (slots, block), 0)
        gated = jnp.zeros((slots, block), F32)
        for k in range(TOP):
            gate = jnp.sum(
                jnp.where(expert == given[k : k + 1, :], probs, 0.0), axis=0, keepdims=True
            )
            gated = jnp.where(slot == targets(given, k), gate, gated)
        column = jnp.broadcast_to(jnp.sum(gated, axis=1, keepdims=True), (slots, 128))
        fill_slots(i, r.gates, column)
        fill_slots(i, r.rows_in, matmul(r.table[i], values).astype(BF16))
        lane = lax.div(lax.broadcasted_iota(jnp.int32, (SLOTS, WIDTH), 1), RANK)
        at = pl.ds(pl.multiple_of(i * SLOTS, SLOTS), SLOTS)
        r.slot_sets[at, :] = (lane == given[SET_ROW : SET_ROW + 1, 0:1]).astype(F32)
        return 0

    lax.fori_loop(0, all_images, dispatch, 0)

    chunks = [
        (
            r.first.at[e], r.first_end.at[e], r.first_mid.at[e], r.first_stage.at[e],
            r.first_final.at[e],
            functools.partial(lambda e, dp, tp: r.first_all.at[dp, tp, e], e),
        )
        for e in range(experts)
    ]
    chunks += [
        (r.second_sum, r.second_end, r.second_mid, r.second_stage, r.second_final,
         lambda dp, tp: r.second_all.at[dp, tp]),
        (r.early_sum, r.early_end, r.early_mid, r.early_stage, r.early_final,
         lambda dp, tp: r.early_all.at[dp, tp]),
        (r.late_sum, r.late_end, r.late_mid, r.late_stage, r.late_final,
         lambda dp, tp: r.late_all.at[dp, tp]),
    ]
    inner, outer_half = place.inner, 1 - place.inner
    to_partner, to_mid = {"ctx": place.partner}, {"ctx": place.other_mid}
    flows, spreads = [], []
    for mine, end, mid, stage, final, slot in chunks:
        flows.append(
            dict(
                outer=wire.copy(mine.at[outer_half], end.at[outer_half], to_partner),
                inner=wire.copy(mine.at[inner], end.at[inner], to_partner),
                cross=wire.copy(stage, mid, to_mid),
                back=wire.copy(final.at[inner], final.at[inner], to_partner),
                share=wire.copy(final.at[inner], final.at[inner], to_mid),
                pass_on=wire.copy(final.at[outer_half], final.at[outer_half], to_partner),
            )
        )
        spreads.append(Spread(place, wire, final, slot))

    def send_end(k):
        @pl.when(place.is_end)
        def _():
            flows[k]["outer"].start()
            flows[k]["inner"].start()

    def mid_first(k):
        mine, end, mid, stage, final, slot = chunks[k]

        @pl.when(place.is_mid)
        def _():
            flows[k]["outer"].wait_recv()
            stage[...] = add_rounded(mine[outer_half], end[outer_half])
            flows[k]["cross"].start()

    def mid_second(k):
        mine, end, mid, stage, final, slot = chunks[k]

        @pl.when(place.is_mid)
        def _():
            flows[k]["inner"].wait_recv()
            flows[k]["cross"].wait_recv()
            final[inner] = add_rounded(mine[inner], end[inner], mid[...])
            flows[k]["share"].start()
            flows[k]["back"].start()

    def settle(k):
        @pl.when(place.is_mid)
        def _():
            flows[k]["share"].wait_recv()
            flows[k]["pass_on"].start()

        @pl.when(place.is_end)
        def _():
            flows[k]["back"].wait_recv()
            flows[k]["pass_on"].wait_recv()

        spreads[k].start()

    stages = (
        mid_first, mid_second, settle,
        lambda k: spreads[k].forward(), lambda k: spreads[k].diagonal(),
    )
    reached = [0] * len(chunks)
    SUM, FINAL, SENT, ONWARD, DONE = range(1, 6)
    second_at, early_at, late_at = experts, experts + 1, experts + 2

    def go(k, stage):
        while reached[k] < stage:
            stages[reached[k]](k)
            reached[k] += 1

    def go_first(*pairs):
        for k, stage in pairs:
            if k < experts:
                go(k, stage)

    def run_expert(e):
        need(("a_first", e), ("b_first", e), ("up", e))
        need(("a_second", e), ("b_second", e), ("down", e))
        a_first, b_first = r.v_first_a[e].reshape(WIDTH, D), r.v_first_b[e].reshape(WIDTH, -1)
        a_second = r.v_second_a[e].reshape(WIDTH, -1)
        b_second = r.v_second_b[e].reshape(WIDTH, D)
        sums = None
        size = min(EXPERT_ROWS, all_images * SLOTS)
        for c in range(all_images * SLOTS // size):
            at = slice(c * size, (c + 1) * size)
            rows = r.rows_in[e, at]
            grads = r.grad_slots[e, at].astype(F32)
            gate = r.gates[e, at][:, 0:1]
            sets = r.slot_sets[at]
            lifted = (times_transposed(rows, a_first) * sets).astype(BF16)
            before = matmul(rows, r.v_up[e]) + matmul(lifted, b_first)
            phi = 0.5 * (1.0 + lax.erf(before * SQRT_HALF))
            active = (before * phi).astype(BF16)
            slope = phi + before * (INV_ROOT_TWO_PI * jnp.exp(-0.5 * before * before))
            lowered = (times_transposed(active, a_second) * sets).astype(BF16)
            out = matmul(active, r.v_down[e]) + matmul(lowered, b_second)
            grad_out = (grads * gate).astype(BF16)
            grad_lowered = (times_transposed(grad_out, b_second) * sets).astype(BF16)
            grad_active = times_transposed(grad_out, r.v_down[e]) + matmul(grad_lowered, a_second)
            grad_before = (grad_active * slope).astype(BF16)
            grad_lifted = (times_transposed(grad_before, b_first) * sets).astype(BF16)
            grad_rows = times_transposed(grad_before, r.v_up[e]) + matmul(grad_lifted, a_first)
            made = [
                inner_rows(lifted, grad_before),
                inner_rows(grad_lowered, active),
                inner_rows(grad_lifted, rows),
                inner_rows(lowered, grad_out),
            ]
            sums = made if sums is None else [a + b for a, b in zip(sums, made)]
            lane = lax.broadcasted_iota(jnp.int32, (size, 128), 1)
            gate_grads = jnp.sum(out * grads, axis=1, keepdims=True)
            gate_grads = jnp.where(lane == owned + e, gate_grads, 0.0).astype(BF16)
            some = slice(c * size // SLOTS, (c + 1) * size // SLOTS)
            to = slice(e * SLOTS, (e + 1) * SLOTS)
            number = size // SLOTS
            r.payload[some, to, 0:D] = grad_rows.astype(BF16).reshape(number, SLOTS, D)
            r.payload[some, to, D:CRITICAL] = gate_grads.reshape(number, SLOTS, 128)
            r.payload[some, to, CRITICAL:] = (out * gate).astype(BF16).reshape(number, SLOTS, D)
        r.first[e, 0] = sums[0].astype(BF16)
        r.first[e, 1] = sums[1].astype(BF16)
        share = D // place.tp_size
        for number in range(2):
            for t in range(place.tp_size):
                r.second[t, number, e] = sums[2 + number][:, t * share : (t + 1) * share].astype(
                    BF16
                )

    for e in range(experts):
        run_expert(e)
        send_end(e)
        go_first(*((e - 1 - n, n + 1) for n in range(3) if e - 1 - n >= 0))

    second_swap = wire.copy(
        r.second.at[place.other_tp], r.second_got, {"tp": place.other_tp}
    )
    swap = wire.copy(r.partial.at[1 - place.core], r.from_sibling, {"dp": place.sibling})

    def combine(core):
        def run(chip, _):
            for n in range(images):
                i = (chip * 2 + core) * images + n
                made = inner_rows(r.table[i], r.payload[i]).astype(BF16)
                for t in range(place.tp_size):
                    r.partial[core, chip, t, n * half : (n + 1) * half, :] = made[
                        t * half : (t + 1) * half
                    ]
            return 0

        lax.fori_loop(0, place.chips, run, 0)

    combine(1 - place.core)
    swap.start()
    combine(place.core)
    swap.wait_recv()
    returns = []
    for at in (slice(0, CRITICAL), slice(CRITICAL, CRITICAL + D)):
        copies = []
        for i, j in place.offsets() + [(0, 0)]:
            dp, tp = place.ahead(i, j)
            chip = lax.div(dp, 2)
            index = i * place.tp_size + j
            both = add_rounded(
                r.partial[place.core, chip, tp, :, at], r.from_sibling[chip, tp, :, at]
            )
            if index:
                r.from_sibling[chip, tp, :, at] = both
                copy = wire.copy(
                    r.from_sibling.at[chip, tp, :, at],
                    r.received.at[index, :, at],
                    {"dp": dp, "tp": tp},
                )
                copy.start()
                copies.append(copy)
            else:
                r.received[0, :, at] = both
        returns.append(copies)
        if not at.start:
            second_swap.start()
    late_sends = [swap] + returns[0] + returns[1]
    last = experts - 1
    go_first((last - 2, SENT), (last - 1, FINAL), (last, SUM))
    go_first((last - 3, ONWARD))
    for copy in returns[0]:
        copy.wait_recv()

    def live_column(i):
        lane = lax.broadcasted_iota(jnp.int32, (half, block), 1)
        row = lax.broadcasted_iota(jnp.int32, (half, block), 0) + place.tp * half
        live = r.ints[i, LIVE_ROW : LIVE_ROW + 1, :].astype(F32)
        return jnp.sum(jnp.where(lane == row, live, 0.0), axis=1, keepdims=True)

    lives = [live_column(i) for i in range(images)]
    total = r.received[0, :, :CRITICAL].astype(F32)
    for k in range(1, r.received.shape[0]):
        total = total + r.received[k, :, :CRITICAL].astype(F32)
    hidden = r.hidden[...]
    grad_probs = total[:, D : D + EXPERTS]
    grad_output = jnp.concatenate(
        [
            r.cot_all[place.dp * images + i, pl.ds(start, half), :].astype(F32) * lives[i]
            for i in range(images)
        ],
        axis=0,
    )
    rows = r.expert_in[...].reshape(count, D)
    router_lift = (times_transposed(rows, router_low) * own_sets).astype(BF16)
    logits = times_transposed(rows, r.router_t[...]) + matmul(router_lift, router_high)
    powers = jnp.exp(logits - jnp.max(logits, axis=-1, keepdims=True))
    gate_probs = powers / jnp.sum(powers, axis=-1, keepdims=True)
    grad_logits = (
        gate_probs * (grad_probs - jnp.sum(grad_probs * gate_probs, axis=-1, keepdims=True))
    ).astype(BF16)
    grad_router_lift = (times_transposed(grad_logits, router_high) * own_sets).astype(BF16)
    grad_expert_in = (
        total[:, :D] + matmul(grad_logits, r.router_t[...]) + matmul(grad_router_lift, router_low)
    )
    _, unit, factor = normalize(hidden, gain_two, shift_two)
    grad_rows = grad_output + normalize_back(grad_expert_in, unit, factor, gain_two)
    r.grad_hidden[...] = grad_rows
    grad_attended = grad_rows.astype(BF16)
    grad_mixing_lift = (times_transposed(grad_attended, mixing_high) * own_sets).astype(BF16)
    grad_heads = (
        matmul(grad_attended, r.mixing_all[...]) + matmul(grad_mixing_lift, mixing_low)
    ).astype(BF16)
    r.heads[...] = grad_heads.reshape(images, half, D)
    mix = r.head_mix[...]
    lane = lax.broadcasted_iota(jnp.int32, (D, 128), 1)
    head = lax.div(lax.broadcasted_iota(jnp.int32, (D, 128), 0), HD)
    ones = (lane == head).astype(F32).astype(BF16)
    delta_rows = split_sum(grad_heads.astype(F32) * mix.astype(F32), ones)
    r.delta[...] = delta_rows
    log_rows = r.logs[...]
    for i in range(images):
        part = slice(i * half, (i + 1) * half)
        pad = jnp.zeros((128 - half, 128), F32)
        turned = [
            jnp.concatenate([v[part], pad], axis=0).T[:HEADS] for v in (log_rows, delta_rows)
        ]
        row = 0
        for rest, number in zip(turned, (3, 2)):
            for _ in range(number):
                top = rest.astype(BF16)
                r.stats[i, row : row + HEADS, :] = top
                rest = rest - top.astype(F32)
                row += HEADS

    def heads_slot(ctx, tp):
        at = pl.multiple_of((ctx * place.tp_size + tp) * half, 16)
        return r.heads_all.at[:, pl.ds(at, half), :]

    chain = Chain(
        place, wire, [r.heads, r.stats],
        [heads_slot, lambda ctx, tp: r.stats_all.at[ctx * place.tp_size + tp]],
        [True, True], True,
    )
    chain.start()

    def spread_start(values, got):
        rows = got.shape[1]
        copies = []
        for k, (dp, tp) in enumerate(place.peers):
            at = pl.ds(pl.multiple_of((dp * place.tp_size + tp) * rows, 16), rows)
            copy = wire.copy(values.at[at], got.at[k], {"dp": dp, "tp": tp})
            copy.start()
            copies.append(copy)
        return copies

    def spread_end(copies, values, got, total):
        rows = got.shape[1]
        for copy in copies:
            copy.wait()
        added = values[pl.ds(pl.multiple_of(place.me * rows, 16), rows), :].astype(F32)
        for k in range(plane - 1):
            added = added + got[k].astype(F32)
        total[...] = added.astype(BF16).reshape(total.shape)

    def put_tiles(target, products):
        tile = 0
        for product in products:
            for n in range(product.shape[1] // 128):
                target[tile * WIDTH : (tile + 1) * WIDTH, :] = product[
                    :, n * 128 : (n + 1) * 128
                ].astype(BF16)
                tile += 1
        if tile * WIDTH < target.shape[0]:
            target[tile * WIDTH :, :] = jnp.zeros(
                (target.shape[0] - tile * WIDTH, 128), BF16
            )

    wide_logits = jnp.concatenate(
        [grad_logits, jnp.zeros((count, 128 - EXPERTS), BF16)], axis=1
    )
    put_tiles(
        r.early,
        (
            inner_rows(grad_mixing_lift, mix),
            inner_rows(r.mixing_lift[...], grad_attended),
            inner_rows(grad_router_lift, rows),
            inner_rows(router_lift, wide_logits),
        ),
    )
    early_spread = spread_start(r.early, r.early_got)
    second_swap.wait()
    r.second_sum[...] = add_rounded(r.second[place.tp], r.second_got[...])
    send_end(second_at)
    go_first((last, FINAL), (last - 1, SENT), (last - 2, ONWARD))
    chain.step(1)
    go_first((last - 3, DONE), (last, SENT))
    chain.step(2)
    go(second_at, SUM)
    go_first((last - 1, ONWARD))
    chain.step(3)
    spread_end(early_spread, r.early, r.early_got, r.early_sum)
    send_end(early_at)
    go(second_at, FINAL)
    go_first((last - 2, DONE))
    chain.finish_own()
    for s in range(1, chain.steps + 1):
        chain.landed(s)

    def heads_back(i, j):
        part = slice(i * half, (i + 1) * half)
        at = slice(j * 2 * HD, (j + 1) * 2 * HD)
        keys_open = r.keys_open[i : i + 1, :] > 0
        own_open = jnp.concatenate([lives[i], lives[i]], axis=0) > 0
        found = jnp.concatenate(
            [r.stats_all[n, i][:, :half].astype(F32) for n in range(r.stats_all.shape[0])], axis=1
        )
        log_t = found[0:HEADS] + found[HEADS : 2 * HEADS] + found[2 * HEADS : 3 * HEADS]
        delta_t = found[3 * HEADS : 4 * HEADS] + found[4 * HEADS :]
        q_all, k_all, v_all = (r.joined[p, i, :, at] for p in range(3))
        g_all = r.heads_all[i, :, at]

        def column(values):
            return jnp.concatenate(
                [values[:, 2 * j : 2 * j + 1], values[:, 2 * j + 1 : 2 * j + 2]], axis=0
            )

        def across(values):
            return jnp.concatenate(
                [
                    jnp.broadcast_to(values[2 * j + n : 2 * j + n + 1, :], (half, values.shape[1]))
                    for n in range(2)
                ],
                axis=0,
            )

        q = stack_pair(r.joined[0, i, own, at], masks, scale)
        g = stack_pair(r.heads[i, :, at], masks)
        scores = jnp.where(keys_open, times_transposed(q, k_all), MASKED)
        probs = jnp.exp(scores - column(r.logs[part]))
        grad_probs_att = times_transposed(g, v_all)
        grad_scores = (probs * (grad_probs_att - column(r.delta[part]))).astype(BF16)
        r.grads[0, part, at] = (join_pair(matmul(grad_scores, k_all), masks) * scale).astype(BF16)
        k = stack_pair(r.joined[1, i, own, at], masks, scale)
        v = stack_pair(r.joined[2, i, own, at], masks)
        scores = jnp.where(own_open, times_transposed(k, q_all), MASKED)
        probs = jnp.exp(scores - across(log_t))
        grad_probs_att = times_transposed(v, g_all)
        grad_scores = (probs * (grad_probs_att - across(delta_t))).astype(BF16)
        r.grads[1, part, at] = (join_pair(matmul(grad_scores, q_all), masks) * scale).astype(BF16)
        r.grads[2, part, at] = join_pair(matmul(probs.astype(BF16), g_all), masks).astype(BF16)

    for i in range(images):
        for j in range(HEADS // 2):
            heads_back(i, j)
        if i == 0:
            go(early_at, SUM)
            go(second_at, SENT)
            go_first((last, ONWARD), (last - 1, DONE))
    go(early_at, FINAL)
    lift = times_transposed(r.grads[0], high(0))
    into = times_transposed(r.grads[0], r.weights_all[0])
    for p in range(1, 3):
        lift = lift + times_transposed(r.grads[p], high(p))
        into = into + times_transposed(r.grads[p], r.weights_all[p])
    lift = (lift * own_sets).astype(BF16)
    lift_in = jnp.concatenate([r.lift_all[i, own, :] for i in range(images)], axis=0)
    put_tiles(
        r.late,
        [inner_rows(lift_in, r.grads[p]) for p in range(3)]
        + [inner_rows(lift, r.own_in[...].reshape(count, D))],
    )
    late_spread = spread_start(r.late, r.late_got)
    go(second_at, ONWARD)
    into = into + matmul(lift, attend_low)
    flat = jnp.concatenate([r.tokens_all[i, own, :] for i in range(images)], axis=0).astype(F32)
    _, unit, factor = normalize(flat, gain_one, shift_one)
    result = r.grad_hidden[...] + normalize_back(into, unit, factor, gain_one)
    r.grad_own[...] = result.astype(BF16).reshape(images, half, D)
    for copy in returns[1]:
        copy.wait_recv()
    total = r.hidden[...]
    for k in range(r.received.shape[0]):
        total = total + r.received[k, :, CRITICAL:].astype(F32)
    r.out_own[...] = total.astype(BF16).reshape(images, half, D)
    outs = []
    for values, gathered in ((r.out_own, r.out_all), (r.grad_own, r.grad_all)):
        spot = gathered.at[:, pl.ds(start, half), :]
        outs.append(wire.copy(values, spot, {"tp": place.other_tp}))
        outs.append(wire.near(values, spot))
    spread_end(late_spread, r.late, r.late_got, r.late_sum)
    send_end(late_at)
    for copy in outs:
        copy.start()
    go(early_at, SENT)
    go_first((last, DONE))
    go(late_at, SUM)
    go(second_at, DONE)
    go(late_at, FINAL)
    go(early_at, ONWARD)
    go(late_at, SENT)
    go(early_at, DONE)
    for k in range(len(chunks)):
        go(k, DONE)

    @pl.when(place.is_end)
    def _():
        for flow in flows:
            flow["outer"].wait_send()
            flow["inner"].wait_send()

    @pl.when(place.is_mid)
    def _():
        for flow in flows:
            for name in ("cross", "back", "share", "pass_on"):
                flow[name].wait_send()

    for spread in spreads:
        spread.finish()
    for spread in [weights, mixing, numbers, router, cotangents, expert_rows] + spreads:
        spread.drain()
    tokens_chain.drain()
    chain.drain()
    for copy in late_sends:
        copy.wait_send()
    for copy in outs:
        copy.wait()
    assert not pending


def run_layer(sizes, **inputs):
    dp, ctx, tp = sizes
    assert ctx == 4 and tp == 2
    plane, chips = dp * tp, dp // 2
    images, block = inputs["tokens"].shape[:2]
    assert images == 2
    half = block // tp
    count, seq, all_images = images * half, ctx * block, dp * images
    experts, _, hidden = inputs["up_weight"].shape
    rows, lanes = inputs["mixing"].shape
    slots = experts * SLOTS
    sent = CRITICAL + D
    early_rows = small_rows(3 * (D // 128) + 1, plane)
    late_rows = small_rows(4 * (D // 128), plane)
    second = (2, experts, WIDTH, D // tp)
    full = dict(
        first=(experts, 2, WIDTH, hidden),
        second=second,
        early=(2, early_rows // 2, 128),
        late=(2, late_rows // 2, 128),
    )
    cut = {name: shape[1:] for name, shape in full.items()}
    cut["first"] = (experts, WIDTH, hidden)
    outputs = {name + "_all": (dp, tp) + shape for name, shape in full.items()}
    outputs.update(out_all=(images, block, D), grad_all=(images, block, D))
    narrow = dict(
        tokens_all=(images, seq, D),
        weights_all=(3, dp * rows, tp * lanes),
        mixing_all=(dp * rows, tp * lanes),
        router_all=(dp,) + inputs["router"].shape,
        router_t=(EXPERTS, D),
        cot_all=(all_images, block, D),
        rows_all=(all_images, block, D),
        v_attend_low=(SETS, RANK, D),
        v_attend_high=(SETS, 3, RANK, D),
        v_mixing_low=(SETS, RANK, D),
        v_mixing_high=(SETS, RANK, D),
        v_router_low=(SETS, RANK, D),
        v_router_high=(SETS, RANK, EXPERTS),
        v_first_a=(experts, SETS, RANK, D),
        v_first_b=(experts, SETS, RANK, hidden),
        v_second_a=(experts, SETS, RANK, hidden),
        v_second_b=(experts, SETS, RANK, D),
        v_up=(experts, D, hidden),
        v_down=(experts, hidden, D),
        lift_all=(images, seq, WIDTH),
        joined=(3, images, seq, D),
        own_in=(images, half, D),
        head_mix=(count, D),
        mixing_lift=(count, WIDTH),
        expert_in=(images, half, D),
        table=(all_images, slots, block),
        grad_slots=(experts, all_images * SLOTS, D),
        rows_in=(experts, all_images * SLOTS, D),
        payload=(all_images, slots, sent),
        partial=(2, chips, tp, count, sent),
        from_sibling=(chips, tp, count, sent),
        received=(chips * tp, count, sent),
        first=full["first"],
        second=(tp,) + second,
        second_got=second,
        second_sum=second,
        early=(plane * early_rows, 128),
        late=(plane * late_rows, 128),
        early_got=(plane - 1, early_rows, 128),
        late_got=(plane - 1, late_rows, 128),
        early_sum=full["early"],
        late_sum=full["late"],
        heads=(images, half, D),
        stats=(images, 5 * HEADS, 128),
        heads_all=(images, seq, D),
        stats_all=(ctx * tp, images, 5 * HEADS, 128),
        grads=(3, count, D),
        out_own=(images, half, D),
        grad_own=(images, half, D),
    )
    for name in full:
        narrow[name + "_end"] = narrow[name + "_final"] = full[name]
        narrow[name + "_mid"] = narrow[name + "_stage"] = cut[name]
    wide = dict(
        logs=(count, 128),
        delta=(count, 128),
        hidden=(count, D),
        grad_hidden=(count, D),
        gates=(experts, all_images * SLOTS, 128),
        slot_sets=(all_images * SLOTS, WIDTH),
        keys_open=(images, seq),
    )
    integers = dict(
        ints=(images, 8, block),
        ints_all=(all_images, 8, block),
        ctx_ints=(ctx, images, 8, block),
    )
    scratch = {}
    for shapes, dtype in ((narrow, BF16), (wide, F32), (integers, jnp.int32)):
        for name, shape in shapes.items():
            scratch[name] = pltpu.VMEM(shape, dtype)
    chunks = experts + 3
    remote = (
        2 * Chain.remote(ctx, 2)
        + (3 + chunks) * Spread.remote(sizes)
        + 3 * Spread.remote(sizes, False)
        + 6 * chunks
        + 2
        + 2 * (chips * tp - 1)
        + 2 * (plane - 1)
        + 2
    )
    scratch["send"] = pltpu.SemaphoreType.DMA((remote,))
    scratch["recv"] = pltpu.SemaphoreType.DMA((remote,))
    scratch["local"] = pltpu.SemaphoreType.DMA((7 + 6 * experts + 6 + chunks + 2 + 2,))
    kinds = dict(
        adapter_set=IN_SMEM, image_mask=IN_SMEM, gains=IN_VMEM, routes_t=IN_VMEM,
        slots_t=IN_VMEM, token_mask=IN_VMEM,
    )
    names = tuple(inputs) + tuple(outputs) + tuple(scratch)
    made = pl.pallas_call(
        functools.partial(layer_kernel, sizes, names),
        out_shape=tuple(jax.ShapeDtypeStruct(shape, BF16) for shape in outputs.values()),
        in_specs=[kinds.get(name, ANY) for name in inputs],
        out_specs=(ANY,) * len(outputs),
        scratch_shapes=tuple(scratch.values()),
        compiler_params=pltpu.CompilerParams(
            collective_id=0, has_side_effects=True, vmem_limit_bytes=62 << 20
        ),
    )(*inputs.values())
    return dict(zip(outputs, made))


def assemble_kernel(
    first, second, early, late, up, down_t, narrow_t, narrow,
    attend_down, attend_up, mixing_down, mixing_up, router_down, router_up,
):
    lanes, part = first.shape[-1], second.shape[-1]
    for tp in range(first.shape[1]):
        for half, out in ((0, up), (1, down_t)):
            out[:, 0, :, tp * lanes : (tp + 1) * lanes] = (
                first[0, tp, 0, half].astype(F32).reshape(SETS, RANK, lanes)
            )
        for half, out in ((0, narrow_t), (1, narrow)):
            out[:, 0, :, tp * part : (tp + 1) * part] = (
                second[0, tp, half, 0].astype(F32).reshape(SETS, RANK, part)
            )

    @pl.when(pl.program_id(0) == 0)
    def _():
        def tile(small, k):
            return small[k * WIDTH : (k + 1) * WIDTH, :].astype(F32).reshape(SETS, RANK, 128)

        count = D // 128
        for p in range(3):
            for k in range(count):
                attend_up[:, p, :, k * 128 : (k + 1) * 128] = tile(late, p * count + k)
        for k in range(count):
            attend_down[:, :, k * 128 : (k + 1) * 128] = tile(late, 3 * count + k)
        for p, out in enumerate((mixing_down, mixing_up, router_down)):
            for k in range(count):
                out[:, :, k * 128 : (k + 1) * 128] = tile(early, p * count + k)
        router_up[...] = tile(early, 3 * count)[:, :, :EXPERTS]


def assemble(first, second, early, late):
    dp, tp, experts, _, width, lanes = first.shape
    part = second.shape[-1]

    def split(e):
        return lax.div(e, experts), lax.rem(e, experts)

    def expert_out(size):
        return (
            jax.ShapeDtypeStruct((SETS, EXPERTS, RANK, size), F32),
            pl.BlockSpec((SETS, 1, RANK, size), lambda e: (0, e, 0, 0)),
        )

    def whole_out(*shape):
        return (
            jax.ShapeDtypeStruct(shape, F32),
            pl.BlockSpec(shape, lambda e: (0,) * len(shape)),
        )

    outs = (
        [expert_out(FF)] * 2
        + [expert_out(D)] * 2
        + [whole_out(SETS, RANK, D), whole_out(SETS, 3, RANK, D)]
        + [whole_out(SETS, RANK, D)] * 3
        + [whole_out(SETS, RANK, EXPERTS)]
    )
    return pl.pallas_call(
        assemble_kernel,
        grid=(EXPERTS,),
        out_shape=[out[0] for out in outs],
        in_specs=[
            pl.BlockSpec(
                (1, tp, 1, 2, width, lanes), lambda e: (split(e)[0], 0, split(e)[1], 0, 0, 0)
            ),
            pl.BlockSpec(
                (1, tp, 2, 1, width, part), lambda e: (split(e)[0], 0, 0, split(e)[1], 0, 0)
            ),
            pl.BlockSpec(early.shape, lambda e: (0, 0)),
            pl.BlockSpec(late.shape, lambda e: (0, 0)),
        ],
        out_specs=[out[1] for out in outs],
        compiler_params=pltpu.CompilerParams(vmem_limit_bytes=32 << 20),
    )(first, second, early, late)


def per_device(
    sizes,
    tokens,
    cotangent,
    routes,
    slot_index,
    token_mask,
    image_mask,
    adapter_set,
    first_gain,
    first_shift,
    second_gain,
    second_shift,
    attend_weight,
    mixing_weight,
    router_weight,
    expand_weight,
    shrink_weight,
    attend_down,
    attend_up,
    mixing_down,
    mixing_up,
    router_down,
    router_up,
    expand_down,
    expand_up,
    shrink_down,
    shrink_up,
):
    def flipped(values):
        return jnp.swapaxes(values, -1, -2)

    made = run_layer(
        sizes,
        tokens=tokens,
        cotangent=cotangent,
        weights=jnp.transpose(attend_weight, (1, 0, 2)),
        mixing=mixing_weight,
        router=flipped(router_weight),
        routes_t=flipped(routes),
        slots_t=flipped(slot_index),
        token_mask=token_mask,
        image_mask=image_mask,
        adapter_set=adapter_set,
        gains=jnp.stack([first_gain, first_shift, second_gain, second_shift]),
        up_weight=expand_weight,
        down_weight=shrink_weight,
        attend_low=flipped(attend_down),
        attend_high=jnp.transpose(attend_up, (0, 2, 1, 3)),
        mixing_low=flipped(mixing_down),
        mixing_high=mixing_up,
        router_low=flipped(router_down),
        router_high=router_up,
        first_a=flipped(expand_down),
        first_b=expand_up,
        second_a=flipped(shrink_down),
        second_b=shrink_up,
    )
    wide = assemble(
        made["first_all"],
        made["second_all"],
        made["early_all"].reshape(-1, 128),
        made["late_all"].reshape(-1, 128),
    )
    return (
        made["out_all"],
        made["grad_all"],
        flipped(wide[4]),
        jnp.transpose(wide[5], (0, 2, 1, 3)),
        flipped(wide[6]),
        wide[7],
        flipped(wide[8]),
        wide[9],
        flipped(wide[2]),
        wide[0],
        flipped(wide[1]),
        wide[3],
    )


def solution(mesh):
    sizes = (mesh.shape["dp"], mesh.shape["ctx"], mesh.shape["tp"])
    tokens_spec = P("dp", "ctx", None)
    in_specs = (
        (tokens_spec,) * 4
        + (P("dp", "ctx"), P("dp"), P("dp"))
        + (P(),) * 4
        + (P("dp", None, "tp"), P("dp", "tp"), P("dp", None))
        + (P("dp", None, "tp"), P("dp", "tp", None))
        + (P(),) * 10
    )
    out_specs = (tokens_spec,) * 2 + (P(),) * 10
    return jax.shard_map(
        functools.partial(per_device, sizes),
        mesh=mesh,
        in_specs=in_specs,
        out_specs=out_specs,
        check_vma=False,
    )
```

```python
import functools
import types

import jax
import jax.numpy as jnp
from jax import lax
from jax.experimental import pallas as pl
from jax.experimental.pallas import tpu as pltpu
from jax.sharding import PartitionSpec as P

D = 512
HEADS = 8
HD = 64
FF = 2048
EXPERTS = 16
TOP = 2
RANK = 16
SETS = 4
CAP = 30
SLOTS = 32
WIDTH = SETS * RANK
LIVE_ROW = 2 * TOP
SET_ROW = LIVE_ROW + 1
CRITICAL = D + 128
EXPERT_ROWS = 256
ASSEMBLED = 2

EPSILON = 1e-06
MASKED = -1e30
SQRT_HALF = 0.7071067811865476
INV_ROOT_TWO_PI = 0.3989422804014327
F32 = jnp.float32
BF16 = jnp.bfloat16
MESH = pl.DeviceIdType.MESH
ANY = pl.BlockSpec(memory_space=pl.ANY)
IN_SMEM = pl.BlockSpec(memory_space=pltpu.SMEM)
IN_VMEM = pl.BlockSpec(memory_space=pltpu.VMEM)


def matmul(left_side, right_side):
    return jnp.dot(left_side, right_side, preferred_element_type=F32)


def inner_rows(left_side, right_side):
    return lax.dot_general(
        left_side, right_side, (((0,), (0,)), ((), ())), preferred_element_type=F32
    )


def times_transposed(left_side, right_side):
    return lax.dot_general(
        left_side, right_side, (((1,), (1,)), ((), ())), preferred_element_type=F32
    )


def normalize(values, gain_row, shift_row):
    centred = values - jnp.mean(values, axis=-1, keepdims=True)
    spread = jnp.mean(centred * centred, axis=-1, keepdims=True)
    factor = lax.rsqrt(spread + EPSILON)
    normed = centred * factor
    return (normed * gain_row + shift_row, normed, factor)


def normalize_back(grad_out, normed, factor, gain_row):
    scaled = grad_out * gain_row
    return factor * (
        scaled
        - jnp.mean(scaled, axis=-1, keepdims=True)
        - normed * jnp.mean(scaled * normed, axis=-1, keepdims=True)
    )


def add_rounded(*parts):
    total = parts[0].astype(F32)
    for part in parts[1:]:
        total = total + part.astype(F32)
    return total.astype(BF16)


def split_sum(values, ones):
    high = values.astype(BF16)
    low = (values - high.astype(F32)).astype(BF16)
    return matmul(high, ones) + matmul(low, ones)


def put_lanes(columns, width):
    lane = lax.broadcasted_iota(jnp.int32, (columns[0].shape[0], width), 1)
    total = jnp.zeros((columns[0].shape[0], width), F32)
    for k, column in enumerate(columns):
        total = jnp.where(lane == k, column, total)
    return total


def half_masks():
    lane = lax.broadcasted_iota(jnp.int32, (1, 2 * HD), 1)
    even = (lane < HD).astype(F32)
    return even, 1.0 - even


def stack_pair(rows, masks, factor=1.0):
    wide = rows.astype(F32) * factor
    return jnp.concatenate([wide * masks[0], wide * masks[1]], axis=0).astype(BF16)


def join_pair(rows, masks):
    half = rows.shape[0] // 2
    return rows[:half] * masks[0] + rows[half:] * masks[1]


SUM, SENT, ONWARD, DONE = range(1, 5)
E0, E1, E2, E3, SECOND, EARLY, LATE = range(-7, 0)
SCHEDULE = (
    (),
    ((E0, SUM),),
    ((E1, SUM),),
    ((E0, SENT), (E2, SUM), (E1, SENT)),
    ((E0, ONWARD), (E3, SUM)),
    ((E2, SENT), (E1, ONWARD)),
    ((E0, DONE), (SECOND, SUM)),
    ((E3, SENT), (E2, ONWARD)),
    ((E1, DONE),),
    ((SECOND, SENT),),
    ((EARLY, SUM), (E3, ONWARD)),
    ((E2, DONE),),
    ((SECOND, ONWARD),),
    ((EARLY, SENT),),
    (
        (E3, DONE), (LATE, SUM), (EARLY, ONWARD), (SECOND, DONE), (LATE, SENT), (EARLY, DONE),
        (LATE, ONWARD), (LATE, DONE),
    ),
)


def small_rows(tiles, plane):
    return -(-tiles * WIDTH // (plane * 16)) * 16


class Wire:
    def __init__(self, send, recv, local):
        self.send, self.recv, self.local = send, recv, local
        self.used = self.used_local = 0

    def copy(self, src, dst, device):
        k = self.used
        self.used += 1
        assert k < self.send.shape[0]
        return pltpu.make_async_remote_copy(
            src_ref=src,
            dst_ref=dst,
            send_sem=self.send.at[k],
            recv_sem=self.recv.at[k],
            device_id=device,
            device_id_type=MESH,
        )

    def near(self, src, dst):
        k = self.used_local
        self.used_local += 1
        assert k < self.local.shape[0]
        return pltpu.make_async_copy(src, dst, self.local.at[k])


class Place:
    def __init__(self, sizes):
        self.dp_size, self.ctx_size, self.tp_size = sizes
        self.chips = self.dp_size // 2
        self.plane = self.dp_size * self.tp_size
        self.dp = lax.axis_index("dp")
        self.ctx = lax.axis_index("ctx")
        self.tp = lax.axis_index("tp")
        self.chip = lax.div(self.dp, 2)
        self.core = lax.rem(self.dp, 2)
        self.sibling = self.chip * 2 + (1 - self.core)
        self.other_tp = lax.rem(self.tp + 1, 2)
        self.me = self.dp * self.tp_size + self.tp
        self.is_mid = jnp.logical_and(self.ctx >= 1, self.ctx <= 2)
        self.is_end = jnp.logical_not(self.is_mid)
        self.inner = lax.div(self.ctx, 2)
        self.partner = jnp.where(self.is_mid, self.inner * 3, 1 + self.inner)
        self.far_mid = 2 - self.inner
        self.far_end = 3 - 3 * self.inner
        self.peers = []
        for k in range(1, self.plane):
            peer = lax.rem(self.me + k, self.plane)
            self.peers.append((lax.div(peer, self.tp_size), lax.rem(peer, self.tp_size)))

    def ahead(self, i, j):
        return (
            lax.rem(self.chip + i, self.chips) * 2 + self.core,
            lax.rem(self.tp + j, self.tp_size),
        )

    def behind(self, i, j):
        return self.ahead(self.chips - i, self.tp_size - j)

    def offsets(self, over_tp=True):
        return [
            (i, j)
            for i in range(self.chips)
            for j in range(self.tp_size if over_tp else 1)
            if i or j
        ]

    def greet(self):
        barrier = pltpu.get_barrier_semaphore()
        for dp, tp in self.peers:
            pl.semaphore_signal(
                barrier, inc=1, device_id={"dp": dp, "tp": tp}, device_id_type=MESH
            )
        for ctx in (self.partner, self.far_mid):
            pl.semaphore_signal(barrier, inc=1, device_id={"ctx": ctx}, device_id_type=MESH)

        @pl.when(self.is_mid)
        def _():
            pl.semaphore_signal(
                barrier, inc=1, device_id={"ctx": self.far_end}, device_id_type=MESH
            )

    def met(self):
        barrier = pltpu.get_barrier_semaphore()
        pl.semaphore_wait(barrier, self.plane + 1 + jnp.where(self.is_mid, 1, 0))


class Spread:
    def __init__(self, place, wire, source, slot, over_tp=True, direct=False, near=True):
        self.place, self.wire, self.source, self.slot = place, wire, source, slot
        self.over_tp = over_tp
        self.relay = over_tp and not direct and place.chips == 2 and place.tp_size == 2
        self.near = near
        self.flights, self.across, self.beside, self.here = [], None, [], None

    def to_sibling(self, source, spot):
        copy = self.wire.copy(source, spot, {"dp": self.place.sibling})
        copy.start()
        self.beside.append(copy)

    def start(self):
        place = self.place
        spot = self.slot(place.dp, place.tp)
        for i, j in place.offsets(self.over_tp):
            if self.relay and i and j:
                continue
            dp, tp = place.ahead(i, j)
            copy = self.wire.copy(self.source, spot, {"dp": dp, "tp": tp})
            copy.start()
            self.flights.append((copy, i, j))
        self.to_sibling(self.source, spot)
        if self.near:
            self.here = self.wire.near(self.source, spot)
            self.here.start()

    def forward(self):
        for copy, i, j in sorted(self.flights, key=lambda f: f[1]):
            copy.wait_recv()
            got = self.slot(*self.place.behind(i, j))
            if self.relay and j:
                dp, tp = self.place.ahead(1, 0)
                self.across = self.wire.copy(got, got, {"dp": dp, "tp": tp})
                self.across.start()
            self.to_sibling(got, got)

    def diagonal(self):
        if self.relay:
            self.across.wait_recv()
            got = self.slot(*self.place.behind(1, 1))
            self.to_sibling(got, got)

    def finish(self):
        for copy in self.beside:
            copy.wait_recv()
        if self.near:
            self.here.wait()

    def drain(self):
        for copy, _, _ in self.flights:
            copy.wait_send()
        if self.relay:
            self.across.wait_send()
        for copy in self.beside:
            copy.wait_send()

    @staticmethod
    def remote(sizes, over_tp=True):
        return 2 * (sizes[0] // 2 * (sizes[2] if over_tp else 1) - 1) + 1


class Chain:
    def __init__(self, place, wire, sources, slots, over, with_own):
        self.place, n = place, place.ctx_size
        self.steps = n - 1
        to_tp = {"tp": place.other_tp}
        self.right, self.left, self.over_right, self.over_left = {}, {}, {}, {}
        self.own, self.here = [], []
        for source, slot in zip(sources, slots):
            spot = slot(place.ctx, place.tp)
            if with_own:
                self.own.append(wire.copy(source, spot, to_tp))
                self.here.append(wire.near(source, spot))
        for s in range(1, n):
            back = [slot(jnp.maximum(place.ctx - (s - 1), 0), place.tp) for slot in slots]
            ahead = [slot(jnp.minimum(place.ctx + (s - 1), n - 1), place.tp) for slot in slots]
            got_right = [slot(jnp.maximum(place.ctx - s, 0), place.tp) for slot in slots]
            got_left = [slot(jnp.minimum(place.ctx + s, n - 1), place.tp) for slot in slots]
            to_right = {"ctx": jnp.minimum(place.ctx + 1, n - 1)}
            to_left = {"ctx": jnp.maximum(place.ctx - 1, 0)}
            self.right[s] = [
                wire.copy(a if s == 1 else b, b, to_right) for a, b in zip(sources, back)
            ]
            self.left[s] = [
                wire.copy(a if s == 1 else b, b, to_left) for a, b in zip(sources, ahead)
            ]
            self.over_right[s] = {
                k: wire.copy(b, b, to_tp) for k, b in enumerate(got_right) if over[k]
            }
            self.over_left[s] = {
                k: wire.copy(b, b, to_tp) for k, b in enumerate(got_left) if over[k]
            }

    def sends_right(self, s):
        return jnp.logical_and(self.place.ctx >= s - 1, self.place.ctx < self.steps)

    def sends_left(self, s):
        return jnp.logical_and(self.place.ctx <= self.steps + 1 - s, self.place.ctx > 0)

    def gets_right(self, s):
        return self.place.ctx >= s

    def gets_left(self, s):
        return self.place.ctx <= self.steps - s

    @staticmethod
    def all_of(copies, verb):
        for copy in copies:
            getattr(copy, verb)()

    def start(self):
        pl.when(self.sends_right(1))(lambda: self.all_of(self.right[1], "start"))
        pl.when(self.sends_left(1))(lambda: self.all_of(self.left[1], "start"))
        self.all_of(self.own + self.here, "start")

    def step(self, s):
        def passed(got, over, sends):
            def run():
                for k, copy in enumerate(got[s]):
                    copy.wait_recv()
                    if s < self.steps:
                        pl.when(sends(s + 1))(got[s + 1][k].start)
                    if k in over[s]:
                        over[s][k].start()

            return run

        pl.when(self.gets_right(s))(passed(self.right, self.over_right, self.sends_right))
        pl.when(self.gets_left(s))(passed(self.left, self.over_left, self.sends_left))

    def landed(self, s):
        pl.when(self.gets_right(s))(lambda: self.all_of(self.over_right[s].values(), "wait_recv"))
        pl.when(self.gets_left(s))(lambda: self.all_of(self.over_left[s].values(), "wait_recv"))

    def finish_own(self):
        self.all_of(self.own, "wait_recv")
        self.all_of(self.here, "wait")

    def drain(self):
        self.all_of(self.own, "wait_send")
        for s in range(1, self.steps + 1):
            pl.when(self.gets_right(s))(lambda: self.all_of(self.over_right[s].values(), "wait_send"))
            pl.when(self.gets_left(s))(lambda: self.all_of(self.over_left[s].values(), "wait_send"))
            pl.when(self.sends_right(s))(lambda: self.all_of(self.right[s], "wait_send"))
            pl.when(self.sends_left(s))(lambda: self.all_of(self.left[s], "wait_send"))

    @staticmethod
    def remote(n, arrays):
        return arrays * (1 + 4 * (n - 1))


def layer_kernel(sizes, names, *refs):
    r = types.SimpleNamespace(**dict(zip(names, refs)))
    place = Place(sizes)
    wire = Wire(r.send, r.recv, r.local)
    plane = place.plane
    images, block = r.tokens.shape[:2]
    half = block // place.tp_size
    count = images * half
    seq = place.ctx_size * block
    experts, _, hidden_units = r.up_weight.shape
    all_images = place.dp_size * images
    owned = place.dp * experts
    start = pl.multiple_of(place.tp * half, 16)
    own_start = pl.multiple_of(place.ctx * block + place.tp * half, 16)
    own = pl.ds(own_start, half)
    masks = half_masks()
    scale = HD**-0.5

    pending = {}

    def load(name, source, target):
        pending[name] = wire.near(source, target)
        pending[name].start()

    def need(*wanted):
        for name in wanted:
            if name in pending:
                pending.pop(name).wait()

    place.greet()
    whole = pl.ds(pl.multiple_of(place.ctx * block, 16), block)
    load("tokens", r.tokens, r.tokens_all.at[:, whole, :])
    for name in (
        "attend_low", "attend_high", "mixing_low", "mixing_high", "router_low", "router_high",
    ):
        load(name, getattr(r, name), getattr(r, "v_" + name))
    r.ints[:, 0:TOP, :] = r.routes_t[...]
    r.ints[:, TOP : 2 * TOP, :] = r.slots_t[...]
    lane_set = lax.div(lax.broadcasted_iota(jnp.int32, (1, WIDTH), 1), RANK)
    picks = []
    for i in range(images):
        r.ints[i, LIVE_ROW : LIVE_ROW + 1, :] = r.token_mask[i : i + 1, :] * r.image_mask[i]
        r.ints[i, SET_ROW:, :] = jnp.full((8 - SET_ROW, block), r.adapter_set[i], jnp.int32)
        picks.append((lane_set == r.adapter_set[i]).astype(F32))
    gain_one, shift_one = r.first_gain[...], r.first_shift[...]
    gain_two, shift_two = r.second_gain[...], r.second_shift[...]

    place.met()

    rows, lanes = r.mixing.shape

    def at_rows(dp):
        return pl.ds(pl.multiple_of(dp * rows, 16), rows)

    def at_lanes(tp):
        return pl.ds(pl.multiple_of(tp * lanes, 128), lanes)

    def token_slot(i, ctx, tp):
        at = pl.multiple_of(ctx * block + tp * half, 16)
        return r.tokens_all.at[i, pl.ds(at, half), :]

    tokens_chain = Chain(
        place, wire,
        [r.tokens.at[i, pl.ds(start, half), :] for i in range(images)] + [r.ints],
        [functools.partial(token_slot, i) for i in range(images)]
        + [lambda ctx, tp: r.ctx_ints.at[ctx]],
        [True] * images + [False], False,
    )
    weights = Spread(
        place, wire, r.weights, lambda dp, tp: r.weights_all.at[:, at_rows(dp), at_lanes(tp)]
    )
    mixing = Spread(
        place, wire, r.mixing, lambda dp, tp: r.mixing_all.at[at_rows(dp), at_lanes(tp)]
    )
    numbers = Spread(
        place, wire, r.ints, lambda dp, tp: r.ints_all.at[pl.ds(dp * 2, 2)], over_tp=False
    )
    router = Spread(place, wire, r.router, lambda dp, tp: r.router_all.at[dp], over_tp=False)
    cotangents = Spread(
        place, wire, r.cotangent, lambda dp, tp: r.cot_all.at[pl.ds(dp * 2, 2)], over_tp=False
    )
    r.ctx_ints[place.ctx] = r.ints[...]
    tokens_chain.start()
    weights.start()
    numbers.start()
    router.start()
    mixing.start()
    cotangents.start()
    wide = pl.ds(pl.multiple_of(place.tp * hidden_units, 128), hidden_units)
    for e in range(experts):
        load(("a_first", e), r.first_a.at[:, owned + e], r.v_first_a.at[e])
        load(("b_first", e), r.first_b.at[:, owned + e, :, wide], r.v_first_b.at[e])
        load(("up", e), r.up_weight.at[e], r.v_up.at[e])
        load(("a_second", e), r.second_a.at[:, owned + e, :, wide], r.v_second_a.at[e])
        load(("b_second", e), r.second_b.at[:, owned + e], r.v_second_b.at[e])
        load(("down", e), r.down_weight.at[e], r.v_down.at[e])
    weights.forward()
    tokens_chain.step(1)
    weights.diagonal()
    tokens_chain.step(2)
    numbers.forward()
    router.forward()
    weights.finish()
    need("tokens", "attend_low", "attend_high")

    block_picks = jnp.concatenate(
        [jnp.broadcast_to(pick, (block, WIDTH)) for pick in picks], axis=0
    )
    own_sets = jnp.concatenate(
        [jnp.broadcast_to(pick, (half, WIDTH)) for pick in picks], axis=0
    )
    attend_low = r.v_attend_low[...].reshape(WIDTH, D)

    def high(p):
        return r.v_attend_high[:, p].reshape(WIDTH, D)

    def project(k, _):
        ctx = place.ctx
        first = jnp.where(ctx == 3, 2, ctx + 1)
        second = jnp.where(ctx == 0, 2, jnp.where(ctx == 1, 0, 1))
        third = jnp.where(ctx < 2, 3, 0)
        which = jnp.where(
            k == 0, ctx, jnp.where(k == 1, first, jnp.where(k == 2, second, third))
        )
        at = pl.ds(pl.multiple_of(which * block, 16), block)
        values = jnp.concatenate([r.tokens_all[i, at, :] for i in range(images)], axis=0)
        normed = normalize(values.astype(F32), gain_one, shift_one)[0].astype(BF16)
        lift = (times_transposed(normed, attend_low) * block_picks).astype(BF16)
        for i in range(images):
            r.lift_all[i, at, :] = lift[i * block : (i + 1) * block]
        for p in range(3):
            made = (matmul(normed, r.weights_all[p]) + matmul(lift, high(p))).astype(BF16)
            for i in range(images):
                r.joined[p, i, at, :] = made[i * block : (i + 1) * block]
        return 0

    def project_blocks(low, up):
        lax.fori_loop(low, up, project, 0)

    project_blocks(0, 1)
    tokens_chain.step(3)
    tokens_chain.landed(1)
    mixing.forward()
    project_blocks(1, 2)
    tokens_chain.landed(2)
    project_blocks(2, 3)
    cotangents.forward()
    mixing.diagonal()
    tokens_chain.landed(3)
    project_blocks(3, 4)
    mixing.finish()
    need("mixing_low", "mixing_high")
    mixing_low = r.v_mixing_low[...].reshape(WIDTH, D)
    mixing_high = r.v_mixing_high[...].reshape(WIDTH, D)

    def open_keys(i):
        return (
            jnp.concatenate(
                [
                    r.ctx_ints[n, i, LIVE_ROW : LIVE_ROW + 1, :]
                    for n in range(place.ctx_size)
                ],
                axis=1,
            )
            > 0
        )

    def rows_slot(i, dp, tp):
        at = pl.multiple_of(tp * half, 16)
        return r.rows_all.at[dp * images + i, pl.ds(at, half), :]

    expert_rows = []
    for i in range(images):
        r.keys_open[i : i + 1, :] = open_keys(i).astype(F32)
        token_rows = r.tokens_all[i, own, :].astype(F32)
        r.own_in[i] = normalize(token_rows, gain_one, shift_one)[0].astype(BF16)
        keys_open = r.keys_open[i : i + 1, :] > 0
        part = slice(i * half, (i + 1) * half)
        logs = []
        for j in range(HEADS // 2):
            at = slice(j * 2 * HD, (j + 1) * 2 * HD)
            q = stack_pair(r.joined[0, i, own, at], masks, scale)
            scores = times_transposed(q, r.joined[1, i, :, at])
            scores = jnp.where(keys_open, scores, MASKED)
            top = jnp.max(scores, axis=-1, keepdims=True)
            powers = jnp.exp(scores - top)
            total = jnp.sum(powers, axis=-1, keepdims=True)
            weights_att = (powers * (1.0 / total)).astype(BF16)
            mixed = join_pair(matmul(weights_att, r.joined[2, i, :, at]), masks)
            r.head_mix[part, at] = mixed.astype(BF16)
            log = jnp.maximum(top + jnp.log(total), -1e29)
            logs += [log[:half], log[half:]]
        r.logs[part, :] = put_lanes(logs, 128)
        mix = r.head_mix[part, :]
        lift = (times_transposed(mix, mixing_low) * picks[i]).astype(BF16)
        r.mixing_lift[part, :] = lift
        hidden = token_rows + times_transposed(mix, r.mixing_all[...]) + matmul(lift, mixing_high)
        r.hidden[part, :] = hidden
        r.expert_in[i] = normalize(hidden, gain_two, shift_two)[0].astype(BF16)
        expert_rows.append(
            Spread(place, wire, r.expert_in.at[i], functools.partial(rows_slot, i), direct=True)
        )
        expert_rows[i].start()

    slots = experts * SLOTS
    cotangents.finish()
    numbers.finish()
    router.finish()
    need("router_low", "router_high")
    router_low = r.v_router_low[...].reshape(WIDTH, D)
    router_high = r.v_router_high[...].reshape(WIDTH, EXPERTS)
    r.router_t[...] = jnp.concatenate([r.router_all[n] for n in range(place.dp_size)], axis=1)

    def targets(given, k):
        route, slot = given[k : k + 1, :], given[TOP + k : TOP + k + 1, :]
        local = route - owned
        here = (local >= 0) & (local < experts) & (slot < CAP)
        return jnp.where(here, local * SLOTS + slot, -1)

    def fill_slots(i, target, values):
        at = pl.ds(pl.multiple_of(i * SLOTS, SLOTS), SLOTS)
        for n in range(experts):
            target[n, at, :] = values[n * SLOTS : (n + 1) * SLOTS]

    def make_table(i, _):
        given = r.ints_all[i]
        slot = lax.broadcasted_iota(jnp.int32, (slots, block), 0)
        hot = jnp.zeros((slots, block), F32)
        for k in range(TOP):
            hot = jnp.where(slot == targets(given, k), 1.0, hot)
        hot = hot.astype(BF16)
        r.table[i] = hot
        fill_slots(i, r.grad_slots, matmul(hot, r.cot_all[i]).astype(BF16))
        return 0

    lax.fori_loop(0, all_images, make_table, 0, unroll=2)
    for spread in expert_rows:
        spread.forward()
    for spread in expert_rows:
        spread.finish()

    def dispatch(i, _):
        values = r.rows_all[i]
        given = r.ints_all[i]
        set_column = lax.div(lax.broadcasted_iota(jnp.int32, (WIDTH, 1), 0), RANK)
        pick = (set_column == given[SET_ROW : SET_ROW + 1, 0:1]).astype(F32)
        lift = (times_transposed(router_low, values) * pick).astype(BF16)
        logits = times_transposed(r.router_t[...], values) + inner_rows(router_high, lift)
        powers = jnp.exp(logits - jnp.max(logits, axis=0, keepdims=True))
        probs = powers / jnp.sum(powers, axis=0, keepdims=True)
        expert = lax.broadcasted_iota(jnp.int32, (EXPERTS, block), 0)
        slot = lax.broadcasted_iota(jnp.int32, (slots, block), 0)
        gated = jnp.zeros((slots, block), F32)
        for k in range(TOP):
            gate = jnp.sum(
                jnp.where(expert == given[k : k + 1, :], probs, 0.0), axis=0, keepdims=True
            )
            gated = jnp.where(slot == targets(given, k), gate, gated)
        column = jnp.broadcast_to(jnp.sum(gated, axis=1, keepdims=True), (slots, 128))
        fill_slots(i, r.gates, column)
        fill_slots(i, r.rows_in, matmul(r.table[i], values).astype(BF16))
        lane = lax.div(lax.broadcasted_iota(jnp.int32, (SLOTS, WIDTH), 1), RANK)
        at = pl.ds(pl.multiple_of(i * SLOTS, SLOTS), SLOTS)
        r.slot_sets[at, :] = (lane == given[SET_ROW : SET_ROW + 1, 0:1]).astype(F32)
        return 0

    lax.fori_loop(0, all_images, dispatch, 0, unroll=4)

    chunks = [
        (
            r.first.at[e], r.first_got.at[e], r.first_final.at[e],
            functools.partial(lambda e, dp, tp: r.first_all.at[dp, tp, e], e),
        )
        for e in range(experts)
    ]
    chunks += [
        (r.second_sum, r.second_in, r.second_final, lambda dp, tp: r.second_all.at[dp, tp]),
        (r.early_sum, r.early_in, r.early_final, lambda dp, tp: r.early_all.at[dp, tp]),
        (r.late_sum, r.late_in, r.late_final, lambda dp, tp: r.late_all.at[dp, tp]),
    ]
    inner, outer = place.inner, 1 - place.inner
    to_partner, to_far = {"ctx": place.partner}, {"ctx": place.far_mid}
    flows, spreads = [], []
    for mine, got, final, slot in chunks:
        flows.append(
            dict(
                beside=wire.copy(mine.at[inner], got.at[0], to_partner),
                across=wire.copy(mine.at[outer], got.at[1], to_far),
                beyond=wire.copy(mine.at[outer], got.at[2], to_far),
                back=wire.copy(final.at[inner], final.at[inner], to_partner),
                share=wire.copy(final.at[inner], final.at[inner], to_far),
                away=wire.copy(final.at[inner], final.at[inner], {"ctx": place.far_end}),
            )
        )
        spreads.append(Spread(place, wire, final, slot))

    def offer(k):
        @pl.when(place.is_end)
        def _():
            flows[k]["beyond"].start()
            flows[k]["beside"].start()

        @pl.when(place.is_mid)
        def _():
            flows[k]["across"].start()

    def total_half(k):
        mine, got, final, slot = chunks[k]

        @pl.when(place.is_mid)
        def _():
            for name in ("beside", "across", "beyond"):
                flows[k][name].wait_recv()
            final[inner] = add_rounded(mine[inner], got[0], got[1], got[2])
            for name in ("away", "share", "back"):
                flows[k][name].start()

    def settle(k):
        @pl.when(place.is_mid)
        def _():
            flows[k]["share"].wait_recv()

        @pl.when(place.is_end)
        def _():
            flows[k]["back"].wait_recv()
            flows[k]["away"].wait_recv()

        spreads[k].start()

    stages = (
        total_half, settle, lambda k: spreads[k].forward(), lambda k: spreads[k].diagonal(),
    )
    reached = [0] * len(chunks)
    second_at, early_at, late_at = experts, experts + 1, experts + 2

    def go(k, stage):
        while reached[k] < stage:
            stages[reached[k]](k)
            reached[k] += 1

    def at_point(point):
        for chunk, stage in SCHEDULE[point]:
            if len(chunks) + chunk >= 0:
                go(len(chunks) + chunk, stage)

    def run_expert(e):
        need(("a_first", e), ("b_first", e), ("up", e))
        need(("a_second", e), ("b_second", e), ("down", e))
        a_first, b_first = r.v_first_a[e].reshape(WIDTH, D), r.v_first_b[e].reshape(WIDTH, -1)
        a_second = r.v_second_a[e].reshape(WIDTH, -1)
        b_second = r.v_second_b[e].reshape(WIDTH, D)
        sums = None
        size = min(EXPERT_ROWS, all_images * SLOTS)
        for c in range(all_images * SLOTS // size):
            at = slice(c * size, (c + 1) * size)
            rows = r.rows_in[e, at]
            grads = r.grad_slots[e, at].astype(F32)
            gate = r.gates[e, at][:, 0:1]
            sets = r.slot_sets[at]
            lifted = (times_transposed(rows, a_first) * sets).astype(BF16)
            before = matmul(rows, r.v_up[e]) + matmul(lifted, b_first)
            phi = 0.5 * (1.0 + lax.erf(before * SQRT_HALF))
            active = (before * phi).astype(BF16)
            slope = phi + before * (INV_ROOT_TWO_PI * jnp.exp(-0.5 * before * before))
            lowered = (times_transposed(active, a_second) * sets).astype(BF16)
            out = matmul(active, r.v_down[e]) + matmul(lowered, b_second)
            grad_out = (grads * gate).astype(BF16)
            grad_lowered = (times_transposed(grad_out, b_second) * sets).astype(BF16)
            grad_active = times_transposed(grad_out, r.v_down[e]) + matmul(grad_lowered, a_second)
            grad_before = (grad_active * slope).astype(BF16)
            grad_lifted = (times_transposed(grad_before, b_first) * sets).astype(BF16)
            grad_rows = times_transposed(grad_before, r.v_up[e]) + matmul(grad_lifted, a_first)
            made = [
                inner_rows(lifted, grad_before),
                inner_rows(grad_lowered, active),
                inner_rows(grad_lifted, rows),
                inner_rows(lowered, grad_out),
            ]
            sums = made if sums is None else [a + b for a, b in zip(sums, made)]
            lane = lax.broadcasted_iota(jnp.int32, (size, 128), 1)
            gate_grads = jnp.sum(out * grads, axis=1, keepdims=True)
            gate_grads = jnp.where(lane == owned + e, gate_grads, 0.0).astype(BF16)
            some = slice(c * size // SLOTS, (c + 1) * size // SLOTS)
            to = slice(e * SLOTS, (e + 1) * SLOTS)
            number = size // SLOTS
            r.payload[some, to, 0:D] = grad_rows.astype(BF16).reshape(number, SLOTS, D)
            r.payload[some, to, D:CRITICAL] = gate_grads.reshape(number, SLOTS, 128)
            r.payload[some, to, CRITICAL:] = (out * gate).astype(BF16).reshape(number, SLOTS, D)
        r.first[e, 0] = sums[0].astype(BF16)
        r.first[e, 1] = sums[1].astype(BF16)
        share = D // place.tp_size
        for number in range(2):
            for t in range(place.tp_size):
                r.second[t, number, e] = sums[2 + number][:, t * share : (t + 1) * share].astype(
                    BF16
                )

    for e in range(experts):
        run_expert(e)
        offer(e)
        if e == experts - 2:
            at_point(0)
    at_point(1)

    second_swap = wire.copy(
        r.second.at[place.other_tp], r.second_got, {"tp": place.other_tp}
    )
    swap = wire.copy(r.partial.at[1 - place.core], r.from_sibling, {"dp": place.sibling})
    second_swap.start()

    def combine(core):
        def run(chip, _):
            for n in range(images):
                i = (chip * 2 + core) * images + n
                made = inner_rows(r.table[i], r.payload[i]).astype(BF16)
                for t in range(place.tp_size):
                    r.partial[core, chip, t, n * half : (n + 1) * half, :] = made[
                        t * half : (t + 1) * half
                    ]
            return 0

        lax.fori_loop(0, place.chips, run, 0)

    combine(1 - place.core)
    swap.start()
    combine(place.core)
    at_point(2)
    second_swap.wait()
    r.second_sum[...] = add_rounded(r.second[place.tp], r.second_got[...])
    offer(second_at)
    swap.wait_recv()
    returns = []
    for at in (slice(0, CRITICAL), slice(CRITICAL, CRITICAL + D)):
        copies = []
        for i, j in place.offsets() + [(0, 0)]:
            dp, tp = place.ahead(i, j)
            chip = lax.div(dp, 2)
            index = i * place.tp_size + j
            both = add_rounded(
                r.partial[place.core, chip, tp, :, at], r.from_sibling[chip, tp, :, at]
            )
            if index:
                r.from_sibling[chip, tp, :, at] = both
                copy = wire.copy(
                    r.from_sibling.at[chip, tp, :, at],
                    r.received.at[index, :, at],
                    {"dp": dp, "tp": tp},
                )
                copy.start()
                copies.append(copy)
            else:
                r.received[0, :, at] = both
        returns.append(copies)
    late_sends = [swap] + returns[0] + returns[1]
    at_point(3)
    for copy in returns[0]:
        copy.wait_recv()

    def live_column(i):
        lane = lax.broadcasted_iota(jnp.int32, (half, block), 1)
        row = lax.broadcasted_iota(jnp.int32, (half, block), 0) + place.tp * half
        live = r.ints[i, LIVE_ROW : LIVE_ROW + 1, :].astype(F32)
        return jnp.sum(jnp.where(lane == row, live, 0.0), axis=1, keepdims=True)

    lives = [live_column(i) for i in range(images)]
    total = r.received[0, :, :CRITICAL].astype(F32)
    for k in range(1, r.received.shape[0]):
        total = total + r.received[k, :, :CRITICAL].astype(F32)
    hidden = r.hidden[...]
    grad_probs = total[:, D : D + EXPERTS]
    grad_output = jnp.concatenate(
        [
            r.cot_all[place.dp * images + i, pl.ds(start, half), :].astype(F32) * lives[i]
            for i in range(images)
        ],
        axis=0,
    )
    rows = r.expert_in[...].reshape(count, D)
    router_lift = (times_transposed(rows, router_low) * own_sets).astype(BF16)
    logits = times_transposed(rows, r.router_t[...]) + matmul(router_lift, router_high)
    powers = jnp.exp(logits - jnp.max(logits, axis=-1, keepdims=True))
    gate_probs = powers / jnp.sum(powers, axis=-1, keepdims=True)
    grad_logits = (
        gate_probs * (grad_probs - jnp.sum(grad_probs * gate_probs, axis=-1, keepdims=True))
    ).astype(BF16)
    grad_router_lift = (times_transposed(grad_logits, router_high) * own_sets).astype(BF16)
    grad_expert_in = (
        total[:, :D] + matmul(grad_logits, r.router_t[...]) + matmul(grad_router_lift, router_low)
    )
    _, unit, factor = normalize(hidden, gain_two, shift_two)
    grad_rows = grad_output + normalize_back(grad_expert_in, unit, factor, gain_two)
    r.grad_hidden[...] = grad_rows
    grad_attended = grad_rows.astype(BF16)
    grad_mixing_lift = (times_transposed(grad_attended, mixing_high) * own_sets).astype(BF16)
    grad_heads = (
        matmul(grad_attended, r.mixing_all[...]) + matmul(grad_mixing_lift, mixing_low)
    ).astype(BF16)
    r.heads[...] = grad_heads.reshape(images, half, D)
    mix = r.head_mix[...]
    lane = lax.broadcasted_iota(jnp.int32, (D, 128), 1)
    head = lax.div(lax.broadcasted_iota(jnp.int32, (D, 128), 0), HD)
    ones = (lane == head).astype(F32).astype(BF16)
    delta_rows = split_sum(grad_heads.astype(F32) * mix.astype(F32), ones)
    r.delta[...] = delta_rows
    log_rows = r.logs[...]
    for i in range(images):
        part = slice(i * half, (i + 1) * half)
        pad = jnp.zeros((128 - half, 128), F32)
        turned = [
            jnp.concatenate([v[part], pad], axis=0).T[:HEADS] for v in (log_rows, delta_rows)
        ]
        row = 0
        for rest, number in zip(turned, (3, 2)):
            for _ in range(number):
                top = rest.astype(BF16)
                r.stats[i, row : row + HEADS, :] = top
                rest = rest - top.astype(F32)
                row += HEADS

    def heads_slot(i, ctx, tp):
        at = pl.multiple_of((ctx * place.tp_size + tp) * half, 16)
        return r.heads_all.at[i, pl.ds(at, half), :]

    chain = Chain(
        place, wire, [r.heads.at[i] for i in range(images)] + [r.stats],
        [functools.partial(heads_slot, i) for i in range(images)]
        + [lambda ctx, tp: r.stats_all.at[ctx * place.tp_size + tp]],
        [True] * (images + 1), True,
    )
    chain.start()

    def spread_start(values, got):
        rows = got.shape[1]
        copies = []
        for k, (dp, tp) in enumerate(place.peers):
            at = pl.ds(pl.multiple_of((dp * place.tp_size + tp) * rows, 16), rows)
            copy = wire.copy(values.at[at], got.at[k], {"dp": dp, "tp": tp})
            copy.start()
            copies.append(copy)
        return copies

    def spread_end(copies, values, got, total):
        rows = got.shape[1]
        for copy in copies:
            copy.wait()
        added = values[pl.ds(pl.multiple_of(place.me * rows, 16), rows), :].astype(F32)
        for k in range(plane - 1):
            added = added + got[k].astype(F32)
        total[...] = added.astype(BF16).reshape(total.shape)

    def put_tiles(target, products):
        tile = 0
        for product in products:
            for n in range(product.shape[1] // 128):
                target[tile * WIDTH : (tile + 1) * WIDTH, :] = product[
                    :, n * 128 : (n + 1) * 128
                ].astype(BF16)
                tile += 1
        if tile * WIDTH < target.shape[0]:
            target[tile * WIDTH :, :] = jnp.zeros(
                (target.shape[0] - tile * WIDTH, 128), BF16
            )

    wide_logits = jnp.concatenate(
        [grad_logits, jnp.zeros((count, 128 - EXPERTS), BF16)], axis=1
    )
    put_tiles(
        r.early,
        (
            inner_rows(grad_mixing_lift, mix),
            inner_rows(r.mixing_lift[...], grad_attended),
            inner_rows(grad_router_lift, rows),
            inner_rows(router_lift, wide_logits),
        ),
    )
    early_spread = spread_start(r.early, r.early_got)
    at_point(4)
    chain.step(1)
    at_point(5)
    chain.step(2)
    at_point(6)
    chain.step(3)
    spread_end(early_spread, r.early, r.early_got, r.early_sum)
    offer(early_at)
    at_point(7)
    chain.finish_own()
    for s in range(1, chain.steps + 1):
        chain.landed(s)

    def to_other(values, gathered):
        spot = gathered.at[:, pl.ds(start, half), :]
        copies = [wire.copy(values, spot, {"tp": place.other_tp}), wire.near(values, spot)]
        for copy in copies:
            copy.start()
        return copies

    for copy in returns[1]:
        copy.wait_recv()
    total = r.hidden[...]
    for k in range(r.received.shape[0]):
        total = total + r.received[k, :, CRITICAL:].astype(F32)
    r.out_own[...] = total.astype(BF16).reshape(images, half, D)
    layer_out = to_other(r.out_own, r.out_all)

    def heads_back(i, j):
        part = slice(i * half, (i + 1) * half)
        at = slice(j * 2 * HD, (j + 1) * 2 * HD)
        keys_open = r.keys_open[i : i + 1, :] > 0
        own_open = jnp.concatenate([lives[i], lives[i]], axis=0) > 0
        found = jnp.concatenate(
            [r.stats_all[n, i][:, :half].astype(F32) for n in range(r.stats_all.shape[0])], axis=1
        )
        log_t = found[0:HEADS] + found[HEADS : 2 * HEADS] + found[2 * HEADS : 3 * HEADS]
        delta_t = found[3 * HEADS : 4 * HEADS] + found[4 * HEADS :]
        q_all, k_all, v_all = (r.joined[p, i, :, at] for p in range(3))
        g_all = r.heads_all[i, :, at]

        def column(values):
            return jnp.concatenate(
                [values[:, 2 * j : 2 * j + 1], values[:, 2 * j + 1 : 2 * j + 2]], axis=0
            )

        def across(values):
            return jnp.concatenate(
                [
                    jnp.broadcast_to(values[2 * j + n : 2 * j + n + 1, :], (half, values.shape[1]))
                    for n in range(2)
                ],
                axis=0,
            )

        q = stack_pair(r.joined[0, i, own, at], masks, scale)
        g = stack_pair(r.heads[i, :, at], masks)
        scores = jnp.where(keys_open, times_transposed(q, k_all), MASKED)
        probs = jnp.exp(scores - column(r.logs[part]))
        grad_probs_att = times_transposed(g, v_all)
        grad_scores = (probs * (grad_probs_att - column(r.delta[part]))).astype(BF16)
        r.grads[0, part, at] = (join_pair(matmul(grad_scores, k_all), masks) * scale).astype(BF16)
        k = stack_pair(r.joined[1, i, own, at], masks, scale)
        v = stack_pair(r.joined[2, i, own, at], masks)
        scores = jnp.where(own_open, times_transposed(k, q_all), MASKED)
        probs = jnp.exp(scores - across(log_t))
        grad_probs_att = times_transposed(v, g_all)
        grad_scores = (probs * (grad_probs_att - across(delta_t))).astype(BF16)
        r.grads[1, part, at] = (join_pair(matmul(grad_scores, q_all), masks) * scale).astype(BF16)
        r.grads[2, part, at] = join_pair(matmul(probs.astype(BF16), g_all), masks).astype(BF16)

    for i in range(images):
        for j in range(HEADS // 2):
            heads_back(i, j)
            if j % 2:
                at_point(8 + 2 * i + j // 2)
    lift = times_transposed(r.grads[0], high(0))
    into = times_transposed(r.grads[0], r.weights_all[0])
    for p in range(1, 3):
        lift = lift + times_transposed(r.grads[p], high(p))
        into = into + times_transposed(r.grads[p], r.weights_all[p])
    lift = (lift * own_sets).astype(BF16)
    lift_in = jnp.concatenate([r.lift_all[i, own, :] for i in range(images)], axis=0)
    put_tiles(
        r.late,
        [inner_rows(lift_in, r.grads[p]) for p in range(3)]
        + [inner_rows(lift, r.own_in[...].reshape(count, D))],
    )
    late_spread = spread_start(r.late, r.late_got)
    at_point(12)
    into = into + matmul(lift, attend_low)
    flat = jnp.concatenate([r.tokens_all[i, own, :] for i in range(images)], axis=0).astype(F32)
    _, unit, factor = normalize(flat, gain_one, shift_one)
    result = r.grad_hidden[...] + normalize_back(into, unit, factor, gain_one)
    r.grad_own[...] = result.astype(BF16).reshape(images, half, D)
    at_point(13)
    tokens_out = to_other(r.grad_own, r.grad_all)
    spread_end(late_spread, r.late, r.late_got, r.late_sum)
    offer(late_at)
    at_point(14)
    for k in range(len(chunks)):
        go(k, DONE)

    @pl.when(place.is_end)
    def _():
        for flow in flows:
            flow["beyond"].wait_send()
            flow["beside"].wait_send()

    @pl.when(place.is_mid)
    def _():
        for flow in flows:
            for name in ("across", "away", "share", "back"):
                flow[name].wait_send()

    for spread in spreads:
        spread.finish()
    for spread in [weights, mixing, numbers, router, cotangents] + expert_rows + spreads:
        spread.drain()
    tokens_chain.drain()
    chain.drain()
    for copy in late_sends:
        copy.wait_send()
    for copy in layer_out + tokens_out:
        copy.wait()
    assert not pending


def run_layer(sizes, **inputs):
    dp, ctx, tp = sizes
    assert ctx == 4 and tp == 2
    plane, chips = dp * tp, dp // 2
    images, block = inputs["tokens"].shape[:2]
    assert images == 2
    half = block // tp
    count, seq, all_images = images * half, ctx * block, dp * images
    experts, _, hidden = inputs["up_weight"].shape
    rows, lanes = inputs["mixing"].shape
    slots = experts * SLOTS
    sent = CRITICAL + D
    early_rows = small_rows(3 * (D // 128) + 1, plane)
    late_rows = small_rows(4 * (D // 128), plane)
    second = (2, experts, WIDTH, D // tp)
    full = dict(
        first=(experts, 2, WIDTH, hidden),
        second=second,
        early=(2, early_rows // 2, 128),
        late=(2, late_rows // 2, 128),
    )
    cut = {name: shape[1:] for name, shape in full.items()}
    cut["first"] = (experts, WIDTH, hidden)
    outputs = {name + "_all": (dp, tp) + shape for name, shape in full.items()}
    outputs.update(out_all=(images, block, D), grad_all=(images, block, D))
    narrow = dict(
        tokens_all=(images, seq, D),
        weights_all=(3, dp * rows, tp * lanes),
        mixing_all=(dp * rows, tp * lanes),
        router_all=(dp,) + inputs["router"].shape,
        router_t=(EXPERTS, D),
        cot_all=(all_images, block, D),
        rows_all=(all_images, block, D),
        v_attend_low=(SETS, RANK, D),
        v_attend_high=(SETS, 3, RANK, D),
        v_mixing_low=(SETS, RANK, D),
        v_mixing_high=(SETS, RANK, D),
        v_router_low=(SETS, RANK, D),
        v_router_high=(SETS, RANK, EXPERTS),
        v_first_a=(experts, SETS, RANK, D),
        v_first_b=(experts, SETS, RANK, hidden),
        v_second_a=(experts, SETS, RANK, hidden),
        v_second_b=(experts, SETS, RANK, D),
        v_up=(experts, D, hidden),
        v_down=(experts, hidden, D),
        lift_all=(images, seq, WIDTH),
        joined=(3, images, seq, D),
        own_in=(images, half, D),
        head_mix=(count, D),
        mixing_lift=(count, WIDTH),
        expert_in=(images, half, D),
        table=(all_images, slots, block),
        grad_slots=(experts, all_images * SLOTS, D),
        rows_in=(experts, all_images * SLOTS, D),
        payload=(all_images, slots, sent),
        partial=(2, chips, tp, count, sent),
        from_sibling=(chips, tp, count, sent),
        received=(chips * tp, count, sent),
        first=full["first"],
        second=(tp,) + second,
        second_got=second,
        second_sum=second,
        early=(plane * early_rows, 128),
        late=(plane * late_rows, 128),
        early_got=(plane - 1, early_rows, 128),
        late_got=(plane - 1, late_rows, 128),
        early_sum=full["early"],
        late_sum=full["late"],
        heads=(images, half, D),
        stats=(images, 5 * HEADS, 128),
        heads_all=(images, seq, D),
        stats_all=(ctx * tp, images, 5 * HEADS, 128),
        grads=(3, count, D),
        out_own=(images, half, D),
        grad_own=(images, half, D),
    )
    for name in full:
        narrow[name + "_final"] = full[name]
        narrow[name + "_in"] = (3,) + cut[name]
    narrow["first_got"] = (experts, 3, WIDTH, hidden)
    del narrow["first_in"]
    wide = dict(
        logs=(count, 128),
        delta=(count, 128),
        hidden=(count, D),
        grad_hidden=(count, D),
        gates=(experts, all_images * SLOTS, 128),
        slot_sets=(all_images * SLOTS, WIDTH),
        keys_open=(images, seq),
    )
    integers = dict(
        ints=(images, 8, block),
        ints_all=(all_images, 8, block),
        ctx_ints=(ctx, images, 8, block),
    )
    scratch = {}
    for shapes, dtype in ((narrow, BF16), (wide, F32), (integers, jnp.int32)):
        for name, shape in shapes.items():
            scratch[name] = pltpu.VMEM(shape, dtype)
    chunks = experts + 3
    remote = (
        2 * Chain.remote(ctx, images + 1)
        + (2 + images + chunks) * Spread.remote(sizes)
        + 3 * Spread.remote(sizes, False)
        + 6 * chunks
        + 2
        + 2 * (chips * tp - 1)
        + 2 * (plane - 1)
        + 2
    )
    scratch["send"] = pltpu.SemaphoreType.DMA((remote,))
    scratch["recv"] = pltpu.SemaphoreType.DMA((remote,))
    scratch["local"] = pltpu.SemaphoreType.DMA((7 + 6 * experts + 5 + images + chunks + images + 1 + 2,))
    kinds = dict(
        adapter_set=IN_SMEM, image_mask=IN_SMEM, routes_t=IN_VMEM, slots_t=IN_VMEM,
        token_mask=IN_VMEM, first_gain=IN_VMEM, first_shift=IN_VMEM, second_gain=IN_VMEM,
        second_shift=IN_VMEM,
    )
    names = tuple(inputs) + tuple(outputs) + tuple(scratch)
    made = pl.pallas_call(
        functools.partial(layer_kernel, sizes, names),
        out_shape=tuple(jax.ShapeDtypeStruct(shape, BF16) for shape in outputs.values()),
        in_specs=[kinds.get(name, ANY) for name in inputs],
        out_specs=(ANY,) * len(outputs),
        scratch_shapes=tuple(scratch.values()),
        compiler_params=pltpu.CompilerParams(
            collective_id=0, has_side_effects=True, vmem_limit_bytes=62 << 20
        ),
    )(*inputs.values())
    return dict(zip(outputs, made))


def assemble_kernel(
    first, second, early, late, out_in, grad_in,
    up, down_t, narrow_t, narrow, attend_down, attend_up, mixing_down, mixing_up, router_down,
    router_up, out, grad,
):
    lanes, part = first.shape[-1], second.shape[-1]
    for n in range(first.shape[2]):
        for tp in range(first.shape[1]):
            for half, target in ((0, up), (1, down_t)):
                target[:, n, :, tp * lanes : (tp + 1) * lanes] = (
                    first[0, tp, n, half].astype(F32).reshape(SETS, RANK, lanes)
                )
            for half, target in ((0, narrow_t), (1, narrow)):
                target[:, n, :, tp * part : (tp + 1) * part] = (
                    second[0, tp, half, n].astype(F32).reshape(SETS, RANK, part)
                )

    @pl.when(pl.program_id(0) == 0)
    def _():
        def tile(small, k):
            return small[k * WIDTH : (k + 1) * WIDTH, :].astype(F32).reshape(SETS, RANK, 128)

        count = D // 128
        for p in range(3):
            for k in range(count):
                attend_up[:, p, :, k * 128 : (k + 1) * 128] = tile(late, p * count + k)
        for k in range(count):
            attend_down[:, :, k * 128 : (k + 1) * 128] = tile(late, 3 * count + k)
        for p, target in enumerate((mixing_down, mixing_up, router_down)):
            for k in range(count):
                target[:, :, k * 128 : (k + 1) * 128] = tile(early, p * count + k)
        router_up[...] = tile(early, 3 * count)[:, :, :EXPERTS]
        out[...] = out_in[...]
        grad[...] = grad_in[...]


def assemble(first, second, early, late, out, grad):
    dp, tp, experts, _, width, lanes = first.shape
    part = second.shape[-1]
    group = min(experts, ASSEMBLED)
    groups = experts // group

    def split(e):
        return lax.div(e, groups), lax.rem(e, groups)

    def expert_out(size):
        return (
            jax.ShapeDtypeStruct((SETS, EXPERTS, RANK, size), F32),
            pl.BlockSpec((SETS, group, RANK, size), lambda e: (0, e, 0, 0)),
        )

    def whole_out(*shape):
        return (
            jax.ShapeDtypeStruct(shape, F32),
            pl.BlockSpec(shape, lambda e: (0,) * len(shape)),
        )

    outs = (
        [expert_out(FF)] * 2
        + [expert_out(D)] * 2
        + [whole_out(SETS, RANK, D), whole_out(SETS, 3, RANK, D)]
        + [whole_out(SETS, RANK, D)] * 3
        + [whole_out(SETS, RANK, EXPERTS)]
        + [(jax.ShapeDtypeStruct(out.shape, BF16), pl.BlockSpec(out.shape, lambda e: (0, 0, 0)))] * 2
    )
    return pl.pallas_call(
        assemble_kernel,
        grid=(EXPERTS // group,),
        out_shape=[out[0] for out in outs],
        in_specs=[
            pl.BlockSpec(
                (1, tp, group, 2, width, lanes), lambda e: (split(e)[0], 0, split(e)[1], 0, 0, 0)
            ),
            pl.BlockSpec(
                (1, tp, 2, group, width, part), lambda e: (split(e)[0], 0, 0, split(e)[1], 0, 0)
            ),
            pl.BlockSpec(early.shape, lambda e: (0, 0)),
            pl.BlockSpec(late.shape, lambda e: (0, 0)),
            pl.BlockSpec(out.shape, lambda e: (0, 0, 0)),
            pl.BlockSpec(grad.shape, lambda e: (0, 0, 0)),
        ],
        out_specs=[out[1] for out in outs],
        compiler_params=pltpu.CompilerParams(vmem_limit_bytes=60 << 20),
    )(first, second, early, late, out, grad)


def per_device(
    sizes,
    tokens,
    cotangent,
    routes,
    slot_index,
    token_mask,
    image_mask,
    adapter_set,
    first_gain,
    first_shift,
    second_gain,
    second_shift,
    attend_weight,
    mixing_weight,
    router_weight,
    expand_weight,
    shrink_weight,
    attend_down,
    attend_up,
    mixing_down,
    mixing_up,
    router_down,
    router_up,
    expand_down,
    expand_up,
    shrink_down,
    shrink_up,
):
    def flipped(values):
        return jnp.swapaxes(values, -1, -2)

    made = run_layer(
        sizes,
        tokens=tokens,
        cotangent=cotangent,
        weights=jnp.transpose(attend_weight, (1, 0, 2)),
        mixing=mixing_weight,
        router=flipped(router_weight),
        routes_t=flipped(routes),
        slots_t=flipped(slot_index),
        token_mask=token_mask,
        image_mask=image_mask,
        adapter_set=adapter_set,
        first_gain=first_gain.reshape(1, D),
        first_shift=first_shift.reshape(1, D),
        second_gain=second_gain.reshape(1, D),
        second_shift=second_shift.reshape(1, D),
        up_weight=expand_weight,
        down_weight=shrink_weight,
        attend_low=flipped(attend_down),
        attend_high=jnp.transpose(attend_up, (0, 2, 1, 3)),
        mixing_low=flipped(mixing_down),
        mixing_high=mixing_up,
        router_low=flipped(router_down),
        router_high=router_up,
        first_a=flipped(expand_down),
        first_b=expand_up,
        second_a=flipped(shrink_down),
        second_b=shrink_up,
    )
    wide = assemble(
        made["first_all"],
        made["second_all"],
        made["early_all"].reshape(-1, 128),
        made["late_all"].reshape(-1, 128),
        made["out_all"],
        made["grad_all"],
    )
    return (
        wide[10],
        wide[11],
        flipped(wide[4]),
        jnp.transpose(wide[5], (0, 2, 1, 3)),
        flipped(wide[6]),
        wide[7],
        flipped(wide[8]),
        wide[9],
        flipped(wide[2]),
        wide[0],
        flipped(wide[1]),
        wide[3],
    )


def solution(mesh):
    sizes = (mesh.shape["dp"], mesh.shape["ctx"], mesh.shape["tp"])
    tokens_spec = P("dp", "ctx", None)
    in_specs = (
        (tokens_spec,) * 4
        + (P("dp", "ctx"), P("dp"), P("dp"))
        + (P(),) * 4
        + (P("dp", None, "tp"), P("dp", "tp"), P("dp", None))
        + (P("dp", None, "tp"), P("dp", "tp", None))
        + (P(),) * 10
    )
    out_specs = (tokens_spec,) * 2 + (P(),) * 10
    return jax.shard_map(
        functools.partial(per_device, sizes),
        mesh=mesh,
        in_specs=in_specs,
        out_specs=out_specs,
        check_vma=False,
    )
```

```python
import functools
import types

import jax
import jax.numpy as jnp
from jax import lax
from jax.experimental import pallas as pl
from jax.experimental.pallas import tpu as pltpu
from jax.sharding import PartitionSpec as P

D = 512
HEADS = 8
HD = 64
FF = 2048
EXPERTS = 16
TOP = 2
RANK = 16
SETS = 4
CAP = 30
SLOTS = 32
WIDTH = SETS * RANK
LIVE_ROW = 2 * TOP
SET_ROW = LIVE_ROW + 1
CRITICAL = D + 128
EXPERT_ROWS = 256
ASSEMBLED = 4

EPSILON = 1e-06
MASKED = -1e30
SQRT_HALF = 0.7071067811865476
INV_ROOT_TWO_PI = 0.3989422804014327
F32 = jnp.float32
BF16 = jnp.bfloat16
MESH = pl.DeviceIdType.MESH
ANY = pl.BlockSpec(memory_space=pl.ANY)
IN_SMEM = pl.BlockSpec(memory_space=pltpu.SMEM)
IN_VMEM = pl.BlockSpec(memory_space=pltpu.VMEM)


def matmul(left_side, right_side):
    return jnp.dot(left_side, right_side, preferred_element_type=F32)


def inner_rows(left_side, right_side):
    return lax.dot_general(
        left_side, right_side, (((0,), (0,)), ((), ())), preferred_element_type=F32
    )


def times_transposed(left_side, right_side):
    return lax.dot_general(
        left_side, right_side, (((1,), (1,)), ((), ())), preferred_element_type=F32
    )


def normalize(values, gain_row, shift_row):
    centred = values - jnp.mean(values, axis=-1, keepdims=True)
    spread = jnp.mean(centred * centred, axis=-1, keepdims=True)
    factor = lax.rsqrt(spread + EPSILON)
    normed = centred * factor
    return (normed * gain_row + shift_row, normed, factor)


def normalize_back(grad_out, normed, factor, gain_row):
    scaled = grad_out * gain_row
    return factor * (
        scaled
        - jnp.mean(scaled, axis=-1, keepdims=True)
        - normed * jnp.mean(scaled * normed, axis=-1, keepdims=True)
    )


def add_rounded(*parts):
    total = parts[0].astype(F32)
    for part in parts[1:]:
        total = total + part.astype(F32)
    return total.astype(BF16)


def split_sum(values, ones):
    high = values.astype(BF16)
    low = (values - high.astype(F32)).astype(BF16)
    return matmul(high, ones) + matmul(low, ones)


def put_lanes(columns, width):
    lane = lax.broadcasted_iota(jnp.int32, (columns[0].shape[0], width), 1)
    total = jnp.zeros((columns[0].shape[0], width), F32)
    for k, column in enumerate(columns):
        total = jnp.where(lane == k, column, total)
    return total


def half_masks():
    lane = lax.broadcasted_iota(jnp.int32, (1, 2 * HD), 1)
    even = (lane < HD).astype(F32)
    return even, 1.0 - even


def stack_pair(rows, masks, factor=1.0):
    wide = rows.astype(F32) * factor
    return jnp.concatenate([wide * masks[0], wide * masks[1]], axis=0).astype(BF16)


def join_pair(rows, masks):
    half = rows.shape[0] // 2
    return rows[:half] * masks[0] + rows[half:] * masks[1]


SUM, SENT, ONWARD, DONE = range(1, 5)
E0, E1, E2, E3, SECOND, EARLY, LATE = range(-7, 0)
SCHEDULE = (
    (),
    ((E0, SUM),),
    ((E1, SUM),),
    ((E0, SENT), (E2, SUM), (E1, SENT)),
    ((E0, ONWARD), (E3, SUM)),
    ((E2, SENT), (E1, ONWARD)),
    ((E0, DONE), (SECOND, SUM)),
    ((E3, SENT), (E2, ONWARD)),
    ((E1, DONE),),
    ((SECOND, SENT),),
    ((EARLY, SUM), (E3, ONWARD)),
    ((E2, DONE),),
    ((SECOND, ONWARD),),
    ((EARLY, SENT),),
    (
        (E3, DONE), (LATE, SUM), (EARLY, ONWARD), (SECOND, DONE), (LATE, SENT), (EARLY, DONE),
        (LATE, ONWARD), (LATE, DONE),
    ),
)


def small_rows(tiles, plane):
    return -(-tiles * WIDTH // (plane * 16)) * 16


class Wire:
    def __init__(self, send, recv, local):
        self.send, self.recv, self.local = send, recv, local
        self.used = self.used_local = 0

    def copy(self, src, dst, device):
        k = self.used
        self.used += 1
        assert k < self.send.shape[0]
        return pltpu.make_async_remote_copy(
            src_ref=src,
            dst_ref=dst,
            send_sem=self.send.at[k],
            recv_sem=self.recv.at[k],
            device_id=device,
            device_id_type=MESH,
        )

    def near(self, src, dst):
        k = self.used_local
        self.used_local += 1
        assert k < self.local.shape[0]
        return pltpu.make_async_copy(src, dst, self.local.at[k])


class Place:
    def __init__(self, sizes):
        self.dp_size, self.ctx_size, self.tp_size = sizes
        self.chips = self.dp_size // 2
        self.plane = self.dp_size * self.tp_size
        self.dp = lax.axis_index("dp")
        self.ctx = lax.axis_index("ctx")
        self.tp = lax.axis_index("tp")
        self.chip = lax.div(self.dp, 2)
        self.core = lax.rem(self.dp, 2)
        self.sibling = self.chip * 2 + (1 - self.core)
        self.other_tp = lax.rem(self.tp + 1, 2)
        self.me = self.dp * self.tp_size + self.tp
        self.is_mid = jnp.logical_and(self.ctx >= 1, self.ctx <= 2)
        self.is_end = jnp.logical_not(self.is_mid)
        self.inner = lax.div(self.ctx, 2)
        self.partner = jnp.where(self.is_mid, self.inner * 3, 1 + self.inner)
        self.far_mid = 2 - self.inner
        self.far_end = 3 - 3 * self.inner
        self.peers = []
        for k in range(1, self.plane):
            peer = lax.rem(self.me + k, self.plane)
            self.peers.append((lax.div(peer, self.tp_size), lax.rem(peer, self.tp_size)))

    def ahead(self, i, j):
        return (
            lax.rem(self.chip + i, self.chips) * 2 + self.core,
            lax.rem(self.tp + j, self.tp_size),
        )

    def behind(self, i, j):
        return self.ahead(self.chips - i, self.tp_size - j)

    def offsets(self, over_tp=True):
        return [
            (i, j)
            for i in range(self.chips)
            for j in range(self.tp_size if over_tp else 1)
            if i or j
        ]

    def greet(self):
        barrier = pltpu.get_barrier_semaphore()
        for dp, tp in self.peers:
            pl.semaphore_signal(
                barrier, inc=1, device_id={"dp": dp, "tp": tp}, device_id_type=MESH
            )
        for ctx in (self.partner, self.far_mid):
            pl.semaphore_signal(barrier, inc=1, device_id={"ctx": ctx}, device_id_type=MESH)

        @pl.when(self.is_mid)
        def _():
            pl.semaphore_signal(
                barrier, inc=1, device_id={"ctx": self.far_end}, device_id_type=MESH
            )

    def met(self):
        barrier = pltpu.get_barrier_semaphore()
        pl.semaphore_wait(barrier, self.plane + 1 + jnp.where(self.is_mid, 1, 0))


class Spread:
    def __init__(self, place, wire, source, slot, over_tp=True, direct=False, near=True):
        self.place, self.wire, self.source, self.slot = place, wire, source, slot
        self.over_tp = over_tp
        self.relay = over_tp and not direct and place.chips == 2 and place.tp_size == 2
        self.near = near
        self.flights, self.across, self.beside, self.here = [], None, [], None

    def to_sibling(self, source, spot):
        copy = self.wire.copy(source, spot, {"dp": self.place.sibling})
        copy.start()
        self.beside.append(copy)

    def start(self):
        place = self.place
        spot = self.slot(place.dp, place.tp)
        for i, j in place.offsets(self.over_tp):
            if self.relay and i and j:
                continue
            dp, tp = place.ahead(i, j)
            copy = self.wire.copy(self.source, spot, {"dp": dp, "tp": tp})
            copy.start()
            self.flights.append((copy, i, j))
        self.to_sibling(self.source, spot)
        if self.near:
            self.here = self.wire.near(self.source, spot)
            self.here.start()

    def forward(self):
        for copy, i, j in sorted(self.flights, key=lambda f: f[1]):
            copy.wait_recv()
            got = self.slot(*self.place.behind(i, j))
            if self.relay and j:
                dp, tp = self.place.ahead(1, 0)
                self.across = self.wire.copy(got, got, {"dp": dp, "tp": tp})
                self.across.start()
            self.to_sibling(got, got)

    def diagonal(self):
        if self.relay:
            self.across.wait_recv()
            got = self.slot(*self.place.behind(1, 1))
            self.to_sibling(got, got)

    def finish(self):
        for copy in self.beside:
            copy.wait_recv()
        if self.near:
            self.here.wait()

    def drain(self):
        for copy, _, _ in self.flights:
            copy.wait_send()
        if self.relay:
            self.across.wait_send()
        for copy in self.beside:
            copy.wait_send()

    @staticmethod
    def remote(sizes, over_tp=True):
        return 2 * (sizes[0] // 2 * (sizes[2] if over_tp else 1) - 1) + 1


class Chain:
    def __init__(self, place, wire, sources, slots, over, with_own):
        self.place, n = place, place.ctx_size
        self.steps = n - 1
        to_tp = {"tp": place.other_tp}
        self.right, self.left, self.over_right, self.over_left = {}, {}, {}, {}
        self.own, self.here = [], []
        for source, slot in zip(sources, slots):
            spot = slot(place.ctx, place.tp)
            if with_own:
                self.own.append(wire.copy(source, spot, to_tp))
                self.here.append(wire.near(source, spot))
        for s in range(1, n):
            back = [slot(jnp.maximum(place.ctx - (s - 1), 0), place.tp) for slot in slots]
            ahead = [slot(jnp.minimum(place.ctx + (s - 1), n - 1), place.tp) for slot in slots]
            got_right = [slot(jnp.maximum(place.ctx - s, 0), place.tp) for slot in slots]
            got_left = [slot(jnp.minimum(place.ctx + s, n - 1), place.tp) for slot in slots]
            to_right = {"ctx": jnp.minimum(place.ctx + 1, n - 1)}
            to_left = {"ctx": jnp.maximum(place.ctx - 1, 0)}
            self.right[s] = [
                wire.copy(a if s == 1 else b, b, to_right) for a, b in zip(sources, back)
            ]
            self.left[s] = [
                wire.copy(a if s == 1 else b, b, to_left) for a, b in zip(sources, ahead)
            ]
            self.over_right[s] = {
                k: wire.copy(b, b, to_tp) for k, b in enumerate(got_right) if over[k]
            }
            self.over_left[s] = {
                k: wire.copy(b, b, to_tp) for k, b in enumerate(got_left) if over[k]
            }

    def sends_right(self, s):
        return jnp.logical_and(self.place.ctx >= s - 1, self.place.ctx < self.steps)

    def sends_left(self, s):
        return jnp.logical_and(self.place.ctx <= self.steps + 1 - s, self.place.ctx > 0)

    def gets_right(self, s):
        return self.place.ctx >= s

    def gets_left(self, s):
        return self.place.ctx <= self.steps - s

    @staticmethod
    def all_of(copies, verb):
        for copy in copies:
            getattr(copy, verb)()

    def start(self):
        pl.when(self.sends_right(1))(lambda: self.all_of(self.right[1], "start"))
        pl.when(self.sends_left(1))(lambda: self.all_of(self.left[1], "start"))
        self.all_of(self.own + self.here, "start")

    def step(self, s):
        def passed(got, over, sends):
            def run():
                for k, copy in enumerate(got[s]):
                    copy.wait_recv()
                    if s < self.steps:
                        pl.when(sends(s + 1))(got[s + 1][k].start)
                    if k in over[s]:
                        over[s][k].start()

            return run

        pl.when(self.gets_right(s))(passed(self.right, self.over_right, self.sends_right))
        pl.when(self.gets_left(s))(passed(self.left, self.over_left, self.sends_left))

    def landed(self, s):
        pl.when(self.gets_right(s))(lambda: self.all_of(self.over_right[s].values(), "wait_recv"))
        pl.when(self.gets_left(s))(lambda: self.all_of(self.over_left[s].values(), "wait_recv"))

    def finish_own(self):
        self.all_of(self.own, "wait_recv")
        self.all_of(self.here, "wait")

    def drain(self):
        self.all_of(self.own, "wait_send")
        for s in range(1, self.steps + 1):
            pl.when(self.gets_right(s))(lambda: self.all_of(self.over_right[s].values(), "wait_send"))
            pl.when(self.gets_left(s))(lambda: self.all_of(self.over_left[s].values(), "wait_send"))
            pl.when(self.sends_right(s))(lambda: self.all_of(self.right[s], "wait_send"))
            pl.when(self.sends_left(s))(lambda: self.all_of(self.left[s], "wait_send"))

    @staticmethod
    def remote(n, arrays):
        return arrays * (1 + 4 * (n - 1))


def layer_kernel(sizes, names, *refs):
    r = types.SimpleNamespace(**dict(zip(names, refs)))
    place = Place(sizes)
    wire = Wire(r.send, r.recv, r.local)
    plane = place.plane
    images, block = r.tokens.shape[:2]
    half = block // place.tp_size
    count = images * half
    seq = place.ctx_size * block
    experts, _, hidden_units = r.up_weight.shape
    all_images = place.dp_size * images
    owned = place.dp * experts
    start = pl.multiple_of(place.tp * half, 16)
    own_start = pl.multiple_of(place.ctx * block + place.tp * half, 16)
    own = pl.ds(own_start, half)
    masks = half_masks()
    scale = HD**-0.5

    pending = {}

    def load(name, source, target):
        pending[name] = wire.near(source, target)
        pending[name].start()

    def need(*wanted):
        for name in wanted:
            if name in pending:
                pending.pop(name).wait()

    place.greet()
    whole = pl.ds(pl.multiple_of(place.ctx * block, 16), block)
    load("tokens", r.tokens, r.tokens_all.at[:, whole, :])
    for name in (
        "attend_low", "attend_high", "mixing_low", "mixing_high", "router_low", "router_high",
    ):
        load(name, getattr(r, name), getattr(r, "v_" + name))
    r.ints[:, 0:TOP, :] = r.routes_t[...]
    r.ints[:, TOP : 2 * TOP, :] = r.slots_t[...]
    lane_set = lax.div(lax.broadcasted_iota(jnp.int32, (1, WIDTH), 1), RANK)
    picks = []
    for i in range(images):
        r.ints[i, LIVE_ROW : LIVE_ROW + 1, :] = r.token_mask[i : i + 1, :] * r.image_mask[i]
        r.ints[i, SET_ROW:, :] = jnp.full((8 - SET_ROW, block), r.adapter_set[i], jnp.int32)
        picks.append((lane_set == r.adapter_set[i]).astype(F32))
    gain_one, shift_one = r.first_gain[...], r.first_shift[...]
    gain_two, shift_two = r.second_gain[...], r.second_shift[...]

    place.met()

    rows, lanes = r.mixing.shape

    def at_rows(dp):
        return pl.ds(pl.multiple_of(dp * rows, 16), rows)

    def at_lanes(tp):
        return pl.ds(pl.multiple_of(tp * lanes, 128), lanes)

    def token_slot(i, ctx, tp):
        at = pl.multiple_of(ctx * block + tp * half, 16)
        return r.tokens_all.at[i, pl.ds(at, half), :]

    tokens_chain = Chain(
        place, wire,
        [r.tokens.at[i, pl.ds(start, half), :] for i in range(images)] + [r.ints],
        [functools.partial(token_slot, i) for i in range(images)]
        + [lambda ctx, tp: r.ctx_ints.at[ctx]],
        [True] * images + [False], False,
    )
    weights = Spread(
        place, wire, r.weights, lambda dp, tp: r.weights_all.at[:, at_rows(dp), at_lanes(tp)]
    )
    mixing = Spread(
        place, wire, r.mixing, lambda dp, tp: r.mixing_all.at[at_rows(dp), at_lanes(tp)]
    )
    numbers = Spread(
        place, wire, r.ints, lambda dp, tp: r.ints_all.at[pl.ds(dp * 2, 2)], over_tp=False
    )
    router = Spread(place, wire, r.router, lambda dp, tp: r.router_all.at[dp], over_tp=False)
    cotangents = Spread(
        place, wire, r.cotangent, lambda dp, tp: r.cot_all.at[pl.ds(dp * 2, 2)], over_tp=False
    )
    r.ctx_ints[place.ctx] = r.ints[...]
    tokens_chain.start()
    weights.start()
    numbers.start()
    router.start()
    mixing.start()
    cotangents.start()
    wide = pl.ds(pl.multiple_of(place.tp * hidden_units, 128), hidden_units)
    for e in range(experts):
        load(("a_first", e), r.first_a.at[:, owned + e], r.v_first_a.at[e])
        load(("b_first", e), r.first_b.at[:, owned + e, :, wide], r.v_first_b.at[e])
        load(("up", e), r.up_weight.at[e], r.v_up.at[e])
        load(("a_second", e), r.second_a.at[:, owned + e, :, wide], r.v_second_a.at[e])
        load(("b_second", e), r.second_b.at[:, owned + e], r.v_second_b.at[e])
        load(("down", e), r.down_weight.at[e], r.v_down.at[e])
    weights.forward()
    tokens_chain.step(1)
    weights.diagonal()
    tokens_chain.step(2)
    numbers.forward()
    router.forward()
    weights.finish()
    need("tokens", "attend_low", "attend_high")

    block_picks = jnp.concatenate(
        [jnp.broadcast_to(pick, (block, WIDTH)) for pick in picks], axis=0
    )
    own_sets = jnp.concatenate(
        [jnp.broadcast_to(pick, (half, WIDTH)) for pick in picks], axis=0
    )
    attend_low = r.v_attend_low[...].reshape(WIDTH, D)

    def high(p):
        return r.v_attend_high[:, p].reshape(WIDTH, D)

    def project(k, _):
        ctx = place.ctx
        first = jnp.where(ctx == 3, 2, ctx + 1)
        second = jnp.where(ctx == 0, 2, jnp.where(ctx == 1, 0, 1))
        third = jnp.where(ctx < 2, 3, 0)
        which = jnp.where(
            k == 0, ctx, jnp.where(k == 1, first, jnp.where(k == 2, second, third))
        )
        at = pl.ds(pl.multiple_of(which * block, 16), block)
        values = jnp.concatenate([r.tokens_all[i, at, :] for i in range(images)], axis=0)
        normed = normalize(values.astype(F32), gain_one, shift_one)[0].astype(BF16)
        lift = (times_transposed(normed, attend_low) * block_picks).astype(BF16)
        for i in range(images):
            r.lift_all[i, at, :] = lift[i * block : (i + 1) * block]
        for p in range(3):
            made = (matmul(normed, r.weights_all[p]) + matmul(lift, high(p))).astype(BF16)
            for i in range(images):
                r.joined[p, i, at, :] = made[i * block : (i + 1) * block]
        return 0

    def project_blocks(low, up):
        lax.fori_loop(low, up, project, 0)

    project_blocks(0, 1)
    tokens_chain.step(3)
    tokens_chain.landed(1)
    mixing.forward()
    project_blocks(1, 2)
    tokens_chain.landed(2)
    project_blocks(2, 3)
    cotangents.forward()
    mixing.diagonal()
    tokens_chain.landed(3)
    project_blocks(3, 4)
    mixing.finish()
    need("mixing_low", "mixing_high")
    mixing_low = r.v_mixing_low[...].reshape(WIDTH, D)
    mixing_high = r.v_mixing_high[...].reshape(WIDTH, D)

    def open_keys(i):
        return (
            jnp.concatenate(
                [
                    r.ctx_ints[n, i, LIVE_ROW : LIVE_ROW + 1, :]
                    for n in range(place.ctx_size)
                ],
                axis=1,
            )
            > 0
        )

    def rows_slot(i, dp, tp):
        at = pl.multiple_of(tp * half, 16)
        return r.rows_all.at[dp * images + i, pl.ds(at, half), :]

    expert_rows = []
    for i in range(images):
        r.keys_open[i : i + 1, :] = open_keys(i).astype(F32)
        token_rows = r.tokens_all[i, own, :].astype(F32)
        r.own_in[i] = normalize(token_rows, gain_one, shift_one)[0].astype(BF16)
        keys_open = r.keys_open[i : i + 1, :] > 0
        part = slice(i * half, (i + 1) * half)
        logs = []
        for j in range(HEADS // 2):
            at = slice(j * 2 * HD, (j + 1) * 2 * HD)
            q = stack_pair(r.joined[0, i, own, at], masks, scale)
            scores = times_transposed(q, r.joined[1, i, :, at])
            scores = jnp.where(keys_open, scores, MASKED)
            top = jnp.max(scores, axis=-1, keepdims=True)
            powers = jnp.exp(scores - top)
            total = jnp.sum(powers, axis=-1, keepdims=True)
            weights_att = (powers * (1.0 / total)).astype(BF16)
            mixed = join_pair(matmul(weights_att, r.joined[2, i, :, at]), masks)
            r.head_mix[part, at] = mixed.astype(BF16)
            log = jnp.maximum(top + jnp.log(total), -1e29)
            logs += [log[:half], log[half:]]
        r.logs[part, :] = put_lanes(logs, 128)
        mix = r.head_mix[part, :]
        lift = (times_transposed(mix, mixing_low) * picks[i]).astype(BF16)
        r.mixing_lift[part, :] = lift
        hidden = token_rows + times_transposed(mix, r.mixing_all[...]) + matmul(lift, mixing_high)
        r.hidden[part, :] = hidden
        r.expert_in[i] = normalize(hidden, gain_two, shift_two)[0].astype(BF16)
        expert_rows.append(
            Spread(place, wire, r.expert_in.at[i], functools.partial(rows_slot, i), direct=True)
        )
        expert_rows[i].start()

    slots = experts * SLOTS
    cotangents.finish()
    numbers.finish()
    router.finish()
    need("router_low", "router_high")
    router_low = r.v_router_low[...].reshape(WIDTH, D)
    router_high = r.v_router_high[...].reshape(WIDTH, EXPERTS)
    r.router_t[...] = jnp.concatenate([r.router_all[n] for n in range(place.dp_size)], axis=1)

    def targets(given, k):
        route, slot = given[k : k + 1, :], given[TOP + k : TOP + k + 1, :]
        local = route - owned
        here = (local >= 0) & (local < experts) & (slot < CAP)
        return jnp.where(here, local * SLOTS + slot, -1)

    def fill_slots(i, target, values):
        at = pl.ds(pl.multiple_of(i * SLOTS, SLOTS), SLOTS)
        for n in range(experts):
            target[n, at, :] = values[n * SLOTS : (n + 1) * SLOTS]

    def make_table(i, _):
        given = r.ints_all[i]
        slot = lax.broadcasted_iota(jnp.int32, (slots, block), 0)
        hot = jnp.zeros((slots, block), F32)
        for k in range(TOP):
            hot = jnp.where(slot == targets(given, k), 1.0, hot)
        hot = hot.astype(BF16)
        r.table[i] = hot
        fill_slots(i, r.grad_slots, matmul(hot, r.cot_all[i]).astype(BF16))
        return 0

    lax.fori_loop(0, all_images, make_table, 0, unroll=2)
    for spread in expert_rows:
        spread.forward()
    for spread in expert_rows:
        spread.finish()

    def dispatch(i, _):
        values = r.rows_all[i]
        given = r.ints_all[i]
        set_column = lax.div(lax.broadcasted_iota(jnp.int32, (WIDTH, 1), 0), RANK)
        pick = (set_column == given[SET_ROW : SET_ROW + 1, 0:1]).astype(F32)
        lift = (times_transposed(router_low, values) * pick).astype(BF16)
        logits = times_transposed(r.router_t[...], values) + inner_rows(router_high, lift)
        powers = jnp.exp(logits - jnp.max(logits, axis=0, keepdims=True))
        probs = powers / jnp.sum(powers, axis=0, keepdims=True)
        expert = lax.broadcasted_iota(jnp.int32, (EXPERTS, block), 0)
        slot = lax.broadcasted_iota(jnp.int32, (slots, block), 0)
        gated = jnp.zeros((slots, block), F32)
        for k in range(TOP):
            gate = jnp.sum(
                jnp.where(expert == given[k : k + 1, :], probs, 0.0), axis=0, keepdims=True
            )
            gated = jnp.where(slot == targets(given, k), gate, gated)
        column = jnp.broadcast_to(jnp.sum(gated, axis=1, keepdims=True), (slots, 128))
        fill_slots(i, r.gates, column)
        fill_slots(i, r.rows_in, matmul(r.table[i], values).astype(BF16))
        lane = lax.div(lax.broadcasted_iota(jnp.int32, (SLOTS, WIDTH), 1), RANK)
        at = pl.ds(pl.multiple_of(i * SLOTS, SLOTS), SLOTS)
        r.slot_sets[at, :] = (lane == given[SET_ROW : SET_ROW + 1, 0:1]).astype(F32)
        return 0

    lax.fori_loop(0, all_images, dispatch, 0, unroll=4)

    chunks = [
        (
            r.first.at[e], r.first_got.at[e], r.first_final.at[e],
            functools.partial(lambda e, dp, tp: r.first_all.at[dp, tp, e], e),
        )
        for e in range(experts)
    ]
    chunks += [
        (r.second_sum, r.second_in, r.second_final, lambda dp, tp: r.second_all.at[dp, tp]),
        (r.early_sum, r.early_in, r.early_final, lambda dp, tp: r.early_all.at[dp, tp]),
        (r.late_sum, r.late_in, r.late_final, lambda dp, tp: r.late_all.at[dp, tp]),
    ]
    second_at, early_at, late_at = experts, experts + 1, experts + 2
    inner, outer = place.inner, 1 - place.inner
    to_partner, to_far = {"ctx": place.partner}, {"ctx": place.far_mid}
    flows, spreads = [], []
    for mine, got, final, slot in chunks:
        flows.append(
            dict(
                beside=wire.copy(mine.at[inner], got.at[0], to_partner),
                across=wire.copy(mine.at[outer], got.at[1], to_far),
                beyond=wire.copy(mine.at[outer], got.at[2], to_far),
                back=wire.copy(final.at[inner], final.at[inner], to_partner),
                share=wire.copy(final.at[inner], final.at[inner], to_far),
                away=wire.copy(final.at[inner], final.at[inner], {"ctx": place.far_end}),
            )
        )
        spreads.append(Spread(place, wire, final, slot, direct=len(spreads) >= early_at))

    def offer(k):
        @pl.when(place.is_end)
        def _():
            flows[k]["beyond"].start()
            flows[k]["beside"].start()

        @pl.when(place.is_mid)
        def _():
            flows[k]["across"].start()

    def total_half(k):
        mine, got, final, slot = chunks[k]

        @pl.when(place.is_mid)
        def _():
            for name in ("beside", "across", "beyond"):
                flows[k][name].wait_recv()
            final[inner] = add_rounded(mine[inner], got[0], got[1], got[2])
            for name in ("away", "share", "back"):
                flows[k][name].start()

    def settle(k):
        @pl.when(place.is_mid)
        def _():
            flows[k]["share"].wait_recv()

        @pl.when(place.is_end)
        def _():
            flows[k]["back"].wait_recv()
            flows[k]["away"].wait_recv()

        spreads[k].start()

    stages = (
        total_half, settle, lambda k: spreads[k].forward(), lambda k: spreads[k].diagonal(),
    )
    reached = [0] * len(chunks)

    def go(k, stage):
        while reached[k] < stage:
            stages[reached[k]](k)
            reached[k] += 1

    def at_point(point):
        for chunk, stage in SCHEDULE[point]:
            if len(chunks) + chunk >= 0:
                go(len(chunks) + chunk, stage)

    def run_expert(e):
        need(("a_first", e), ("b_first", e), ("up", e))
        need(("a_second", e), ("b_second", e), ("down", e))
        a_first, b_first = r.v_first_a[e].reshape(WIDTH, D), r.v_first_b[e].reshape(WIDTH, -1)
        a_second = r.v_second_a[e].reshape(WIDTH, -1)
        b_second = r.v_second_b[e].reshape(WIDTH, D)
        sums = None
        size = min(EXPERT_ROWS, all_images * SLOTS)
        for c in range(all_images * SLOTS // size):
            at = slice(c * size, (c + 1) * size)
            rows = r.rows_in[e, at]
            grads = r.grad_slots[e, at].astype(F32)
            gate = r.gates[e, at][:, 0:1]
            sets = r.slot_sets[at]
            lifted = (times_transposed(rows, a_first) * sets).astype(BF16)
            before = matmul(rows, r.v_up[e]) + matmul(lifted, b_first)
            phi = 0.5 * (1.0 + lax.erf(before * SQRT_HALF))
            active = (before * phi).astype(BF16)
            slope = phi + before * (INV_ROOT_TWO_PI * jnp.exp(-0.5 * before * before))
            lowered = (times_transposed(active, a_second) * sets).astype(BF16)
            out = matmul(active, r.v_down[e]) + matmul(lowered, b_second)
            grad_out = (grads * gate).astype(BF16)
            grad_lowered = (times_transposed(grad_out, b_second) * sets).astype(BF16)
            grad_active = times_transposed(grad_out, r.v_down[e]) + matmul(grad_lowered, a_second)
            grad_before = (grad_active * slope).astype(BF16)
            grad_lifted = (times_transposed(grad_before, b_first) * sets).astype(BF16)
            grad_rows = times_transposed(grad_before, r.v_up[e]) + matmul(grad_lifted, a_first)
            made = [
                inner_rows(lifted, grad_before),
                inner_rows(grad_lowered, active),
                inner_rows(grad_lifted, rows),
                inner_rows(lowered, grad_out),
            ]
            sums = made if sums is None else [a + b for a, b in zip(sums, made)]
            lane = lax.broadcasted_iota(jnp.int32, (size, 128), 1)
            gate_grads = jnp.sum(out * grads, axis=1, keepdims=True)
            gate_grads = jnp.where(lane == owned + e, gate_grads, 0.0).astype(BF16)
            some = slice(c * size // SLOTS, (c + 1) * size // SLOTS)
            to = slice(e * SLOTS, (e + 1) * SLOTS)
            number = size // SLOTS
            r.payload[some, to, 0:D] = grad_rows.astype(BF16).reshape(number, SLOTS, D)
            r.payload[some, to, D:CRITICAL] = gate_grads.reshape(number, SLOTS, 128)
            r.payload[some, to, CRITICAL:] = (out * gate).astype(BF16).reshape(number, SLOTS, D)
        r.first[e, 0] = sums[0].astype(BF16)
        r.first[e, 1] = sums[1].astype(BF16)
        share = D // place.tp_size
        for number in range(2):
            for t in range(place.tp_size):
                r.second[t, number, e] = sums[2 + number][:, t * share : (t + 1) * share].astype(
                    BF16
                )

    for e in range(experts):
        run_expert(e)
        offer(e)
        if e == experts - 2:
            at_point(0)
    at_point(1)

    second_swap = wire.copy(
        r.second.at[place.other_tp], r.second_got, {"tp": place.other_tp}
    )
    second_swap.start()
    first_lanes, other_lanes = slice(0, CRITICAL), slice(CRITICAL, CRITICAL + D)
    swaps = [
        wire.copy(
            r.partial.at[1 - place.core, :, :, :, at],
            r.from_sibling.at[:, :, :, at],
            {"dp": place.sibling},
        )
        for at in (first_lanes, other_lanes)
    ]

    def combine(core, at):
        def run(chip, _):
            for n in range(images):
                i = (chip * 2 + core) * images + n
                made = inner_rows(r.table[i], r.payload[i, :, at]).astype(BF16)
                for t in range(place.tp_size):
                    r.partial[core, chip, t, n * half : (n + 1) * half, at] = made[
                        t * half : (t + 1) * half
                    ]
            return 0

        lax.fori_loop(0, place.chips, run, 0, unroll=2)

    def send_back(at):
        copies = []
        for i, j in place.offsets() + [(0, 0)]:
            dp, tp = place.ahead(i, j)
            chip = lax.div(dp, 2)
            index = i * place.tp_size + j
            both = add_rounded(
                r.partial[place.core, chip, tp, :, at], r.from_sibling[chip, tp, :, at]
            )
            if index:
                r.from_sibling[chip, tp, :, at] = both
                copy = wire.copy(
                    r.from_sibling.at[chip, tp, :, at],
                    r.received.at[index, :, at],
                    {"dp": dp, "tp": tp},
                )
                copy.start()
                copies.append(copy)
            else:
                r.received[0, :, at] = both
        return copies

    combine(1 - place.core, first_lanes)
    swaps[0].start()
    combine(place.core, first_lanes)
    at_point(2)
    swaps[0].wait_recv()
    returns = [send_back(first_lanes)]
    combine(1 - place.core, other_lanes)
    swaps[1].start()
    combine(place.core, other_lanes)
    second_swap.wait()
    r.second_sum[...] = add_rounded(r.second[place.tp], r.second_got[...])
    offer(second_at)
    swaps[1].wait_recv()
    returns.append(send_back(other_lanes))
    late_sends = swaps + returns[0] + returns[1]
    at_point(3)
    for copy in returns[0]:
        copy.wait_recv()

    def live_column(i):
        lane = lax.broadcasted_iota(jnp.int32, (half, block), 1)
        row = lax.broadcasted_iota(jnp.int32, (half, block), 0) + place.tp * half
        live = r.ints[i, LIVE_ROW : LIVE_ROW + 1, :].astype(F32)
        return jnp.sum(jnp.where(lane == row, live, 0.0), axis=1, keepdims=True)

    lives = [live_column(i) for i in range(images)]
    total = r.received[0, :, :CRITICAL].astype(F32)
    for k in range(1, r.received.shape[0]):
        total = total + r.received[k, :, :CRITICAL].astype(F32)
    hidden = r.hidden[...]
    grad_probs = total[:, D : D + EXPERTS]
    grad_output = jnp.concatenate(
        [
            r.cot_all[place.dp * images + i, pl.ds(start, half), :].astype(F32) * lives[i]
            for i in range(images)
        ],
        axis=0,
    )
    rows = r.expert_in[...].reshape(count, D)
    router_lift = (times_transposed(rows, router_low) * own_sets).astype(BF16)
    logits = times_transposed(rows, r.router_t[...]) + matmul(router_lift, router_high)
    powers = jnp.exp(logits - jnp.max(logits, axis=-1, keepdims=True))
    gate_probs = powers / jnp.sum(powers, axis=-1, keepdims=True)
    grad_logits = (
        gate_probs * (grad_probs - jnp.sum(grad_probs * gate_probs, axis=-1, keepdims=True))
    ).astype(BF16)
    grad_router_lift = (times_transposed(grad_logits, router_high) * own_sets).astype(BF16)
    grad_expert_in = (
        total[:, :D] + matmul(grad_logits, r.router_t[...]) + matmul(grad_router_lift, router_low)
    )
    _, unit, factor = normalize(hidden, gain_two, shift_two)
    grad_rows = grad_output + normalize_back(grad_expert_in, unit, factor, gain_two)
    r.grad_hidden[...] = grad_rows
    grad_attended = grad_rows.astype(BF16)
    grad_mixing_lift = (times_transposed(grad_attended, mixing_high) * own_sets).astype(BF16)
    grad_heads = (
        matmul(grad_attended, r.mixing_all[...]) + matmul(grad_mixing_lift, mixing_low)
    ).astype(BF16)
    r.heads[...] = grad_heads.reshape(images, half, D)
    mix = r.head_mix[...]
    lane = lax.broadcasted_iota(jnp.int32, (D, 128), 1)
    head = lax.div(lax.broadcasted_iota(jnp.int32, (D, 128), 0), HD)
    ones = (lane == head).astype(F32).astype(BF16)
    delta_rows = split_sum(grad_heads.astype(F32) * mix.astype(F32), ones)
    r.delta[...] = delta_rows
    log_rows = r.logs[...]
    for i in range(images):
        part = slice(i * half, (i + 1) * half)
        pad = jnp.zeros((128 - half, 128), F32)
        turned = [
            jnp.concatenate([v[part], pad], axis=0).T[:HEADS] for v in (log_rows, delta_rows)
        ]
        row = 0
        for rest, number in zip(turned, (3, 2)):
            for _ in range(number):
                top = rest.astype(BF16)
                r.stats[i, row : row + HEADS, :] = top
                rest = rest - top.astype(F32)
                row += HEADS

    def heads_slot(i, ctx, tp):
        at = pl.multiple_of((ctx * place.tp_size + tp) * half, 16)
        return r.heads_all.at[i, pl.ds(at, half), :]

    chain = Chain(
        place, wire, [r.heads.at[i] for i in range(images)] + [r.stats],
        [functools.partial(heads_slot, i) for i in range(images)]
        + [lambda ctx, tp: r.stats_all.at[ctx * place.tp_size + tp]],
        [True] * (images + 1), True,
    )
    chain.start()

    def spread_start(values, got):
        rows = got.shape[1]
        copies = []
        for k, (dp, tp) in enumerate(place.peers):
            at = pl.ds(pl.multiple_of((dp * place.tp_size + tp) * rows, 16), rows)
            copy = wire.copy(values.at[at], got.at[k], {"dp": dp, "tp": tp})
            copy.start()
            copies.append(copy)
        return copies

    def spread_end(copies, values, got, total):
        rows = got.shape[1]
        for copy in copies:
            copy.wait()
        added = values[pl.ds(pl.multiple_of(place.me * rows, 16), rows), :].astype(F32)
        for k in range(plane - 1):
            added = added + got[k].astype(F32)
        total[...] = added.astype(BF16).reshape(total.shape)

    def put_tiles(target, products):
        tile = 0
        for product in products:
            for n in range(product.shape[1] // 128):
                target[tile * WIDTH : (tile + 1) * WIDTH, :] = product[
                    :, n * 128 : (n + 1) * 128
                ].astype(BF16)
                tile += 1
        if tile * WIDTH < target.shape[0]:
            target[tile * WIDTH :, :] = jnp.zeros(
                (target.shape[0] - tile * WIDTH, 128), BF16
            )

    wide_logits = jnp.concatenate(
        [grad_logits, jnp.zeros((count, 128 - EXPERTS), BF16)], axis=1
    )
    put_tiles(
        r.early,
        (
            inner_rows(grad_mixing_lift, mix),
            inner_rows(r.mixing_lift[...], grad_attended),
            inner_rows(grad_router_lift, rows),
            inner_rows(router_lift, wide_logits),
        ),
    )
    early_spread = spread_start(r.early, r.early_got)
    at_point(4)
    chain.step(1)
    at_point(5)
    chain.step(2)
    at_point(6)
    chain.step(3)
    spread_end(early_spread, r.early, r.early_got, r.early_sum)
    offer(early_at)
    at_point(7)
    chain.finish_own()
    for s in range(1, chain.steps + 1):
        chain.landed(s)

    def to_other(values, gathered):
        spot = gathered.at[:, pl.ds(start, half), :]
        copies = [wire.copy(values, spot, {"tp": place.other_tp}), wire.near(values, spot)]
        for copy in copies:
            copy.start()
        return copies

    for copy in returns[1]:
        copy.wait_recv()
    total = r.hidden[...]
    for k in range(r.received.shape[0]):
        total = total + r.received[k, :, CRITICAL:].astype(F32)
    r.out_own[...] = total.astype(BF16).reshape(images, half, D)
    layer_out = to_other(r.out_own, r.out_all)

    def heads_back(i, j):
        part = slice(i * half, (i + 1) * half)
        at = slice(j * 2 * HD, (j + 1) * 2 * HD)
        keys_open = r.keys_open[i : i + 1, :] > 0
        own_open = jnp.concatenate([lives[i], lives[i]], axis=0) > 0
        found = jnp.concatenate(
            [r.stats_all[n, i][:, :half].astype(F32) for n in range(r.stats_all.shape[0])], axis=1
        )
        log_t = found[0:HEADS] + found[HEADS : 2 * HEADS] + found[2 * HEADS : 3 * HEADS]
        delta_t = found[3 * HEADS : 4 * HEADS] + found[4 * HEADS :]
        q_all, k_all, v_all = (r.joined[p, i, :, at] for p in range(3))
        g_all = r.heads_all[i, :, at]

        def column(values):
            return jnp.concatenate(
                [values[:, 2 * j : 2 * j + 1], values[:, 2 * j + 1 : 2 * j + 2]], axis=0
            )

        def across(values):
            return jnp.concatenate(
                [
                    jnp.broadcast_to(values[2 * j + n : 2 * j + n + 1, :], (half, values.shape[1]))
                    for n in range(2)
                ],
                axis=0,
            )

        q = stack_pair(r.joined[0, i, own, at], masks, scale)
        g = stack_pair(r.heads[i, :, at], masks)
        scores = jnp.where(keys_open, times_transposed(q, k_all), MASKED)
        probs = jnp.exp(scores - column(r.logs[part]))
        grad_probs_att = times_transposed(g, v_all)
        grad_scores = (probs * (grad_probs_att - column(r.delta[part]))).astype(BF16)
        r.grads[0, part, at] = (join_pair(matmul(grad_scores, k_all), masks) * scale).astype(BF16)
        k = stack_pair(r.joined[1, i, own, at], masks, scale)
        v = stack_pair(r.joined[2, i, own, at], masks)
        scores = jnp.where(own_open, times_transposed(k, q_all), MASKED)
        probs = jnp.exp(scores - across(log_t))
        grad_probs_att = times_transposed(v, g_all)
        grad_scores = (probs * (grad_probs_att - across(delta_t))).astype(BF16)
        r.grads[1, part, at] = (join_pair(matmul(grad_scores, q_all), masks) * scale).astype(BF16)
        r.grads[2, part, at] = join_pair(matmul(probs.astype(BF16), g_all), masks).astype(BF16)

    for i in range(images):
        for j in range(HEADS // 2):
            heads_back(i, j)
            if j % 2:
                at_point(8 + 2 * i + j // 2)
    lift = times_transposed(r.grads[0], high(0))
    into = times_transposed(r.grads[0], r.weights_all[0])
    for p in range(1, 3):
        lift = lift + times_transposed(r.grads[p], high(p))
        into = into + times_transposed(r.grads[p], r.weights_all[p])
    lift = (lift * own_sets).astype(BF16)
    lift_in = jnp.concatenate([r.lift_all[i, own, :] for i in range(images)], axis=0)
    put_tiles(
        r.late,
        [inner_rows(lift_in, r.grads[p]) for p in range(3)]
        + [inner_rows(lift, r.own_in[...].reshape(count, D))],
    )
    late_spread = spread_start(r.late, r.late_got)
    at_point(12)
    into = into + matmul(lift, attend_low)
    flat = jnp.concatenate([r.tokens_all[i, own, :] for i in range(images)], axis=0).astype(F32)
    _, unit, factor = normalize(flat, gain_one, shift_one)
    result = r.grad_hidden[...] + normalize_back(into, unit, factor, gain_one)
    r.grad_own[...] = result.astype(BF16).reshape(images, half, D)
    at_point(13)
    tokens_out = to_other(r.grad_own, r.grad_all)
    spread_end(late_spread, r.late, r.late_got, r.late_sum)
    offer(late_at)
    at_point(14)
    for k in range(len(chunks)):
        go(k, DONE)

    @pl.when(place.is_end)
    def _():
        for flow in flows:
            flow["beyond"].wait_send()
            flow["beside"].wait_send()

    @pl.when(place.is_mid)
    def _():
        for flow in flows:
            for name in ("across", "away", "share", "back"):
                flow[name].wait_send()

    for spread in spreads:
        spread.finish()
    for spread in [weights, mixing, numbers, router, cotangents] + expert_rows + spreads:
        spread.drain()
    tokens_chain.drain()
    chain.drain()
    for copy in late_sends:
        copy.wait_send()
    for copy in layer_out + tokens_out:
        copy.wait()
    assert not pending


def run_layer(sizes, **inputs):
    dp, ctx, tp = sizes
    assert ctx == 4 and tp == 2
    plane, chips = dp * tp, dp // 2
    images, block = inputs["tokens"].shape[:2]
    assert images == 2
    half = block // tp
    count, seq, all_images = images * half, ctx * block, dp * images
    experts, _, hidden = inputs["up_weight"].shape
    rows, lanes = inputs["mixing"].shape
    slots = experts * SLOTS
    sent = CRITICAL + D
    early_rows = small_rows(3 * (D // 128) + 1, plane)
    late_rows = small_rows(4 * (D // 128), plane)
    second = (2, experts, WIDTH, D // tp)
    full = dict(
        first=(experts, 2, WIDTH, hidden),
        second=second,
        early=(2, early_rows // 2, 128),
        late=(2, late_rows // 2, 128),
    )
    cut = {name: shape[1:] for name, shape in full.items()}
    cut["first"] = (experts, WIDTH, hidden)
    outputs = {name + "_all": (dp, tp) + shape for name, shape in full.items()}
    outputs.update(out_all=(images, block, D), grad_all=(images, block, D))
    narrow = dict(
        tokens_all=(images, seq, D),
        weights_all=(3, dp * rows, tp * lanes),
        mixing_all=(dp * rows, tp * lanes),
        router_all=(dp,) + inputs["router"].shape,
        router_t=(EXPERTS, D),
        cot_all=(all_images, block, D),
        rows_all=(all_images, block, D),
        v_attend_low=(SETS, RANK, D),
        v_attend_high=(SETS, 3, RANK, D),
        v_mixing_low=(SETS, RANK, D),
        v_mixing_high=(SETS, RANK, D),
        v_router_low=(SETS, RANK, D),
        v_router_high=(SETS, RANK, EXPERTS),
        v_first_a=(experts, SETS, RANK, D),
        v_first_b=(experts, SETS, RANK, hidden),
        v_second_a=(experts, SETS, RANK, hidden),
        v_second_b=(experts, SETS, RANK, D),
        v_up=(experts, D, hidden),
        v_down=(experts, hidden, D),
        lift_all=(images, seq, WIDTH),
        joined=(3, images, seq, D),
        own_in=(images, half, D),
        head_mix=(count, D),
        mixing_lift=(count, WIDTH),
        expert_in=(images, half, D),
        table=(all_images, slots, block),
        grad_slots=(experts, all_images * SLOTS, D),
        rows_in=(experts, all_images * SLOTS, D),
        payload=(all_images, slots, sent),
        partial=(2, chips, tp, count, sent),
        from_sibling=(chips, tp, count, sent),
        received=(chips * tp, count, sent),
        first=full["first"],
        second=(tp,) + second,
        second_got=second,
        second_sum=second,
        early=(plane * early_rows, 128),
        late=(plane * late_rows, 128),
        early_got=(plane - 1, early_rows, 128),
        late_got=(plane - 1, late_rows, 128),
        early_sum=full["early"],
        late_sum=full["late"],
        heads=(images, half, D),
        stats=(images, 5 * HEADS, 128),
        heads_all=(images, seq, D),
        stats_all=(ctx * tp, images, 5 * HEADS, 128),
        grads=(3, count, D),
        out_own=(images, half, D),
        grad_own=(images, half, D),
    )
    for name in full:
        narrow[name + "_final"] = full[name]
        narrow[name + "_in"] = (3,) + cut[name]
    narrow["first_got"] = (experts, 3, WIDTH, hidden)
    del narrow["first_in"]
    wide = dict(
        logs=(count, 128),
        delta=(count, 128),
        hidden=(count, D),
        grad_hidden=(count, D),
        gates=(experts, all_images * SLOTS, 128),
        slot_sets=(all_images * SLOTS, WIDTH),
        keys_open=(images, seq),
    )
    integers = dict(
        ints=(images, 8, block),
        ints_all=(all_images, 8, block),
        ctx_ints=(ctx, images, 8, block),
    )
    scratch = {}
    for shapes, dtype in ((narrow, BF16), (wide, F32), (integers, jnp.int32)):
        for name, shape in shapes.items():
            scratch[name] = pltpu.VMEM(shape, dtype)
    chunks = experts + 3
    remote = (
        2 * Chain.remote(ctx, images + 1)
        + (2 + images + chunks) * Spread.remote(sizes)
        + 3 * Spread.remote(sizes, False)
        + 6 * chunks
        + 3
        + 2 * (chips * tp - 1)
        + 2 * (plane - 1)
        + 2
    )
    scratch["send"] = pltpu.SemaphoreType.DMA((remote,))
    scratch["recv"] = pltpu.SemaphoreType.DMA((remote,))
    scratch["local"] = pltpu.SemaphoreType.DMA((7 + 6 * experts + 5 + images + chunks + images + 1 + 2,))
    kinds = dict(
        adapter_set=IN_SMEM, image_mask=IN_SMEM, routes_t=IN_VMEM, slots_t=IN_VMEM,
        token_mask=IN_VMEM, first_gain=IN_VMEM, first_shift=IN_VMEM, second_gain=IN_VMEM,
        second_shift=IN_VMEM,
    )
    names = tuple(inputs) + tuple(outputs) + tuple(scratch)
    made = pl.pallas_call(
        functools.partial(layer_kernel, sizes, names),
        out_shape=tuple(jax.ShapeDtypeStruct(shape, BF16) for shape in outputs.values()),
        in_specs=[kinds.get(name, ANY) for name in inputs],
        out_specs=(ANY,) * len(outputs),
        scratch_shapes=tuple(scratch.values()),
        compiler_params=pltpu.CompilerParams(
            collective_id=0, has_side_effects=True, vmem_limit_bytes=62 << 20
        ),
    )(*inputs.values())
    return dict(zip(outputs, made))


def assemble_kernel(
    first, second, early, late, out_in, grad_in,
    up, down_t, narrow_t, narrow, attend_down, attend_up, mixing_down, mixing_up, router_down,
    router_up, out, grad,
):
    lanes, part = first.shape[-1], second.shape[-1]
    for n in range(first.shape[2]):
        for tp in range(first.shape[1]):
            for half, target in ((0, up), (1, down_t)):
                target[:, n, :, tp * lanes : (tp + 1) * lanes] = (
                    first[0, tp, n, half].astype(F32).reshape(SETS, RANK, lanes)
                )
            for half, target in ((0, narrow_t), (1, narrow)):
                target[:, n, :, tp * part : (tp + 1) * part] = (
                    second[0, tp, half, n].astype(F32).reshape(SETS, RANK, part)
                )

    @pl.when(pl.program_id(0) == 0)
    def _():
        def tile(small, k):
            return small[k * WIDTH : (k + 1) * WIDTH, :].astype(F32).reshape(SETS, RANK, 128)

        count = D // 128
        for p in range(3):
            for k in range(count):
                attend_up[:, p, :, k * 128 : (k + 1) * 128] = tile(late, p * count + k)
        for k in range(count):
            attend_down[:, :, k * 128 : (k + 1) * 128] = tile(late, 3 * count + k)
        for p, target in enumerate((mixing_down, mixing_up, router_down)):
            for k in range(count):
                target[:, :, k * 128 : (k + 1) * 128] = tile(early, p * count + k)
        router_up[...] = tile(early, 3 * count)[:, :, :EXPERTS]
        out[...] = out_in[...]
        grad[...] = grad_in[...]


def assemble(first, second, early, late, out, grad):
    dp, tp, experts, _, width, lanes = first.shape
    part = second.shape[-1]
    group = min(experts, ASSEMBLED)
    groups = experts // group

    def split(e):
        return lax.div(e, groups), lax.rem(e, groups)

    def expert_out(size):
        return (
            jax.ShapeDtypeStruct((SETS, EXPERTS, RANK, size), F32),
            pl.BlockSpec((SETS, group, RANK, size), lambda e: (0, e, 0, 0)),
        )

    def whole_out(*shape):
        return (
            jax.ShapeDtypeStruct(shape, F32),
            pl.BlockSpec(shape, lambda e: (0,) * len(shape)),
        )

    outs = (
        [expert_out(FF)] * 2
        + [expert_out(D)] * 2
        + [whole_out(SETS, RANK, D), whole_out(SETS, 3, RANK, D)]
        + [whole_out(SETS, RANK, D)] * 3
        + [whole_out(SETS, RANK, EXPERTS)]
        + [(jax.ShapeDtypeStruct(out.shape, BF16), pl.BlockSpec(out.shape, lambda e: (0, 0, 0)))] * 2
    )
    return pl.pallas_call(
        assemble_kernel,
        grid=(EXPERTS // group,),
        out_shape=[out[0] for out in outs],
        in_specs=[
            pl.BlockSpec(
                (1, tp, group, 2, width, lanes), lambda e: (split(e)[0], 0, split(e)[1], 0, 0, 0)
            ),
            pl.BlockSpec(
                (1, tp, 2, group, width, part), lambda e: (split(e)[0], 0, 0, split(e)[1], 0, 0)
            ),
            pl.BlockSpec(early.shape, lambda e: (0, 0)),
            pl.BlockSpec(late.shape, lambda e: (0, 0)),
            pl.BlockSpec(out.shape, lambda e: (0, 0, 0)),
            pl.BlockSpec(grad.shape, lambda e: (0, 0, 0)),
        ],
        out_specs=[out[1] for out in outs],
        compiler_params=pltpu.CompilerParams(vmem_limit_bytes=60 << 20),
    )(first, second, early, late, out, grad)


def per_device(
    sizes,
    tokens,
    cotangent,
    routes,
    slot_index,
    token_mask,
    image_mask,
    adapter_set,
    first_gain,
    first_shift,
    second_gain,
    second_shift,
    attend_weight,
    mixing_weight,
    router_weight,
    expand_weight,
    shrink_weight,
    attend_down,
    attend_up,
    mixing_down,
    mixing_up,
    router_down,
    router_up,
    expand_down,
    expand_up,
    shrink_down,
    shrink_up,
):
    def flipped(values):
        return jnp.swapaxes(values, -1, -2)

    made = run_layer(
        sizes,
        tokens=tokens,
        cotangent=cotangent,
        weights=jnp.transpose(attend_weight, (1, 0, 2)),
        mixing=mixing_weight,
        router=flipped(router_weight),
        routes_t=flipped(routes),
        slots_t=flipped(slot_index),
        token_mask=token_mask,
        image_mask=image_mask,
        adapter_set=adapter_set,
        first_gain=first_gain.reshape(1, D),
        first_shift=first_shift.reshape(1, D),
        second_gain=second_gain.reshape(1, D),
        second_shift=second_shift.reshape(1, D),
        up_weight=expand_weight,
        down_weight=shrink_weight,
        attend_low=flipped(attend_down),
        attend_high=jnp.transpose(attend_up, (0, 2, 1, 3)),
        mixing_low=flipped(mixing_down),
        mixing_high=mixing_up,
        router_low=flipped(router_down),
        router_high=router_up,
        first_a=flipped(expand_down),
        first_b=expand_up,
        second_a=flipped(shrink_down),
        second_b=shrink_up,
    )
    wide = assemble(
        made["first_all"],
        made["second_all"],
        made["early_all"].reshape(-1, 128),
        made["late_all"].reshape(-1, 128),
        made["out_all"],
        made["grad_all"],
    )
    return (
        wide[10],
        wide[11],
        flipped(wide[4]),
        jnp.transpose(wide[5], (0, 2, 1, 3)),
        flipped(wide[6]),
        wide[7],
        flipped(wide[8]),
        wide[9],
        flipped(wide[2]),
        wide[0],
        flipped(wide[1]),
        wide[3],
    )


def solution(mesh):
    sizes = (mesh.shape["dp"], mesh.shape["ctx"], mesh.shape["tp"])
    tokens_spec = P("dp", "ctx", None)
    in_specs = (
        (tokens_spec,) * 4
        + (P("dp", "ctx"), P("dp"), P("dp"))
        + (P(),) * 4
        + (P("dp", None, "tp"), P("dp", "tp"), P("dp", None))
        + (P("dp", None, "tp"), P("dp", "tp", None))
        + (P(),) * 10
    )
    out_specs = (tokens_spec,) * 2 + (P(),) * 10
    return jax.shard_map(
        functools.partial(per_device, sizes),
        mesh=mesh,
        in_specs=in_specs,
        out_specs=out_specs,
        check_vma=False,
    )
```

```python
import functools
import types

import jax
import jax.numpy as jnp
from jax import lax
from jax.experimental import pallas as pl
from jax.experimental.pallas import tpu as pltpu
from jax.sharding import PartitionSpec as P

D = 512
HEADS = 8
HD = 64
FF = 2048
EXPERTS = 16
TOP = 2
RANK = 16
SETS = 4
CAP = 30
SLOTS = 32
WIDTH = SETS * RANK
LIVE_ROW = 2 * TOP
SET_ROW = LIVE_ROW + 1
CRITICAL = D + 128
EXPERT_ROWS = 256
ASSEMBLED = 4

EPSILON = 1e-06
MASKED = -1e30
SQRT_HALF = 0.7071067811865476
INV_ROOT_TWO_PI = 0.3989422804014327
F32 = jnp.float32
BF16 = jnp.bfloat16
MESH = pl.DeviceIdType.MESH
ANY = pl.BlockSpec(memory_space=pl.ANY)
IN_SMEM = pl.BlockSpec(memory_space=pltpu.SMEM)
IN_VMEM = pl.BlockSpec(memory_space=pltpu.VMEM)


def matmul(left_side, right_side):
    return jnp.dot(left_side, right_side, preferred_element_type=F32)


def inner_rows(left_side, right_side):
    return lax.dot_general(
        left_side, right_side, (((0,), (0,)), ((), ())), preferred_element_type=F32
    )


def times_transposed(left_side, right_side):
    return lax.dot_general(
        left_side, right_side, (((1,), (1,)), ((), ())), preferred_element_type=F32
    )


def normalize(values, gain_row, shift_row):
    centred = values - jnp.mean(values, axis=-1, keepdims=True)
    spread = jnp.mean(centred * centred, axis=-1, keepdims=True)
    factor = lax.rsqrt(spread + EPSILON)
    normed = centred * factor
    return (normed * gain_row + shift_row, normed, factor)


def normalize_back(grad_out, normed, factor, gain_row):
    scaled = grad_out * gain_row
    return factor * (
        scaled
        - jnp.mean(scaled, axis=-1, keepdims=True)
        - normed * jnp.mean(scaled * normed, axis=-1, keepdims=True)
    )


def add_rounded(*parts):
    total = parts[0].astype(F32)
    for part in parts[1:]:
        total = total + part.astype(F32)
    return total.astype(BF16)


def split_sum(values, ones):
    high = values.astype(BF16)
    low = (values - high.astype(F32)).astype(BF16)
    return matmul(high, ones) + matmul(low, ones)


def put_lanes(columns, width):
    lane = lax.broadcasted_iota(jnp.int32, (columns[0].shape[0], width), 1)
    total = jnp.zeros((columns[0].shape[0], width), F32)
    for k, column in enumerate(columns):
        total = jnp.where(lane == k, column, total)
    return total


def half_masks():
    lane = lax.broadcasted_iota(jnp.int32, (1, 2 * HD), 1)
    even = (lane < HD).astype(F32)
    return even, 1.0 - even


def stack_pair(rows, masks, factor=1.0):
    wide = rows.astype(F32) * factor
    return jnp.concatenate([wide * masks[0], wide * masks[1]], axis=0).astype(BF16)


def join_pair(rows, masks):
    half = rows.shape[0] // 2
    return rows[:half] * masks[0] + rows[half:] * masks[1]


SUM, SENT, ONWARD, DONE = range(1, 5)
E0, E1, E2, E3, SECOND, EARLY, LATE = range(-7, 0)
SCHEDULE = (
    (),
    ((E0, SUM),),
    ((E1, SUM),),
    ((E0, SENT), (E2, SUM), (E1, SENT)),
    ((E0, ONWARD), (E3, SUM)),
    ((E2, SENT), (E1, ONWARD)),
    ((E0, DONE), (SECOND, SUM)),
    ((E3, SENT), (E2, ONWARD)),
    ((E1, DONE),),
    ((SECOND, SENT),),
    ((EARLY, SUM), (E3, ONWARD)),
    ((E2, DONE),),
    ((SECOND, ONWARD),),
    ((EARLY, SENT),),
    (
        (E3, DONE), (LATE, SUM), (EARLY, ONWARD), (SECOND, DONE), (LATE, SENT), (EARLY, DONE),
        (LATE, ONWARD), (LATE, DONE),
    ),
)


def small_rows(tiles, plane):
    return -(-tiles * WIDTH // (plane * 16)) * 16


class Wire:
    def __init__(self, send, recv, local):
        self.send, self.recv, self.local = send, recv, local
        self.used = self.used_local = 0

    def copy(self, src, dst, device):
        k = self.used
        self.used += 1
        assert k < self.send.shape[0]
        return pltpu.make_async_remote_copy(
            src_ref=src,
            dst_ref=dst,
            send_sem=self.send.at[k],
            recv_sem=self.recv.at[k],
            device_id=device,
            device_id_type=MESH,
        )

    def near(self, src, dst):
        k = self.used_local
        self.used_local += 1
        assert k < self.local.shape[0]
        return pltpu.make_async_copy(src, dst, self.local.at[k])


class Place:
    def __init__(self, sizes):
        self.dp_size, self.ctx_size, self.tp_size = sizes
        self.chips = self.dp_size // 2
        self.plane = self.dp_size * self.tp_size
        self.dp = lax.axis_index("dp")
        self.ctx = lax.axis_index("ctx")
        self.tp = lax.axis_index("tp")
        self.chip = lax.div(self.dp, 2)
        self.core = lax.rem(self.dp, 2)
        self.sibling = self.chip * 2 + (1 - self.core)
        self.other_tp = lax.rem(self.tp + 1, 2)
        self.me = self.dp * self.tp_size + self.tp
        self.is_mid = jnp.logical_and(self.ctx >= 1, self.ctx <= 2)
        self.is_end = jnp.logical_not(self.is_mid)
        self.inner = lax.div(self.ctx, 2)
        self.partner = jnp.where(self.is_mid, self.inner * 3, 1 + self.inner)
        self.far_mid = 2 - self.inner
        self.far_end = 3 - 3 * self.inner
        self.peers = []
        for k in range(1, self.plane):
            peer = lax.rem(self.me + k, self.plane)
            self.peers.append((lax.div(peer, self.tp_size), lax.rem(peer, self.tp_size)))

    def ahead(self, i, j):
        return (
            lax.rem(self.chip + i, self.chips) * 2 + self.core,
            lax.rem(self.tp + j, self.tp_size),
        )

    def behind(self, i, j):
        return self.ahead(self.chips - i, self.tp_size - j)

    def offsets(self, over_tp=True):
        return [
            (i, j)
            for i in range(self.chips)
            for j in range(self.tp_size if over_tp else 1)
            if i or j
        ]

    def greet(self):
        barrier = pltpu.get_barrier_semaphore()
        for dp, tp in self.peers:
            pl.semaphore_signal(
                barrier, inc=1, device_id={"dp": dp, "tp": tp}, device_id_type=MESH
            )
        for ctx in (self.partner, self.far_mid):
            pl.semaphore_signal(barrier, inc=1, device_id={"ctx": ctx}, device_id_type=MESH)

        @pl.when(self.is_mid)
        def _():
            pl.semaphore_signal(
                barrier, inc=1, device_id={"ctx": self.far_end}, device_id_type=MESH
            )

    def met(self):
        barrier = pltpu.get_barrier_semaphore()
        pl.semaphore_wait(barrier, self.plane + 1 + jnp.where(self.is_mid, 1, 0))


class Spread:
    def __init__(
        self, place, wire, source, slot, over_tp=True, direct=False, near=True, turn=False
    ):
        self.turn = turn
        self.place, self.wire, self.source, self.slot = place, wire, source, slot
        self.over_tp = over_tp
        self.relay = over_tp and not direct and place.chips == 2 and place.tp_size == 2
        self.near = near
        self.flights, self.across, self.beside, self.here = [], None, [], None

    def to_sibling(self, source, spot):
        copy = self.wire.copy(source, spot, {"dp": self.place.sibling})
        copy.start()
        self.beside.append(copy)

    def start(self):
        place = self.place
        spot = self.slot(place.dp, place.tp)
        for i, j in place.offsets(self.over_tp):
            if self.relay and i and j:
                continue
            dp, tp = place.ahead(i, j)
            copy = self.wire.copy(self.source, spot, {"dp": dp, "tp": tp})
            copy.start()
            self.flights.append((copy, i, j))
        self.to_sibling(self.source, spot)
        if self.near:
            self.here = self.wire.near(self.source, spot)
            self.here.start()

    def forward(self):
        for copy, i, j in sorted(self.flights, key=lambda f: f[1]):
            copy.wait_recv()
            got = self.slot(*self.place.behind(i, j))
            if self.relay and (i if self.turn else j):
                dp, tp = self.place.ahead(0, 1) if self.turn else self.place.ahead(1, 0)
                self.across = self.wire.copy(got, got, {"dp": dp, "tp": tp})
                self.across.start()
            self.to_sibling(got, got)

    def diagonal(self):
        if self.relay:
            self.across.wait_recv()
            got = self.slot(*self.place.behind(1, 1))
            self.to_sibling(got, got)

    def finish(self):
        for copy in self.beside:
            copy.wait_recv()
        if self.near:
            self.here.wait()

    def drain(self):
        for copy, _, _ in self.flights:
            copy.wait_send()
        if self.relay:
            self.across.wait_send()
        for copy in self.beside:
            copy.wait_send()

    @staticmethod
    def remote(sizes, over_tp=True):
        return 2 * (sizes[0] // 2 * (sizes[2] if over_tp else 1) - 1) + 1


class Chain:
    def __init__(self, place, wire, sources, slots, over, with_own):
        self.place, n = place, place.ctx_size
        self.steps = n - 1
        to_tp = {"tp": place.other_tp}
        self.right, self.left, self.over_right, self.over_left = {}, {}, {}, {}
        self.own, self.here = [], []
        for source, slot in zip(sources, slots):
            spot = slot(place.ctx, place.tp)
            if with_own:
                self.own.append(wire.copy(source, spot, to_tp))
                self.here.append(wire.near(source, spot))
        for s in range(1, n):
            back = [slot(jnp.maximum(place.ctx - (s - 1), 0), place.tp) for slot in slots]
            ahead = [slot(jnp.minimum(place.ctx + (s - 1), n - 1), place.tp) for slot in slots]
            got_right = [slot(jnp.maximum(place.ctx - s, 0), place.tp) for slot in slots]
            got_left = [slot(jnp.minimum(place.ctx + s, n - 1), place.tp) for slot in slots]
            to_right = {"ctx": jnp.minimum(place.ctx + 1, n - 1)}
            to_left = {"ctx": jnp.maximum(place.ctx - 1, 0)}
            self.right[s] = [
                wire.copy(a if s == 1 else b, b, to_right) for a, b in zip(sources, back)
            ]
            self.left[s] = [
                wire.copy(a if s == 1 else b, b, to_left) for a, b in zip(sources, ahead)
            ]
            self.over_right[s] = {
                k: wire.copy(b, b, to_tp) for k, b in enumerate(got_right) if over[k]
            }
            self.over_left[s] = {
                k: wire.copy(b, b, to_tp) for k, b in enumerate(got_left) if over[k]
            }

    def sends_right(self, s):
        return jnp.logical_and(self.place.ctx >= s - 1, self.place.ctx < self.steps)

    def sends_left(self, s):
        return jnp.logical_and(self.place.ctx <= self.steps + 1 - s, self.place.ctx > 0)

    def gets_right(self, s):
        return self.place.ctx >= s

    def gets_left(self, s):
        return self.place.ctx <= self.steps - s

    @staticmethod
    def all_of(copies, verb):
        for copy in copies:
            getattr(copy, verb)()

    def start(self):
        pl.when(self.sends_right(1))(lambda: self.all_of(self.right[1], "start"))
        pl.when(self.sends_left(1))(lambda: self.all_of(self.left[1], "start"))
        self.all_of(self.own + self.here, "start")

    def step(self, s):
        def passed(got, over, sends):
            def run():
                for k, copy in enumerate(got[s]):
                    copy.wait_recv()
                    if s < self.steps:
                        pl.when(sends(s + 1))(got[s + 1][k].start)
                    if k in over[s]:
                        over[s][k].start()

            return run

        pl.when(self.gets_right(s))(passed(self.right, self.over_right, self.sends_right))
        pl.when(self.gets_left(s))(passed(self.left, self.over_left, self.sends_left))

    def landed(self, s):
        pl.when(self.gets_right(s))(lambda: self.all_of(self.over_right[s].values(), "wait_recv"))
        pl.when(self.gets_left(s))(lambda: self.all_of(self.over_left[s].values(), "wait_recv"))

    def finish_own(self):
        self.all_of(self.own, "wait_recv")
        self.all_of(self.here, "wait")

    def drain(self):
        self.all_of(self.own, "wait_send")
        for s in range(1, self.steps + 1):
            pl.when(self.gets_right(s))(lambda: self.all_of(self.over_right[s].values(), "wait_send"))
            pl.when(self.gets_left(s))(lambda: self.all_of(self.over_left[s].values(), "wait_send"))
            pl.when(self.sends_right(s))(lambda: self.all_of(self.right[s], "wait_send"))
            pl.when(self.sends_left(s))(lambda: self.all_of(self.left[s], "wait_send"))

    @staticmethod
    def remote(n, arrays):
        return arrays * (1 + 4 * (n - 1))


def layer_kernel(sizes, names, *refs):
    r = types.SimpleNamespace(**dict(zip(names, refs)))
    place = Place(sizes)
    wire = Wire(r.send, r.recv, r.local)
    plane = place.plane
    images, block = r.tokens.shape[:2]
    half = block // place.tp_size
    count = images * half
    seq = place.ctx_size * block
    experts, _, hidden_units = r.up_weight.shape
    all_images = place.dp_size * images
    owned = place.dp * experts
    start = pl.multiple_of(place.tp * half, 16)
    own_start = pl.multiple_of(place.ctx * block + place.tp * half, 16)
    own = pl.ds(own_start, half)
    masks = half_masks()
    scale = HD**-0.5

    pending = {}

    def load(name, source, target):
        pending[name] = wire.near(source, target)
        pending[name].start()

    def need(*wanted):
        for name in wanted:
            if name in pending:
                pending.pop(name).wait()

    place.greet()
    whole = pl.ds(pl.multiple_of(place.ctx * block, 16), block)
    load("tokens", r.tokens, r.tokens_all.at[:, whole, :])
    for name in (
        "attend_low", "attend_high", "mixing_low", "mixing_high", "router_low", "router_high",
    ):
        load(name, getattr(r, name), getattr(r, "v_" + name))
    r.ints[:, 0:TOP, :] = r.routes_t[...]
    r.ints[:, TOP : 2 * TOP, :] = r.slots_t[...]
    lane_set = lax.div(lax.broadcasted_iota(jnp.int32, (1, WIDTH), 1), RANK)
    picks = []
    for i in range(images):
        r.ints[i, LIVE_ROW : LIVE_ROW + 1, :] = r.token_mask[i : i + 1, :] * r.image_mask[i]
        r.ints[i, SET_ROW:, :] = jnp.full((8 - SET_ROW, block), r.adapter_set[i], jnp.int32)
        picks.append((lane_set == r.adapter_set[i]).astype(F32))
    gain_one, shift_one = r.first_gain[...], r.first_shift[...]
    gain_two, shift_two = r.second_gain[...], r.second_shift[...]

    place.met()

    rows, lanes = r.mixing.shape

    def at_rows(dp):
        return pl.ds(pl.multiple_of(dp * rows, 16), rows)

    def at_lanes(tp):
        return pl.ds(pl.multiple_of(tp * lanes, 128), lanes)

    def token_slot(i, ctx, tp):
        at = pl.multiple_of(ctx * block + tp * half, 16)
        return r.tokens_all.at[i, pl.ds(at, half), :]

    tokens_chain = Chain(
        place, wire,
        [r.tokens.at[i, pl.ds(start, half), :] for i in range(images)] + [r.ints],
        [functools.partial(token_slot, i) for i in range(images)]
        + [lambda ctx, tp: r.ctx_ints.at[ctx]],
        [True] * images + [False], False,
    )
    weights = Spread(
        place, wire, r.weights, lambda dp, tp: r.weights_all.at[:, at_rows(dp), at_lanes(tp)]
    )
    mixing = Spread(
        place, wire, r.mixing, lambda dp, tp: r.mixing_all.at[at_rows(dp), at_lanes(tp)]
    )
    numbers = Spread(
        place, wire, r.ints, lambda dp, tp: r.ints_all.at[pl.ds(dp * 2, 2)], over_tp=False
    )
    router = Spread(place, wire, r.router, lambda dp, tp: r.router_all.at[dp], over_tp=False)
    cotangents = Spread(
        place, wire, r.cotangent, lambda dp, tp: r.cot_all.at[pl.ds(dp * 2, 2)], over_tp=False
    )
    r.ctx_ints[place.ctx] = r.ints[...]
    tokens_chain.start()
    weights.start()
    numbers.start()
    router.start()
    mixing.start()
    wide = pl.ds(pl.multiple_of(place.tp * hidden_units, 128), hidden_units)
    for e in range(experts):
        load(("a_first", e), r.first_a.at[:, owned + e], r.v_first_a.at[e])
        load(("b_first", e), r.first_b.at[:, owned + e, :, wide], r.v_first_b.at[e])
        load(("up", e), r.up_weight.at[e], r.v_up.at[e])
        load(("a_second", e), r.second_a.at[:, owned + e, :, wide], r.v_second_a.at[e])
        load(("b_second", e), r.second_b.at[:, owned + e], r.v_second_b.at[e])
        load(("down", e), r.down_weight.at[e], r.v_down.at[e])
    weights.forward()
    tokens_chain.step(1)
    weights.diagonal()
    tokens_chain.step(2)
    numbers.forward()
    router.forward()
    weights.finish()
    need("tokens", "attend_low", "attend_high")

    block_picks = jnp.concatenate(
        [jnp.broadcast_to(pick, (block, WIDTH)) for pick in picks], axis=0
    )
    own_sets = jnp.concatenate(
        [jnp.broadcast_to(pick, (half, WIDTH)) for pick in picks], axis=0
    )
    attend_low = r.v_attend_low[...].reshape(WIDTH, D)

    def high(p):
        return r.v_attend_high[:, p].reshape(WIDTH, D)

    def project(k, _):
        ctx = place.ctx
        first = jnp.where(ctx == 3, 2, ctx + 1)
        second = jnp.where(ctx == 0, 2, jnp.where(ctx == 1, 0, 1))
        third = jnp.where(ctx < 2, 3, 0)
        which = jnp.where(
            k == 0, ctx, jnp.where(k == 1, first, jnp.where(k == 2, second, third))
        )
        at = pl.ds(pl.multiple_of(which * block, 16), block)
        values = jnp.concatenate([r.tokens_all[i, at, :] for i in range(images)], axis=0)
        normed = normalize(values.astype(F32), gain_one, shift_one)[0].astype(BF16)
        lift = (times_transposed(normed, attend_low) * block_picks).astype(BF16)
        for i in range(images):
            r.lift_all[i, at, :] = lift[i * block : (i + 1) * block]
        for p in range(3):
            made = (matmul(normed, r.weights_all[p]) + matmul(lift, high(p))).astype(BF16)
            for i in range(images):
                r.joined[p, i, at, :] = made[i * block : (i + 1) * block]
        return 0

    def project_blocks(low, up):
        lax.fori_loop(low, up, project, 0)

    project_blocks(0, 1)
    tokens_chain.step(3)
    tokens_chain.landed(1)
    mixing.forward()
    project_blocks(1, 2)
    cotangents.start()
    tokens_chain.landed(2)
    project_blocks(2, 3)
    tokens_chain.landed(3)
    project_blocks(3, 4)

    def open_keys(i):
        return (
            jnp.concatenate(
                [
                    r.ctx_ints[n, i, LIVE_ROW : LIVE_ROW + 1, :]
                    for n in range(place.ctx_size)
                ],
                axis=1,
            )
            > 0
        )

    def rows_slot(i, dp, tp):
        at = pl.multiple_of(tp * half, 16)
        return r.rows_all.at[dp * images + i, pl.ds(at, half), :]

    expert_rows = []
    for i in range(images):
        r.keys_open[i : i + 1, :] = open_keys(i).astype(F32)
        token_rows = r.tokens_all[i, own, :].astype(F32)
        r.own_in[i] = normalize(token_rows, gain_one, shift_one)[0].astype(BF16)
        keys_open = r.keys_open[i : i + 1, :] > 0
        part = slice(i * half, (i + 1) * half)
        logs = []
        for j in range(HEADS // 2):
            at = slice(j * 2 * HD, (j + 1) * 2 * HD)
            q = stack_pair(r.joined[0, i, own, at], masks, scale)
            scores = times_transposed(q, r.joined[1, i, :, at])
            scores = jnp.where(keys_open, scores, MASKED)
            top = jnp.max(scores, axis=-1, keepdims=True)
            powers = jnp.exp(scores - top)
            total = jnp.sum(powers, axis=-1, keepdims=True)
            weights_att = (powers * (1.0 / total)).astype(BF16)
            mixed = join_pair(matmul(weights_att, r.joined[2, i, :, at]), masks)
            r.head_mix[part, at] = mixed.astype(BF16)
            log = jnp.maximum(top + jnp.log(total), -1e29)
            logs += [log[:half], log[half:]]
        r.logs[part, :] = put_lanes(logs, 128)
        if i == 0:
            mixing.diagonal()
            mixing.finish()
            need("mixing_low", "mixing_high")
            mixing_low = r.v_mixing_low[...].reshape(WIDTH, D)
            mixing_high = r.v_mixing_high[...].reshape(WIDTH, D)
        mix = r.head_mix[part, :]
        lift = (times_transposed(mix, mixing_low) * picks[i]).astype(BF16)
        r.mixing_lift[part, :] = lift
        hidden = token_rows + times_transposed(mix, r.mixing_all[...]) + matmul(lift, mixing_high)
        r.hidden[part, :] = hidden
        r.expert_in[i] = normalize(hidden, gain_two, shift_two)[0].astype(BF16)
        expert_rows.append(
            Spread(place, wire, r.expert_in.at[i], functools.partial(rows_slot, i), direct=True)
        )
        expert_rows[i].start()

    slots = experts * SLOTS
    cotangents.forward()
    cotangents.finish()
    numbers.finish()
    router.finish()
    need("router_low", "router_high")
    router_low = r.v_router_low[...].reshape(WIDTH, D)
    router_high = r.v_router_high[...].reshape(WIDTH, EXPERTS)
    r.router_t[...] = jnp.concatenate([r.router_all[n] for n in range(place.dp_size)], axis=1)

    def targets(given, k):
        route, slot = given[k : k + 1, :], given[TOP + k : TOP + k + 1, :]
        local = route - owned
        here = (local >= 0) & (local < experts) & (slot < CAP)
        return jnp.where(here, local * SLOTS + slot, -1)

    def fill_slots(i, target, values):
        at = pl.ds(pl.multiple_of(i * SLOTS, SLOTS), SLOTS)
        for n in range(experts):
            target[n, at, :] = values[n * SLOTS : (n + 1) * SLOTS]

    def make_table(i, _):
        given = r.ints_all[i]
        slot = lax.broadcasted_iota(jnp.int32, (slots, block), 0)
        hot = jnp.zeros((slots, block), F32)
        for k in range(TOP):
            hot = jnp.where(slot == targets(given, k), 1.0, hot)
        hot = hot.astype(BF16)
        r.table[i] = hot
        fill_slots(i, r.grad_slots, matmul(hot, r.cot_all[i]).astype(BF16))
        return 0

    lax.fori_loop(0, all_images, make_table, 0, unroll=2)
    for spread in expert_rows:
        spread.forward()
    for spread in expert_rows:
        spread.finish()

    def dispatch(i, _):
        values = r.rows_all[i]
        given = r.ints_all[i]
        set_column = lax.div(lax.broadcasted_iota(jnp.int32, (WIDTH, 1), 0), RANK)
        pick = (set_column == given[SET_ROW : SET_ROW + 1, 0:1]).astype(F32)
        lift = (times_transposed(router_low, values) * pick).astype(BF16)
        logits = times_transposed(r.router_t[...], values) + inner_rows(router_high, lift)
        powers = jnp.exp(logits - jnp.max(logits, axis=0, keepdims=True))
        probs = powers / jnp.sum(powers, axis=0, keepdims=True)
        expert = lax.broadcasted_iota(jnp.int32, (EXPERTS, block), 0)
        slot = lax.broadcasted_iota(jnp.int32, (slots, block), 0)
        gated = jnp.zeros((slots, block), F32)
        for k in range(TOP):
            gate = jnp.sum(
                jnp.where(expert == given[k : k + 1, :], probs, 0.0), axis=0, keepdims=True
            )
            gated = jnp.where(slot == targets(given, k), gate, gated)
        column = jnp.broadcast_to(jnp.sum(gated, axis=1, keepdims=True), (slots, 128))
        fill_slots(i, r.gates, column)
        fill_slots(i, r.rows_in, matmul(r.table[i], values).astype(BF16))
        lane = lax.div(lax.broadcasted_iota(jnp.int32, (SLOTS, WIDTH), 1), RANK)
        at = pl.ds(pl.multiple_of(i * SLOTS, SLOTS), SLOTS)
        r.slot_sets[at, :] = (lane == given[SET_ROW : SET_ROW + 1, 0:1]).astype(F32)
        return 0

    lax.fori_loop(0, all_images, dispatch, 0, unroll=4)

    chunks = [
        (
            r.first.at[e], r.first_got.at[e], r.first_final.at[e],
            functools.partial(lambda e, dp, tp: r.first_all.at[dp, tp, e], e),
        )
        for e in range(experts)
    ]
    chunks += [
        (r.second_sum, r.second_in, r.second_final, lambda dp, tp: r.second_all.at[dp, tp]),
        (r.early_sum, r.early_in, r.early_final, lambda dp, tp: r.early_all.at[dp, tp]),
        (r.late_sum, r.late_in, r.late_final, lambda dp, tp: r.late_all.at[dp, tp]),
    ]
    second_at, early_at, late_at = experts, experts + 1, experts + 2
    inner, outer = place.inner, 1 - place.inner
    to_partner, to_far = {"ctx": place.partner}, {"ctx": place.far_mid}
    flows, spreads = [], []
    for mine, got, final, slot in chunks:
        flows.append(
            dict(
                beside=wire.copy(mine.at[inner], got.at[0], to_partner),
                across=wire.copy(mine.at[outer], got.at[1], to_far),
                beyond=wire.copy(mine.at[outer], got.at[2], to_far),
                back=wire.copy(final.at[inner], final.at[inner], to_partner),
                share=wire.copy(final.at[inner], final.at[inner], to_far),
                away=wire.copy(final.at[inner], final.at[inner], {"ctx": place.far_end}),
            )
        )
        k = len(spreads)
        spreads.append(
            Spread(place, wire, final, slot, direct=k >= early_at, turn=k == second_at)
        )

    def offer(k):
        @pl.when(place.is_end)
        def _():
            flows[k]["beyond"].start()
            flows[k]["beside"].start()

        @pl.when(place.is_mid)
        def _():
            flows[k]["across"].start()

    def total_half(k):
        mine, got, final, slot = chunks[k]

        @pl.when(place.is_mid)
        def _():
            for name in ("beside", "across", "beyond"):
                flows[k][name].wait_recv()
            final[inner] = add_rounded(mine[inner], got[0], got[1], got[2])
            for name in ("away", "share", "back"):
                flows[k][name].start()

    def settle(k):
        @pl.when(place.is_mid)
        def _():
            flows[k]["share"].wait_recv()

        @pl.when(place.is_end)
        def _():
            flows[k]["back"].wait_recv()
            flows[k]["away"].wait_recv()

        spreads[k].start()

    stages = (
        total_half, settle, lambda k: spreads[k].forward(), lambda k: spreads[k].diagonal(),
    )
    reached = [0] * len(chunks)

    def go(k, stage):
        while reached[k] < stage:
            stages[reached[k]](k)
            reached[k] += 1

    def at_point(point):
        for chunk, stage in SCHEDULE[point]:
            if len(chunks) + chunk >= 0:
                go(len(chunks) + chunk, stage)

    def run_expert(e):
        need(("a_first", e), ("b_first", e), ("up", e))
        need(("a_second", e), ("b_second", e), ("down", e))
        a_first, b_first = r.v_first_a[e].reshape(WIDTH, D), r.v_first_b[e].reshape(WIDTH, -1)
        a_second = r.v_second_a[e].reshape(WIDTH, -1)
        b_second = r.v_second_b[e].reshape(WIDTH, D)
        sums = None
        size = min(EXPERT_ROWS, all_images * SLOTS)
        for c in range(all_images * SLOTS // size):
            at = slice(c * size, (c + 1) * size)
            rows = r.rows_in[e, at]
            grads = r.grad_slots[e, at].astype(F32)
            gate = r.gates[e, at][:, 0:1]
            sets = r.slot_sets[at]
            lifted = (times_transposed(rows, a_first) * sets).astype(BF16)
            before = matmul(rows, r.v_up[e]) + matmul(lifted, b_first)
            phi = 0.5 * (1.0 + lax.erf(before * SQRT_HALF))
            active = (before * phi).astype(BF16)
            slope = phi + before * (INV_ROOT_TWO_PI * jnp.exp(-0.5 * before * before))
            lowered = (times_transposed(active, a_second) * sets).astype(BF16)
            out = matmul(active, r.v_down[e]) + matmul(lowered, b_second)
            grad_out = (grads * gate).astype(BF16)
            grad_lowered = (times_transposed(grad_out, b_second) * sets).astype(BF16)
            grad_active = times_transposed(grad_out, r.v_down[e]) + matmul(grad_lowered, a_second)
            grad_before = (grad_active * slope).astype(BF16)
            grad_lifted = (times_transposed(grad_before, b_first) * sets).astype(BF16)
            grad_rows = times_transposed(grad_before, r.v_up[e]) + matmul(grad_lifted, a_first)
            made = [
                inner_rows(lifted, grad_before),
                inner_rows(grad_lowered, active),
                inner_rows(grad_lifted, rows),
                inner_rows(lowered, grad_out),
            ]
            sums = made if sums is None else [a + b for a, b in zip(sums, made)]
            lane = lax.broadcasted_iota(jnp.int32, (size, 128), 1)
            gate_grads = jnp.sum(out * grads, axis=1, keepdims=True)
            gate_grads = jnp.where(lane == owned + e, gate_grads, 0.0).astype(BF16)
            some = slice(c * size // SLOTS, (c + 1) * size // SLOTS)
            to = slice(e * SLOTS, (e + 1) * SLOTS)
            number = size // SLOTS
            r.payload[some, to, 0:D] = grad_rows.astype(BF16).reshape(number, SLOTS, D)
            r.payload[some, to, D:CRITICAL] = gate_grads.reshape(number, SLOTS, 128)
            r.payload[some, to, CRITICAL:] = (out * gate).astype(BF16).reshape(number, SLOTS, D)
        r.first[e, 0] = sums[0].astype(BF16)
        r.first[e, 1] = sums[1].astype(BF16)
        share = D // place.tp_size
        for number in range(2):
            for t in range(place.tp_size):
                r.second[t, number, e] = sums[2 + number][:, t * share : (t + 1) * share].astype(
                    BF16
                )

    for e in range(experts):
        run_expert(e)
        offer(e)
        if e == experts - 2:
            at_point(0)
    at_point(1)

    second_swap = wire.copy(
        r.second.at[place.other_tp], r.second_got, {"tp": place.other_tp}
    )
    second_swap.start()
    first_lanes, other_lanes = slice(0, CRITICAL), slice(CRITICAL, CRITICAL + D)
    swaps = [
        wire.copy(
            r.partial.at[1 - place.core, :, :, :, at],
            r.from_sibling.at[:, :, :, at],
            {"dp": place.sibling},
        )
        for at in (first_lanes, other_lanes)
    ]

    def combine(core, at):
        def run(chip, _):
            for n in range(images):
                i = (chip * 2 + core) * images + n
                made = inner_rows(r.table[i], r.payload[i, :, at]).astype(BF16)
                for t in range(place.tp_size):
                    r.partial[core, chip, t, n * half : (n + 1) * half, at] = made[
                        t * half : (t + 1) * half
                    ]
            return 0

        lax.fori_loop(0, place.chips, run, 0, unroll=2)

    def send_back(at):
        copies = []
        for i, j in place.offsets() + [(0, 0)]:
            dp, tp = place.ahead(i, j)
            chip = lax.div(dp, 2)
            index = i * place.tp_size + j
            both = add_rounded(
                r.partial[place.core, chip, tp, :, at], r.from_sibling[chip, tp, :, at]
            )
            if index:
                r.from_sibling[chip, tp, :, at] = both
                copy = wire.copy(
                    r.from_sibling.at[chip, tp, :, at],
                    r.received.at[index, :, at],
                    {"dp": dp, "tp": tp},
                )
                copy.start()
                copies.append(copy)
            else:
                r.received[0, :, at] = both
        return copies

    combine(1 - place.core, first_lanes)
    swaps[0].start()
    combine(place.core, first_lanes)
    at_point(2)
    swaps[0].wait_recv()
    returns = [send_back(first_lanes)]
    combine(1 - place.core, other_lanes)
    swaps[1].start()
    combine(place.core, other_lanes)
    second_swap.wait()
    r.second_sum[...] = add_rounded(r.second[place.tp], r.second_got[...])
    offer(second_at)
    swaps[1].wait_recv()
    returns.append(send_back(other_lanes))
    late_sends = swaps + returns[0] + returns[1]
    at_point(3)
    for copy in returns[0]:
        copy.wait_recv()

    def live_column(i):
        lane = lax.broadcasted_iota(jnp.int32, (half, block), 1)
        row = lax.broadcasted_iota(jnp.int32, (half, block), 0) + place.tp * half
        live = r.ints[i, LIVE_ROW : LIVE_ROW + 1, :].astype(F32)
        return jnp.sum(jnp.where(lane == row, live, 0.0), axis=1, keepdims=True)

    lives = [live_column(i) for i in range(images)]
    total = r.received[0, :, :CRITICAL].astype(F32)
    for k in range(1, r.received.shape[0]):
        total = total + r.received[k, :, :CRITICAL].astype(F32)
    hidden = r.hidden[...]
    grad_probs = total[:, D : D + EXPERTS]
    grad_output = jnp.concatenate(
        [
            r.cot_all[place.dp * images + i, pl.ds(start, half), :].astype(F32) * lives[i]
            for i in range(images)
        ],
        axis=0,
    )
    rows = r.expert_in[...].reshape(count, D)
    router_lift = (times_transposed(rows, router_low) * own_sets).astype(BF16)
    logits = times_transposed(rows, r.router_t[...]) + matmul(router_lift, router_high)
    powers = jnp.exp(logits - jnp.max(logits, axis=-1, keepdims=True))
    gate_probs = powers / jnp.sum(powers, axis=-1, keepdims=True)
    grad_logits = (
        gate_probs * (grad_probs - jnp.sum(grad_probs * gate_probs, axis=-1, keepdims=True))
    ).astype(BF16)
    grad_router_lift = (times_transposed(grad_logits, router_high) * own_sets).astype(BF16)
    grad_expert_in = (
        total[:, :D] + matmul(grad_logits, r.router_t[...]) + matmul(grad_router_lift, router_low)
    )
    _, unit, factor = normalize(hidden, gain_two, shift_two)
    grad_rows = grad_output + normalize_back(grad_expert_in, unit, factor, gain_two)
    r.grad_hidden[...] = grad_rows
    grad_attended = grad_rows.astype(BF16)
    grad_mixing_lift = (times_transposed(grad_attended, mixing_high) * own_sets).astype(BF16)
    grad_heads = (
        matmul(grad_attended, r.mixing_all[...]) + matmul(grad_mixing_lift, mixing_low)
    ).astype(BF16)
    r.heads[...] = grad_heads.reshape(images, half, D)
    mix = r.head_mix[...]
    lane = lax.broadcasted_iota(jnp.int32, (D, 128), 1)
    head = lax.div(lax.broadcasted_iota(jnp.int32, (D, 128), 0), HD)
    ones = (lane == head).astype(F32).astype(BF16)
    delta_rows = split_sum(grad_heads.astype(F32) * mix.astype(F32), ones)
    r.delta[...] = delta_rows
    log_rows = r.logs[...]
    for i in range(images):
        part = slice(i * half, (i + 1) * half)
        pad = jnp.zeros((128 - half, 128), F32)
        turned = [
            jnp.concatenate([v[part], pad], axis=0).T[:HEADS] for v in (log_rows, delta_rows)
        ]
        row = 0
        for rest, number in zip(turned, (3, 2)):
            for _ in range(number):
                top = rest.astype(BF16)
                r.stats[i, row : row + HEADS, :] = top
                rest = rest - top.astype(F32)
                row += HEADS

    def heads_slot(i, ctx, tp):
        at = pl.multiple_of((ctx * place.tp_size + tp) * half, 16)
        return r.heads_all.at[i, pl.ds(at, half), :]

    chain = Chain(
        place, wire, [r.heads.at[i] for i in range(images)] + [r.stats],
        [functools.partial(heads_slot, i) for i in range(images)]
        + [lambda ctx, tp: r.stats_all.at[ctx * place.tp_size + tp]],
        [True] * (images + 1), True,
    )
    chain.start()

    def spread_start(values, got):
        rows = got.shape[1]
        copies = []
        for k, (dp, tp) in enumerate(place.peers):
            at = pl.ds(pl.multiple_of((dp * place.tp_size + tp) * rows, 16), rows)
            copy = wire.copy(values.at[at], got.at[k], {"dp": dp, "tp": tp})
            copy.start()
            copies.append(copy)
        return copies

    def spread_end(copies, values, got, total):
        rows = got.shape[1]
        for copy in copies:
            copy.wait()
        added = values[pl.ds(pl.multiple_of(place.me * rows, 16), rows), :].astype(F32)
        for k in range(plane - 1):
            added = added + got[k].astype(F32)
        total[...] = added.astype(BF16).reshape(total.shape)

    def put_tiles(target, products):
        tile = 0
        for product in products:
            for n in range(product.shape[1] // 128):
                target[tile * WIDTH : (tile + 1) * WIDTH, :] = product[
                    :, n * 128 : (n + 1) * 128
                ].astype(BF16)
                tile += 1
        if tile * WIDTH < target.shape[0]:
            target[tile * WIDTH :, :] = jnp.zeros(
                (target.shape[0] - tile * WIDTH, 128), BF16
            )

    wide_logits = jnp.concatenate(
        [grad_logits, jnp.zeros((count, 128 - EXPERTS), BF16)], axis=1
    )
    put_tiles(
        r.early,
        (
            inner_rows(grad_mixing_lift, mix),
            inner_rows(r.mixing_lift[...], grad_attended),
            inner_rows(grad_router_lift, rows),
            inner_rows(router_lift, wide_logits),
        ),
    )
    early_spread = spread_start(r.early, r.early_got)
    at_point(4)
    chain.step(1)
    at_point(5)
    chain.step(2)
    at_point(6)
    chain.step(3)
    spread_end(early_spread, r.early, r.early_got, r.early_sum)
    offer(early_at)
    at_point(7)
    chain.finish_own()
    for s in range(1, chain.steps + 1):
        chain.landed(s)

    def to_other(values, gathered):
        spot = gathered.at[:, pl.ds(start, half), :]
        copies = [wire.copy(values, spot, {"tp": place.other_tp}), wire.near(values, spot)]
        for copy in copies:
            copy.start()
        return copies

    for copy in returns[1]:
        copy.wait_recv()
    total = r.hidden[...]
    for k in range(r.received.shape[0]):
        total = total + r.received[k, :, CRITICAL:].astype(F32)
    r.out_own[...] = total.astype(BF16).reshape(images, half, D)
    layer_out = to_other(r.out_own, r.out_all)

    def heads_back(i, j):
        part = slice(i * half, (i + 1) * half)
        at = slice(j * 2 * HD, (j + 1) * 2 * HD)
        keys_open = r.keys_open[i : i + 1, :] > 0
        own_open = jnp.concatenate([lives[i], lives[i]], axis=0) > 0
        found = jnp.concatenate(
            [r.stats_all[n, i][:, :half].astype(F32) for n in range(r.stats_all.shape[0])], axis=1
        )
        log_t = found[0:HEADS] + found[HEADS : 2 * HEADS] + found[2 * HEADS : 3 * HEADS]
        delta_t = found[3 * HEADS : 4 * HEADS] + found[4 * HEADS :]
        q_all, k_all, v_all = (r.joined[p, i, :, at] for p in range(3))
        g_all = r.heads_all[i, :, at]

        def column(values):
            return jnp.concatenate(
                [values[:, 2 * j : 2 * j + 1], values[:, 2 * j + 1 : 2 * j + 2]], axis=0
            )

        def across(values):
            return jnp.concatenate(
                [
                    jnp.broadcast_to(values[2 * j + n : 2 * j + n + 1, :], (half, values.shape[1]))
                    for n in range(2)
                ],
                axis=0,
            )

        q = stack_pair(r.joined[0, i, own, at], masks, scale)
        g = stack_pair(r.heads[i, :, at], masks)
        scores = jnp.where(keys_open, times_transposed(q, k_all), MASKED)
        probs = jnp.exp(scores - column(r.logs[part]))
        grad_probs_att = times_transposed(g, v_all)
        grad_scores = (probs * (grad_probs_att - column(r.delta[part]))).astype(BF16)
        r.grads[0, part, at] = (join_pair(matmul(grad_scores, k_all), masks) * scale).astype(BF16)
        k = stack_pair(r.joined[1, i, own, at], masks, scale)
        v = stack_pair(r.joined[2, i, own, at], masks)
        scores = jnp.where(own_open, times_transposed(k, q_all), MASKED)
        probs = jnp.exp(scores - across(log_t))
        grad_probs_att = times_transposed(v, g_all)
        grad_scores = (probs * (grad_probs_att - across(delta_t))).astype(BF16)
        r.grads[1, part, at] = (join_pair(matmul(grad_scores, q_all), masks) * scale).astype(BF16)
        r.grads[2, part, at] = join_pair(matmul(probs.astype(BF16), g_all), masks).astype(BF16)

    for i in range(images):
        for j in range(HEADS // 2):
            heads_back(i, j)
            if j % 2:
                at_point(8 + 2 * i + j // 2)
    lift = times_transposed(r.grads[0], high(0))
    into = times_transposed(r.grads[0], r.weights_all[0])
    for p in range(1, 3):
        lift = lift + times_transposed(r.grads[p], high(p))
        into = into + times_transposed(r.grads[p], r.weights_all[p])
    lift = (lift * own_sets).astype(BF16)
    lift_in = jnp.concatenate([r.lift_all[i, own, :] for i in range(images)], axis=0)
    put_tiles(
        r.late,
        [inner_rows(lift_in, r.grads[p]) for p in range(3)]
        + [inner_rows(lift, r.own_in[...].reshape(count, D))],
    )
    late_spread = spread_start(r.late, r.late_got)
    at_point(12)
    into = into + matmul(lift, attend_low)
    flat = jnp.concatenate([r.tokens_all[i, own, :] for i in range(images)], axis=0).astype(F32)
    _, unit, factor = normalize(flat, gain_one, shift_one)
    result = r.grad_hidden[...] + normalize_back(into, unit, factor, gain_one)
    r.grad_own[...] = result.astype(BF16).reshape(images, half, D)
    at_point(13)
    tokens_out = to_other(r.grad_own, r.grad_all)
    spread_end(late_spread, r.late, r.late_got, r.late_sum)
    offer(late_at)
    at_point(14)
    for k in range(len(chunks)):
        go(k, DONE)

    @pl.when(place.is_end)
    def _():
        for flow in flows:
            flow["beyond"].wait_send()
            flow["beside"].wait_send()

    @pl.when(place.is_mid)
    def _():
        for flow in flows:
            for name in ("across", "away", "share", "back"):
                flow[name].wait_send()

    for spread in spreads:
        spread.finish()
    for spread in [weights, mixing, numbers, router, cotangents] + expert_rows + spreads:
        spread.drain()
    tokens_chain.drain()
    chain.drain()
    for copy in late_sends:
        copy.wait_send()
    for copy in layer_out + tokens_out:
        copy.wait()
    assert not pending


def run_layer(sizes, **inputs):
    dp, ctx, tp = sizes
    assert ctx == 4 and tp == 2
    plane, chips = dp * tp, dp // 2
    images, block = inputs["tokens"].shape[:2]
    assert images == 2
    half = block // tp
    count, seq, all_images = images * half, ctx * block, dp * images
    experts, _, hidden = inputs["up_weight"].shape
    rows, lanes = inputs["mixing"].shape
    slots = experts * SLOTS
    sent = CRITICAL + D
    early_rows = small_rows(3 * (D // 128) + 1, plane)
    late_rows = small_rows(4 * (D // 128), plane)
    second = (2, experts, WIDTH, D // tp)
    full = dict(
        first=(experts, 2, WIDTH, hidden),
        second=second,
        early=(2, early_rows // 2, 128),
        late=(2, late_rows // 2, 128),
    )
    cut = {name: shape[1:] for name, shape in full.items()}
    cut["first"] = (experts, WIDTH, hidden)
    outputs = {name + "_all": (dp, tp) + shape for name, shape in full.items()}
    outputs.update(out_all=(images, block, D), grad_all=(images, block, D))
    narrow = dict(
        tokens_all=(images, seq, D),
        weights_all=(3, dp * rows, tp * lanes),
        mixing_all=(dp * rows, tp * lanes),
        router_all=(dp,) + inputs["router"].shape,
        router_t=(EXPERTS, D),
        cot_all=(all_images, block, D),
        rows_all=(all_images, block, D),
        v_attend_low=(SETS, RANK, D),
        v_attend_high=(SETS, 3, RANK, D),
        v_mixing_low=(SETS, RANK, D),
        v_mixing_high=(SETS, RANK, D),
        v_router_low=(SETS, RANK, D),
        v_router_high=(SETS, RANK, EXPERTS),
        v_first_a=(experts, SETS, RANK, D),
        v_first_b=(experts, SETS, RANK, hidden),
        v_second_a=(experts, SETS, RANK, hidden),
        v_second_b=(experts, SETS, RANK, D),
        v_up=(experts, D, hidden),
        v_down=(experts, hidden, D),
        lift_all=(images, seq, WIDTH),
        joined=(3, images, seq, D),
        own_in=(images, half, D),
        head_mix=(count, D),
        mixing_lift=(count, WIDTH),
        expert_in=(images, half, D),
        table=(all_images, slots, block),
        grad_slots=(experts, all_images * SLOTS, D),
        rows_in=(experts, all_images * SLOTS, D),
        payload=(all_images, slots, sent),
        partial=(2, chips, tp, count, sent),
        from_sibling=(chips, tp, count, sent),
        received=(chips * tp, count, sent),
        first=full["first"],
        second=(tp,) + second,
        second_got=second,
        second_sum=second,
        early=(plane * early_rows, 128),
        late=(plane * late_rows, 128),
        early_got=(plane - 1, early_rows, 128),
        late_got=(plane - 1, late_rows, 128),
        early_sum=full["early"],
        late_sum=full["late"],
        heads=(images, half, D),
        stats=(images, 5 * HEADS, 128),
        heads_all=(images, seq, D),
        stats_all=(ctx * tp, images, 5 * HEADS, 128),
        grads=(3, count, D),
        out_own=(images, half, D),
        grad_own=(images, half, D),
    )
    for name in full:
        narrow[name + "_final"] = full[name]
        narrow[name + "_in"] = (3,) + cut[name]
    narrow["first_got"] = (experts, 3, WIDTH, hidden)
    del narrow["first_in"]
    wide = dict(
        logs=(count, 128),
        delta=(count, 128),
        hidden=(count, D),
        grad_hidden=(count, D),
        gates=(experts, all_images * SLOTS, 128),
        slot_sets=(all_images * SLOTS, WIDTH),
        keys_open=(images, seq),
    )
    integers = dict(
        ints=(images, 8, block),
        ints_all=(all_images, 8, block),
        ctx_ints=(ctx, images, 8, block),
    )
    scratch = {}
    for shapes, dtype in ((narrow, BF16), (wide, F32), (integers, jnp.int32)):
        for name, shape in shapes.items():
            scratch[name] = pltpu.VMEM(shape, dtype)
    chunks = experts + 3
    remote = (
        2 * Chain.remote(ctx, images + 1)
        + (2 + images + chunks) * Spread.remote(sizes)
        + 3 * Spread.remote(sizes, False)
        + 6 * chunks
        + 3
        + 2 * (chips * tp - 1)
        + 2 * (plane - 1)
        + 2
    )
    scratch["send"] = pltpu.SemaphoreType.DMA((remote,))
    scratch["recv"] = pltpu.SemaphoreType.DMA((remote,))
    scratch["local"] = pltpu.SemaphoreType.DMA((7 + 6 * experts + 5 + images + chunks + images + 1 + 2,))
    kinds = dict(
        adapter_set=IN_SMEM, image_mask=IN_SMEM, routes_t=IN_VMEM, slots_t=IN_VMEM,
        token_mask=IN_VMEM, first_gain=IN_VMEM, first_shift=IN_VMEM, second_gain=IN_VMEM,
        second_shift=IN_VMEM,
    )
    names = tuple(inputs) + tuple(outputs) + tuple(scratch)
    made = pl.pallas_call(
        functools.partial(layer_kernel, sizes, names),
        out_shape=tuple(jax.ShapeDtypeStruct(shape, BF16) for shape in outputs.values()),
        in_specs=[kinds.get(name, ANY) for name in inputs],
        out_specs=(ANY,) * len(outputs),
        scratch_shapes=tuple(scratch.values()),
        compiler_params=pltpu.CompilerParams(
            collective_id=0, has_side_effects=True, vmem_limit_bytes=62 << 20
        ),
    )(*inputs.values())
    return dict(zip(outputs, made))


def assemble_kernel(
    first, second, early, late, out_in, grad_in,
    up, down_t, narrow_t, narrow, attend_down, attend_up, mixing_down, mixing_up, router_down,
    router_up, out, grad,
):
    lanes, part = first.shape[-1], second.shape[-1]
    for n in range(first.shape[2]):
        for tp in range(first.shape[1]):
            for half, target in ((0, up), (1, down_t)):
                target[:, n, :, tp * lanes : (tp + 1) * lanes] = (
                    first[0, tp, n, half].astype(F32).reshape(SETS, RANK, lanes)
                )
            for half, target in ((0, narrow_t), (1, narrow)):
                target[:, n, :, tp * part : (tp + 1) * part] = (
                    second[0, tp, half, n].astype(F32).reshape(SETS, RANK, part)
                )

    @pl.when(pl.program_id(0) == 0)
    def _():
        def tile(small, k):
            return small[k * WIDTH : (k + 1) * WIDTH, :].astype(F32).reshape(SETS, RANK, 128)

        count = D // 128
        for p in range(3):
            for k in range(count):
                attend_up[:, p, :, k * 128 : (k + 1) * 128] = tile(late, p * count + k)
        for k in range(count):
            attend_down[:, :, k * 128 : (k + 1) * 128] = tile(late, 3 * count + k)
        for p, target in enumerate((mixing_down, mixing_up, router_down)):
            for k in range(count):
                target[:, :, k * 128 : (k + 1) * 128] = tile(early, p * count + k)
        router_up[...] = tile(early, 3 * count)[:, :, :EXPERTS]
        out[...] = out_in[...]
        grad[...] = grad_in[...]


def assemble(first, second, early, late, out, grad):
    dp, tp, experts, _, width, lanes = first.shape
    part = second.shape[-1]
    group = min(experts, ASSEMBLED)
    groups = experts // group

    def split(e):
        return lax.div(e, groups), lax.rem(e, groups)

    def expert_out(size):
        return (
            jax.ShapeDtypeStruct((SETS, EXPERTS, RANK, size), F32),
            pl.BlockSpec((SETS, group, RANK, size), lambda e: (0, e, 0, 0)),
        )

    def whole_out(*shape):
        return (
            jax.ShapeDtypeStruct(shape, F32),
            pl.BlockSpec(shape, lambda e: (0,) * len(shape)),
        )

    outs = (
        [expert_out(FF)] * 2
        + [expert_out(D)] * 2
        + [whole_out(SETS, RANK, D), whole_out(SETS, 3, RANK, D)]
        + [whole_out(SETS, RANK, D)] * 3
        + [whole_out(SETS, RANK, EXPERTS)]
        + [(jax.ShapeDtypeStruct(out.shape, BF16), pl.BlockSpec(out.shape, lambda e: (0, 0, 0)))] * 2
    )
    return pl.pallas_call(
        assemble_kernel,
        grid=(EXPERTS // group,),
        out_shape=[out[0] for out in outs],
        in_specs=[
            pl.BlockSpec(
                (1, tp, group, 2, width, lanes), lambda e: (split(e)[0], 0, split(e)[1], 0, 0, 0)
            ),
            pl.BlockSpec(
                (1, tp, 2, group, width, part), lambda e: (split(e)[0], 0, 0, split(e)[1], 0, 0)
            ),
            pl.BlockSpec(early.shape, lambda e: (0, 0)),
            pl.BlockSpec(late.shape, lambda e: (0, 0)),
            pl.BlockSpec(out.shape, lambda e: (0, 0, 0)),
            pl.BlockSpec(grad.shape, lambda e: (0, 0, 0)),
        ],
        out_specs=[out[1] for out in outs],
        compiler_params=pltpu.CompilerParams(vmem_limit_bytes=60 << 20),
    )(first, second, early, late, out, grad)


def per_device(
    sizes,
    tokens,
    cotangent,
    routes,
    slot_index,
    token_mask,
    image_mask,
    adapter_set,
    first_gain,
    first_shift,
    second_gain,
    second_shift,
    attend_weight,
    mixing_weight,
    router_weight,
    expand_weight,
    shrink_weight,
    attend_down,
    attend_up,
    mixing_down,
    mixing_up,
    router_down,
    router_up,
    expand_down,
    expand_up,
    shrink_down,
    shrink_up,
):
    def flipped(values):
        return jnp.swapaxes(values, -1, -2)

    made = run_layer(
        sizes,
        tokens=tokens,
        cotangent=cotangent,
        weights=jnp.transpose(attend_weight, (1, 0, 2)),
        mixing=mixing_weight,
        router=flipped(router_weight),
        routes_t=flipped(routes),
        slots_t=flipped(slot_index),
        token_mask=token_mask,
        image_mask=image_mask,
        adapter_set=adapter_set,
        first_gain=first_gain.reshape(1, D),
        first_shift=first_shift.reshape(1, D),
        second_gain=second_gain.reshape(1, D),
        second_shift=second_shift.reshape(1, D),
        up_weight=expand_weight,
        down_weight=shrink_weight,
        attend_low=flipped(attend_down),
        attend_high=jnp.transpose(attend_up, (0, 2, 1, 3)),
        mixing_low=flipped(mixing_down),
        mixing_high=mixing_up,
        router_low=flipped(router_down),
        router_high=router_up,
        first_a=flipped(expand_down),
        first_b=expand_up,
        second_a=flipped(shrink_down),
        second_b=shrink_up,
    )
    wide = assemble(
        made["first_all"],
        made["second_all"],
        made["early_all"].reshape(-1, 128),
        made["late_all"].reshape(-1, 128),
        made["out_all"],
        made["grad_all"],
    )
    return (
        wide[10],
        wide[11],
        flipped(wide[4]),
        jnp.transpose(wide[5], (0, 2, 1, 3)),
        flipped(wide[6]),
        wide[7],
        flipped(wide[8]),
        wide[9],
        flipped(wide[2]),
        wide[0],
        flipped(wide[1]),
        wide[3],
    )


def solution(mesh):
    sizes = (mesh.shape["dp"], mesh.shape["ctx"], mesh.shape["tp"])
    tokens_spec = P("dp", "ctx", None)
    in_specs = (
        (tokens_spec,) * 4
        + (P("dp", "ctx"), P("dp"), P("dp"))
        + (P(),) * 4
        + (P("dp", None, "tp"), P("dp", "tp"), P("dp", None))
        + (P("dp", None, "tp"), P("dp", "tp", None))
        + (P(),) * 10
    )
    out_specs = (tokens_spec,) * 2 + (P(),) * 10
    return jax.shard_map(
        functools.partial(per_device, sizes),
        mesh=mesh,
        in_specs=in_specs,
        out_specs=out_specs,
        check_vma=False,
    )
```

```python
import functools
import types

import jax
import jax.numpy as jnp
from jax import lax
from jax.experimental import pallas as pl
from jax.experimental.pallas import tpu as pltpu
from jax.sharding import PartitionSpec as P

D = 512
HEADS = 8
HD = 64
FF = 2048
EXPERTS = 16
TOP = 2
RANK = 16
SETS = 4
CAP = 30
SLOTS = 32
WIDTH = SETS * RANK
LIVE_ROW = 2 * TOP
SET_ROW = LIVE_ROW + 1
CRITICAL = D + 128
EXPERT_ROWS = 256
ASSEMBLED = 4

EPSILON = 1e-06
MASKED = -1e30
SQRT_HALF = 0.7071067811865476
INV_ROOT_TWO_PI = 0.3989422804014327
F32 = jnp.float32
BF16 = jnp.bfloat16
MESH = pl.DeviceIdType.MESH
ANY = pl.BlockSpec(memory_space=pl.ANY)
IN_SMEM = pl.BlockSpec(memory_space=pltpu.SMEM)
IN_VMEM = pl.BlockSpec(memory_space=pltpu.VMEM)


def matmul(left_side, right_side):
    return jnp.dot(left_side, right_side, preferred_element_type=F32)


def inner_rows(left_side, right_side):
    return lax.dot_general(
        left_side, right_side, (((0,), (0,)), ((), ())), preferred_element_type=F32
    )


def times_transposed(left_side, right_side):
    return lax.dot_general(
        left_side, right_side, (((1,), (1,)), ((), ())), preferred_element_type=F32
    )


def normalize(values, gain_row, shift_row):
    centred = values - jnp.mean(values, axis=-1, keepdims=True)
    spread = jnp.mean(centred * centred, axis=-1, keepdims=True)
    factor = lax.rsqrt(spread + EPSILON)
    normed = centred * factor
    return (normed * gain_row + shift_row, normed, factor)


def normalize_back(grad_out, normed, factor, gain_row):
    scaled = grad_out * gain_row
    return factor * (
        scaled
        - jnp.mean(scaled, axis=-1, keepdims=True)
        - normed * jnp.mean(scaled * normed, axis=-1, keepdims=True)
    )


def add_rounded(*parts):
    total = parts[0].astype(F32)
    for part in parts[1:]:
        total = total + part.astype(F32)
    return total.astype(BF16)


def split_sum(values, ones):
    high = values.astype(BF16)
    low = (values - high.astype(F32)).astype(BF16)
    return matmul(high, ones) + matmul(low, ones)


def put_lanes(columns, width):
    lane = lax.broadcasted_iota(jnp.int32, (columns[0].shape[0], width), 1)
    total = jnp.zeros((columns[0].shape[0], width), F32)
    for k, column in enumerate(columns):
        total = jnp.where(lane == k, column, total)
    return total


def half_masks():
    lane = lax.broadcasted_iota(jnp.int32, (1, 2 * HD), 1)
    even = (lane < HD).astype(F32)
    return even, 1.0 - even


def stack_pair(rows, masks, factor=1.0):
    wide = rows.astype(F32) * factor
    return jnp.concatenate([wide * masks[0], wide * masks[1]], axis=0).astype(BF16)


def join_pair(rows, masks):
    half = rows.shape[0] // 2
    return rows[:half] * masks[0] + rows[half:] * masks[1]


SUM, SENT, ONWARD, DONE = range(1, 5)
E0, E1, E2, E3, SECOND, EARLY, LATE = range(-7, 0)
SCHEDULE = (
    (),
    ((E0, SUM),),
    ((E1, SUM),),
    ((E0, SENT), (E2, SUM), (E1, SENT)),
    ((E0, ONWARD), (E3, SUM)),
    ((E2, SENT), (E1, ONWARD)),
    ((E0, DONE), (SECOND, SUM)),
    ((E3, SENT), (E2, ONWARD)),
    ((E1, DONE),),
    ((SECOND, SENT),),
    ((EARLY, SUM), (E3, ONWARD)),
    ((E2, DONE),),
    ((SECOND, ONWARD),),
    ((EARLY, SENT),),
    (
        (LATE, SUM), (E3, DONE), (EARLY, ONWARD), (LATE, SENT), (SECOND, DONE), (EARLY, DONE),
        (LATE, ONWARD), (LATE, DONE),
    ),
)


def small_rows(tiles, plane):
    return -(-tiles * WIDTH // (plane * 16)) * 16


class Wire:
    def __init__(self, send, recv, local):
        self.send, self.recv, self.local = send, recv, local
        self.used = self.used_local = 0

    def copy(self, src, dst, device):
        k = self.used
        self.used += 1
        assert k < self.send.shape[0]
        return pltpu.make_async_remote_copy(
            src_ref=src,
            dst_ref=dst,
            send_sem=self.send.at[k],
            recv_sem=self.recv.at[k],
            device_id=device,
            device_id_type=MESH,
        )

    def near(self, src, dst):
        k = self.used_local
        self.used_local += 1
        assert k < self.local.shape[0]
        return pltpu.make_async_copy(src, dst, self.local.at[k])


class Place:
    def __init__(self, sizes):
        self.dp_size, self.ctx_size, self.tp_size = sizes
        self.chips = self.dp_size // 2
        self.plane = self.dp_size * self.tp_size
        self.dp = lax.axis_index("dp")
        self.ctx = lax.axis_index("ctx")
        self.tp = lax.axis_index("tp")
        self.chip = lax.div(self.dp, 2)
        self.core = lax.rem(self.dp, 2)
        self.sibling = self.chip * 2 + (1 - self.core)
        self.other_tp = lax.rem(self.tp + 1, 2)
        self.me = self.dp * self.tp_size + self.tp
        self.is_mid = jnp.logical_and(self.ctx >= 1, self.ctx <= 2)
        self.is_end = jnp.logical_not(self.is_mid)
        self.inner = lax.div(self.ctx, 2)
        self.partner = jnp.where(self.is_mid, self.inner * 3, 1 + self.inner)
        self.far_mid = 2 - self.inner
        self.far_end = 3 - 3 * self.inner
        self.peers = []
        for k in range(1, self.plane):
            peer = lax.rem(self.me + k, self.plane)
            self.peers.append((lax.div(peer, self.tp_size), lax.rem(peer, self.tp_size)))

    def ahead(self, i, j):
        return (
            lax.rem(self.chip + i, self.chips) * 2 + self.core,
            lax.rem(self.tp + j, self.tp_size),
        )

    def behind(self, i, j):
        return self.ahead(self.chips - i, self.tp_size - j)

    def offsets(self, over_tp=True):
        return [
            (i, j)
            for i in range(self.chips)
            for j in range(self.tp_size if over_tp else 1)
            if i or j
        ]

    def greet(self):
        barrier = pltpu.get_barrier_semaphore()
        for dp, tp in self.peers:
            pl.semaphore_signal(
                barrier, inc=1, device_id={"dp": dp, "tp": tp}, device_id_type=MESH
            )
        for ctx in (self.partner, self.far_mid):
            pl.semaphore_signal(barrier, inc=1, device_id={"ctx": ctx}, device_id_type=MESH)

        @pl.when(self.is_mid)
        def _():
            pl.semaphore_signal(
                barrier, inc=1, device_id={"ctx": self.far_end}, device_id_type=MESH
            )

    def met(self):
        barrier = pltpu.get_barrier_semaphore()
        pl.semaphore_wait(barrier, self.plane + 1 + jnp.where(self.is_mid, 1, 0))


class Spread:
    def __init__(
        self, place, wire, source, slot, over_tp=True, direct=False, near=True, turn=False
    ):
        self.turn = turn
        self.place, self.wire, self.source, self.slot = place, wire, source, slot
        self.over_tp = over_tp
        self.relay = over_tp and not direct and place.chips == 2 and place.tp_size == 2
        self.near = near
        self.flights, self.across, self.beside, self.here = [], None, [], None

    def to_sibling(self, source, spot):
        copy = self.wire.copy(source, spot, {"dp": self.place.sibling})
        copy.start()
        self.beside.append(copy)

    def start(self):
        place = self.place
        spot = self.slot(place.dp, place.tp)
        for i, j in place.offsets(self.over_tp):
            if self.relay and i and j:
                continue
            dp, tp = place.ahead(i, j)
            copy = self.wire.copy(self.source, spot, {"dp": dp, "tp": tp})
            copy.start()
            self.flights.append((copy, i, j))
        self.to_sibling(self.source, spot)
        if self.near:
            self.here = self.wire.near(self.source, spot)
            self.here.start()

    def forward(self):
        for copy, i, j in sorted(self.flights, key=lambda f: f[1]):
            copy.wait_recv()
            got = self.slot(*self.place.behind(i, j))
            if self.relay and (i if self.turn else j):
                dp, tp = self.place.ahead(0, 1) if self.turn else self.place.ahead(1, 0)
                self.across = self.wire.copy(got, got, {"dp": dp, "tp": tp})
                self.across.start()
            self.to_sibling(got, got)

    def diagonal(self):
        if self.relay:
            self.across.wait_recv()
            got = self.slot(*self.place.behind(1, 1))
            self.to_sibling(got, got)

    def finish(self):
        for copy in self.beside:
            copy.wait_recv()
        if self.near:
            self.here.wait()

    def drain(self):
        for copy, _, _ in self.flights:
            copy.wait_send()
        if self.relay:
            self.across.wait_send()
        for copy in self.beside:
            copy.wait_send()

    @staticmethod
    def remote(sizes, over_tp=True):
        return 2 * (sizes[0] // 2 * (sizes[2] if over_tp else 1) - 1) + 1


class Chain:
    def __init__(self, place, wire, sources, slots, over, with_own):
        self.place, n = place, place.ctx_size
        self.steps = n - 1
        to_tp = {"tp": place.other_tp}
        self.right, self.left, self.over_right, self.over_left = {}, {}, {}, {}
        self.own, self.here = [], []
        for source, slot in zip(sources, slots):
            spot = slot(place.ctx, place.tp)
            if with_own:
                self.own.append(wire.copy(source, spot, to_tp))
                self.here.append(wire.near(source, spot))
        for s in range(1, n):
            back = [slot(jnp.maximum(place.ctx - (s - 1), 0), place.tp) for slot in slots]
            ahead = [slot(jnp.minimum(place.ctx + (s - 1), n - 1), place.tp) for slot in slots]
            got_right = [slot(jnp.maximum(place.ctx - s, 0), place.tp) for slot in slots]
            got_left = [slot(jnp.minimum(place.ctx + s, n - 1), place.tp) for slot in slots]
            to_right = {"ctx": jnp.minimum(place.ctx + 1, n - 1)}
            to_left = {"ctx": jnp.maximum(place.ctx - 1, 0)}
            self.right[s] = [
                wire.copy(a if s == 1 else b, b, to_right) for a, b in zip(sources, back)
            ]
            self.left[s] = [
                wire.copy(a if s == 1 else b, b, to_left) for a, b in zip(sources, ahead)
            ]
            self.over_right[s] = {
                k: wire.copy(b, b, to_tp) for k, b in enumerate(got_right) if over[k]
            }
            self.over_left[s] = {
                k: wire.copy(b, b, to_tp) for k, b in enumerate(got_left) if over[k]
            }

    def sends_right(self, s):
        return jnp.logical_and(self.place.ctx >= s - 1, self.place.ctx < self.steps)

    def sends_left(self, s):
        return jnp.logical_and(self.place.ctx <= self.steps + 1 - s, self.place.ctx > 0)

    def gets_right(self, s):
        return self.place.ctx >= s

    def gets_left(self, s):
        return self.place.ctx <= self.steps - s

    @staticmethod
    def all_of(copies, verb):
        for copy in copies:
            getattr(copy, verb)()

    def start(self):
        pl.when(self.sends_right(1))(lambda: self.all_of(self.right[1], "start"))
        pl.when(self.sends_left(1))(lambda: self.all_of(self.left[1], "start"))
        self.all_of(self.own + self.here, "start")

    def step(self, s):
        def passed(got, over, sends):
            def run():
                for k, copy in enumerate(got[s]):
                    copy.wait_recv()
                    if s < self.steps:
                        pl.when(sends(s + 1))(got[s + 1][k].start)
                    if k in over[s]:
                        over[s][k].start()

            return run

        pl.when(self.gets_right(s))(passed(self.right, self.over_right, self.sends_right))
        pl.when(self.gets_left(s))(passed(self.left, self.over_left, self.sends_left))

    def landed(self, s):
        pl.when(self.gets_right(s))(lambda: self.all_of(self.over_right[s].values(), "wait_recv"))
        pl.when(self.gets_left(s))(lambda: self.all_of(self.over_left[s].values(), "wait_recv"))

    def finish_own(self):
        self.all_of(self.own, "wait_recv")
        self.all_of(self.here, "wait")

    def drain(self):
        self.all_of(self.own, "wait_send")
        for s in range(1, self.steps + 1):
            pl.when(self.gets_right(s))(lambda: self.all_of(self.over_right[s].values(), "wait_send"))
            pl.when(self.gets_left(s))(lambda: self.all_of(self.over_left[s].values(), "wait_send"))
            pl.when(self.sends_right(s))(lambda: self.all_of(self.right[s], "wait_send"))
            pl.when(self.sends_left(s))(lambda: self.all_of(self.left[s], "wait_send"))

    @staticmethod
    def remote(n, arrays):
        return arrays * (1 + 4 * (n - 1))


def layer_kernel(sizes, names, *refs):
    r = types.SimpleNamespace(**dict(zip(names, refs)))
    place = Place(sizes)
    wire = Wire(r.send, r.recv, r.local)
    plane = place.plane
    images, block = r.tokens.shape[:2]
    half = block // place.tp_size
    count = images * half
    seq = place.ctx_size * block
    experts, _, hidden_units = r.up_weight.shape
    all_images = place.dp_size * images
    owned = place.dp * experts
    start = pl.multiple_of(place.tp * half, 16)
    own_start = pl.multiple_of(place.ctx * block + place.tp * half, 16)
    own = pl.ds(own_start, half)
    masks = half_masks()
    scale = HD**-0.5

    pending = {}

    def load(name, source, target):
        pending[name] = wire.near(source, target)
        pending[name].start()

    def need(*wanted):
        for name in wanted:
            if name in pending:
                pending.pop(name).wait()

    place.greet()
    whole = pl.ds(pl.multiple_of(place.ctx * block, 16), block)
    load("tokens", r.tokens, r.tokens_all.at[:, whole, :])
    for name in (
        "attend_low", "attend_high", "mixing_low", "mixing_high", "router_low", "router_high",
    ):
        load(name, getattr(r, name), getattr(r, "v_" + name))
    r.ints[:, 0:TOP, :] = r.routes_t[...]
    r.ints[:, TOP : 2 * TOP, :] = r.slots_t[...]
    lane_set = lax.div(lax.broadcasted_iota(jnp.int32, (1, WIDTH), 1), RANK)
    picks = []
    for i in range(images):
        r.ints[i, LIVE_ROW : LIVE_ROW + 1, :] = r.token_mask[i : i + 1, :] * r.image_mask[i]
        r.ints[i, SET_ROW:, :] = jnp.full((8 - SET_ROW, block), r.adapter_set[i], jnp.int32)
        picks.append((lane_set == r.adapter_set[i]).astype(F32))
    gain_one, shift_one = r.first_gain[...], r.first_shift[...]
    gain_two, shift_two = r.second_gain[...], r.second_shift[...]

    place.met()

    rows, lanes = r.mixing.shape

    def at_rows(dp):
        return pl.ds(pl.multiple_of(dp * rows, 16), rows)

    def at_lanes(tp):
        return pl.ds(pl.multiple_of(tp * lanes, 128), lanes)

    def token_slot(i, ctx, tp):
        at = pl.multiple_of(ctx * block + tp * half, 16)
        return r.tokens_all.at[i, pl.ds(at, half), :]

    tokens_chain = Chain(
        place, wire,
        [r.tokens.at[i, pl.ds(start, half), :] for i in range(images)] + [r.ints],
        [functools.partial(token_slot, i) for i in range(images)]
        + [lambda ctx, tp: r.ctx_ints.at[ctx]],
        [True] * images + [False], False,
    )
    weights = Spread(
        place, wire, r.weights, lambda dp, tp: r.weights_all.at[:, at_rows(dp), at_lanes(tp)]
    )
    mixing = Spread(
        place, wire, r.mixing, lambda dp, tp: r.mixing_all.at[at_rows(dp), at_lanes(tp)]
    )
    numbers = Spread(
        place, wire, r.ints, lambda dp, tp: r.ints_all.at[pl.ds(dp * 2, 2)], over_tp=False
    )
    router = Spread(place, wire, r.router, lambda dp, tp: r.router_all.at[dp], over_tp=False)
    cotangents = Spread(
        place, wire, r.cotangent, lambda dp, tp: r.cot_all.at[pl.ds(dp * 2, 2)], over_tp=False
    )
    r.ctx_ints[place.ctx] = r.ints[...]
    tokens_chain.start()
    weights.start()
    numbers.start()
    router.start()
    mixing.start()
    wide = pl.ds(pl.multiple_of(place.tp * hidden_units, 128), hidden_units)
    for e in range(experts):
        load(("a_first", e), r.first_a.at[:, owned + e], r.v_first_a.at[e])
        load(("b_first", e), r.first_b.at[:, owned + e, :, wide], r.v_first_b.at[e])
        load(("up", e), r.up_weight.at[e], r.v_up.at[e])
        load(("a_second", e), r.second_a.at[:, owned + e, :, wide], r.v_second_a.at[e])
        load(("b_second", e), r.second_b.at[:, owned + e], r.v_second_b.at[e])
        load(("down", e), r.down_weight.at[e], r.v_down.at[e])
    weights.forward()
    tokens_chain.step(1)
    weights.diagonal()
    tokens_chain.step(2)
    numbers.forward()
    router.forward()
    weights.finish()
    need("tokens", "attend_low", "attend_high")

    block_picks = jnp.concatenate(
        [jnp.broadcast_to(pick, (block, WIDTH)) for pick in picks], axis=0
    )
    own_sets = jnp.concatenate(
        [jnp.broadcast_to(pick, (half, WIDTH)) for pick in picks], axis=0
    )
    attend_low = r.v_attend_low[...].reshape(WIDTH, D)

    def high(p):
        return r.v_attend_high[:, p].reshape(WIDTH, D)

    def project(k, _):
        ctx = place.ctx
        first = jnp.where(ctx == 3, 2, ctx + 1)
        second = jnp.where(ctx == 0, 2, jnp.where(ctx == 1, 0, 1))
        third = jnp.where(ctx < 2, 3, 0)
        which = jnp.where(
            k == 0, ctx, jnp.where(k == 1, first, jnp.where(k == 2, second, third))
        )
        at = pl.ds(pl.multiple_of(which * block, 16), block)
        values = jnp.concatenate([r.tokens_all[i, at, :] for i in range(images)], axis=0)
        normed = normalize(values.astype(F32), gain_one, shift_one)[0].astype(BF16)
        lift = (times_transposed(normed, attend_low) * block_picks).astype(BF16)
        for i in range(images):
            r.lift_all[i, at, :] = lift[i * block : (i + 1) * block]
        for p in range(3):
            made = (matmul(normed, r.weights_all[p]) + matmul(lift, high(p))).astype(BF16)
            for i in range(images):
                r.joined[p, i, at, :] = made[i * block : (i + 1) * block]
        return 0

    def project_blocks(low, up):
        lax.fori_loop(low, up, project, 0)

    project_blocks(0, 1)
    tokens_chain.step(3)
    tokens_chain.landed(1)
    mixing.forward()
    project_blocks(1, 2)
    cotangents.start()
    tokens_chain.landed(2)
    project_blocks(2, 3)
    tokens_chain.landed(3)
    project_blocks(3, 4)

    def open_keys(i):
        return (
            jnp.concatenate(
                [
                    r.ctx_ints[n, i, LIVE_ROW : LIVE_ROW + 1, :]
                    for n in range(place.ctx_size)
                ],
                axis=1,
            )
            > 0
        )

    def rows_slot(i, dp, tp):
        at = pl.multiple_of(tp * half, 16)
        return r.rows_all.at[dp * images + i, pl.ds(at, half), :]

    expert_rows = []
    for i in range(images):
        r.keys_open[i : i + 1, :] = open_keys(i).astype(F32)
        token_rows = r.tokens_all[i, own, :].astype(F32)
        r.own_in[i] = normalize(token_rows, gain_one, shift_one)[0].astype(BF16)
        keys_open = r.keys_open[i : i + 1, :] > 0
        part = slice(i * half, (i + 1) * half)
        logs = []
        for j in range(HEADS // 2):
            at = slice(j * 2 * HD, (j + 1) * 2 * HD)
            q = stack_pair(r.joined[0, i, own, at], masks, scale)
            scores = times_transposed(q, r.joined[1, i, :, at])
            scores = jnp.where(keys_open, scores, MASKED)
            top = jnp.max(scores, axis=-1, keepdims=True)
            powers = jnp.exp(scores - top)
            total = jnp.sum(powers, axis=-1, keepdims=True)
            weights_att = (powers * (1.0 / total)).astype(BF16)
            mixed = join_pair(matmul(weights_att, r.joined[2, i, :, at]), masks)
            r.head_mix[part, at] = mixed.astype(BF16)
            log = jnp.maximum(top + jnp.log(total), -1e29)
            logs += [log[:half], log[half:]]
        r.logs[part, :] = put_lanes(logs, 128)
        if i == 0:
            mixing.diagonal()
            mixing.finish()
            need("mixing_low", "mixing_high")
            mixing_low = r.v_mixing_low[...].reshape(WIDTH, D)
            mixing_high = r.v_mixing_high[...].reshape(WIDTH, D)
        mix = r.head_mix[part, :]
        lift = (times_transposed(mix, mixing_low) * picks[i]).astype(BF16)
        r.mixing_lift[part, :] = lift
        hidden = token_rows + times_transposed(mix, r.mixing_all[...]) + matmul(lift, mixing_high)
        r.hidden[part, :] = hidden
        r.expert_in[i] = normalize(hidden, gain_two, shift_two)[0].astype(BF16)
        expert_rows.append(
            Spread(place, wire, r.expert_in.at[i], functools.partial(rows_slot, i), direct=True)
        )
        expert_rows[i].start()

    slots = experts * SLOTS
    cotangents.forward()
    cotangents.finish()
    numbers.finish()
    router.finish()
    need("router_low", "router_high")
    router_low = r.v_router_low[...].reshape(WIDTH, D)
    router_high = r.v_router_high[...].reshape(WIDTH, EXPERTS)
    r.router_t[...] = jnp.concatenate([r.router_all[n] for n in range(place.dp_size)], axis=1)

    def targets(given, k):
        route, slot = given[k : k + 1, :], given[TOP + k : TOP + k + 1, :]
        local = route - owned
        here = (local >= 0) & (local < experts) & (slot < CAP)
        return jnp.where(here, local * SLOTS + slot, -1)

    def fill_slots(i, target, values):
        at = pl.ds(pl.multiple_of(i * SLOTS, SLOTS), SLOTS)
        for n in range(experts):
            target[n, at, :] = values[n * SLOTS : (n + 1) * SLOTS]

    def make_table(i, _):
        given = r.ints_all[i]
        slot = lax.broadcasted_iota(jnp.int32, (slots, block), 0)
        hot = jnp.zeros((slots, block), F32)
        for k in range(TOP):
            hot = jnp.where(slot == targets(given, k), 1.0, hot)
        hot = hot.astype(BF16)
        r.table[i] = hot
        fill_slots(i, r.grad_slots, matmul(hot, r.cot_all[i]).astype(BF16))
        return 0

    lax.fori_loop(0, all_images, make_table, 0, unroll=4)
    for spread in expert_rows:
        spread.forward()
    for spread in expert_rows:
        spread.finish()

    def dispatch(i, _):
        values = r.rows_all[i]
        given = r.ints_all[i]
        set_column = lax.div(lax.broadcasted_iota(jnp.int32, (WIDTH, 1), 0), RANK)
        pick = (set_column == given[SET_ROW : SET_ROW + 1, 0:1]).astype(F32)
        lift = (times_transposed(router_low, values) * pick).astype(BF16)
        logits = times_transposed(r.router_t[...], values) + inner_rows(router_high, lift)
        powers = jnp.exp(logits - jnp.max(logits, axis=0, keepdims=True))
        probs = powers / jnp.sum(powers, axis=0, keepdims=True)
        expert = lax.broadcasted_iota(jnp.int32, (EXPERTS, block), 0)
        slot = lax.broadcasted_iota(jnp.int32, (slots, block), 0)
        gated = jnp.zeros((slots, block), F32)
        for k in range(TOP):
            gate = jnp.sum(
                jnp.where(expert == given[k : k + 1, :], probs, 0.0), axis=0, keepdims=True
            )
            gated = jnp.where(slot == targets(given, k), gate, gated)
        column = jnp.broadcast_to(jnp.sum(gated, axis=1, keepdims=True), (slots, 128))
        fill_slots(i, r.gates, column)
        fill_slots(i, r.rows_in, matmul(r.table[i], values).astype(BF16))
        lane = lax.div(lax.broadcasted_iota(jnp.int32, (SLOTS, WIDTH), 1), RANK)
        at = pl.ds(pl.multiple_of(i * SLOTS, SLOTS), SLOTS)
        r.slot_sets[at, :] = (lane == given[SET_ROW : SET_ROW + 1, 0:1]).astype(F32)
        return 0

    lax.fori_loop(0, all_images, dispatch, 0, unroll=8)

    chunks = [
        (
            r.first.at[e], r.first_got.at[e], r.first_final.at[e],
            functools.partial(lambda e, dp, tp: r.first_all.at[dp, tp, e], e),
        )
        for e in range(experts)
    ]
    chunks += [
        (r.second_sum, r.second_in, r.second_final, lambda dp, tp: r.second_all.at[dp, tp]),
        (r.early_sum, r.early_in, r.early_final, lambda dp, tp: r.early_all.at[dp, tp]),
        (r.late_sum, r.late_in, r.late_final, lambda dp, tp: r.late_all.at[dp, tp]),
    ]
    second_at, early_at, late_at = experts, experts + 1, experts + 2
    inner, outer = place.inner, 1 - place.inner
    to_partner, to_far = {"ctx": place.partner}, {"ctx": place.far_mid}
    flows, spreads = [], []
    for mine, got, final, slot in chunks:
        flows.append(
            dict(
                beside=wire.copy(mine.at[inner], got.at[0], to_partner),
                across=wire.copy(mine.at[outer], got.at[1], to_far),
                beyond=wire.copy(mine.at[outer], got.at[2], to_far),
                back=wire.copy(final.at[inner], final.at[inner], to_partner),
                share=wire.copy(final.at[inner], final.at[inner], to_far),
                away=wire.copy(final.at[inner], final.at[inner], {"ctx": place.far_end}),
            )
        )
        k = len(spreads)
        spreads.append(
            Spread(place, wire, final, slot, direct=k >= early_at, turn=k == second_at)
        )

    def offer(k):
        @pl.when(place.is_end)
        def _():
            flows[k]["beyond"].start()
            flows[k]["beside"].start()

        @pl.when(place.is_mid)
        def _():
            flows[k]["across"].start()

    def total_half(k):
        mine, got, final, slot = chunks[k]

        @pl.when(place.is_mid)
        def _():
            for name in ("beside", "across", "beyond"):
                flows[k][name].wait_recv()
            final[inner] = add_rounded(mine[inner], got[0], got[1], got[2])
            for name in ("away", "share", "back"):
                flows[k][name].start()

    def settle(k):
        @pl.when(place.is_mid)
        def _():
            flows[k]["share"].wait_recv()

        @pl.when(place.is_end)
        def _():
            flows[k]["back"].wait_recv()
            flows[k]["away"].wait_recv()

        spreads[k].start()

    stages = (
        total_half, settle, lambda k: spreads[k].forward(), lambda k: spreads[k].diagonal(),
    )
    reached = [0] * len(chunks)

    def go(k, stage):
        while reached[k] < stage:
            stages[reached[k]](k)
            reached[k] += 1

    def at_point(point):
        for chunk, stage in SCHEDULE[point]:
            if len(chunks) + chunk >= 0:
                go(len(chunks) + chunk, stage)

    def run_expert(e):
        need(("a_first", e), ("b_first", e), ("up", e))
        need(("a_second", e), ("b_second", e), ("down", e))
        a_first, b_first = r.v_first_a[e].reshape(WIDTH, D), r.v_first_b[e].reshape(WIDTH, -1)
        a_second = r.v_second_a[e].reshape(WIDTH, -1)
        b_second = r.v_second_b[e].reshape(WIDTH, D)
        sums = None
        size = min(EXPERT_ROWS, all_images * SLOTS)
        for c in range(all_images * SLOTS // size):
            at = slice(c * size, (c + 1) * size)
            rows = r.rows_in[e, at]
            grads = r.grad_slots[e, at].astype(F32)
            gate = r.gates[e, at][:, 0:1]
            sets = r.slot_sets[at]
            lifted = (times_transposed(rows, a_first) * sets).astype(BF16)
            before = matmul(rows, r.v_up[e]) + matmul(lifted, b_first)
            phi = 0.5 * (1.0 + lax.erf(before * SQRT_HALF))
            active = (before * phi).astype(BF16)
            slope = phi + before * (INV_ROOT_TWO_PI * jnp.exp(-0.5 * before * before))
            lowered = (times_transposed(active, a_second) * sets).astype(BF16)
            out = matmul(active, r.v_down[e]) + matmul(lowered, b_second)
            grad_out = (grads * gate).astype(BF16)
            grad_lowered = (times_transposed(grad_out, b_second) * sets).astype(BF16)
            grad_active = times_transposed(grad_out, r.v_down[e]) + matmul(grad_lowered, a_second)
            grad_before = (grad_active * slope).astype(BF16)
            grad_lifted = (times_transposed(grad_before, b_first) * sets).astype(BF16)
            grad_rows = times_transposed(grad_before, r.v_up[e]) + matmul(grad_lifted, a_first)
            made = [
                inner_rows(lifted, grad_before),
                inner_rows(grad_lowered, active),
                inner_rows(grad_lifted, rows),
                inner_rows(lowered, grad_out),
            ]
            sums = made if sums is None else [a + b for a, b in zip(sums, made)]
            lane = lax.broadcasted_iota(jnp.int32, (size, 128), 1)
            gate_grads = jnp.sum(out * grads, axis=1, keepdims=True)
            gate_grads = jnp.where(lane == owned + e, gate_grads, 0.0).astype(BF16)
            some = slice(c * size // SLOTS, (c + 1) * size // SLOTS)
            to = slice(e * SLOTS, (e + 1) * SLOTS)
            number = size // SLOTS
            r.payload[some, to, 0:D] = grad_rows.astype(BF16).reshape(number, SLOTS, D)
            r.payload[some, to, D:CRITICAL] = gate_grads.reshape(number, SLOTS, 128)
            r.payload[some, to, CRITICAL:] = (out * gate).astype(BF16).reshape(number, SLOTS, D)
        r.first[e, 0] = sums[0].astype(BF16)
        r.first[e, 1] = sums[1].astype(BF16)
        share = D // place.tp_size
        for number in range(2):
            for t in range(place.tp_size):
                r.second[t, number, e] = sums[2 + number][:, t * share : (t + 1) * share].astype(
                    BF16
                )

    for e in range(experts):
        run_expert(e)
        offer(e)
        if e == experts - 2:
            at_point(0)
    at_point(1)

    second_swap = wire.copy(
        r.second.at[place.other_tp], r.second_got, {"tp": place.other_tp}
    )
    second_swap.start()
    first_lanes, other_lanes = slice(0, CRITICAL), slice(CRITICAL, CRITICAL + D)
    swaps = [
        wire.copy(
            r.partial.at[1 - place.core, :, :, :, at],
            r.from_sibling.at[:, :, :, at],
            {"dp": place.sibling},
        )
        for at in (first_lanes, other_lanes)
    ]

    def combine(core, at):
        def run(chip, _):
            for n in range(images):
                i = (chip * 2 + core) * images + n
                made = inner_rows(r.table[i], r.payload[i, :, at]).astype(BF16)
                for t in range(place.tp_size):
                    r.partial[core, chip, t, n * half : (n + 1) * half, at] = made[
                        t * half : (t + 1) * half
                    ]
            return 0

        lax.fori_loop(0, place.chips, run, 0, unroll=2)

    def send_back(at):
        copies = []
        for i, j in place.offsets() + [(0, 0)]:
            dp, tp = place.ahead(i, j)
            chip = lax.div(dp, 2)
            index = i * place.tp_size + j
            both = add_rounded(
                r.partial[place.core, chip, tp, :, at], r.from_sibling[chip, tp, :, at]
            )
            if index:
                r.from_sibling[chip, tp, :, at] = both
                copy = wire.copy(
                    r.from_sibling.at[chip, tp, :, at],
                    r.received.at[index, :, at],
                    {"dp": dp, "tp": tp},
                )
                copy.start()
                copies.append(copy)
            else:
                r.received[0, :, at] = both
        return copies

    combine(1 - place.core, first_lanes)
    swaps[0].start()
    combine(place.core, first_lanes)
    at_point(2)
    swaps[0].wait_recv()
    returns = [send_back(first_lanes)]
    combine(1 - place.core, other_lanes)
    swaps[1].start()
    combine(place.core, other_lanes)
    second_swap.wait()
    r.second_sum[...] = add_rounded(r.second[place.tp], r.second_got[...])
    offer(second_at)
    swaps[1].wait_recv()
    returns.append(send_back(other_lanes))
    late_sends = swaps + returns[0] + returns[1]
    at_point(3)
    for copy in returns[0]:
        copy.wait_recv()

    def live_column(i):
        lane = lax.broadcasted_iota(jnp.int32, (half, block), 1)
        row = lax.broadcasted_iota(jnp.int32, (half, block), 0) + place.tp * half
        live = r.ints[i, LIVE_ROW : LIVE_ROW + 1, :].astype(F32)
        return jnp.sum(jnp.where(lane == row, live, 0.0), axis=1, keepdims=True)

    lives = [live_column(i) for i in range(images)]
    total = r.received[0, :, :CRITICAL].astype(F32)
    for k in range(1, r.received.shape[0]):
        total = total + r.received[k, :, :CRITICAL].astype(F32)
    hidden = r.hidden[...]
    grad_probs = total[:, D : D + EXPERTS]
    grad_output = jnp.concatenate(
        [
            r.cot_all[place.dp * images + i, pl.ds(start, half), :].astype(F32) * lives[i]
            for i in range(images)
        ],
        axis=0,
    )
    rows = r.expert_in[...].reshape(count, D)
    router_lift = (times_transposed(rows, router_low) * own_sets).astype(BF16)
    logits = times_transposed(rows, r.router_t[...]) + matmul(router_lift, router_high)
    powers = jnp.exp(logits - jnp.max(logits, axis=-1, keepdims=True))
    gate_probs = powers / jnp.sum(powers, axis=-1, keepdims=True)
    grad_logits = (
        gate_probs * (grad_probs - jnp.sum(grad_probs * gate_probs, axis=-1, keepdims=True))
    ).astype(BF16)
    grad_router_lift = (times_transposed(grad_logits, router_high) * own_sets).astype(BF16)
    grad_expert_in = (
        total[:, :D] + matmul(grad_logits, r.router_t[...]) + matmul(grad_router_lift, router_low)
    )
    _, unit, factor = normalize(hidden, gain_two, shift_two)
    grad_rows = grad_output + normalize_back(grad_expert_in, unit, factor, gain_two)
    r.grad_hidden[...] = grad_rows
    grad_attended = grad_rows.astype(BF16)
    grad_mixing_lift = (times_transposed(grad_attended, mixing_high) * own_sets).astype(BF16)
    grad_heads = (
        matmul(grad_attended, r.mixing_all[...]) + matmul(grad_mixing_lift, mixing_low)
    ).astype(BF16)
    r.heads[...] = grad_heads.reshape(images, half, D)
    mix = r.head_mix[...]
    lane = lax.broadcasted_iota(jnp.int32, (D, 128), 1)
    head = lax.div(lax.broadcasted_iota(jnp.int32, (D, 128), 0), HD)
    ones = (lane == head).astype(F32).astype(BF16)
    delta_rows = split_sum(grad_heads.astype(F32) * mix.astype(F32), ones)
    r.delta[...] = delta_rows
    log_rows = r.logs[...]
    for i in range(images):
        part = slice(i * half, (i + 1) * half)
        pad = jnp.zeros((128 - half, 128), F32)
        turned = [
            jnp.concatenate([v[part], pad], axis=0).T[:HEADS] for v in (log_rows, delta_rows)
        ]
        row = 0
        for rest, number in zip(turned, (3, 2)):
            for _ in range(number):
                top = rest.astype(BF16)
                r.stats[i, row : row + HEADS, :] = top
                rest = rest - top.astype(F32)
                row += HEADS

    def heads_slot(i, ctx, tp):
        at = pl.multiple_of((ctx * place.tp_size + tp) * half, 16)
        return r.heads_all.at[i, pl.ds(at, half), :]

    chain = Chain(
        place, wire, [r.heads.at[i] for i in range(images)] + [r.stats],
        [functools.partial(heads_slot, i) for i in range(images)]
        + [lambda ctx, tp: r.stats_all.at[ctx * place.tp_size + tp]],
        [True] * (images + 1), True,
    )
    chain.start()

    def spread_start(values, got):
        rows = got.shape[1]
        copies = []
        for k, (dp, tp) in enumerate(place.peers):
            at = pl.ds(pl.multiple_of((dp * place.tp_size + tp) * rows, 16), rows)
            copy = wire.copy(values.at[at], got.at[k], {"dp": dp, "tp": tp})
            copy.start()
            copies.append(copy)
        return copies

    def spread_end(copies, values, got, total):
        rows = got.shape[1]
        for copy in copies:
            copy.wait()
        added = values[pl.ds(pl.multiple_of(place.me * rows, 16), rows), :].astype(F32)
        for k in range(plane - 1):
            added = added + got[k].astype(F32)
        total[...] = added.astype(BF16).reshape(total.shape)

    def put_tiles(target, products):
        tile = 0
        for product in products:
            for n in range(product.shape[1] // 128):
                target[tile * WIDTH : (tile + 1) * WIDTH, :] = product[
                    :, n * 128 : (n + 1) * 128
                ].astype(BF16)
                tile += 1
        if tile * WIDTH < target.shape[0]:
            target[tile * WIDTH :, :] = jnp.zeros(
                (target.shape[0] - tile * WIDTH, 128), BF16
            )

    wide_logits = jnp.concatenate(
        [grad_logits, jnp.zeros((count, 128 - EXPERTS), BF16)], axis=1
    )
    put_tiles(
        r.early,
        (
            inner_rows(grad_mixing_lift, mix),
            inner_rows(r.mixing_lift[...], grad_attended),
            inner_rows(grad_router_lift, rows),
            inner_rows(router_lift, wide_logits),
        ),
    )
    early_spread = spread_start(r.early, r.early_got)
    at_point(4)
    chain.step(1)
    at_point(5)
    chain.step(2)
    at_point(6)
    chain.step(3)
    spread_end(early_spread, r.early, r.early_got, r.early_sum)
    offer(early_at)
    at_point(7)
    chain.finish_own()
    for s in range(1, chain.steps + 1):
        chain.landed(s)

    def to_other(values, gathered):
        spot = gathered.at[:, pl.ds(start, half), :]
        copies = [wire.copy(values, spot, {"tp": place.other_tp}), wire.near(values, spot)]
        for copy in copies:
            copy.start()
        return copies

    for copy in returns[1]:
        copy.wait_recv()
    total = r.hidden[...]
    for k in range(r.received.shape[0]):
        total = total + r.received[k, :, CRITICAL:].astype(F32)
    r.out_own[...] = total.astype(BF16).reshape(images, half, D)
    layer_out = to_other(r.out_own, r.out_all)

    def heads_back(i, j):
        part = slice(i * half, (i + 1) * half)
        at = slice(j * 2 * HD, (j + 1) * 2 * HD)
        keys_open = r.keys_open[i : i + 1, :] > 0
        own_open = jnp.concatenate([lives[i], lives[i]], axis=0) > 0
        found = jnp.concatenate(
            [r.stats_all[n, i][:, :half].astype(F32) for n in range(r.stats_all.shape[0])], axis=1
        )
        log_t = found[0:HEADS] + found[HEADS : 2 * HEADS] + found[2 * HEADS : 3 * HEADS]
        delta_t = found[3 * HEADS : 4 * HEADS] + found[4 * HEADS :]
        q_all, k_all, v_all = (r.joined[p, i, :, at] for p in range(3))
        g_all = r.heads_all[i, :, at]

        def column(values):
            return jnp.concatenate(
                [values[:, 2 * j : 2 * j + 1], values[:, 2 * j + 1 : 2 * j + 2]], axis=0
            )

        def across(values):
            return jnp.concatenate(
                [
                    jnp.broadcast_to(values[2 * j + n : 2 * j + n + 1, :], (half, values.shape[1]))
                    for n in range(2)
                ],
                axis=0,
            )

        q = stack_pair(r.joined[0, i, own, at], masks, scale)
        g = stack_pair(r.heads[i, :, at], masks)
        scores = jnp.where(keys_open, times_transposed(q, k_all), MASKED)
        probs = jnp.exp(scores - column(r.logs[part]))
        grad_probs_att = times_transposed(g, v_all)
        grad_scores = (probs * (grad_probs_att - column(r.delta[part]))).astype(BF16)
        r.grads[0, part, at] = (join_pair(matmul(grad_scores, k_all), masks) * scale).astype(BF16)
        k = stack_pair(r.joined[1, i, own, at], masks, scale)
        v = stack_pair(r.joined[2, i, own, at], masks)
        scores = jnp.where(own_open, times_transposed(k, q_all), MASKED)
        probs = jnp.exp(scores - across(log_t))
        grad_probs_att = times_transposed(v, g_all)
        grad_scores = (probs * (grad_probs_att - across(delta_t))).astype(BF16)
        r.grads[1, part, at] = (join_pair(matmul(grad_scores, q_all), masks) * scale).astype(BF16)
        r.grads[2, part, at] = join_pair(matmul(probs.astype(BF16), g_all), masks).astype(BF16)

    for i in range(images):
        for j in range(HEADS // 2):
            heads_back(i, j)
            if j % 2:
                at_point(8 + 2 * i + j // 2)
    lift = times_transposed(r.grads[0], high(0))
    into = times_transposed(r.grads[0], r.weights_all[0])
    for p in range(1, 3):
        lift = lift + times_transposed(r.grads[p], high(p))
        into = into + times_transposed(r.grads[p], r.weights_all[p])
    lift = (lift * own_sets).astype(BF16)
    lift_in = jnp.concatenate([r.lift_all[i, own, :] for i in range(images)], axis=0)
    put_tiles(
        r.late,
        [inner_rows(lift_in, r.grads[p]) for p in range(3)]
        + [inner_rows(lift, r.own_in[...].reshape(count, D))],
    )
    late_spread = spread_start(r.late, r.late_got)
    at_point(12)
    into = into + matmul(lift, attend_low)
    flat = jnp.concatenate([r.tokens_all[i, own, :] for i in range(images)], axis=0).astype(F32)
    _, unit, factor = normalize(flat, gain_one, shift_one)
    result = r.grad_hidden[...] + normalize_back(into, unit, factor, gain_one)
    r.grad_own[...] = result.astype(BF16).reshape(images, half, D)
    at_point(13)
    tokens_out = to_other(r.grad_own, r.grad_all)
    spread_end(late_spread, r.late, r.late_got, r.late_sum)
    offer(late_at)
    at_point(14)
    for k in range(len(chunks)):
        go(k, DONE)

    @pl.when(place.is_end)
    def _():
        for flow in flows:
            flow["beyond"].wait_send()
            flow["beside"].wait_send()

    @pl.when(place.is_mid)
    def _():
        for flow in flows:
            for name in ("across", "away", "share", "back"):
                flow[name].wait_send()

    for spread in spreads:
        spread.finish()
    for spread in [weights, mixing, numbers, router, cotangents] + expert_rows + spreads:
        spread.drain()
    tokens_chain.drain()
    chain.drain()
    for copy in late_sends:
        copy.wait_send()
    for copy in layer_out + tokens_out:
        copy.wait()
    assert not pending


def run_layer(sizes, **inputs):
    dp, ctx, tp = sizes
    assert ctx == 4 and tp == 2
    plane, chips = dp * tp, dp // 2
    images, block = inputs["tokens"].shape[:2]
    assert images == 2
    half = block // tp
    count, seq, all_images = images * half, ctx * block, dp * images
    experts, _, hidden = inputs["up_weight"].shape
    rows, lanes = inputs["mixing"].shape
    slots = experts * SLOTS
    sent = CRITICAL + D
    early_rows = small_rows(3 * (D // 128) + 1, plane)
    late_rows = small_rows(4 * (D // 128), plane)
    second = (2, experts, WIDTH, D // tp)
    full = dict(
        first=(experts, 2, WIDTH, hidden),
        second=second,
        early=(2, early_rows // 2, 128),
        late=(2, late_rows // 2, 128),
    )
    cut = {name: shape[1:] for name, shape in full.items()}
    cut["first"] = (experts, WIDTH, hidden)
    outputs = {name + "_all": (dp, tp) + shape for name, shape in full.items()}
    outputs.update(out_all=(images, block, D), grad_all=(images, block, D))
    narrow = dict(
        tokens_all=(images, seq, D),
        weights_all=(3, dp * rows, tp * lanes),
        mixing_all=(dp * rows, tp * lanes),
        router_all=(dp,) + inputs["router"].shape,
        router_t=(EXPERTS, D),
        cot_all=(all_images, block, D),
        rows_all=(all_images, block, D),
        v_attend_low=(SETS, RANK, D),
        v_attend_high=(SETS, 3, RANK, D),
        v_mixing_low=(SETS, RANK, D),
        v_mixing_high=(SETS, RANK, D),
        v_router_low=(SETS, RANK, D),
        v_router_high=(SETS, RANK, EXPERTS),
        v_first_a=(experts, SETS, RANK, D),
        v_first_b=(experts, SETS, RANK, hidden),
        v_second_a=(experts, SETS, RANK, hidden),
        v_second_b=(experts, SETS, RANK, D),
        v_up=(experts, D, hidden),
        v_down=(experts, hidden, D),
        lift_all=(images, seq, WIDTH),
        joined=(3, images, seq, D),
        own_in=(images, half, D),
        head_mix=(count, D),
        mixing_lift=(count, WIDTH),
        expert_in=(images, half, D),
        table=(all_images, slots, block),
        grad_slots=(experts, all_images * SLOTS, D),
        rows_in=(experts, all_images * SLOTS, D),
        payload=(all_images, slots, sent),
        partial=(2, chips, tp, count, sent),
        from_sibling=(chips, tp, count, sent),
        received=(chips * tp, count, sent),
        first=full["first"],
        second=(tp,) + second,
        second_got=second,
        second_sum=second,
        early=(plane * early_rows, 128),
        late=(plane * late_rows, 128),
        early_got=(plane - 1, early_rows, 128),
        late_got=(plane - 1, late_rows, 128),
        early_sum=full["early"],
        late_sum=full["late"],
        heads=(images, half, D),
        stats=(images, 5 * HEADS, 128),
        heads_all=(images, seq, D),
        stats_all=(ctx * tp, images, 5 * HEADS, 128),
        grads=(3, count, D),
        out_own=(images, half, D),
        grad_own=(images, half, D),
    )
    for name in full:
        narrow[name + "_final"] = full[name]
        narrow[name + "_in"] = (3,) + cut[name]
    narrow["first_got"] = (experts, 3, WIDTH, hidden)
    del narrow["first_in"]
    wide = dict(
        logs=(count, 128),
        delta=(count, 128),
        hidden=(count, D),
        grad_hidden=(count, D),
        gates=(experts, all_images * SLOTS, 128),
        slot_sets=(all_images * SLOTS, WIDTH),
        keys_open=(images, seq),
    )
    integers = dict(
        ints=(images, 8, block),
        ints_all=(all_images, 8, block),
        ctx_ints=(ctx, images, 8, block),
    )
    scratch = {}
    for shapes, dtype in ((narrow, BF16), (wide, F32), (integers, jnp.int32)):
        for name, shape in shapes.items():
            scratch[name] = pltpu.VMEM(shape, dtype)
    chunks = experts + 3
    remote = (
        2 * Chain.remote(ctx, images + 1)
        + (2 + images + chunks) * Spread.remote(sizes)
        + 3 * Spread.remote(sizes, False)
        + 6 * chunks
        + 3
        + 2 * (chips * tp - 1)
        + 2 * (plane - 1)
        + 2
    )
    scratch["send"] = pltpu.SemaphoreType.DMA((remote,))
    scratch["recv"] = pltpu.SemaphoreType.DMA((remote,))
    scratch["local"] = pltpu.SemaphoreType.DMA((7 + 6 * experts + 5 + images + chunks + images + 1 + 2,))
    kinds = dict(
        adapter_set=IN_SMEM, image_mask=IN_SMEM, routes_t=IN_VMEM, slots_t=IN_VMEM,
        token_mask=IN_VMEM, first_gain=IN_VMEM, first_shift=IN_VMEM, second_gain=IN_VMEM,
        second_shift=IN_VMEM,
    )
    names = tuple(inputs) + tuple(outputs) + tuple(scratch)
    made = pl.pallas_call(
        functools.partial(layer_kernel, sizes, names),
        out_shape=tuple(jax.ShapeDtypeStruct(shape, BF16) for shape in outputs.values()),
        in_specs=[kinds.get(name, ANY) for name in inputs],
        out_specs=(ANY,) * len(outputs),
        scratch_shapes=tuple(scratch.values()),
        compiler_params=pltpu.CompilerParams(
            collective_id=0, has_side_effects=True, vmem_limit_bytes=62 << 20
        ),
    )(*inputs.values())
    return dict(zip(outputs, made))


def assemble_kernel(
    first, second, early, late, out_in, grad_in,
    up, down_t, narrow_t, narrow, attend_down, attend_up, mixing_down, mixing_up, router_down,
    router_up, out, grad,
):
    lanes, part = first.shape[-1], second.shape[-1]
    for n in range(first.shape[2]):
        for tp in range(first.shape[1]):
            for half, target in ((0, up), (1, down_t)):
                target[:, n, :, tp * lanes : (tp + 1) * lanes] = (
                    first[0, tp, n, half].astype(F32).reshape(SETS, RANK, lanes)
                )
            for half, target in ((0, narrow_t), (1, narrow)):
                target[:, n, :, tp * part : (tp + 1) * part] = (
                    second[0, tp, half, n].astype(F32).reshape(SETS, RANK, part)
                )

    @pl.when(pl.program_id(0) == 0)
    def _():
        def tile(small, k):
            return small[k * WIDTH : (k + 1) * WIDTH, :].astype(F32).reshape(SETS, RANK, 128)

        count = D // 128
        for p in range(3):
            for k in range(count):
                attend_up[:, p, :, k * 128 : (k + 1) * 128] = tile(late, p * count + k)
        for k in range(count):
            attend_down[:, :, k * 128 : (k + 1) * 128] = tile(late, 3 * count + k)
        for p, target in enumerate((mixing_down, mixing_up, router_down)):
            for k in range(count):
                target[:, :, k * 128 : (k + 1) * 128] = tile(early, p * count + k)
        router_up[...] = tile(early, 3 * count)[:, :, :EXPERTS]
        out[...] = out_in[...]
        grad[...] = grad_in[...]


def assemble(first, second, early, late, out, grad):
    dp, tp, experts, _, width, lanes = first.shape
    part = second.shape[-1]
    group = min(experts, ASSEMBLED)
    groups = experts // group

    def split(e):
        return lax.div(e, groups), lax.rem(e, groups)

    def expert_out(size):
        return (
            jax.ShapeDtypeStruct((SETS, EXPERTS, RANK, size), F32),
            pl.BlockSpec((SETS, group, RANK, size), lambda e: (0, e, 0, 0)),
        )

    def whole_out(*shape):
        return (
            jax.ShapeDtypeStruct(shape, F32),
            pl.BlockSpec(shape, lambda e: (0,) * len(shape)),
        )

    outs = (
        [expert_out(FF)] * 2
        + [expert_out(D)] * 2
        + [whole_out(SETS, RANK, D), whole_out(SETS, 3, RANK, D)]
        + [whole_out(SETS, RANK, D)] * 3
        + [whole_out(SETS, RANK, EXPERTS)]
        + [(jax.ShapeDtypeStruct(out.shape, BF16), pl.BlockSpec(out.shape, lambda e: (0, 0, 0)))] * 2
    )
    return pl.pallas_call(
        assemble_kernel,
        grid=(EXPERTS // group,),
        out_shape=[out[0] for out in outs],
        in_specs=[
            pl.BlockSpec(
                (1, tp, group, 2, width, lanes), lambda e: (split(e)[0], 0, split(e)[1], 0, 0, 0)
            ),
            pl.BlockSpec(
                (1, tp, 2, group, width, part), lambda e: (split(e)[0], 0, 0, split(e)[1], 0, 0)
            ),
            pl.BlockSpec(early.shape, lambda e: (0, 0)),
            pl.BlockSpec(late.shape, lambda e: (0, 0)),
            pl.BlockSpec(out.shape, lambda e: (0, 0, 0)),
            pl.BlockSpec(grad.shape, lambda e: (0, 0, 0)),
        ],
        out_specs=[out[1] for out in outs],
        compiler_params=pltpu.CompilerParams(vmem_limit_bytes=60 << 20),
    )(first, second, early, late, out, grad)


def per_device(
    sizes,
    tokens,
    cotangent,
    routes,
    slot_index,
    token_mask,
    image_mask,
    adapter_set,
    first_gain,
    first_shift,
    second_gain,
    second_shift,
    attend_weight,
    mixing_weight,
    router_weight,
    expand_weight,
    shrink_weight,
    attend_down,
    attend_up,
    mixing_down,
    mixing_up,
    router_down,
    router_up,
    expand_down,
    expand_up,
    shrink_down,
    shrink_up,
):
    def flipped(values):
        return jnp.swapaxes(values, -1, -2)

    made = run_layer(
        sizes,
        tokens=tokens,
        cotangent=cotangent,
        weights=jnp.transpose(attend_weight, (1, 0, 2)),
        mixing=mixing_weight,
        router=flipped(router_weight),
        routes_t=flipped(routes),
        slots_t=flipped(slot_index),
        token_mask=token_mask,
        image_mask=image_mask,
        adapter_set=adapter_set,
        first_gain=first_gain.reshape(1, D),
        first_shift=first_shift.reshape(1, D),
        second_gain=second_gain.reshape(1, D),
        second_shift=second_shift.reshape(1, D),
        up_weight=expand_weight,
        down_weight=shrink_weight,
        attend_low=flipped(attend_down),
        attend_high=jnp.transpose(attend_up, (0, 2, 1, 3)),
        mixing_low=flipped(mixing_down),
        mixing_high=mixing_up,
        router_low=flipped(router_down),
        router_high=router_up,
        first_a=flipped(expand_down),
        first_b=expand_up,
        second_a=flipped(shrink_down),
        second_b=shrink_up,
    )
    wide = assemble(
        made["first_all"],
        made["second_all"],
        made["early_all"].reshape(-1, 128),
        made["late_all"].reshape(-1, 128),
        made["out_all"],
        made["grad_all"],
    )
    return (
        wide[10],
        wide[11],
        flipped(wide[4]),
        jnp.transpose(wide[5], (0, 2, 1, 3)),
        flipped(wide[6]),
        wide[7],
        flipped(wide[8]),
        wide[9],
        flipped(wide[2]),
        wide[0],
        flipped(wide[1]),
        wide[3],
    )


def solution(mesh):
    sizes = (mesh.shape["dp"], mesh.shape["ctx"], mesh.shape["tp"])
    tokens_spec = P("dp", "ctx", None)
    in_specs = (
        (tokens_spec,) * 4
        + (P("dp", "ctx"), P("dp"), P("dp"))
        + (P(),) * 4
        + (P("dp", None, "tp"), P("dp", "tp"), P("dp", None))
        + (P("dp", None, "tp"), P("dp", "tp", None))
        + (P(),) * 10
    )
    out_specs = (tokens_spec,) * 2 + (P(),) * 10
    return jax.shard_map(
        functools.partial(per_device, sizes),
        mesh=mesh,
        in_specs=in_specs,
        out_specs=out_specs,
        check_vma=False,
    )
```
